32 devices in a mesh: dp: 8 (over z, y), mp: 4 (over x, core).
Axes of the slice: x: 2, y: 2, z: 4, core: 2. Of those that a mesh axis runs over, the one named last changes fastest.
Arguments:
- hidden_in: bfloat16 [16384, 768], P('dp'), may hold values from -6 to 6
- cotangent: bfloat16 [16384, 768], P('dp'), may hold values from -6 to 6
- w_query: bfloat16 [768, 768], P('dp', 'mp'), may hold values from -0.3125 to 0.3125
- w_key: bfloat16 [768, 768], P('dp', 'mp'), may hold values from -0.21875 to 0.21875
- w_value: bfloat16 [768, 768], P('dp', 'mp'), may hold values from -0.21875 to 0.21875
- w_output: bfloat16 [768, 768], P('mp', 'dp'), may hold values from -0.4375 to 0.4375
- w_inner: bfloat16 [768, 3072], P('dp', 'mp'), may hold values from -0.21875 to 0.21875
- w_outer: bfloat16 [3072, 768], P('mp', 'dp'), may hold values from -0.109375 to 0.109375
- biases: bfloat16 [4, 768], P(None, 'dp'), may hold values from -3 to 3
- gains: bfloat16 [2, 768], P(None, 'dp'), may hold values from 0.5 to 1.5
- shifts: bfloat16 [2, 768], P(None, 'dp'), may hold values from -2 to 2
- inner_bias: bfloat16 [3072], P('dp'), may hold values from -3 to 3
- lengths: int32 [10], replicated, may hold values from 1024 to 2048, as said below
- padding: int32 [16384], P('dp'), may hold values from 0 to 1, as said below
- cluster_perm: int32 [12, 16384], P('mp', 'dp'), may hold values from 0 to 16383, as said below
Outputs:
- hidden_out: bfloat16 [16384, 768], P('dp')
- grad_hidden: bfloat16 [16384, 768], P('dp')
- grad_query: float32 [768, 768], P('dp', 'mp')
- grad_key: float32 [768, 768], P('dp', 'mp')
- grad_value: float32 [768, 768], P('dp', 'mp')
- grad_output: float32 [768, 768], P('mp', 'dp')
- grad_inner: float32 [768, 3072], P('dp', 'mp')
- grad_outer: float32 [3072, 768], P('mp', 'dp')
- grad_biases: float32 [4, 768], P(None, 'dp')
- grad_gains: float32 [2, 768], P(None, 'dp')
- grad_shifts: float32 [2, 768], P(None, 'dp')
- grad_inner_bias: float32 [3072], P('dp')
The draws below stay inside these ranges and needn't reach their ends.
Inputs may be any that keep to these rules, and one draw needn't show every extreme that they name: In each run of 8 indices of dp, 10 lengths that, each rounded up to a multiple of 128, sum to 16384; in each run one of them is exactly 2048. `padding`: A row that is the p-th of its document's rows on its device, on index d of dp, is 1 exactly when p * 8 + (d mod 8) is under the document's length. `cluster_perm`: for each head a permutation of the token numbers; each cluster holds tokens of one document only, 16 from each device of its run; of the tokens held by one index of dp, exactly 256 have slots among those of each index r of dp (slots r * 2048 to (r + 1) * 2048 - 1).
All inputs are finite; a program needn't handle non-finite values.
Results may differ from the reference program's by a relative error of at most 0.015.
Values may be sent and summed in bfloat16 or wider, within the bound.
No kernel may reach another device: no remote copies, remote signals or barrier semaphores. Data moves between devices by JAX's collectives and lax.ppermute only.
A program may use at most 128 MiB of HBM per device.

```python
import math
import jax
import jax.numpy as jnp
from jax import lax

D = 768
HEADS = 12
HEAD_DIM = 64
FF = 3072
CLUSTER = 128
DOC_LEAST = 1024
TOK_DEV = 2048
TOKENS = 16384
STRIPE = 8
DOCS_GROUP = 10
N_DP = 8


def run_lengths(key):
    least_units = DOC_LEAST // CLUSTER
    run_units = STRIPE * TOK_DEV // CLUSTER
    spare_units = run_units - (DOCS_GROUP + 1) * least_units
    free_spots = (DOCS_GROUP - 1) * least_units
    key_pick, key_roll, key_pad = jax.random.split(key, 3)
    chosen = (jax.random.permutation(key_pick, free_spots) < spare_units).astype(jnp.int32)
    extra_units = jnp.sum(chosen.reshape(DOCS_GROUP - 1, least_units), axis=1)
    doc_units = jnp.concatenate([jnp.full((1,), 2 * least_units, jnp.int32), least_units + extra_units])
    doc_units = jnp.roll(doc_units, jax.random.randint(key_roll, (), 0, DOCS_GROUP))
    pad_cut = jax.random.randint(key_pad, (DOCS_GROUP,), 0, CLUSTER)
    pad_cut = jnp.where((doc_units > least_units) & (doc_units < 2 * least_units), pad_cut, 0)
    return (doc_units * CLUSTER - pad_cut).astype(jnp.int32)


def doc_lengths(key):
    run_count = TOKENS // TOK_DEV // STRIPE
    return jax.vmap(run_lengths)(jax.random.split(key, run_count)).reshape(-1)


def row_layout(lengths):
    run_count = TOKENS // TOK_DEV // STRIPE
    padded = (lengths + CLUSTER - 1) // CLUSTER * CLUSTER
    local_rows = (padded // STRIPE).reshape(run_count, DOCS_GROUP)
    local_ends = jnp.cumsum(local_rows, axis=1)
    local_starts = local_ends - local_rows
    row_place = jnp.arange(TOK_DEV)
    doc_local = jnp.sum((row_place[None, :, None] >= local_ends[:, None, :]).astype(jnp.int32), axis=2)
    start_row = jnp.take_along_axis(local_starts, doc_local, axis=1)
    doc_length = jnp.take_along_axis(lengths.reshape(run_count, DOCS_GROUP), doc_local, axis=1)
    return (doc_local, start_row, doc_length)


def draw_lengths(key, part):
    return doc_lengths(jax.random.fold_in(key, 11))


def draw_padding(key, part):
    lengths = doc_lengths(jax.random.fold_in(key, 11))
    devices = TOKENS // TOK_DEV
    doc_local, start_row, doc_length = row_layout(lengths)
    device_run = jnp.arange(devices) // STRIPE
    row_place = jnp.arange(TOK_DEV)[None, :]
    doc_place = (row_place - start_row[device_run]) * STRIPE + (jnp.arange(devices) % STRIPE)[:, None]
    return (doc_place < doc_length[device_run]).astype(jnp.int32).reshape(TOKENS)


def draw_cluster_perm(key, part):
    lengths = doc_lengths(jax.random.fold_in(key, 11))
    devices = TOKENS // TOK_DEV
    run_count = devices // STRIPE
    per_device = CLUSTER // STRIPE
    run_clusters = STRIPE * TOK_DEV // CLUSTER
    quota = run_clusters // devices
    doc_local, start_row, doc_length = row_layout(lengths)
    device_run = jnp.arange(devices) // STRIPE
    doc_dev = doc_local[device_run]
    start_dev = start_row[device_run]
    key_rank, key_run, key_owner = jax.random.split(jax.random.fold_in(key, 23), 3)
    rank_order = jax.vmap(lambda subkey: jax.random.permutation(subkey, TOK_DEV))(jax.random.split(key_rank, HEADS * devices)).reshape(HEADS, devices, TOK_DEV)
    score = doc_dev[None] * TOK_DEV + rank_order
    order = jnp.argsort(score, axis=2)
    inverse = jnp.argsort(order, axis=2)
    within_doc = inverse - start_dev[None]
    cluster_run = start_dev[None] * STRIPE // CLUSTER + within_doc // per_device
    inner_slot = (jnp.arange(devices) % STRIPE)[None, :, None] * per_device + within_doc % per_device
    run_perm = jax.vmap(lambda subkey: jax.random.permutation(subkey, run_clusters))(jax.random.split(key_run, HEADS * run_count)).reshape(HEADS, run_count, run_clusters)
    head_index = jnp.arange(HEADS)[:, None, None]
    dealt = run_perm[head_index, device_run[None, :, None], cluster_run]
    owner = dealt // quota
    turn = dealt % quota
    owner_order = jax.vmap(lambda subkey: jax.random.permutation(subkey, TOK_DEV // CLUSTER))(jax.random.split(key_owner, HEADS * devices)).reshape(HEADS, devices, TOK_DEV // CLUSTER)
    position = owner_order[head_index, owner, device_run[None, :, None] * quota + turn]
    return (owner * TOK_DEV + position * CLUSTER + inner_slot).reshape(HEADS, TOKENS).astype(jnp.int32)


def steps_of(rng, shape, pieces, smallest, largest):
    def one(axis_at, shards_of):
        heights = jax.random.uniform(jax.random.fold_in(jax.random.fold_in(rng, 6), axis_at), (shards_of,), jnp.float32, smallest / len(pieces), largest / len(pieces))
        return jnp.repeat(jnp.exp(heights), shape[axis_at] // shards_of).reshape((-1,) + (1,) * (len(shape) - axis_at - 1))

    level = one(*pieces[0])
    for cut in pieces[1:]:
        level = level * one(*cut)
    return level


def noise(stream_key, dims, width, bound, pieces=(), held_as=jnp.bfloat16):
    loudness = steps_of(stream_key, dims, pieces, -0.22, 0.18) if pieces else 1.0
    values = jax.random.normal(stream_key, dims, jnp.float32) * width * loudness
    return jnp.minimum(jnp.maximum(values, -bound), bound).astype(held_as)


def setup_inputs(seed: int = 0) -> dict:
    key_of = jax.random.split(jax.random.key(seed), 16)
    hidden_in = noise(key_of[0], (TOKENS, D), 1.0, 6.0, ((0, 8),))
    cotangent = noise(key_of[1], (TOKENS, D), 1.0, 6.0, ((0, 8),))
    w_query = noise(key_of[2], (D, D), (D // 2) ** -0.5, 0.3125, ((0, 8), (1, 4)))
    w_key = noise(key_of[3], (D, D), D ** -0.5, 0.21875, ((0, 8), (1, 4)))
    w_value = noise(key_of[4], (D, D), D ** -0.5, 0.21875, ((0, 8), (1, 4)))
    w_output = noise(key_of[5], (D, D), (D // 4) ** -0.5, 0.4375, ((0, 4), (1, 8)))
    w_inner = noise(key_of[6], (D, FF), D ** -0.5, 0.21875, ((0, 8), (1, 4)))
    w_outer = noise(key_of[7], (FF, D), FF ** -0.5, 0.109375, ((0, 4), (1, 8)))
    biases = noise(key_of[8], (4, D), 0.5, 3.0, ((1, 8),))
    gains = jnp.clip(1.0 + 0.1 * jax.random.normal(key_of[9], (2, D), jnp.float32), 0.5, 1.5).astype(jnp.bfloat16)
    shifts = noise(key_of[10], (2, D), 0.3, 2.0, ((1, 8),))
    inner_bias = noise(key_of[11], (FF,), 0.5, 3.0, ((0, 8),))
    lengths = draw_lengths(jax.random.fold_in(key_of[15], 71), 0)
    padding = draw_padding(jax.random.fold_in(key_of[15], 71), 0)
    cluster_perm = draw_cluster_perm(jax.random.fold_in(key_of[15], 71), 0)
    return {"hidden_in": hidden_in, "cotangent": cotangent, "w_query": w_query, "w_key": w_key, "w_value": w_value, "w_output": w_output, "w_inner": w_inner, "w_outer": w_outer, "biases": biases, "gains": gains, "shifts": shifts, "inner_bias": inner_bias, "lengths": lengths, "padding": padding, "cluster_perm": cluster_perm}


@jax.custom_vjp
def low(v):
    return lax.optimization_barrier(v.astype(jnp.bfloat16)).astype(jnp.float32)

@jax.custom_vjp
def low_back(v):
    return v

def low_keep(v):
    return (low(v), None)

def low_pass(kept, grad):
    return (grad,)

def back_keep(v):
    return (v, None)

def back_low(kept, grad):
    return (low(grad),)
low.defvjp(low_keep, low_pass)
low_back.defvjp(back_keep, back_low)
highest = lax.Precision.HIGHEST
epsilon = 1e-05
masked_fill = -1e+30

def norm_rows(hidden, gain_row, shift_row):
    average = lax.optimization_barrier(jnp.mean(hidden, axis=-1, keepdims=True))
    centred = hidden - average
    variance = lax.optimization_barrier(jnp.mean(centred * centred, axis=-1, keepdims=True))
    return centred * lax.rsqrt(variance + epsilon) * gain_row + shift_row

def block_layer(hidden, w_query, w_key, w_value, w_output, w_inner, w_outer, biases, gains, shifts, inner_bias, document, padding, slot_token, cluster_perm):

    def split_heads(row_data):
        return row_data.reshape(row_data.shape[0], HEADS, HEAD_DIM).transpose(1, 0, 2)
    queries = low(low_back(jnp.dot(hidden, w_query, precision=highest) + biases[0]))
    key_rows = low(low_back(jnp.dot(hidden, w_key, precision=highest)))
    values = low(low_back(jnp.dot(hidden, w_value, precision=highest) + biases[1]))

    def one_head(inputs):
        head_query, head_key, head_value, head_slots, head_perm = inputs
        query_blocks = head_query[head_slots].reshape(-1, CLUSTER, HEAD_DIM)
        key_blocks = head_key[head_slots].reshape(-1, CLUSTER, HEAD_DIM)
        value_blocks = head_value[head_slots].reshape(-1, CLUSTER, HEAD_DIM)
        doc_blocks = document[head_slots].reshape(-1, CLUSTER)
        valid_blocks = padding[head_slots].reshape(-1, CLUSTER)
        same_doc = doc_blocks[:, :, None] == doc_blocks[:, None, :]
        permitted = same_doc & (valid_blocks == 1)[:, None, :] | jnp.eye(CLUSTER, dtype=bool)[None]
        score_scale = 1.0 / math.sqrt(HEAD_DIM)
        raw_scores = jnp.einsum('bid,bjd->bij', query_blocks, key_blocks, precision=highest) * score_scale
        scores = jnp.where(permitted, low_back(raw_scores), masked_fill)
        soft_weights = jax.nn.softmax(scores, axis=-1)
        mixed_rows = jnp.einsum('bij,bjd->bid', low(soft_weights), value_blocks, precision=highest)
        mixed_rows = low(low_back(mixed_rows.reshape(-1, HEAD_DIM)))
        return mixed_rows[head_perm]
    attended = lax.map(jax.checkpoint(one_head), (split_heads(queries), split_heads(key_rows), split_heads(values), slot_token, cluster_perm))
    attended = attended.transpose(1, 0, 2).reshape(hidden.shape[0], HEADS * HEAD_DIM)
    branch = low_back(jnp.dot(attended, w_output, precision=highest) + biases[2])
    first = norm_rows(hidden + branch, gains[0], shifts[0])
    pre_act = low_back(jnp.dot(low(first), w_inner, precision=highest) + inner_bias)
    activated = low(jax.nn.gelu(pre_act, approximate=False))
    ffn_out = low_back(jnp.dot(activated, w_outer, precision=highest) + biases[3])
    return norm_rows(first + ffn_out, gains[1], shifts[1])

def reference(hidden_in, cotangent, w_query, w_key, w_value, w_output, w_inner, w_outer, biases, gains, shifts, inner_bias, lengths, padding, cluster_perm):
    run_count = N_DP // STRIPE
    padded = (lengths + CLUSTER - 1) // CLUSTER * CLUSTER
    local_rows = (padded // STRIPE).reshape(run_count, DOCS_GROUP)
    local_ends = jnp.cumsum(local_rows, axis=1).astype(jnp.int32)
    positions = jnp.arange(TOKENS, dtype=jnp.int32)
    run_of = (positions // TOK_DEV // STRIPE).astype(jnp.int32)
    row_place = (positions % TOK_DEV).astype(jnp.int32)
    ends_here = local_ends[run_of]
    document = (run_of * DOCS_GROUP + lax.optimization_barrier(jnp.sum((row_place[:, None] >= ends_here).astype(jnp.int32), axis=1))).astype(jnp.int32)
    head_index = jnp.arange(HEADS, dtype=jnp.int32)[:, None]
    slot_token = jnp.zeros((HEADS, TOKENS), jnp.int32).at[head_index, cluster_perm].set(jnp.broadcast_to(positions, (HEADS, TOKENS)))
    floats = [array.astype(jnp.float32) for array in (hidden_in, w_query, w_key, w_value, w_output, w_inner, w_outer, biases, gains, shifts, inner_bias)]

    def forward_fn(*params):
        return block_layer(*params, document, padding, slot_token, cluster_perm)
    result, pullback = jax.vjp(forward_fn, *floats)
    grads = pullback(cotangent.astype(jnp.float32))
    return (result.astype(jnp.bfloat16), grads[0].astype(jnp.bfloat16), grads[1], grads[2], grads[3], grads[4], grads[5], grads[6], grads[7], grads[8], grads[9], grads[10])
```

```python
from functools import partial
import math

import jax
import jax.numpy as jnp
from jax import lax
from jax.experimental import pallas as pl
from jax.experimental.pallas import tpu as pltpu
from jax.sharding import PartitionSpec as P

D = 768
HEAD_DIM = 64
FF = 3072
CLUSTER = 128
LANES = 128
EPSILON = 1e-05
MASKED = -1e30
SCALE = 1.0 / math.sqrt(HEAD_DIM)

bf16 = jnp.bfloat16
f32 = jnp.float32
i32 = jnp.int32


def nn(a, b):
    return lax.dot_general(a, b, (((1,), (0,)), ((), ())), preferred_element_type=f32)


def nt(a, b):
    return lax.dot_general(a, b, (((1,), (1,)), ((), ())), preferred_element_type=f32)


def tn(a, b):
    return lax.dot_general(a, b, (((0,), (0,)), ((), ())), preferred_element_type=f32)


def lane_iota(rows, lanes=LANES):
    return lax.broadcasted_iota(i32, (rows, lanes), 1)


def sublane_iota(rows, lanes=LANES):
    return lax.broadcasted_iota(i32, (rows, lanes), 0)


def as_column(row):
    parts = [
        jnp.broadcast_to(row[:, i * LANES : (i + 1) * LANES], (LANES, LANES)).T
        for i in range(row.shape[1] // LANES)
    ]
    return parts[0] if len(parts) == 1 else jnp.concatenate(parts, axis=0)


class Layout:
    def __init__(self, peers, tokens, heads):
        self.peers, self.tokens, self.heads = peers, tokens, heads
        self.stripe = min(16, peers)
        self.runs = peers // self.stripe
        self.per_dev = CLUSTER // self.stripe
        self.rows_peer = tokens // peers
        self.half_rows = self.rows_peer // 2
        self.pairs = self.half_rows // self.per_dev
        self.packed = tokens // 2
        self.clusters = peers * tokens // CLUSTER
        self.peers_chunk = 256 // self.half_rows
        self.data_rows = 9 * self.half_rows


def place_kernel(lay, perm_ref, code_ref):
    groups = lay.clusters
    strict = (sublane_iota(LANES) > lane_iota(LANES)).astype(f32).astype(bf16)
    shift = CLUSTER.bit_length() - 1
    blocks = lay.tokens // LANES
    for h in range(lay.heads):

        def members(b):
            row = perm_ref[h : h + 1, pl.ds(pl.multiple_of(b * LANES, LANES), LANES)]
            column = as_column(lax.shift_right_logical(row, shift))
            wide = jnp.concatenate([column] * (groups // LANES), axis=1)
            return (wide == lane_iota(LANES, groups)).astype(f32)

        if lay.runs == 1:
            base = (lane_iota(1, groups) * lay.per_dev).astype(f32)
        else:
            counts = lax.fori_loop(
                0,
                blocks,
                lambda b, c: c + jnp.sum(members(b), axis=0, keepdims=True),
                jnp.zeros((1, groups), f32),
            )
            before = (sublane_iota(groups, groups) < lane_iota(groups, groups)).astype(f32)
            base = nn(jnp.broadcast_to(counts, (16, groups)).astype(bf16), before.astype(bf16))[:1]

        def step(b, carry):
            member = members(b)
            ahead = nn(strict, member.astype(bf16)) + carry
            rank = jnp.sum(member * ahead, axis=1, keepdims=True).astype(i32)
            peer = rank // lay.rows_peer
            rest = rank - peer * lay.rows_peer
            half = (rest >= lay.half_rows).astype(i32)
            packed = peer * lay.half_rows + rest - half * lay.half_rows
            lane = lane_iota(LANES)
            code = jnp.where(lane == 0, packed, jnp.where(lane == 1, half, 0))
            code_ref[h, :, pl.ds(pl.multiple_of(b * LANES, LANES), LANES)] = code.T[:8]
            return carry + jnp.sum(member, axis=0, keepdims=True)

        lax.fori_loop(0, blocks, step, base)


def place_tokens(lay, perm):
    return pl.pallas_call(
        partial(place_kernel, lay),
        out_shape=jax.ShapeDtypeStruct((lay.heads, 8, lay.tokens), i32),
        name="place_tokens",
    )(perm)


def scatter_matrix(code_ref, h, first, rows, tokens):
    packed = code_ref[h, 0:1, :]
    wanted = sublane_iota(rows, tokens) + first
    return jnp.where(jnp.broadcast_to(packed, (rows, tokens)) == wanted, 1.0, 0.0).astype(bf16)


def gather_matrix(column, packed_rows):
    rows = column.shape[0]
    lane = lane_iota(rows)
    parts = [
        jnp.where(column == lane + k * LANES, 1.0, 0.0).astype(bf16)
        for k in range(packed_rows // LANES)
    ]
    return jnp.concatenate(parts, axis=1)


def project_kernel(lay, x_ref, w_ref, bias_ref, code_ref, pad_ref, out_ref, rows_ref, flag_ref):
    h = pl.program_id(0)
    lane_half = (lane_iota(256) >= HEAD_DIM).astype(i32)

    def project(c, _):
        at = pl.ds(pl.multiple_of(c * 256, 256), 256)
        values = nn(x_ref[at, :], w_ref[...]) + bias_ref[0:1, :]
        half = as_column(code_ref[0, 1:2, at])
        keep = half == lane_half
        for x in range(3):
            part = values[:, x * LANES : (x + 1) * LANES]
            rows_ref[at, x * LANES : (x + 1) * LANES] = jnp.where(keep, part, 0.0).astype(bf16)
        live = as_column(pad_ref[0:1, at])
        flags = jnp.where((lane_iota(256) == half) & (live == 1), 1.0, 0.0)
        rows_ref[at, 3 * LANES :] = flags.astype(bf16)
        return 0

    lax.fori_loop(0, lay.tokens // 256, project, 0)

    def sort(j, _):
        chosen = scatter_matrix(code_ref, 0, j * 256, 256, lay.tokens)
        moved = nn(chosen, rows_ref[...])
        peers = pl.ds(j * lay.peers_chunk, lay.peers_chunk)
        for x in range(3):
            part = moved[:, x * LANES : (x + 1) * LANES]
            part = part.reshape(lay.peers_chunk, lay.half_rows, LANES).astype(bf16)
            first = pl.multiple_of((h * 3 + x) * lay.half_rows, 16)
            out_ref[peers, pl.ds(first, lay.half_rows), :] = part
        flags = moved[:, 3 * LANES :]
        for i in range(2):
            at = pl.ds(pl.multiple_of(j * 256 + i * LANES, LANES), LANES)
            flag_ref[h, :, at] = flags[i * LANES : (i + 1) * LANES, :].T[:8]
        return 0

    lax.fori_loop(0, lay.packed // 256, sort, 0)

    @pl.when(h == lay.heads - 1)
    def _():
        for p in range(lay.peers):
            at = slice(p * lay.half_rows, (p + 1) * lay.half_rows)
            rows = [flag_ref[k, 0:2, at] for k in range(lay.heads)]
            block = jnp.concatenate(rows + [jnp.zeros((16 - 2 * lay.heads, lay.half_rows), f32)], axis=0)
            if lay.half_rows < LANES:
                block = jnp.concatenate(
                    [block, jnp.zeros((16, LANES - lay.half_rows), f32)], axis=1
                )
            out_ref[p, lay.data_rows : lay.data_rows + 16, :] = block.astype(bf16)


def project_rows(lay, x, weights, bias, code, pad):
    width = 3 * LANES
    return pl.pallas_call(
        partial(project_kernel, lay),
        grid=(lay.heads,),
        in_specs=[
            pl.BlockSpec((lay.tokens, D), lambda h: (0, 0)),
            pl.BlockSpec((D, width), lambda h: (0, h)),
            pl.BlockSpec((1, width), lambda h: (0, h)),
            pl.BlockSpec((1, 8, lay.tokens), lambda h: (h, 0, 0)),
            pl.BlockSpec((1, lay.tokens), lambda h: (0, 0)),
        ],
        out_specs=pl.BlockSpec((lay.peers, lay.data_rows + 16, LANES), lambda h: (0, 0, 0)),
        out_shape=jax.ShapeDtypeStruct((lay.peers, lay.data_rows + 16, LANES), bf16),
        scratch_shapes=[
            pltpu.VMEM((lay.tokens, 4 * LANES), bf16),
            pltpu.VMEM((lay.heads, 8, lay.packed), f32),
        ],
        name="project_rows",
    )(x, weights, bias, code, pad)


def pair_rows(lay, ref, first, run, p):
    block = ref[run * lay.stripe : (run + 1) * lay.stripe, first : first + lay.half_rows, :]
    if lay.per_dev % 16:
        block = block.astype(f32)
    block = block[:, p * lay.per_dev : (p + 1) * lay.per_dev, :]
    return block.reshape(CLUSTER, LANES).astype(bf16)


def put_pair(lay, ref, first, run, p, rows):
    at = slice(first + p * lay.per_dev, first + (p + 1) * lay.per_dev)
    rows = rows.reshape(lay.stripe, lay.per_dev, LANES).astype(ref.dtype)
    ref[run * lay.stripe : (run + 1) * lay.stripe, at, :] = rows


def live_rows(lay, flag_ref, h):
    flags = flag_ref[...].astype(f32)
    row = lax.broadcasted_iota(i32, flags.shape, 1)
    wide = lay.pairs * LANES
    lane = lane_iota(LANES, wide)
    inner = lane % LANES
    source = (lane // LANES) * lay.per_dev + inner % lay.per_dev
    spread = jnp.where(sublane_iota(LANES, wide) == source, 1.0, 0.0).astype(bf16)
    out = []
    for half in range(2):
        chosen = jnp.sum(jnp.where(row == 2 * h + half, flags, 0.0), axis=1)
        if lay.peers < 16:
            chosen = jnp.concatenate([chosen, jnp.zeros((16 - lay.peers, LANES), f32)], axis=0)
        moved = nn(chosen.astype(bf16), spread)
        rows = []
        for run in range(lay.runs):
            part = moved[run * lay.stripe : (run + 1) * lay.stripe]
            own = (lane_iota(lay.stripe, wide) % LANES) // lay.per_dev == sublane_iota(lay.stripe, wide)
            rows.append(jnp.sum(jnp.where(own, part, 0.0), axis=0, keepdims=True))
        out.append(rows)
    return out


def split_lanes(rows):
    low = lane_iota(rows.shape[0], rows.shape[1]) < HEAD_DIM
    zero = jnp.zeros_like(rows)
    return jnp.where(low, rows, zero), jnp.where(low, zero, rows)


def soft_weights(queries, keys, live):
    scores = nt(queries, keys) * SCALE
    allowed = (live > 0.5) | (lane_iota(CLUSTER) == sublane_iota(CLUSTER))
    scores = jnp.where(allowed, scores, MASKED)
    grown = jnp.exp(scores - jnp.max(scores, axis=1, keepdims=True))
    return grown / jnp.sum(grown, axis=1, keepdims=True)


def attend_kernel(lay, rows_ref, flag_ref, out_ref):
    live = live_rows(lay, flag_ref, pl.program_id(0))
    low = lane_iota(CLUSTER) < HEAD_DIM
    for run in range(lay.runs):
        for p in range(lay.pairs):
            q, k, v = (pair_rows(lay, rows_ref, x * lay.half_rows, run, p) for x in range(3))
            mixed = []
            for half, part in enumerate(split_lanes(q)):
                soft = soft_weights(part, k, live[half][run][:, p * LANES : (p + 1) * LANES])
                mixed.append(nn(soft.astype(bf16), v))
            put_pair(lay, out_ref, 0, run, p, jnp.where(low, mixed[0], mixed[1]))


def exchange_specs(lay):
    return (
        pl.BlockSpec((lay.peers, 3 * lay.half_rows, LANES), lambda h: (0, h, 0)),
        pl.BlockSpec((lay.peers, 16, LANES), lambda h: (0, lay.data_rows // 16, 0)),
        pl.BlockSpec((lay.peers, lay.half_rows, LANES), lambda h: (0, h, 0)),
    )


def attend(lay, arrived):
    rows, flags, single = exchange_specs(lay)
    return pl.pallas_call(
        partial(attend_kernel, lay),
        grid=(lay.heads,),
        in_specs=[rows, flags],
        out_specs=single,
        out_shape=jax.ShapeDtypeStruct((lay.peers, lay.heads * lay.half_rows, LANES), bf16),
        name="attend",
    )(arrived, arrived)


def attend_back_kernel(lay, rows_ref, flag_ref, grad_ref, out_ref, sum_ref):
    live = live_rows(lay, flag_ref, pl.program_id(0))
    low = lane_iota(CLUSTER) < HEAD_DIM
    sums = [jnp.zeros((1, LANES), f32)] * 2
    for run in range(lay.runs):
        for p in range(lay.pairs):
            q, k, v = (pair_rows(lay, rows_ref, x * lay.half_rows, run, p) for x in range(3))
            g = pair_rows(lay, grad_ref, 0, run, p)
            parts = []
            for half, (qh, gh) in enumerate(zip(split_lanes(q), split_lanes(g))):
                soft = soft_weights(qh, k, live[half][run][:, p * LANES : (p + 1) * LANES])
                grad_soft = nt(gh, v)
                delta = jnp.sum(soft * grad_soft, axis=1, keepdims=True)
                grad = (soft * (grad_soft - delta)).astype(bf16)
                parts.append((nn(grad, k), tn(grad, q), tn(soft.astype(bf16), g)))
            one, two = parts
            grad_q = (jnp.where(low, one[0], two[0]) * SCALE).astype(bf16)
            grad_k = (jnp.where(low, one[1], two[1]) * SCALE).astype(bf16)
            grad_v = jnp.where(low, one[2], two[2]).astype(bf16)
            for x, rows in enumerate((grad_q, grad_k, grad_v)):
                put_pair(lay, out_ref, x * lay.half_rows, run, p, rows)
            sums[0] = sums[0] + jnp.sum(grad_q.astype(f32), axis=0, keepdims=True)
            sums[1] = sums[1] + jnp.sum(grad_v.astype(f32), axis=0, keepdims=True)
    sum_ref[0] = jnp.concatenate(sums + [jnp.zeros((6, LANES), f32)], axis=0)


def attend_back(lay, arrived, grads):
    rows, flags, single = exchange_specs(lay)
    return pl.pallas_call(
        partial(attend_back_kernel, lay),
        grid=(lay.heads,),
        in_specs=[rows, flags, single],
        out_specs=[rows, pl.BlockSpec((1, 8, LANES), lambda h: (h, 0, 0))],
        out_shape=[
            jax.ShapeDtypeStruct((lay.peers, lay.data_rows, LANES), bf16),
            jax.ShapeDtypeStruct((lay.heads, 8, LANES), f32),
        ],
        name="attend_back",
    )(arrived, arrived, grads)


def unsort_kernel(lay, rows_ref, code_ref, out_ref):
    rows = rows_ref[...].reshape(lay.packed, LANES)
    low = lane_iota(256) < HEAD_DIM

    def quarter(q, _):
        sides = []
        for side in range(2):
            at = pl.ds(pl.multiple_of(q * 512 + side * 256, 256), 256)
            column = as_column(code_ref[0, 0:1, at])
            half = as_column(code_ref[0, 1:2, at])
            found = nn(gather_matrix(column, lay.packed), rows)
            sides.append(jnp.where(half == side, found, pltpu.roll(found, HEAD_DIM, 1)))
        out_ref[q] = jnp.where(low, sides[0], sides[1]).astype(bf16)
        return 0

    lax.fori_loop(0, lay.tokens // 512, quarter, 0)


def unsort_rows(lay, returned, code):
    quarters = lay.tokens // 512
    return pl.pallas_call(
        partial(unsort_kernel, lay),
        grid=(lay.heads,),
        in_specs=[
            pl.BlockSpec((lay.peers, lay.half_rows, LANES), lambda h: (0, h, 0)),
            pl.BlockSpec((1, 8, lay.tokens), lambda h: (h, 0, 0)),
        ],
        out_specs=pl.BlockSpec((quarters, 256, LANES), lambda h: (0, 0, h)),
        out_shape=jax.ShapeDtypeStruct((quarters, 256, lay.heads * LANES), bf16),
        name="unsort_rows",
    )(returned, code)


def sort_kernel(lay, grad_ref, code_ref, out_ref, rows_ref):
    low = lane_iota(256) < HEAD_DIM
    lane_half = (lane_iota(256) >= HEAD_DIM).astype(i32)

    def quarter(q, _):
        block = grad_ref[q].astype(f32)
        turned = pltpu.roll(block, HEAD_DIM, 1)
        for side in range(2):
            at = pl.ds(pl.multiple_of(q * 512 + side * 256, 256), 256)
            half = as_column(code_ref[0, 1:2, at])
            both = jnp.where(low, block, turned) if side == 0 else jnp.where(low, turned, block)
            rows_ref[at, :] = jnp.where(half == lane_half, both, 0.0).astype(bf16)
        return 0

    lax.fori_loop(0, lay.tokens // 512, quarter, 0)

    def sort(j, _):
        chosen = scatter_matrix(code_ref, 0, j * 256, 256, lay.tokens)
        moved = nn(chosen, rows_ref[...]).astype(bf16)
        peers = pl.ds(j * lay.peers_chunk, lay.peers_chunk)
        out_ref[peers] = moved.astype(f32).reshape(lay.peers_chunk, lay.half_rows, LANES).astype(bf16)
        return 0

    lax.fori_loop(0, lay.packed // 256, sort, 0)


def sort_rows(lay, grads, code):
    quarters = lay.tokens // 512
    return pl.pallas_call(
        partial(sort_kernel, lay),
        grid=(lay.heads,),
        in_specs=[
            pl.BlockSpec((quarters, 256, LANES), lambda h: (0, 0, h)),
            pl.BlockSpec((1, 8, lay.tokens), lambda h: (h, 0, 0)),
        ],
        out_specs=pl.BlockSpec((lay.peers, lay.half_rows, LANES), lambda h: (0, h, 0)),
        out_shape=jax.ShapeDtypeStruct((lay.peers, lay.heads * lay.half_rows, LANES), bf16),
        scratch_shapes=[pltpu.VMEM((lay.tokens, LANES), bf16)],
        name="sort_rows",
    )(grads, code)


def mean_rows(v):
    return jnp.sum(v, axis=1, keepdims=True) * (1.0 / D)


def norm_forward(rows):
    centred = rows - mean_rows(rows)
    inv = lax.rsqrt(mean_rows(centred * centred) + EPSILON)
    return centred * inv, inv


def norm_backward(scaled, normed, inv):
    return inv * (scaled - mean_rows(scaled) - normed * mean_rows(scaled * normed))


def middle_kernel(
    quarter_ref,
    att_ref,
    hidden_ref,
    cot_ref,
    par_ref,
    wo_ref,
    wf_ref,
    out_ref,
    act_ref,
    pre_ref,
    low_ref,
    ffn_grad_ref,
    branch_grad_ref,
    h1_ref,
    att_grad_ref,
    vec_ref,
    first_ref,
    normed_ref,
    inv_ref,
    slope_ref,
    sum_ref,
    h2_ref,
):
    step = pl.program_id(0)
    parts = att_ref.shape[0]

    @pl.when(step == 0)
    def _():
        vec_ref[...] = jnp.zeros_like(vec_ref)
        for side in range(2):
            branch = jnp.zeros((256, D), f32)
            for m in range(parts):
                att = att_ref[m]
                lane = lane_iota(256, att.shape[1]) % LANES
                own = (lane < HEAD_DIM) if side == 0 else (lane >= HEAD_DIM)
                branch = branch + nt(jnp.where(own, att, jnp.zeros_like(att)), wo_ref[m])
            at = slice(side * 256, side * 256 + 256)
            rows = hidden_ref[at, :].astype(f32) + (branch + par_ref[2:3, :])
            normed, inv = norm_forward(rows)
            first = normed * par_ref[4:5, :] + par_ref[6:7, :]
            first_ref[at, :] = first
            normed_ref[at, :] = normed
            inv_ref[at, :] = jnp.broadcast_to(inv, (256, LANES))
            low_ref[at, :] = first.astype(bf16)
        sum_ref[...] = jnp.zeros_like(sum_ref)

    @pl.when((step >= 1) & (step <= 4))
    def _():
        j = step - 1
        for side in range(2):
            at = slice(side * 256, side * 256 + 256)
            pre = nn(low_ref[at, :], wf_ref[0, :, :D]) + par_ref[pl.ds(8 + j, 1), :]
            cdf = 0.5 * (1.0 + lax.erf(pre * (1.0 / math.sqrt(2.0))))
            slope_ref[j, at, :] = cdf + pre * jnp.exp(-0.5 * pre * pre) * (1.0 / math.sqrt(2.0 * math.pi))
            act = (pre * cdf).astype(bf16)
            act_ref[at, :] = act
            sum_ref[at, :] += nt(act, wf_ref[0, :, D:])

    @pl.when(step == 4)
    def _():
        for side in range(4):
            at = slice(side * 128, side * 128 + 128)
            rows = first_ref[at, :] + (sum_ref[at, :] + par_ref[3:4, :])
            normed, inv = norm_forward(rows)
            out_ref[at, :] = (normed * par_ref[5:6, :] + par_ref[7:8, :]).astype(bf16)
            cot = cot_ref[at, :].astype(f32)
            grad = norm_backward(cot * par_ref[5:6, :], normed, inv)
            grad_low = grad.astype(bf16)
            h2_ref[at, :] = grad
            ffn_grad_ref[at, :] = grad_low
            vec_ref[3:4, :] += jnp.sum(grad_low.astype(f32), axis=0, keepdims=True)
            vec_ref[5:6, :] += jnp.sum(cot * normed, axis=0, keepdims=True)
            vec_ref[7:8, :] += jnp.sum(cot, axis=0, keepdims=True)
        sum_ref[...] = jnp.zeros_like(sum_ref)

    @pl.when(step >= 5)
    def _():
        j = 8 - step
        total = jnp.zeros((1, D), f32)
        for side in range(2):
            at = slice(side * 256, side * 256 + 256)
            grad_act = nn(ffn_grad_ref[at, :], wf_ref[0, :, D:])
            grad_pre = (grad_act * slope_ref[j, at, :]).astype(bf16)
            pre_ref[at, :] = grad_pre
            total = total + jnp.sum(grad_pre.astype(f32), axis=0, keepdims=True)
            sum_ref[at, :] += nt(grad_pre, wf_ref[0, :, :D])
        vec_ref[pl.ds(8 + j, 1), :] = total

    @pl.when(step == 8)
    def _():
        for side in range(4):
            at = slice(side * 128, side * 128 + 128)
            grad_first = h2_ref[at, :] + sum_ref[at, :]
            normed = normed_ref[at, :]
            grad = norm_backward(grad_first * par_ref[4:5, :], normed, inv_ref[at, 0:1])
            grad_low = grad.astype(bf16)
            h1_ref[at, :] = grad
            branch_grad_ref[at, :] = grad_low
            vec_ref[2:3, :] += jnp.sum(grad_low.astype(f32), axis=0, keepdims=True)
            vec_ref[4:5, :] += jnp.sum(grad_first * normed, axis=0, keepdims=True)
            vec_ref[6:7, :] += jnp.sum(grad_first, axis=0, keepdims=True)
        for m in range(parts):
            both = [nn(branch_grad_ref[s * 256 : s * 256 + 256, :], wo_ref[m]) for s in range(2)]
            lane = lane_iota(256, both[0].shape[1]) % LANES
            att_grad_ref[m] = jnp.where(lane < HEAD_DIM, both[0], both[1]).astype(bf16)


def middle(lay, quarter, att, hidden, cotangent, params, weights):
    parts, _, width = att.shape
    rows = 512

    def up(s, q):
        return (0, jnp.clip(s - 1, 0, 3))

    def down(s, q):
        return (0, jnp.clip(8 - s, 0, 3))

    def both(s, q):
        return (jnp.where(s <= 4, jnp.clip(s - 1, 0, 3), 8 - s), 0, 0)

    def whole(rank):
        return lambda s, q: (0,) * rank

    spec = pltpu.PrefetchScalarGridSpec(
        num_scalar_prefetch=1,
        grid=(9,),
        in_specs=[
            pl.BlockSpec((parts, 256, width), whole(3)),
            pl.BlockSpec((rows, D), lambda s, q: (q[0], 0)),
            pl.BlockSpec((rows, D), lambda s, q: (q[0], 0)),
            pl.BlockSpec((16, D), whole(2)),
            pl.BlockSpec((parts, D, width), lambda s, q: (0, 0, 4)),
            pl.BlockSpec((1, D, 2 * D), both),
        ],
        out_specs=[
            pl.BlockSpec((rows, D), whole(2)),
            pl.BlockSpec((rows, D), up),
            pl.BlockSpec((rows, D), down),
            pl.BlockSpec((rows, D), whole(2)),
            pl.BlockSpec((rows, D), whole(2)),
            pl.BlockSpec((rows, D), whole(2)),
            pl.BlockSpec((rows, D), whole(2)),
            pl.BlockSpec((parts, 256, width), whole(3)),
            pl.BlockSpec((16, D), whole(2)),
        ],
        scratch_shapes=[
            pltpu.VMEM((rows, D), f32),
            pltpu.VMEM((rows, D), f32),
            pltpu.VMEM((rows, LANES), f32),
            pltpu.VMEM((4, rows, D), f32),
            pltpu.VMEM((rows, D), f32),
            pltpu.VMEM((rows, D), f32),
        ],
    )
    return pl.pallas_call(
        middle_kernel,
        grid_spec=spec,
        out_shape=[
            jax.ShapeDtypeStruct((rows, D), bf16),
            jax.ShapeDtypeStruct((rows, FF), bf16),
            jax.ShapeDtypeStruct((rows, FF), bf16),
            jax.ShapeDtypeStruct((rows, D), bf16),
            jax.ShapeDtypeStruct((rows, D), bf16),
            jax.ShapeDtypeStruct((rows, D), bf16),
            jax.ShapeDtypeStruct((rows, D), f32),
            jax.ShapeDtypeStruct((parts, 256, width), bf16),
            jax.ShapeDtypeStruct((16, D), f32),
        ],
        compiler_params=pltpu.CompilerParams(vmem_limit_bytes=60 * 1024 * 1024),
        name="middle",
    )(quarter, att, hidden, cotangent, params, weights, weights)


def weight_grad_kernel(act_ref, pre_ref, low_ref, ffn_ref, branch_ref, att_ref, out_ref):
    out_ref[:, :D] = tn(low_ref[...], pre_ref[...]).astype(bf16)
    out_ref[:, D : 2 * D] = tn(ffn_ref[...], act_ref[...]).astype(bf16)
    low, high = att_ref[0], att_ref[0]
    lane = lane_iota(256, low.shape[1]) % LANES
    low = jnp.where(lane < HEAD_DIM, low, jnp.zeros_like(low))
    high = jnp.where(lane < HEAD_DIM, jnp.zeros_like(high), high)
    out_ref[:, 2 * D :] = (tn(branch_ref[:256, :], low) + tn(branch_ref[256:, :], high)).astype(bf16)


def weight_grads(act, pre, low, ffn_grad, branch_grad, att):
    parts, _, width = att.shape
    rows = act.shape[0]
    total = 2 * D + width
    whole = pl.BlockSpec((rows, D), lambda j: (0, 0))
    return pl.pallas_call(
        weight_grad_kernel,
        grid=(parts,),
        in_specs=[
            pl.BlockSpec((rows, D), lambda j: (0, j)),
            pl.BlockSpec((rows, D), lambda j: (0, j)),
            whole,
            whole,
            whole,
            pl.BlockSpec((1, 256, width), lambda j: (j, 0, 0)),
        ],
        out_specs=pl.BlockSpec((D, total), lambda j: (j, 0)),
        out_shape=jax.ShapeDtypeStruct((parts * D, total), bf16),
        compiler_params=pltpu.CompilerParams(vmem_limit_bytes=40 * 1024 * 1024),
        name="weight_grads",
    )(act, pre, low, ffn_grad, branch_grad, att)


def collect_kernel(lay, rows_ref, code_ref, x_ref, w_ref, hidden_ref, grad_ref, total_ref):
    chunk = pl.program_id(0)
    low = lane_iota(256) < HEAD_DIM
    firsts, seconds = [], []
    for h in range(lay.heads):
        column = as_column(code_ref[h, 0:1, :])
        half = as_column(code_ref[h, 1:2, :])
        planes = [
            rows_ref[:, (h * 3 + x) * lay.half_rows : (h * 3 + x + 1) * lay.half_rows, :].reshape(
                lay.packed, LANES
            )
            for x in range(3)
        ]
        found = nn(gather_matrix(column, lay.packed), jnp.concatenate(planes, axis=1))
        one, two = [], []
        for x in range(3):
            part = found[:, x * LANES : (x + 1) * LANES]
            turned = pltpu.roll(part, HEAD_DIM, 1)
            one.append(jnp.where(half == 0, part, turned))
            two.append(jnp.where(half == 1, part, turned))
        firsts.append(one)
        seconds.append(two)
    tiles = [jnp.where(low, firsts[h][0], seconds[h][1]) for h in range(lay.heads)]
    for h in range(0, lay.heads, 2):
        right = seconds[h + 1][2] if h + 1 < lay.heads else jnp.zeros((256, LANES), f32)
        tiles.append(jnp.where(low, firsts[h][2], right))
    dense = jnp.concatenate(tiles, axis=1).astype(bf16)
    hidden_ref[...] = nt(dense, w_ref[...]).astype(bf16)
    part = tn(x_ref[...], dense)

    @pl.when(chunk == 0)
    def _():
        total_ref[...] = part

    @pl.when(chunk > 0)
    def _():
        total_ref[...] += part

    @pl.when(chunk == pl.num_programs(0) - 1)
    def _():
        grad_ref[...] = total_ref[...].astype(bf16)


def collect(lay, returned, code, x, weights):
    width = weights.shape[1]
    return pl.pallas_call(
        partial(collect_kernel, lay),
        grid=(lay.tokens // 256,),
        in_specs=[
            pl.BlockSpec((lay.peers, lay.data_rows, LANES), lambda c: (0, 0, 0)),
            pl.BlockSpec((lay.heads, 8, 256), lambda c: (0, 0, c)),
            pl.BlockSpec((256, D), lambda c: (c, 0)),
            pl.BlockSpec((D, width), lambda c: (0, 0)),
        ],
        out_specs=[
            pl.BlockSpec((256, D), lambda c: (c, 0)),
            pl.BlockSpec((D, width), lambda c: (0, 0)),
        ],
        out_shape=[
            jax.ShapeDtypeStruct((lay.tokens, D), bf16),
            jax.ShapeDtypeStruct((D, width), bf16),
        ],
        scratch_shapes=[pltpu.VMEM((D, width), f32)],
        compiler_params=pltpu.CompilerParams(vmem_limit_bytes=40 * 1024 * 1024),
        name="collect",
    )(returned, code, x, weights)


def over_rows(rows):
    return lax.all_to_all(rows, "dp", split_axis=0, concat_axis=0, tiled=True)


def over_heads(rows):
    return lax.all_to_all(rows, "mp", split_axis=0, concat_axis=0, tiled=True)


def swap(rows, flip):
    return lax.ppermute(rows, "mp", [(i, i ^ flip) for i in range(lax.axis_size("mp"))])


def share_quarters(rows, place):
    whole = jnp.zeros((4,) + rows.shape, rows.dtype)
    other = swap(rows, 2)
    two = jnp.stack([rows, other])
    four = swap(two, 1)
    whole = lax.dynamic_update_index_in_dim(whole, rows, place, 0)
    whole = lax.dynamic_update_index_in_dim(whole, other, place ^ 2, 0)
    whole = lax.dynamic_update_index_in_dim(whole, four[0], place ^ 1, 0)
    whole = lax.dynamic_update_index_in_dim(whole, four[1], place ^ 3, 0)
    return whole.reshape((4 * rows.shape[0],) + rows.shape[1:])


def add_quarters(rows, place):
    size = rows.shape[0] // 4
    grid = rows.reshape(2, 2, size, rows.shape[1])
    core, far = place % 2, place // 2
    mine = lax.dynamic_index_in_dim(grid, core, 1, keepdims=False)
    theirs = lax.dynamic_index_in_dim(grid, 1 - core, 1, keepdims=False)
    chip = mine.astype(f32) + swap(theirs, 1).astype(f32)
    send = lax.dynamic_index_in_dim(chip, 1 - far, 0, keepdims=False).astype(bf16)
    keep = lax.dynamic_index_in_dim(chip, far, 0, keepdims=False)
    return keep + swap(send, 2).astype(f32)


def on_device(
    hidden_in,
    cotangent,
    w_query,
    w_key,
    w_value,
    w_output,
    w_inner,
    w_outer,
    biases,
    gains,
    shifts,
    inner_bias,
    lengths,
    padding,
    cluster_perm,
):
    peers = lax.axis_size("dp")
    tokens = hidden_in.shape[0]
    heads = cluster_perm.shape[0]
    lay = Layout(peers, tokens, heads)
    place = lax.axis_index("mp")
    row_block = lax.axis_index("dp")
    depth = w_query.shape[0]
    head_width = heads * HEAD_DIM

    out_t = jnp.broadcast_to(
        w_output.T.reshape(depth, heads, 1, HEAD_DIM), (depth, heads, 2, HEAD_DIM)
    ).reshape(depth, heads * LANES)
    shard = jnp.concatenate([w_inner, w_outer.T, out_t], axis=1)
    middle_w = lax.all_gather(shard, ("mp", "dp"), axis=0, tiled=True).reshape(4, D, -1)

    small = jnp.concatenate(
        [biases, gains, shifts, inner_bias.reshape(4, depth)], axis=0
    )
    width = 3 * head_width
    per_head = jnp.concatenate(
        [w.reshape(depth, heads, 1, HEAD_DIM) for w in (w_query, w_key, w_value)], axis=2
    ).reshape(depth, width)
    tail = small.reshape(-1)
    tail_rows = -(-tail.shape[0] // width)
    tail = jnp.pad(tail, (0, tail_rows * width - tail.shape[0])).reshape(tail_rows, width)
    got = lax.all_gather(jnp.concatenate([per_head, tail], axis=0), "dp", axis=0, tiled=False)
    weights = got[:, :depth].reshape(D, heads, 3, HEAD_DIM)
    vectors = got[:, depth:].reshape(peers, -1)[:, : 12 * depth].astype(f32)
    params = vectors.reshape(peers, 12, depth)[:, :8].transpose(1, 0, 2).reshape(8, D)
    inner = vectors.reshape(peers, 12, depth)[:, 8:].reshape(4, D)
    params = jnp.concatenate([params, inner, jnp.zeros((4, D), f32)], axis=0)
    doubled = jnp.broadcast_to(
        weights[:, :, :, None, :], (D, heads, 3, 2, HEAD_DIM)
    ).reshape(D, heads * 3 * LANES)
    own = lax.dynamic_slice_in_dim(params[:2], place * head_width, head_width, 1)
    own = own.reshape(2, heads, HEAD_DIM)
    own = jnp.stack([own[0], jnp.zeros_like(own[0]), own[1]], axis=1)
    own = jnp.broadcast_to(own[:, :, None, :], (heads, 3, 2, HEAD_DIM)).reshape(1, -1)

    code = place_tokens(lay, cluster_perm)
    sent = project_rows(lay, hidden_in, doubled, own, code, padding.reshape(1, tokens))
    arrived = over_rows(sent)
    mixed = attend(lay, arrived)
    att = over_heads(unsort_rows(lay, over_rows(mixed), code))
    (
        out_quarter,
        act,
        pre_grad,
        first_low,
        ffn_grad,
        branch_grad,
        grad_h1,
        att_grad,
        vec,
    ) = middle(lay, place.reshape(1), att, hidden_in, cotangent, params, middle_w)

    packed = weight_grads(act, pre_grad, first_low, ffn_grad, branch_grad, att)
    reduced = lax.psum_scatter(packed, ("mp", "dp"), scatter_dimension=0, tiled=True).astype(f32)
    hidden_out = share_quarters(out_quarter, place)

    grads = over_rows(sort_rows(lay, over_heads(att_grad), code))
    slot_grads, bias_sums = attend_back(lay, arrived, grads)

    head_sums = bias_sums[:, :2].reshape(heads, 2, 2, HEAD_DIM).sum(axis=2)
    head_sums = head_sums.transpose(1, 0, 2).reshape(2, head_width)
    vec = lax.dynamic_update_slice(vec[:12], head_sums, (0, place * head_width))
    vec = lax.psum(vec, ("dp", "mp"))

    ordered = jnp.concatenate(
        [
            weights[:, :, :2].reshape(D, 2 * head_width),
            weights[:, :, 2].reshape(D, head_width),
            jnp.zeros((D, (-width) % LANES), bf16),
        ],
        axis=1,
    )
    hidden_part, head_grad = collect(lay, over_rows(slot_grads), code, hidden_in, ordered)
    grad_hidden = share_quarters((add_quarters(hidden_part, place) + grad_h1).astype(bf16), place)

    terms = over_rows(head_grad.reshape(peers, depth, -1))
    total = jnp.sum(terms.astype(f32), axis=0)
    query_key = total[:, : 2 * head_width].reshape(depth, heads, 2, HEAD_DIM)
    grad_query = query_key[:, :, 0].reshape(depth, head_width)
    grad_key = query_key[:, :, 1].reshape(depth, head_width)
    grad_value = total[:, 2 * head_width : width]

    grad_out = reduced[:, 2 * D :].reshape(depth, heads, 2, HEAD_DIM).sum(axis=2)
    small = lax.dynamic_slice_in_dim(vec[:8], row_block * depth, depth, 1)
    grad_inner_bias = lax.dynamic_slice_in_dim(
        vec[8:].reshape(FF), row_block * (FF // peers), FF // peers, 0
    )
    return (
        hidden_out,
        grad_hidden,
        grad_query,
        grad_key,
        grad_value,
        grad_out.reshape(depth, head_width).T,
        reduced[:, :D],
        reduced[:, D : 2 * D].T,
        small[:4],
        small[4:6],
        small[6:8],
        grad_inner_bias,
    )


def solution(mesh):
    placed = (
        P("dp", None),
        P("dp", None),
        P("dp", "mp"),
        P("dp", "mp"),
        P("dp", "mp"),
        P("mp", "dp"),
        P("dp", "mp"),
        P("mp", "dp"),
        P(None, "dp"),
        P(None, "dp"),
        P(None, "dp"),
        P("dp"),
        P(),
        P("dp"),
        P("mp", "dp"),
    )
    return jax.shard_map(
        on_device,
        mesh=mesh,
        in_specs=placed,
        out_specs=(
            P("dp", None),
            P("dp", None),
            P("dp", "mp"),
            P("dp", "mp"),
            P("dp", "mp"),
            P("mp", "dp"),
            P("dp", "mp"),
            P("mp", "dp"),
            P(None, "dp"),
            P(None, "dp"),
            P(None, "dp"),
            P("dp"),
        ),
        check_vma=False,
    )
```

```python
from functools import partial
import math

import jax
import jax.numpy as jnp
from jax import lax
from jax.experimental import pallas as pl
from jax.experimental.pallas import tpu as pltpu
from jax.sharding import PartitionSpec as P

D = 768
HEAD_DIM = 64
FF = 3072
CLUSTER = 128
LANES = 128
EPSILON = 1e-05
MASKED = -1e30
SCALE = 1.0 / math.sqrt(HEAD_DIM)

bf16 = jnp.bfloat16
f32 = jnp.float32
i32 = jnp.int32

VMEM = 60 * 1024 * 1024
QUICK = pl.CostEstimate(flops=1000, bytes_accessed=1000, transcendentals=0)


def nn(a, b):
    return lax.dot_general(a, b, (((1,), (0,)), ((), ())), preferred_element_type=f32)


def nt(a, b):
    return lax.dot_general(a, b, (((1,), (1,)), ((), ())), preferred_element_type=f32)


def tn(a, b):
    return lax.dot_general(a, b, (((0,), (0,)), ((), ())), preferred_element_type=f32)


def lane_iota(rows, lanes=LANES):
    return lax.broadcasted_iota(i32, (rows, lanes), 1)


def sublane_iota(rows, lanes=LANES):
    return lax.broadcasted_iota(i32, (rows, lanes), 0)


def as_column(row):
    parts = [
        jnp.broadcast_to(row[:, i * LANES : (i + 1) * LANES], (LANES, LANES)).T
        for i in range(row.shape[1] // LANES)
    ]
    return parts[0] if len(parts) == 1 else jnp.concatenate(parts, axis=0)


class Layout:
    def __init__(self, peers, tokens, heads):
        self.peers, self.tokens, self.heads = peers, tokens, heads
        self.stripe = min(16, peers)
        self.runs = peers // self.stripe
        self.per_dev = CLUSTER // self.stripe
        self.rows_peer = tokens // peers
        self.half_rows = self.rows_peer // 2
        self.pairs = self.half_rows // self.per_dev
        self.packed = tokens // 2
        self.clusters = peers * tokens // CLUSTER
        self.data_rows = 9 * self.half_rows
        self.direct = self.half_rows == LANES
        self.arrays = peers if self.direct else 1

    def peer(self, me, s):
        return (me ^ s) if self.direct else s

    def shapes(self, rows, dtype=bf16):
        lead = () if self.direct else (self.peers,)
        return [jax.ShapeDtypeStruct(lead + (rows, LANES), dtype)] * self.arrays

    def specs(self, rows, at):
        if self.direct:
            return [pl.BlockSpec((rows, LANES), lambda *g: (at(*g), 0))] * self.arrays
        return [pl.BlockSpec((self.peers, rows, LANES), lambda *g: (0, at(*g), 0))]

    def view(self, refs, s):
        return refs[s] if self.direct else refs[0].at[s]


def only(at):
    return lambda *g: at


def place_kernel(lay, perm_ref, code_ref):
    groups = lay.clusters
    shift = CLUSTER.bit_length() - 1
    blocks = lay.tokens // LANES
    before = sublane_iota(LANES, 2 * LANES)
    after = lane_iota(LANES, 2 * LANES)
    ahead_of = jnp.where((before < after) | (after >= LANES), 1.0, 0.0).astype(bf16)

    def members(h, b):
        row = lax.shift_right_logical(perm_ref[h : h + 1, b * LANES : (b + 1) * LANES], shift)
        return jnp.broadcast_to(row, (groups, LANES)) == sublane_iota(groups)

    for h in range(lay.heads):
        if lay.runs == 1:
            carry = (sublane_iota(groups) * lay.per_dev).astype(f32)
        else:
            counts = jnp.zeros((groups, LANES), f32)
            for b in range(blocks):
                member = jnp.where(members(h, b), 1.0, 0.0).astype(bf16)
                counts = counts + nn(member, ahead_of)[:, LANES:]
            lower = jnp.where(
                sublane_iota(groups, groups) > lane_iota(groups, groups), 1.0, 0.0
            ).astype(bf16)
            carry = nn(lower, counts.astype(bf16))
        for b in range(blocks):
            member = members(h, b)
            found = nn(jnp.where(member, 1.0, 0.0).astype(bf16), ahead_of)
            rank = jnp.sum(jnp.where(member, found[:, :LANES] + carry, 0.0), axis=0, keepdims=True)
            carry = carry + found[:, LANES:]
            rank = rank.astype(i32)
            peer = lax.shift_right_logical(rank, lay.rows_peer.bit_length() - 1)
            rest = rank & (lay.rows_peer - 1)
            half = lax.shift_right_logical(rest, lay.half_rows.bit_length() - 1)
            packed = peer * lay.half_rows + (rest & (lay.half_rows - 1))
            at = slice(b * LANES, (b + 1) * LANES)
            code_ref[h, 0:1, at] = packed
            code_ref[h, 1:2, at] = half


def place_tokens(lay, perm):
    return pl.pallas_call(
        partial(place_kernel, lay),
        out_shape=jax.ShapeDtypeStruct((lay.heads, 8, lay.tokens), i32),
        name="place_tokens",
        cost_estimate=QUICK,
    )(perm)


def one_hot(equal):
    return jnp.where(equal, 1.0, 0.0).astype(bf16)


def scatter_matrix(lay, me, packed, s, blocks):
    rows = blocks * lay.half_rows
    if lay.direct:
        parts = [
            one_hot(
                jnp.broadcast_to(packed, (lay.half_rows, lay.tokens))
                == sublane_iota(lay.half_rows, lay.tokens) + lay.peer(me, s + i) * lay.half_rows
            )
            for i in range(blocks)
        ]
        return jnp.concatenate(parts, axis=0)
    wanted = sublane_iota(rows, lay.tokens) + s * lay.half_rows
    return one_hot(jnp.broadcast_to(packed, (rows, lay.tokens)) == wanted)


def gather_matrix(lay, me, column):
    lane = lane_iota(column.shape[0])
    parts = [
        one_hot(column == lane + lay.peer(me, k) * LANES) for k in range(lay.packed // LANES)
    ]
    return jnp.concatenate(parts, axis=1)


def block_rows(lay, refs, first):
    at = slice(first, first + lay.half_rows)
    if lay.direct:
        return jnp.concatenate([refs[s][at, :] for s in range(lay.peers)], axis=0)
    return refs[0][:, at, :].astype(f32).reshape(lay.packed, LANES).astype(bf16)


def put_blocks(lay, refs, s, blocks, first, rows):
    at = slice(first, first + lay.half_rows) if isinstance(first, int) else pl.ds(first, lay.half_rows)
    if lay.direct:
        for i in range(blocks):
            refs[s + i][at, :] = rows[i * LANES : (i + 1) * LANES].astype(bf16)
    else:
        rows = rows.astype(f32).reshape(blocks, lay.half_rows, LANES).astype(bf16)
        refs[0][s : s + blocks, at, :] = rows


def project_kernel(lay, steps, place_ref, x_ref, w_ref, bias_ref, code_ref, pad_ref, *rest):
    outs = rest[: lay.arrays]
    rows_ref, flag_ref = rest[lay.arrays :]
    step = pl.program_id(0)
    me = place_ref[0]
    width = 4 * LANES

    @pl.when(step < steps)
    def _():
        at = pl.ds(pl.multiple_of(step * 256, 256), 256)
        values = nn(x_ref[...], w_ref[...]) + bias_ref[0:1, :]
        low = lane_iota(256) < HEAD_DIM
        lane_half = jnp.where(low, 0, 1)
        live = as_column(pad_ref[0:1, at])
        tiles = [values[:, i * LANES : (i + 1) * LANES] for i in range(values.shape[1] // LANES)]
        turned = [pltpu.roll(tile, HEAD_DIM, 1) for tile in tiles]
        for h in range(lay.heads):
            half = as_column(code_ref[h, 1:2, at])
            keep = half == lane_half
            v, side = lay.heads + h // 2, h % 2
            planes = (
                jnp.where(low, tiles[h], turned[h]),
                jnp.where(low, turned[h], tiles[h]),
                jnp.where(low, tiles[v], turned[v]) if side == 0 else jnp.where(low, turned[v], tiles[v]),
            )
            for x, plane in enumerate(planes):
                rows_ref[h, at, x * LANES : (x + 1) * LANES] = jnp.where(keep, plane, 0.0).astype(bf16)
            flags = jnp.where((lane_iota(256) == half) & (live == 1), 1.0, 0.0)
            rows_ref[h, at, 3 * LANES :] = flags.astype(bf16)

    count = 4 if lay.direct else 32
    for h in range(lay.heads):

        @pl.when(step == steps + h)
        def _():
            for s in range(0, lay.peers, count):
                chosen = scatter_matrix(lay, me, code_ref[h, 0:1, :], s, count)
                moved = nn(chosen, rows_ref[h])
                for x in range(3):
                    put_blocks(
                        lay, outs, s, count, (h * 3 + x) * lay.half_rows,
                        moved[:, x * LANES : (x + 1) * LANES],
                    )
                for i in range(count * lay.half_rows // LANES):
                    at = slice(s * lay.half_rows + i * LANES, s * lay.half_rows + (i + 1) * LANES)
                    flag_ref[h, :, at] = moved[i * LANES : (i + 1) * LANES, 3 * LANES :].T[:8]

    @pl.when(step == steps + lay.heads - 1)
    def _():
        for s in range(lay.peers):
            at = slice(s * lay.half_rows, (s + 1) * lay.half_rows)
            rows = [flag_ref[k, 0:2, at] for k in range(lay.heads)]
            block = jnp.concatenate(rows + [jnp.zeros((16 - 2 * lay.heads, lay.half_rows), f32)], axis=0)
            if lay.half_rows < LANES:
                block = jnp.concatenate(
                    [block, jnp.zeros((16, LANES - lay.half_rows), f32)], axis=1
                )
            lay.view(outs, s)[lay.data_rows : lay.data_rows + 16, :] = block.astype(bf16)


def project_rows(lay, places, x, weights, bias, code, pad):
    width = weights.shape[1]
    steps = lay.tokens // 256
    spec = pltpu.PrefetchScalarGridSpec(
        num_scalar_prefetch=1,
        grid=(steps + lay.heads,),
        in_specs=[
            pl.BlockSpec((256, D), lambda s, _: (jnp.minimum(s, steps - 1), 0)),
            pl.BlockSpec((D, width), lambda s, _: (0, 0)),
            pl.BlockSpec((8, width), lambda s, _: (0, 0)),
            pl.BlockSpec((lay.heads, 8, lay.tokens), lambda s, _: (0, 0, 0)),
            pl.BlockSpec((1, lay.tokens), lambda s, _: (0, 0)),
        ],
        out_specs=lay.specs(lay.data_rows + 16, only(0)),
        scratch_shapes=[
            pltpu.VMEM((lay.heads, lay.tokens, 4 * LANES), bf16),
            pltpu.VMEM((lay.heads, 8, lay.packed), f32),
        ],
    )
    return pl.pallas_call(
        partial(project_kernel, lay, steps),
        grid_spec=spec,
        out_shape=lay.shapes(lay.data_rows + 16),
        compiler_params=pltpu.CompilerParams(vmem_limit_bytes=VMEM),
        name="project_rows",
        cost_estimate=QUICK,
    )(places, x, weights, bias, code, pad)


def pair_rows(lay, refs, first, run, p):
    at = slice(first + p * lay.per_dev, first + (p + 1) * lay.per_dev)
    if lay.direct:
        return jnp.concatenate([refs[s][at, :] for s in range(lay.stripe)], axis=0)
    block = refs[0][run * lay.stripe : (run + 1) * lay.stripe, first : first + lay.half_rows, :]
    block = block.astype(f32)[:, p * lay.per_dev : (p + 1) * lay.per_dev, :]
    return block.reshape(CLUSTER, LANES).astype(bf16)


def put_pair(lay, refs, first, run, p, rows):
    at = slice(first + p * lay.per_dev, first + (p + 1) * lay.per_dev)
    for s in range(lay.stripe):
        part = rows[s * lay.per_dev : (s + 1) * lay.per_dev]
        lay.view(refs, run * lay.stripe + s)[at, :] = part.astype(bf16)


def live_columns(lay, flags, h):
    pick = one_hot(sublane_iota(16, 2 * LANES) == 2 * h + lane_iota(16, 2 * LANES) // LANES)
    return [tn(lay.view(flags, s)[...], pick) for s in range(lay.peers)]


def allowed_pair(lay, columns, run, p):
    at = slice(p * lay.per_dev, (p + 1) * lay.per_dev)
    live = jnp.concatenate([columns[run * lay.stripe + s][at] for s in range(lay.stripe)], axis=0)
    live = jnp.concatenate([live[:, :LANES], live[:, LANES:]], axis=0)
    same = sublane_iota(2 * CLUSTER) % CLUSTER == lane_iota(2 * CLUSTER)
    return (live > 0.5) | same


def stack_halves(rows):
    low = lane_iota(rows.shape[0], rows.shape[1]) < HEAD_DIM
    zero = jnp.zeros_like(rows)
    return jnp.concatenate([jnp.where(low, rows, zero), jnp.where(low, zero, rows)], axis=0)


def each_half(fold, rows):
    one, two = (
        jnp.broadcast_to(fold(part, axis=0, keepdims=True), part.shape)
        for part in (rows[:CLUSTER], rows[CLUSTER:])
    )
    return jnp.concatenate([one, two], axis=0)


def inverse_sum(rows, axis, keepdims):
    return 1.0 / jnp.sum(rows, axis=axis, keepdims=keepdims)


def soft_weights(queries, keys, allowed):
    scores = jnp.where(allowed, nt(keys, queries) * SCALE, MASKED)
    grown = jnp.exp(scores - each_half(jnp.max, scores))
    return grown * each_half(inverse_sum, grown)


def attend_kernel(lay, *refs):
    rows, flags, outs = (refs[i * lay.arrays : (i + 1) * lay.arrays] for i in range(3))
    live = live_columns(lay, flags, pl.program_id(0))
    for run in range(lay.runs):
        for p in range(lay.pairs):
            q, k, v = (pair_rows(lay, rows, x * lay.half_rows, run, p) for x in range(3))
            soft = soft_weights(q, stack_halves(k), allowed_pair(lay, live, run, p))
            put_pair(lay, outs, 0, run, p, tn(soft.astype(bf16), stack_halves(v)))


def attend(lay, arrived):
    head = lambda h: h
    return pl.pallas_call(
        partial(attend_kernel, lay),
        grid=(lay.heads,),
        in_specs=lay.specs(3 * lay.half_rows, head) + lay.specs(16, only(lay.data_rows // 16)),
        out_specs=lay.specs(lay.half_rows, head),
        out_shape=lay.shapes(lay.heads * lay.half_rows),
        name="attend",
        cost_estimate=QUICK,
    )(*arrived, *arrived)


def attend_back_kernel(lay, *refs):
    rows, flags, grads, outs = (refs[i * lay.arrays : (i + 1) * lay.arrays] for i in range(4))
    sum_ref = refs[-1]
    live = live_columns(lay, flags, pl.program_id(0))
    low = lane_iota(CLUSTER) < HEAD_DIM
    sums = [jnp.zeros((1, LANES), f32)] * 2
    for run in range(lay.runs):
        for p in range(lay.pairs):
            q, k, v = (pair_rows(lay, rows, x * lay.half_rows, run, p) for x in range(3))
            g = pair_rows(lay, grads, 0, run, p)
            keys = stack_halves(k)
            soft = soft_weights(q, keys, allowed_pair(lay, live, run, p))
            grad_soft = nt(stack_halves(v), g)
            delta = each_half(jnp.sum, soft * grad_soft)
            grad = (soft * (grad_soft - delta)).astype(bf16)
            grad_q = (tn(grad, keys) * SCALE).astype(bf16)
            part = nn(grad, q)
            grad_k = (jnp.where(low, part[:CLUSTER], part[CLUSTER:]) * SCALE).astype(bf16)
            part = nn(soft.astype(bf16), g)
            grad_v = jnp.where(low, part[:CLUSTER], part[CLUSTER:]).astype(bf16)
            for x, part in enumerate((grad_q, grad_k, grad_v)):
                put_pair(lay, outs, x * lay.half_rows, run, p, part)
            sums[0] = sums[0] + jnp.sum(grad_q.astype(f32), axis=0, keepdims=True)
            sums[1] = sums[1] + jnp.sum(grad_v.astype(f32), axis=0, keepdims=True)
    sum_ref[0] = jnp.concatenate(sums + [jnp.zeros((6, LANES), f32)], axis=0)


def attend_back(lay, arrived, grads):
    head = lambda h: h
    three = lay.specs(3 * lay.half_rows, head)
    out = pl.pallas_call(
        partial(attend_back_kernel, lay),
        grid=(lay.heads,),
        in_specs=three
        + lay.specs(16, only(lay.data_rows // 16))
        + lay.specs(lay.half_rows, head),
        out_specs=three + [pl.BlockSpec((1, 8, LANES), lambda h: (h, 0, 0))],
        out_shape=lay.shapes(lay.data_rows)
        + [jax.ShapeDtypeStruct((lay.heads, 8, LANES), f32)],
        name="attend_back",
        cost_estimate=QUICK,
    )(*arrived, *arrived, *grads)
    return out[:-1], out[-1]


def side_rows(quarter, side):
    return pl.ds(pl.multiple_of(quarter * 512 + side * 256, 256), 256)


def unsort_kernel(lay, place_ref, *refs):
    rows_refs, code_ref, outs = refs[: lay.arrays], refs[lay.arrays], refs[lay.arrays + 1 :]
    rows = block_rows(lay, rows_refs, 0)
    low = lane_iota(256) < HEAD_DIM
    me, place = place_ref[0], place_ref[1]

    for t in range(4):
        sides = []
        for side in range(2):
            at = side_rows(place ^ t, side)
            column = as_column(code_ref[0, 0:1, at])
            half = as_column(code_ref[0, 1:2, at])
            found = nn(gather_matrix(lay, me, column), rows)
            sides.append(jnp.where(half == side, found, pltpu.roll(found, HEAD_DIM, 1)))
        outs[t][...] = jnp.where(low, sides[0], sides[1]).astype(bf16)


def unsort_rows(lay, places, returned, code):
    spec = pltpu.PrefetchScalarGridSpec(
        num_scalar_prefetch=1,
        grid=(lay.heads,),
        in_specs=lay.specs(lay.half_rows, lambda h, _: h)
        + [pl.BlockSpec((1, 8, lay.tokens), lambda h, _: (h, 0, 0))],
        out_specs=[pl.BlockSpec((256, LANES), lambda h, _: (0, h))] * 4,
    )
    return pl.pallas_call(
        partial(unsort_kernel, lay),
        grid_spec=spec,
        out_shape=[jax.ShapeDtypeStruct((256, lay.heads * LANES), bf16)] * 4,
        name="unsort_rows",
        cost_estimate=QUICK,
    )(places, *returned, code)


def sort_kernel(lay, place_ref, *refs):
    grads, code_ref, outs, rows_ref = refs[:4], refs[4], refs[5:-1], refs[-1]
    low = lane_iota(256) < HEAD_DIM
    lane_half = jnp.where(low, 0, 1)
    me, place = place_ref[0], place_ref[1]

    for t in range(4):
        block = grads[t][...].astype(f32)
        turned = pltpu.roll(block, HEAD_DIM, 1)
        for side in range(2):
            at = side_rows(place ^ t, side)
            half = as_column(code_ref[0, 1:2, at])
            both = jnp.where(low, block, turned) if side == 0 else jnp.where(low, turned, block)
            rows_ref[at, :] = jnp.where(half == lane_half, both, 0.0).astype(bf16)

    count = 4 if lay.direct else 32
    for s in range(0, lay.peers, count):
        chosen = scatter_matrix(lay, me, code_ref[0, 0:1, :], s, count)
        put_blocks(lay, outs, s, count, 0, nn(chosen, rows_ref[...]))


def sort_rows(lay, places, grads, code):
    spec = pltpu.PrefetchScalarGridSpec(
        num_scalar_prefetch=1,
        grid=(lay.heads,),
        in_specs=[pl.BlockSpec((256, LANES), lambda h, _: (0, h))] * 4
        + [pl.BlockSpec((1, 8, lay.tokens), lambda h, _: (h, 0, 0))],
        out_specs=lay.specs(lay.half_rows, lambda h, _: h),
        scratch_shapes=[pltpu.VMEM((lay.tokens, LANES), bf16)],
    )
    return pl.pallas_call(
        partial(sort_kernel, lay),
        grid_spec=spec,
        out_shape=lay.shapes(lay.heads * lay.half_rows),
        name="sort_rows",
        cost_estimate=QUICK,
    )(places, *grads, code)


def pack_kernel(
    query_ref, key_ref, value_ref, output_ref, inner_ref, outer_ref,
    bias_ref, gain_ref, shift_ref, inner_bias_ref, piece_ref, shard_ref, outer_out_ref,
):
    depth, width = query_ref.shape
    heads = width // HEAD_DIM
    query, key, value = (ref[...].astype(f32) for ref in (query_ref, key_ref, value_ref))
    cut = [slice(h * HEAD_DIM, (h + 1) * HEAD_DIM) for h in range(heads)]
    columns = [part for at in cut for part in (query[:, at], key[:, at])] + [value]
    have = 3 * width
    fill = piece_ref.shape[1] - have
    if fill:
        columns.append(jnp.zeros((depth, fill), f32))
    piece_ref[:depth, :] = jnp.concatenate(columns, axis=1).astype(bf16)
    inner_bias = inner_bias_ref[...].astype(f32)
    vectors = jnp.concatenate(
        [ref[...].astype(f32) for ref in (bias_ref, gain_ref, shift_ref)]
        + [inner_bias[:, i * depth : (i + 1) * depth] for i in range(4)]
        + [jnp.zeros((4, depth), f32)],
        axis=0,
    )
    vectors = jnp.concatenate([vectors, jnp.zeros((16, piece_ref.shape[1] - depth), f32)], axis=1)
    piece_ref[depth:, :] = vectors.astype(bf16)
    shard_ref[:, :D] = inner_ref[...]
    outer_out_ref[...] = outer_ref[...]
    turned = output_ref[...].astype(f32).T
    shard_ref[:, D:] = jnp.concatenate(
        [turned[:, at] for at in cut for _ in range(2)], axis=1
    ).astype(bf16)


def pack_weights(*arrays):
    depth, width = arrays[0].shape
    columns = -(-3 * width // LANES) * LANES
    return pl.pallas_call(
        pack_kernel,
        out_shape=[
            jax.ShapeDtypeStruct((depth + 16, columns), bf16),
            jax.ShapeDtypeStruct((depth, D + 2 * width), bf16),
            jax.ShapeDtypeStruct((depth, D), bf16),
        ],
        name="pack_weights",
        cost_estimate=QUICK,
    )(*arrays)


def assemble_kernel(lay, place_ref, *refs):
    pieces, (weight_ref, bias_ref, par_ref, part_ref) = refs[: lay.peers], refs[lay.peers :]
    me, place = place_ref[0], place_ref[1]
    depth = D // lay.peers
    for s in range(lay.peers):
        d = me ^ s
        weight_ref[pl.ds(pl.multiple_of(d * depth, 16), depth), :] = pieces[s][:depth, :]
        part_ref[d] = pieces[s][depth:, :LANES].astype(f32)

    def whole(row, rows=1, peers=range(lay.peers)):
        return jnp.concatenate(
            [part_ref[d, row + i : row + i + 1, :depth] for d in peers for i in range(rows)], axis=1
        )

    vectors = [whole(r) for r in range(8)]
    each = lay.peers // 4
    vectors += [whole(8, 4, range(j * each, (j + 1) * each)) for j in range(4)]
    par_ref[...] = jnp.concatenate(vectors + [jnp.zeros((4, D), f32)], axis=0)
    width = lay.heads * HEAD_DIM

    def own(vector):
        out = vector[:, :width]
        for p in range(1, D // width):
            out = jnp.where(place == p, vector[:, p * width : (p + 1) * width], out)
        return out

    query = own(vectors[0])
    zero = jnp.zeros((1, HEAD_DIM), f32)
    columns = [
        part for h in range(lay.heads) for part in (query[:, h * HEAD_DIM : (h + 1) * HEAD_DIM], zero)
    ] + [own(vectors[1])]
    fill = bias_ref.shape[1] - 3 * width
    if fill:
        columns.append(jnp.zeros((1, fill), f32))
    bias_ref[...] = jnp.broadcast_to(jnp.concatenate(columns, axis=1), bias_ref.shape)


def assemble_weights(lay, places, pieces):
    columns = pieces[0].shape[1]
    vmem = pl.BlockSpec(memory_space=pltpu.VMEM)
    return pl.pallas_call(
        partial(assemble_kernel, lay),
        in_specs=[pl.BlockSpec(memory_space=pltpu.SMEM)] + [vmem] * lay.peers,
        out_specs=[vmem] * 3,
        out_shape=[
            jax.ShapeDtypeStruct((D, columns), bf16),
            jax.ShapeDtypeStruct((8, columns), f32),
            jax.ShapeDtypeStruct((16, D), f32),
        ],
        scratch_shapes=[pltpu.VMEM((lay.peers, 16, LANES), f32)],
        name="assemble_weights",
        cost_estimate=QUICK,
    )(places, *pieces)


def mean_rows(v):
    return jnp.sum(v, axis=1, keepdims=True) * (1.0 / D)


def norm_forward(rows):
    centred = rows - mean_rows(rows)
    inv = lax.rsqrt(mean_rows(centred * centred) + EPSILON)
    return centred * inv, inv


def norm_backward(scaled, normed, inv):
    return inv * (scaled - mean_rows(scaled) - normed * mean_rows(scaled * normed))


def middle_kernel(
    place_ref,
    att0,
    att1,
    att2,
    att3,
    hidden_ref,
    cot_ref,
    par_ref,
    w0,
    w1,
    w2,
    w3,
    v0,
    v1,
    v2,
    v3,
    out_ref,
    act_ref,
    pre_ref,
    low_ref,
    ffn_grad_ref,
    branch_grad_ref,
    h1_ref,
    grad0,
    grad1,
    grad2,
    grad3,
    vec_ref,
    first_ref,
    normed_ref,
    inv_ref,
    slope_ref,
    sum_ref,
    h2_ref,
    weight_ref,
    sems,
):
    step = pl.program_id(0)
    place = place_ref[1]
    project = slice(2 * D, None)

    def fetch(t, part):
        width = att0.shape[1]
        source = (w0, w1, w2, w3)[t].at[:, D:], (w0, w1, w2, w3)[t].at[:, :D], (v0, v1, v2, v3)[t]
        target = pl.ds(2 * D, width), pl.ds(0, D), pl.ds(D, D)
        return pltpu.make_async_copy(
            source[part], weight_ref.at[t, :, target[part]], sems.at[part, t]
        )

    for t in range(4):

        @pl.when(step == t + 1)
        def _():
            fetch(t, 1).wait()
            fetch(t, 2).wait()

    @pl.when(step == 0)
    def _():
        for t in range(4):
            fetch(t, 0).start()
        for t in range(4):
            fetch(t, 1).start()
            fetch(t, 2).start()
        for t in range(4):
            fetch(t, 0).wait()
        vec_ref[...] = jnp.zeros_like(vec_ref)
        for side in range(2):
            branch = jnp.zeros((256, D), f32)
            for t, att_ref in enumerate((att0, att1, att2, att3)):
                att = att_ref[...]
                lane = lane_iota(256, att.shape[1]) % LANES
                own = (lane < HEAD_DIM) if side == 0 else (lane >= HEAD_DIM)
                branch = branch + nt(jnp.where(own, att, jnp.zeros_like(att)), weight_ref[t, :, project])
            at = slice(side * 256, side * 256 + 256)
            rows = hidden_ref[at, :].astype(f32) + (branch + par_ref[2:3, :])
            normed, inv = norm_forward(rows)
            first = normed * par_ref[4:5, :] + par_ref[6:7, :]
            first_ref[at, :] = first
            normed_ref[at, :] = normed
            inv_ref[at, :] = jnp.broadcast_to(inv, (256, LANES))
            low_ref[at, :] = first.astype(bf16)
        sum_ref[...] = jnp.zeros_like(sum_ref)

    @pl.when((step >= 1) & (step <= 4))
    def _():
        j = step - 1
        for side in range(2):
            at = slice(side * 256, side * 256 + 256)
            pre = nn(low_ref[at, :], weight_ref[j, :, :D]) + par_ref[pl.ds(8 + (place ^ j), 1), :]
            cdf = 0.5 * (1.0 + lax.erf(pre * (1.0 / math.sqrt(2.0))))
            slope_ref[j, at, :] = cdf + pre * jnp.exp(-0.5 * pre * pre) * (1.0 / math.sqrt(2.0 * math.pi))
            act = (pre * cdf).astype(bf16)
            act_ref[at, :] = act
            sum_ref[at, :] += nt(act, weight_ref[j, :, D : 2 * D])

    @pl.when(step == 4)
    def _():
        for side in range(4):
            at = slice(side * 128, side * 128 + 128)
            rows = first_ref[at, :] + (sum_ref[at, :] + par_ref[3:4, :])
            normed, inv = norm_forward(rows)
            out_ref[at, :] = (normed * par_ref[5:6, :] + par_ref[7:8, :]).astype(bf16)
            cot = cot_ref[at, :].astype(f32)
            grad = norm_backward(cot * par_ref[5:6, :], normed, inv)
            grad_low = grad.astype(bf16)
            h2_ref[at, :] = grad
            ffn_grad_ref[at, :] = grad_low
            vec_ref[3:4, :] += jnp.sum(grad_low.astype(f32), axis=0, keepdims=True)
            vec_ref[5:6, :] += jnp.sum(cot * normed, axis=0, keepdims=True)
            vec_ref[7:8, :] += jnp.sum(cot, axis=0, keepdims=True)
        sum_ref[...] = jnp.zeros_like(sum_ref)

    @pl.when(step >= 5)
    def _():
        j = 8 - step
        total = jnp.zeros((1, D), f32)
        for side in range(2):
            at = slice(side * 256, side * 256 + 256)
            grad_act = nn(ffn_grad_ref[at, :], weight_ref[j, :, D : 2 * D])
            grad_pre = (grad_act * slope_ref[j, at, :]).astype(bf16)
            pre_ref[at, :] = grad_pre
            total = total + jnp.sum(grad_pre.astype(f32), axis=0, keepdims=True)
            sum_ref[at, :] += nt(grad_pre, weight_ref[j, :, :D])
        vec_ref[pl.ds(8 + (place ^ j), 1), :] = total

    @pl.when(step == 8)
    def _():
        for side in range(4):
            at = slice(side * 128, side * 128 + 128)
            grad_first = h2_ref[at, :] + sum_ref[at, :]
            normed = normed_ref[at, :]
            grad = norm_backward(grad_first * par_ref[4:5, :], normed, inv_ref[at, 0:1])
            grad_low = grad.astype(bf16)
            h1_ref[at, :] = grad
            branch_grad_ref[at, :] = grad_low
            vec_ref[2:3, :] += jnp.sum(grad_low.astype(f32), axis=0, keepdims=True)
            vec_ref[4:5, :] += jnp.sum(grad_first * normed, axis=0, keepdims=True)
            vec_ref[6:7, :] += jnp.sum(grad_first, axis=0, keepdims=True)
        for t, grad_ref in enumerate((grad0, grad1, grad2, grad3)):
            both = [
                nn(branch_grad_ref[s * 256 : s * 256 + 256, :], weight_ref[t, :, project])
                for s in range(2)
            ]
            lane = lane_iota(256, both[0].shape[1]) % LANES
            grad_ref[...] = jnp.where(lane < HEAD_DIM, both[0], both[1]).astype(bf16)


def middle(places, att, hidden, cotangent, params, weights):
    width = att[0].shape[1]
    rows = 512

    def up(s, q):
        return (0, jnp.clip(s - 1, 0, 3))

    def down(s, q):
        return (0, jnp.clip(8 - s, 0, 3))

    def whole(rank):
        return lambda s, q: (0,) * rank

    square = pl.BlockSpec((rows, D), whole(2))
    exchanged = pl.BlockSpec((256, width), whole(2))
    spec = pltpu.PrefetchScalarGridSpec(
        num_scalar_prefetch=1,
        grid=(9,),
        in_specs=[exchanged] * 4
        + [
            pl.BlockSpec((rows, D), lambda s, q: (q[1], 0)),
            pl.BlockSpec((rows, D), lambda s, q: (q[1], 0)),
            pl.BlockSpec((16, D), whole(2)),
        ]
        + [pl.BlockSpec(memory_space=pl.ANY)] * 8,
        out_specs=[
            square,
            pl.BlockSpec((rows, D), up),
            pl.BlockSpec((rows, D), down),
            square,
            square,
            square,
            square,
        ]
        + [exchanged] * 4
        + [pl.BlockSpec((16, D), whole(2))],
        scratch_shapes=[
            pltpu.VMEM((rows, D), f32),
            pltpu.VMEM((rows, D), f32),
            pltpu.VMEM((rows, LANES), f32),
            pltpu.VMEM((4, rows, D), f32),
            pltpu.VMEM((rows, D), f32),
            pltpu.VMEM((rows, D), f32),
            pltpu.VMEM((4, D, 2 * D + width), bf16),
            pltpu.SemaphoreType.DMA((3, 4)),
        ],
    )
    out = pl.pallas_call(
        middle_kernel,
        grid_spec=spec,
        out_shape=[
            jax.ShapeDtypeStruct((rows, D), bf16),
            jax.ShapeDtypeStruct((rows, FF), bf16),
            jax.ShapeDtypeStruct((rows, FF), bf16),
            jax.ShapeDtypeStruct((rows, D), bf16),
            jax.ShapeDtypeStruct((rows, D), bf16),
            jax.ShapeDtypeStruct((rows, D), bf16),
            jax.ShapeDtypeStruct((rows, D), f32),
        ]
        + [jax.ShapeDtypeStruct((256, width), bf16)] * 4
        + [jax.ShapeDtypeStruct((16, D), f32)],
        compiler_params=pltpu.CompilerParams(vmem_limit_bytes=VMEM),
        name="middle",
        cost_estimate=QUICK,
    )(places, *att, hidden, cotangent, params, *weights)
    return out[:7], out[7:11], out[11]


def weight_grad_kernel(place_ref, act_ref, pre_ref, low_ref, ffn_ref, branch_ref, *refs):
    att_refs, out_ref = refs[:-1], refs[-1]
    out_ref[:, :D] = tn(low_ref[...], pre_ref[...]).astype(bf16)
    out_ref[:, D : 2 * D] = tn(ffn_ref[...], act_ref[...]).astype(bf16)
    for t in range(4):

        @pl.when(pl.program_id(0) == t)
        def _():
            att = att_refs[t][...]
            low = lane_iota(256, att.shape[1]) % LANES < HEAD_DIM
            zero = jnp.zeros_like(att)
            part = tn(branch_ref[:256, :], jnp.where(low, att, zero))
            part = part + tn(branch_ref[256:, :], jnp.where(low, zero, att))
            out_ref[:, 2 * D :] = part.astype(bf16)


def weight_grads(places, saved, att):
    act, pre, low, ffn_grad, branch_grad = saved
    rows = act.shape[0]
    width = att[0].shape[1]
    total = 2 * D + width
    whole = pl.BlockSpec((rows, D), lambda t, q: (0, 0))
    part = pl.BlockSpec((rows, D), lambda t, q: (0, t))
    spec = pltpu.PrefetchScalarGridSpec(
        num_scalar_prefetch=1,
        grid=(4,),
        in_specs=[part] * 2
        + [whole] * 3
        + [pl.BlockSpec((256, width), lambda t, q: (0, 0))] * 4,
        out_specs=pl.BlockSpec((D, total), lambda t, q: (q[1] ^ t, 0)),
    )
    return pl.pallas_call(
        weight_grad_kernel,
        grid_spec=spec,
        out_shape=jax.ShapeDtypeStruct((4 * D, total), bf16),
        compiler_params=pltpu.CompilerParams(vmem_limit_bytes=VMEM),
        name="weight_grads",
        cost_estimate=QUICK,
    )(places, act, pre, low, ffn_grad, branch_grad, *att)


def token_chunk(lay, g, c, place):
    core = place % 2
    half = jnp.where(c < 2, 1 - core, core)
    return half * (lay.tokens // 512) + g * 2 + c % 2


def collect_kernel(lay, g, place_ref, *refs):
    rows_refs = refs[: lay.arrays]
    code_ref, w_ref, h1_ref, other_ref, mine_ref, dense_ref = refs[lay.arrays :]
    chunk = pl.program_id(0)
    me, place = place_ref[0], place_ref[1]
    low = lane_iota(256) < HEAD_DIM
    firsts, seconds = [], []
    for h in range(lay.heads):
        column = as_column(code_ref[h, 0:1, :])
        half = as_column(code_ref[h, 1:2, :])
        planes = [block_rows(lay, rows_refs, (h * 3 + x) * lay.half_rows) for x in range(3)]
        found = nn(gather_matrix(lay, me, column), jnp.concatenate(planes, axis=1))
        one, two = [], []
        for x in range(3):
            part = found[:, x * LANES : (x + 1) * LANES]
            turned = pltpu.roll(part, HEAD_DIM, 1)
            one.append(jnp.where(half == 0, part, turned))
            two.append(jnp.where(half == 1, part, turned))
        firsts.append(one)
        seconds.append(two)
    tiles = [jnp.where(low, firsts[h][0], seconds[h][1]) for h in range(lay.heads)]
    for h in range(0, lay.heads, 2):
        right = seconds[h + 1][2] if h + 1 < lay.heads else jnp.zeros((256, LANES), f32)
        tiles.append(jnp.where(low, firsts[h][2], right))
    dense = jnp.concatenate(tiles, axis=1).astype(bf16)
    dense_ref[...] = dense
    part = nt(dense, w_ref[...])
    at = token_chunk(lay, g, chunk, place)
    own = (at // 2 == place).astype(f32)
    part = part + own * h1_ref[pl.ds(pl.multiple_of(at % 2 * 256, 256), 256), :]

    @pl.when(chunk < 2)
    def _():
        other_ref[...] = part.astype(bf16)

    @pl.when(chunk >= 2)
    def _():
        mine_ref[...] = part.astype(bf16)


def collect(lay, g, places, returned, code, weights, grad_h1):
    width = weights.shape[1]
    spec = pltpu.PrefetchScalarGridSpec(
        num_scalar_prefetch=1,
        grid=(4,),
        in_specs=lay.specs(lay.data_rows, only(0))
        + [
            pl.BlockSpec((lay.heads, 8, 256), lambda c, q: (0, 0, token_chunk(lay, g, c, q[1]))),
            pl.BlockSpec((D, width), lambda c, q: (0, 0)),
            pl.BlockSpec((512, D), lambda c, q: (0, 0)),
        ],
        out_specs=[
            pl.BlockSpec((256, D), lambda c, q: (jnp.minimum(c, 1), 0)),
            pl.BlockSpec((256, D), lambda c, q: (jnp.maximum(c - 2, 0), 0)),
            pl.BlockSpec((256, width), lambda c, q: (c, 0)),
        ],
    )
    return pl.pallas_call(
        partial(collect_kernel, lay, g),
        grid_spec=spec,
        out_shape=[
            jax.ShapeDtypeStruct((512, D), bf16),
            jax.ShapeDtypeStruct((512, D), bf16),
            jax.ShapeDtypeStruct((1024, width), bf16),
        ],
        compiler_params=pltpu.CompilerParams(vmem_limit_bytes=VMEM),
        name="collect",
        cost_estimate=QUICK,
    )(places, *returned, code, weights, grad_h1)


def head_grad_kernel(lay, place_ref, x_ref, dense0_ref, dense1_ref, vec_ref, *refs):
    outs, total_ref = refs[: lay.arrays], refs[-1]
    step = pl.program_id(0)

    @pl.when(step == 0)
    def _():
        total_ref[...] = tn(x_ref[...], dense0_ref[...])

    @pl.when((step > 0) & (step < 4))
    def _():
        total_ref[...] += tn(x_ref[...], dense0_ref[...])

    @pl.when(step >= 4)
    def _():
        total_ref[...] += tn(x_ref[...], dense1_ref[...])

    @pl.when(step == 7)
    def _():
        depth = D // lay.peers
        if not lay.direct:
            outs[0][...] = total_ref[...].astype(bf16)
            return
        for s in range(lay.peers):
            d = place_ref[0] ^ s
            outs[s][:depth, :] = total_ref[pl.ds(pl.multiple_of(d * depth, 8), depth), :].astype(bf16)
            vector = vec_ref[d]
            high = vector.astype(bf16).astype(f32)
            width = total_ref.shape[1]
            outs[s][depth:, :] = jnp.concatenate(
                [high, vector - high, jnp.zeros((16, width - 2 * LANES), f32)], axis=1
            ).astype(bf16)


def head_grads(lay, places, x, dense, vec):
    width = dense[0].shape[1]
    depth = D // lay.peers

    def token(s, q):
        return (token_chunk(lay, s // 4, s % 4, q[1]), 0)

    rows = depth + 16 if lay.direct else D
    whole = lambda s, q: (0, 0)
    spec = pltpu.PrefetchScalarGridSpec(
        num_scalar_prefetch=1,
        grid=(8,),
        in_specs=[
            pl.BlockSpec((256, D), token),
            pl.BlockSpec((256, width), lambda s, q: (jnp.minimum(s, 3), 0)),
            pl.BlockSpec((256, width), lambda s, q: (jnp.maximum(s - 4, 0), 0)),
            pl.BlockSpec(vec.shape, lambda s, q: (0, 0, 0)),
        ],
        out_specs=[pl.BlockSpec((rows, width), whole)] * lay.arrays,
        scratch_shapes=[pltpu.VMEM((D, width), f32)],
    )
    return pl.pallas_call(
        partial(head_grad_kernel, lay),
        grid_spec=spec,
        out_shape=[jax.ShapeDtypeStruct((rows, width), bf16)] * lay.arrays,
        compiler_params=pltpu.CompilerParams(vmem_limit_bytes=VMEM),
        name="head_grads",
        cost_estimate=QUICK,
    )(places, x, *dense, vec)


def finish_heads_kernel(*refs):
    parts, outs = refs[:-7], refs[-7:]
    depth, width = outs[0].shape
    heads = width // HEAD_DIM
    total = parts[0][...].astype(f32)
    for ref in parts[1:]:
        total = total + ref[...].astype(f32)
    grads = total[:depth]
    cut = [slice(h * LANES, h * LANES + HEAD_DIM) for h in range(heads)]
    outs[0][...] = jnp.concatenate([grads[:, at] for at in cut], axis=1)
    cut = [slice(h * LANES + HEAD_DIM, (h + 1) * LANES) for h in range(heads)]
    outs[1][...] = jnp.concatenate([grads[:, at] for at in cut], axis=1)
    outs[2][...] = grads[:, 2 * width : 3 * width]
    vectors = total[depth:, :depth] + total[depth:, LANES : LANES + depth]
    outs[3][...] = vectors[:4]
    outs[4][...] = vectors[4:6]
    outs[5][...] = vectors[6:8]
    outs[6][...] = vectors[8:12]


def finish_heads(parts, depth, width):
    shapes = [(depth, width)] * 3 + [(4, depth), (2, depth), (2, depth), (4, depth)]
    return pl.pallas_call(
        finish_heads_kernel,
        out_shape=[jax.ShapeDtypeStruct(s, f32) for s in shapes],
        name="finish_heads",
        cost_estimate=QUICK,
    )(*parts)


def finish_middle_kernel(grad_ref, inner_ref, outer_ref, output_ref):
    inner_ref[...] = grad_ref[:, :D].astype(f32)
    outer_ref[...] = grad_ref[:, D : 2 * D].astype(f32)
    rest = grad_ref[:, 2 * D :].astype(f32)
    planes = [rest[:, i * LANES : (i + 1) * LANES] for i in range(rest.shape[1] // LANES)]
    folded = [p[:, :HEAD_DIM] + p[:, HEAD_DIM:] for p in planes]
    output_ref[...] = jnp.concatenate(folded, axis=1).T


def finish_middle(grads):
    depth, total = grads.shape
    return pl.pallas_call(
        finish_middle_kernel,
        out_shape=[
            jax.ShapeDtypeStruct((depth, D), f32),
            jax.ShapeDtypeStruct((depth, D), f32),
            jax.ShapeDtypeStruct(((total - 2 * D) // 2, depth), f32),
        ],
        name="finish_middle",
        cost_estimate=QUICK,
    )(grads)


def order_kernel(place_ref, *refs):
    for i in range(4):

        @pl.when(pl.program_id(0) == i)
        def _():
            refs[4][...] = refs[i][...]


def order_quarters(order, quarters):
    rows, width = quarters[0].shape
    cuts = 2
    cut = rows // cuts

    def source(i):
        return lambda s, r, q: (jnp.where(s == i, r, jnp.where(s < i, 0, cuts - 1)), 0)

    spec = pltpu.PrefetchScalarGridSpec(
        num_scalar_prefetch=1,
        grid=(4, cuts),
        in_specs=[pl.BlockSpec((cut, width), source(i)) for i in range(4)],
        out_specs=pl.BlockSpec((cut, width), lambda s, r, q: (q[s] * cuts + r, 0)),
    )
    return pl.pallas_call(
        order_kernel,
        grid_spec=spec,
        out_shape=jax.ShapeDtypeStruct((4 * rows, width), quarters[0].dtype),
        name="order_quarters",
        cost_estimate=QUICK,
    )(order, *quarters)


def over_rows(lay, blocks):
    if not lay.direct:
        return [lax.all_to_all(blocks[0], "dp", split_axis=0, concat_axis=0, tiled=True)]
    out = [blocks[0]]
    for s in range(1, lay.peers):
        out.append(lax.ppermute(blocks[s], "dp", [(i, i ^ s) for i in range(lay.peers)]))
    return out


def in_hbm(rows):
    return pltpu.with_memory_space_constraint(rows, pltpu.HBM)


def after(value, *others):
    return lax.optimization_barrier((value, *others))[0]


def swap(rows, flip):
    return lax.ppermute(rows, "mp", [(i, i ^ flip) for i in range(4)])


def over_heads(blocks):
    return [blocks[0]] + [swap(blocks[t], t) for t in range(1, 4)]


def on_device(
    hidden_in,
    cotangent,
    w_query,
    w_key,
    w_value,
    w_output,
    w_inner,
    w_outer,
    biases,
    gains,
    shifts,
    inner_bias,
    lengths,
    padding,
    cluster_perm,
):
    peers = lax.axis_size("dp")
    tokens = hidden_in.shape[0]
    heads = cluster_perm.shape[0]
    lay = Layout(peers, tokens, heads)
    place = lax.axis_index("mp")
    me = lax.axis_index("dp")
    places = jnp.stack([me, place]).astype(i32)
    hidden_in = in_hbm(hidden_in)
    depth = w_query.shape[0]
    width = heads * HEAD_DIM

    piece, shard, outer_shard = pack_weights(
        w_query, w_key, w_value, w_output, w_inner, w_outer.T,
        biases, gains, shifts, inner_bias.reshape(1, -1),
    )
    inner_w = lax.all_gather(shard, "dp", axis=0, tiled=True)
    outer_w = lax.all_gather(outer_shard, "dp", axis=0, tiled=True)
    if lay.direct:
        weights, bias, params = assemble_weights(lay, places, over_rows(lay, [piece] * peers))
    else:
        weights, bias, params = gather_weights(lay, place, piece)

    weights = in_hbm(weights)
    code = in_hbm(place_tokens(lay, cluster_perm))
    sent = project_rows(lay, places, hidden_in, weights, bias, code, padding.reshape(1, tokens))
    inner_w = after(inner_w, sent[0])
    far_inner = swap(inner_w, 2)
    arrived = over_rows(lay, sent)
    outer_w = after(outer_w, *arrived)
    far_outer = swap(outer_w, 2)
    mixed = over_rows(lay, attend(lay, arrived))
    far_inner, far_outer = after(far_inner, *mixed), after(far_outer, *mixed)
    middle_w = [inner_w, swap(inner_w, 1), far_inner, swap(far_inner, 1)]
    middle_w += [outer_w, swap(outer_w, 1), far_outer, swap(far_outer, 1)]
    att = over_heads(unsort_rows(lay, places, mixed, code))
    saved, att_grad, vec = middle(places, att, hidden_in, cotangent, params, middle_w)
    out_quarter, act, pre_grad, first_low, ffn_grad, branch_grad, grad_h1 = saved
    saved = tuple(in_hbm(a) for a in (act, pre_grad, first_low, ffn_grad, branch_grad))
    att = [in_hbm(a) for a in att]

    got = over_heads(att_grad)
    far = swap(out_quarter, 2)
    summed = weight_grads(places, saved, att)
    grad_h1 = in_hbm(grad_h1)
    summed = lax.psum_scatter(summed, "mp", scatter_dimension=0, tiled=True)
    grads = over_rows(lay, sort_rows(lay, places, got, code))
    grads[0] = after(grads[0], far)
    slot_grads, bias_sums = attend_back(lay, arrived, grads)

    returned = over_rows(lay, slot_grads)
    reduced = lax.psum_scatter(
        after(summed, *returned), "dp", scatter_dimension=0, tiled=True
    )
    hidden_out = order_quarters(
        jnp.stack([place, place ^ 2, place ^ 1, place ^ 3]).astype(i32),
        [out_quarter, after(far, slot_grads[0]), swap(out_quarter, 1), swap(far, 1)],
    )
    head_sums = bias_sums[:, :2].reshape(heads, 2, 2, HEAD_DIM).sum(axis=2)
    head_sums = head_sums.transpose(1, 0, 2).reshape(2, width)
    vec = lax.dynamic_update_slice(vec[:12], head_sums, (0, place * width))
    vec = vec + swap(vec, 1)
    vec = vec + swap(vec, 2)
    vec = jnp.concatenate(
        [vec[:8].reshape(8, peers, depth).transpose(1, 0, 2), vec[8:].reshape(peers, 4, depth)],
        axis=1,
    )
    spread = jnp.pad(vec, ((0, 0), (0, 4), (0, (-depth) % LANES)))
    ready_code = after(code, hidden_out, spread)
    groups = [
        collect(lay, g, places, returned, ready_code, weights, grad_h1) for g in range(2)
    ]
    chips = [
        (mine.astype(f32) + swap(other, 1).astype(f32)).astype(bf16) for other, mine, _ in groups
    ]
    terms = head_grads(lay, places, hidden_in, [dense for _, _, dense in groups], spread)
    if lay.direct:
        ends = finish_heads(over_rows(lay, terms), depth, width)
    else:
        ends = reduce_heads(terms[0], vec, depth, width)
    ready = [
        (after(chip, ends[0]).astype(f32) + swap(chip, 2).astype(f32)).astype(bf16)
        for chip in chips
    ]
    core = place % 2
    grad_hidden = order_quarters(
        jnp.stack([2 * core, 2 * core + 1, 2 - 2 * core, 3 - 2 * core]).astype(i32),
        ready + [swap(part, 1) for part in ready],
    )

    grad_inner, grad_outer, grad_output = finish_middle(reduced)
    return (
        hidden_out,
        grad_hidden,
        ends[0],
        ends[1],
        ends[2],
        grad_output,
        grad_inner,
        grad_outer.T,
        ends[3],
        ends[4],
        ends[5],
        ends[6].reshape(-1),
    )


def gather_weights(lay, place, piece):
    depth = D // lay.peers
    width = lay.heads * HEAD_DIM
    got = lax.all_gather(piece, "dp", axis=0, tiled=False)
    weights = got[:, :depth].reshape(D, -1)
    vectors = got[:, depth : depth + 12, :depth].astype(f32)
    params = vectors[:, :8].transpose(1, 0, 2).reshape(8, D)
    params = jnp.concatenate([params, vectors[:, 8:].reshape(4, D), jnp.zeros((4, D), f32)], axis=0)
    own = lax.dynamic_slice_in_dim(params[:2], place * width, width, 1)
    query = own[0].reshape(lay.heads, HEAD_DIM)
    query = jnp.concatenate([query, jnp.zeros_like(query)], axis=1).reshape(-1)
    row = jnp.concatenate([query, own[1], jnp.zeros(weights.shape[1] - 3 * width, f32)])
    return weights, jnp.broadcast_to(row[None], (8, row.shape[0])), params


def reduce_heads(grads, vec, depth, width):
    total = lax.psum_scatter(grads, "dp", scatter_dimension=0, tiled=True).astype(f32)
    pairs = total[:, : 2 * width].reshape(depth, -1, 2, HEAD_DIM)
    small = lax.psum_scatter(vec, "dp", scatter_dimension=0, tiled=False)
    return (
        pairs[:, :, 0].reshape(depth, width),
        pairs[:, :, 1].reshape(depth, width),
        total[:, 2 * width : 3 * width],
        small[:4],
        small[4:6],
        small[6:8],
        small[8:],
    )


def solution(mesh):
    placed = (
        P("dp", None),
        P("dp", None),
        P("dp", "mp"),
        P("dp", "mp"),
        P("dp", "mp"),
        P("mp", "dp"),
        P("dp", "mp"),
        P("mp", "dp"),
        P(None, "dp"),
        P(None, "dp"),
        P(None, "dp"),
        P("dp"),
        P(),
        P("dp"),
        P("mp", "dp"),
    )
    return jax.shard_map(
        on_device,
        mesh=mesh,
        in_specs=placed,
        out_specs=(
            P("dp", None),
            P("dp", None),
            P("dp", "mp"),
            P("dp", "mp"),
            P("dp", "mp"),
            P("mp", "dp"),
            P("dp", "mp"),
            P("mp", "dp"),
            P(None, "dp"),
            P(None, "dp"),
            P(None, "dp"),
            P("dp"),
        ),
        check_vma=False,
    )
```

```python
from functools import partial
import math

import jax
import jax.numpy as jnp
from jax import lax
from jax.experimental import pallas as pl
from jax.experimental.pallas import tpu as pltpu
from jax.sharding import PartitionSpec as P

D = 768
HEAD_DIM = 64
FF = 3072
CLUSTER = 128
LANES = 128
EPSILON = 1e-05
MASKED = -1e30
SCALE = 1.0 / math.sqrt(HEAD_DIM)

bf16 = jnp.bfloat16
f32 = jnp.float32
i32 = jnp.int32

VMEM = 60 * 1024 * 1024


def cost(us):
    return pl.CostEstimate(flops=int(1e9 * us), bytes_accessed=int(3e6 * us), transcendentals=0)


QUICK = cost(0.001)
ATTEND_US = 46
COLLECT_US = 30
COLLECT_ROWS = 512
SPREAD_US = 6
HEAD_GRADS_US = 12


def nn(a, b):
    return lax.dot_general(a, b, (((1,), (0,)), ((), ())), preferred_element_type=f32)


def nt(a, b):
    return lax.dot_general(a, b, (((1,), (1,)), ((), ())), preferred_element_type=f32)


def tn(a, b):
    return lax.dot_general(a, b, (((0,), (0,)), ((), ())), preferred_element_type=f32)


def lane_iota(rows, lanes=LANES):
    return lax.broadcasted_iota(i32, (rows, lanes), 1)


def sublane_iota(rows, lanes=LANES):
    return lax.broadcasted_iota(i32, (rows, lanes), 0)


def as_column(row):
    parts = [
        jnp.broadcast_to(row[:, i * LANES : (i + 1) * LANES], (LANES, LANES)).T
        for i in range(row.shape[1] // LANES)
    ]
    return parts[0] if len(parts) == 1 else jnp.concatenate(parts, axis=0)


class Layout:
    def __init__(self, peers, tokens, heads):
        self.peers, self.tokens, self.heads = peers, tokens, heads
        self.stripe = min(16, peers)
        self.runs = peers // self.stripe
        self.per_dev = CLUSTER // self.stripe
        self.rows_peer = tokens // peers
        self.half_rows = self.rows_peer // 2
        self.pairs = self.half_rows // self.per_dev
        self.packed = tokens // 2
        self.clusters = peers * tokens // CLUSTER
        self.data_rows = 9 * self.half_rows
        self.direct = self.half_rows == LANES
        self.arrays = peers if self.direct else 1

    def peer(self, me, s):
        return (me ^ s) if self.direct else s

    def shapes(self, rows, dtype=bf16):
        lead = () if self.direct else (self.peers,)
        return [jax.ShapeDtypeStruct(lead + (rows, LANES), dtype)] * self.arrays

    def specs(self, rows, at):
        if self.direct:
            return [pl.BlockSpec((rows, LANES), lambda *g: (at(*g), 0))] * self.arrays
        return [pl.BlockSpec((self.peers, rows, LANES), lambda *g: (0, at(*g), 0))]

    def view(self, refs, s):
        return refs[s] if self.direct else refs[0].at[s]


def only(at):
    return lambda *g: at


def place_kernel(lay, perm_ref, code_ref):
    groups = lay.clusters
    shift = CLUSTER.bit_length() - 1
    blocks = lay.tokens // LANES
    before = sublane_iota(LANES, 2 * LANES)
    after = lane_iota(LANES, 2 * LANES)
    ahead_of = jnp.where((before < after) | (after >= LANES), 1.0, 0.0).astype(bf16)

    def members(h, b):
        row = lax.shift_right_logical(perm_ref[h : h + 1, b * LANES : (b + 1) * LANES], shift)
        return jnp.broadcast_to(row, (groups, LANES)) == sublane_iota(groups)

    for h in range(lay.heads):
        if lay.runs == 1:
            carry = (sublane_iota(groups) * lay.per_dev).astype(f32)
        else:
            counts = jnp.zeros((groups, LANES), f32)
            for b in range(blocks):
                member = jnp.where(members(h, b), 1.0, 0.0).astype(bf16)
                counts = counts + nn(member, ahead_of)[:, LANES:]
            lower = jnp.where(
                sublane_iota(groups, groups) > lane_iota(groups, groups), 1.0, 0.0
            ).astype(bf16)
            carry = nn(lower, counts.astype(bf16))
        for b in range(blocks):
            member = members(h, b)
            found = nn(jnp.where(member, 1.0, 0.0).astype(bf16), ahead_of)
            rank = jnp.sum(jnp.where(member, found[:, :LANES] + carry, 0.0), axis=0, keepdims=True)
            carry = carry + found[:, LANES:]
            rank = rank.astype(i32)
            peer = lax.shift_right_logical(rank, lay.rows_peer.bit_length() - 1)
            rest = rank & (lay.rows_peer - 1)
            half = lax.shift_right_logical(rest, lay.half_rows.bit_length() - 1)
            packed = peer * lay.half_rows + (rest & (lay.half_rows - 1))
            at = slice(b * LANES, (b + 1) * LANES)
            code_ref[h, 0:1, at] = packed
            code_ref[h, 1:2, at] = half


def place_tokens(lay, perm):
    return pl.pallas_call(
        partial(place_kernel, lay),
        out_shape=jax.ShapeDtypeStruct((lay.heads, 8, lay.tokens), i32),
        name="place_tokens",
        cost_estimate=QUICK,
    )(perm)


def one_hot(equal):
    return jnp.where(equal, 1.0, 0.0).astype(bf16)


def scatter_matrix(lay, me, packed, s, blocks):
    rows = blocks * lay.half_rows
    if lay.direct:
        parts = [
            one_hot(
                jnp.broadcast_to(packed, (lay.half_rows, lay.tokens))
                == sublane_iota(lay.half_rows, lay.tokens) + lay.peer(me, s + i) * lay.half_rows
            )
            for i in range(blocks)
        ]
        return jnp.concatenate(parts, axis=0)
    wanted = sublane_iota(rows, lay.tokens) + s * lay.half_rows
    return one_hot(jnp.broadcast_to(packed, (rows, lay.tokens)) == wanted)


def gather_matrix(lay, me, column):
    lane = lane_iota(column.shape[0])
    parts = [
        one_hot(column == lane + lay.peer(me, k) * LANES) for k in range(lay.packed // LANES)
    ]
    return jnp.concatenate(parts, axis=1)


def block_rows(lay, refs, first):
    at = slice(first, first + lay.half_rows)
    if lay.direct:
        return jnp.concatenate([refs[s][at, :] for s in range(lay.peers)], axis=0)
    return refs[0][:, at, :].astype(f32).reshape(lay.packed, LANES).astype(bf16)


def put_blocks(lay, refs, s, blocks, first, rows):
    at = slice(first, first + lay.half_rows) if isinstance(first, int) else pl.ds(first, lay.half_rows)
    if lay.direct:
        for i in range(blocks):
            refs[s + i][at, :] = rows[i * LANES : (i + 1) * LANES].astype(bf16)
    else:
        rows = rows.astype(f32).reshape(blocks, lay.half_rows, LANES).astype(bf16)
        refs[0][s : s + blocks, at, :] = rows


ROWS = 512
COUNT = 4


def project_kernel(lay, steps, place_ref, x_ref, w_ref, bias_ref, code_ref, pad_ref, *rest):
    outs = rest[: lay.arrays]
    rows_ref, flag_ref = rest[lay.arrays :]
    step = pl.program_id(0)
    me = place_ref[0]
    width = 4 * LANES

    @pl.when(step < steps)
    def _():
        at = pl.ds(pl.multiple_of(step * ROWS, ROWS), ROWS)
        values = nn(x_ref[...], w_ref[...]) + bias_ref[0:1, :]
        low = lane_iota(ROWS) < HEAD_DIM
        lane_half = jnp.where(low, 0, 1)
        live = as_column(pad_ref[0:1, at])
        tiles = [values[:, i * LANES : (i + 1) * LANES] for i in range(values.shape[1] // LANES)]
        turned = [pltpu.roll(tile, HEAD_DIM, 1) for tile in tiles]
        for h in range(lay.heads):
            half = as_column(code_ref[h, 1:2, at])
            keep = half == lane_half
            v, side = lay.heads + h // 2, h % 2
            planes = (
                jnp.where(low, tiles[h], turned[h]),
                jnp.where(low, turned[h], tiles[h]),
                jnp.where(low, tiles[v], turned[v]) if side == 0 else jnp.where(low, turned[v], tiles[v]),
            )
            for x, plane in enumerate(planes):
                rows_ref[h, at, x * LANES : (x + 1) * LANES] = jnp.where(keep, plane, 0.0).astype(bf16)
            flags = jnp.where((lane_iota(ROWS) == half) & (live == 1), 1.0, 0.0)
            rows_ref[h, at, 3 * LANES :] = flags.astype(bf16)

    count = COUNT if lay.direct else 32
    for h in range(lay.heads):

        @pl.when(step == steps + h)
        def _():
            for s in range(0, lay.peers, count):
                chosen = scatter_matrix(lay, me, code_ref[h, 0:1, :], s, count)
                moved = nn(chosen, rows_ref[h])
                for x in range(3):
                    put_blocks(
                        lay, outs, s, count, (h * 3 + x) * lay.half_rows,
                        moved[:, x * LANES : (x + 1) * LANES],
                    )
                for i in range(count * lay.half_rows // LANES):
                    at = slice(s * lay.half_rows + i * LANES, s * lay.half_rows + (i + 1) * LANES)
                    flag_ref[h, :, at] = moved[i * LANES : (i + 1) * LANES, 3 * LANES :].T[:8]

    @pl.when(step == steps + lay.heads - 1)
    def _():
        for s in range(lay.peers):
            at = slice(s * lay.half_rows, (s + 1) * lay.half_rows)
            rows = [flag_ref[k, 0:2, at] for k in range(lay.heads)]
            block = jnp.concatenate(rows + [jnp.zeros((16 - 2 * lay.heads, lay.half_rows), f32)], axis=0)
            if lay.half_rows < LANES:
                block = jnp.concatenate(
                    [block, jnp.zeros((16, LANES - lay.half_rows), f32)], axis=1
                )
            lay.view(outs, s)[lay.data_rows : lay.data_rows + 16, :] = block.astype(bf16)


def project_rows(lay, places, x, weights, bias, code, pad):
    width = weights.shape[1]
    steps = lay.tokens // ROWS
    spec = pltpu.PrefetchScalarGridSpec(
        num_scalar_prefetch=1,
        grid=(steps + lay.heads,),
        in_specs=[
            pl.BlockSpec((ROWS, D), lambda s, _: (jnp.minimum(s, steps - 1), 0)),
            pl.BlockSpec((D, width), lambda s, _: (0, 0)),
            pl.BlockSpec((8, width), lambda s, _: (0, 0)),
            pl.BlockSpec((lay.heads, 8, lay.tokens), lambda s, _: (0, 0, 0)),
            pl.BlockSpec((1, lay.tokens), lambda s, _: (0, 0)),
        ],
        out_specs=lay.specs(lay.data_rows + 16, only(0)),
        scratch_shapes=[
            pltpu.VMEM((lay.heads, lay.tokens, 4 * LANES), bf16),
            pltpu.VMEM((lay.heads, 8, lay.packed), f32),
        ],
    )
    return pl.pallas_call(
        partial(project_kernel, lay, steps),
        grid_spec=spec,
        out_shape=lay.shapes(lay.data_rows + 16),
        compiler_params=pltpu.CompilerParams(vmem_limit_bytes=VMEM),
        name="project_rows",
        cost_estimate=QUICK,
    )(places, x, weights, bias, code, pad)


def pair_rows(lay, refs, first, run, p):
    at = slice(first + p * lay.per_dev, first + (p + 1) * lay.per_dev)
    if lay.direct:
        return jnp.concatenate([refs[s][at, :] for s in range(lay.stripe)], axis=0)
    block = refs[0][run * lay.stripe : (run + 1) * lay.stripe, first : first + lay.half_rows, :]
    block = block.astype(f32)[:, p * lay.per_dev : (p + 1) * lay.per_dev, :]
    return block.reshape(CLUSTER, LANES).astype(bf16)


def put_pair(lay, refs, first, run, p, rows):
    at = slice(first + p * lay.per_dev, first + (p + 1) * lay.per_dev)
    for s in range(lay.stripe):
        part = rows[s * lay.per_dev : (s + 1) * lay.per_dev]
        lay.view(refs, run * lay.stripe + s)[at, :] = part.astype(bf16)


def live_columns(lay, flags, h):
    pick = one_hot(sublane_iota(16, 2 * LANES) == 2 * h + lane_iota(16, 2 * LANES) // LANES)
    return [tn(lay.view(flags, s)[...], pick) for s in range(lay.peers)]


def allowed_pair(lay, columns, run, p):
    at = slice(p * lay.per_dev, (p + 1) * lay.per_dev)
    live = jnp.concatenate([columns[run * lay.stripe + s][at] for s in range(lay.stripe)], axis=0)
    live = jnp.concatenate([live[:, :LANES], live[:, LANES:]], axis=0)
    same = sublane_iota(2 * CLUSTER) % CLUSTER == lane_iota(2 * CLUSTER)
    return (live > 0.5) | same


def stack_halves(rows):
    low = lane_iota(rows.shape[0], rows.shape[1]) < HEAD_DIM
    zero = jnp.zeros_like(rows)
    return jnp.concatenate([jnp.where(low, rows, zero), jnp.where(low, zero, rows)], axis=0)


def each_half(fold, rows):
    one, two = (
        jnp.broadcast_to(fold(part, axis=0, keepdims=True), part.shape)
        for part in (rows[:CLUSTER], rows[CLUSTER:])
    )
    return jnp.concatenate([one, two], axis=0)


def inverse_sum(rows, axis, keepdims):
    return 1.0 / jnp.sum(rows, axis=axis, keepdims=keepdims)


def soft_weights(queries, keys, allowed):
    scores = jnp.where(allowed, nt(keys, queries) * SCALE, MASKED)
    grown = jnp.exp(scores - each_half(jnp.max, scores))
    return grown * each_half(inverse_sum, grown)


def attend_kernel(lay, *refs):
    rows, flags, outs = (refs[i * lay.arrays : (i + 1) * lay.arrays] for i in range(3))
    live = live_columns(lay, flags, pl.program_id(0))
    for run in range(lay.runs):
        for p in range(lay.pairs):
            q, k, v = (pair_rows(lay, rows, x * lay.half_rows, run, p) for x in range(3))
            soft = soft_weights(q, stack_halves(k), allowed_pair(lay, live, run, p))
            put_pair(lay, outs, 0, run, p, tn(soft.astype(bf16), stack_halves(v)))


def attend(lay, arrived):
    head = lambda h: h
    return pl.pallas_call(
        partial(attend_kernel, lay),
        grid=(lay.heads,),
        in_specs=lay.specs(3 * lay.half_rows, head) + lay.specs(16, only(lay.data_rows // 16)),
        out_specs=lay.specs(lay.half_rows, head),
        out_shape=lay.shapes(lay.heads * lay.half_rows),
        name="attend",
        cost_estimate=cost(ATTEND_US),
    )(*arrived, *arrived)


def attend_back_kernel(lay, *refs):
    rows, flags, grads, outs = (refs[i * lay.arrays : (i + 1) * lay.arrays] for i in range(4))
    sum_ref = refs[-1]
    live = live_columns(lay, flags, pl.program_id(0))
    low = lane_iota(CLUSTER) < HEAD_DIM
    sums = [jnp.zeros((1, LANES), f32)] * 2
    for run in range(lay.runs):
        for p in range(lay.pairs):
            q, k, v = (pair_rows(lay, rows, x * lay.half_rows, run, p) for x in range(3))
            g = pair_rows(lay, grads, 0, run, p)
            keys = stack_halves(k)
            soft = soft_weights(q, keys, allowed_pair(lay, live, run, p))
            grad_soft = nt(stack_halves(v), g)
            delta = each_half(jnp.sum, soft * grad_soft)
            grad = (soft * (grad_soft - delta)).astype(bf16)
            grad_q = (tn(grad, keys) * SCALE).astype(bf16)
            part = nn(grad, q)
            grad_k = (jnp.where(low, part[:CLUSTER], part[CLUSTER:]) * SCALE).astype(bf16)
            part = nn(soft.astype(bf16), g)
            grad_v = jnp.where(low, part[:CLUSTER], part[CLUSTER:]).astype(bf16)
            for x, part in enumerate((grad_q, grad_k, grad_v)):
                put_pair(lay, outs, x * lay.half_rows, run, p, part)
            sums[0] = sums[0] + jnp.sum(grad_q.astype(f32), axis=0, keepdims=True)
            sums[1] = sums[1] + jnp.sum(grad_v.astype(f32), axis=0, keepdims=True)
    sum_ref[0] = jnp.concatenate(sums + [jnp.zeros((6, LANES), f32)], axis=0)


def attend_back(lay, arrived, grads):
    head = lambda h: h
    three = lay.specs(3 * lay.half_rows, head)
    out = pl.pallas_call(
        partial(attend_back_kernel, lay),
        grid=(lay.heads,),
        in_specs=three
        + lay.specs(16, only(lay.data_rows // 16))
        + lay.specs(lay.half_rows, head),
        out_specs=three + [pl.BlockSpec((1, 8, LANES), lambda h: (h, 0, 0))],
        out_shape=lay.shapes(lay.data_rows)
        + [jax.ShapeDtypeStruct((lay.heads, 8, LANES), f32)],
        name="attend_back",
        cost_estimate=QUICK,
    )(*arrived, *arrived, *grads)
    return list(out[:-1]), out[-1]


def side_rows(quarter, side):
    return pl.ds(pl.multiple_of(quarter * 512 + side * 256, 256), 256)


def unsort_kernel(lay, place_ref, *refs):
    rows_refs, code_ref, outs = refs[: lay.arrays], refs[lay.arrays], refs[lay.arrays + 1 :]
    rows = block_rows(lay, rows_refs, 0)
    low = lane_iota(256) < HEAD_DIM
    me, place = place_ref[0], place_ref[1]

    for t in range(4):
        sides = []
        for side in range(2):
            at = side_rows(place ^ t, side)
            column = as_column(code_ref[0, 0:1, at])
            half = as_column(code_ref[0, 1:2, at])
            found = nn(gather_matrix(lay, me, column), rows)
            sides.append(jnp.where(half == side, found, pltpu.roll(found, HEAD_DIM, 1)))
        outs[t][...] = jnp.where(low, sides[0], sides[1]).astype(bf16)


def unsort_rows(lay, places, returned, code):
    spec = pltpu.PrefetchScalarGridSpec(
        num_scalar_prefetch=1,
        grid=(lay.heads,),
        in_specs=lay.specs(lay.half_rows, lambda h, _: h)
        + [pl.BlockSpec((1, 8, lay.tokens), lambda h, _: (h, 0, 0))],
        out_specs=[pl.BlockSpec((256, LANES), lambda h, _: (0, h))] * 4,
    )
    return pl.pallas_call(
        partial(unsort_kernel, lay),
        grid_spec=spec,
        out_shape=[jax.ShapeDtypeStruct((256, lay.heads * LANES), bf16)] * 4,
        name="unsort_rows",
        cost_estimate=QUICK,
    )(places, *returned, code)


def sort_kernel(lay, place_ref, *refs):
    grads, code_ref, outs, rows_ref = refs[:4], refs[4], refs[5:-1], refs[-1]
    low = lane_iota(256) < HEAD_DIM
    lane_half = jnp.where(low, 0, 1)
    me, place = place_ref[0], place_ref[1]

    for t in range(4):
        block = grads[t][...].astype(f32)
        turned = pltpu.roll(block, HEAD_DIM, 1)
        for side in range(2):
            at = side_rows(place ^ t, side)
            half = as_column(code_ref[0, 1:2, at])
            both = jnp.where(low, block, turned) if side == 0 else jnp.where(low, turned, block)
            rows_ref[at, :] = jnp.where(half == lane_half, both, 0.0).astype(bf16)

    count = 4 if lay.direct else 32
    for s in range(0, lay.peers, count):
        chosen = scatter_matrix(lay, me, code_ref[0, 0:1, :], s, count)
        put_blocks(lay, outs, s, count, 0, nn(chosen, rows_ref[...]))


def sort_rows(lay, places, grads, code):
    spec = pltpu.PrefetchScalarGridSpec(
        num_scalar_prefetch=1,
        grid=(lay.heads,),
        in_specs=[pl.BlockSpec((256, LANES), lambda h, _: (0, h))] * 4
        + [pl.BlockSpec((1, 8, lay.tokens), lambda h, _: (h, 0, 0))],
        out_specs=lay.specs(lay.half_rows, lambda h, _: h),
        scratch_shapes=[pltpu.VMEM((lay.tokens, LANES), bf16)],
    )
    return pl.pallas_call(
        partial(sort_kernel, lay),
        grid_spec=spec,
        out_shape=lay.shapes(lay.heads * lay.half_rows),
        name="sort_rows",
        cost_estimate=QUICK,
    )(places, *grads, code)


def pack_kernel(
    query_ref, key_ref, value_ref, output_ref, inner_ref, outer_ref,
    bias_ref, gain_ref, shift_ref, inner_bias_ref, piece_ref, shard_ref,
):
    depth, width = query_ref.shape
    heads = width // HEAD_DIM
    query, key, value = (ref[...].astype(f32) for ref in (query_ref, key_ref, value_ref))
    cut = [slice(h * HEAD_DIM, (h + 1) * HEAD_DIM) for h in range(heads)]
    columns = [part for at in cut for part in (query[:, at], key[:, at])] + [value]
    have = 3 * width
    fill = -have % LANES
    if fill:
        columns.append(jnp.zeros((depth, fill), f32))
    columns = jnp.concatenate(columns, axis=1).astype(bf16)
    piece_ref[:depth, : have + fill] = columns
    inner_bias = inner_bias_ref[...].astype(f32)
    vectors = jnp.concatenate(
        [ref[...].astype(f32) for ref in (bias_ref, gain_ref, shift_ref)]
        + [inner_bias[:, i * depth : (i + 1) * depth] for i in range(4)]
        + [jnp.zeros((4, depth), f32)],
        axis=0,
    )
    if depth < LANES:
        vectors = jnp.concatenate([vectors, jnp.zeros((16, LANES - depth), f32)], axis=1)
    piece_ref[:16, have + fill :] = vectors.astype(bf16)
    shard_ref[:, :D] = inner_ref[...]
    turned = output_ref[...].astype(f32).T
    shard_ref[:, D : 2 * D] = outer_ref[...]
    shard_ref[:, 2 * D :] = jnp.concatenate(
        [turned[:, at] for at in cut for _ in range(2)], axis=1
    ).astype(bf16)


def pack_weights(*arrays):
    depth, width = arrays[0].shape
    columns = -(-3 * width // LANES) * LANES
    return pl.pallas_call(
        pack_kernel,
        out_shape=[
            jax.ShapeDtypeStruct((max(depth, 16), columns + LANES), bf16),
            jax.ShapeDtypeStruct((depth, 2 * D + 2 * width), bf16),
        ],
        name="pack_weights",
        cost_estimate=QUICK,
    )(*arrays)


def assemble_kernel(lay, place_ref, *refs):
    pieces, (weight_ref, bias_ref, par_ref, part_ref) = refs[: lay.peers], refs[lay.peers :]
    me, place = place_ref[0], place_ref[1]
    depth = D // lay.peers
    for s in range(lay.peers):
        d = me ^ s
        at = pl.ds(pl.multiple_of(d * depth, 16), depth)
        columns = weight_ref.shape[1]
        weight_ref[at, :] = pieces[s][:, :columns]
        part_ref[d] = pieces[s][:16, columns:].astype(f32)

    def whole(row, rows=1, peers=range(lay.peers)):
        return jnp.concatenate(
            [part_ref[d, row + i : row + i + 1, :depth] for d in peers for i in range(rows)], axis=1
        )

    vectors = [whole(r) for r in range(8)]
    each = lay.peers // 4
    vectors += [whole(8, 4, range(j * each, (j + 1) * each)) for j in range(4)]
    par_ref[...] = jnp.concatenate(vectors + [jnp.zeros((4, D), f32)], axis=0)
    width = lay.heads * HEAD_DIM

    def own(vector):
        out = vector[:, :width]
        for p in range(1, D // width):
            out = jnp.where(place == p, vector[:, p * width : (p + 1) * width], out)
        return out

    query = own(vectors[0])
    zero = jnp.zeros((1, HEAD_DIM), f32)
    columns = [
        part for h in range(lay.heads) for part in (query[:, h * HEAD_DIM : (h + 1) * HEAD_DIM], zero)
    ] + [own(vectors[1])]
    fill = bias_ref.shape[1] - 3 * width
    if fill:
        columns.append(jnp.zeros((1, fill), f32))
    bias_ref[...] = jnp.broadcast_to(jnp.concatenate(columns, axis=1), bias_ref.shape)


def assemble_weights(lay, places, pieces):
    columns = pieces[0].shape[1] - LANES
    vmem = pl.BlockSpec(memory_space=pltpu.VMEM)
    return pl.pallas_call(
        partial(assemble_kernel, lay),
        in_specs=[pl.BlockSpec(memory_space=pltpu.SMEM)] + [vmem] * lay.peers,
        out_specs=[vmem] * 3,
        out_shape=[
            jax.ShapeDtypeStruct((D, columns), bf16),
            jax.ShapeDtypeStruct((8, columns), f32),
            jax.ShapeDtypeStruct((16, D), f32),
        ],
        scratch_shapes=[pltpu.VMEM((lay.peers, 16, LANES), f32)],
        name="assemble_weights",
        cost_estimate=QUICK,
    )(places, *pieces)


def mean_rows(v):
    return jnp.sum(v, axis=1, keepdims=True) * (1.0 / D)


def norm_forward(rows):
    centred = rows - mean_rows(rows)
    inv = lax.rsqrt(mean_rows(centred * centred) + EPSILON)
    return centred * inv, inv


def norm_backward(scaled, normed, inv):
    return inv * (scaled - mean_rows(scaled) - normed * mean_rows(scaled * normed))


TALL = 512


def middle_kernel(
    place_ref,
    att0,
    att1,
    att2,
    att3,
    hidden_ref,
    cot_ref,
    par_ref,
    w0,
    w1,
    w2,
    w3,
    out_ref,
    act_ref,
    pre_ref,
    low_ref,
    ffn_grad_ref,
    branch_grad_ref,
    h1_ref,
    grad0,
    grad1,
    grad2,
    grad3,
    vec_ref,
    first_ref,
    normed_ref,
    inv_ref,
    slope_ref,
    sum_ref,
    h2_ref,
    weight_ref,
    sems,
):
    step = pl.program_id(0)
    place = place_ref[1]
    project = slice(2 * D, None)

    def fetch(t, part):
        width = att0.shape[1]
        at = (pl.ds(2 * D, width), pl.ds(0, 2 * D))[part]
        source = (w0, w1, w2, w3)[t]
        return pltpu.make_async_copy(source.at[:, at], weight_ref.at[t, :, at], sems.at[part, t])

    for t in range(4):

        @pl.when(step == t + 1)
        def _():
            fetch(t, 1).wait()

    @pl.when(step == 0)
    def _():
        for t in range(4):
            fetch(t, 0).start()
        for t in range(4):
            fetch(t, 1).start()
        for t in range(4):
            fetch(t, 0).wait()
        vec_ref[...] = jnp.zeros_like(vec_ref)
        for side in range(2):
            branch = jnp.zeros((256, D), f32)
            for t, att_ref in enumerate((att0, att1, att2, att3)):
                att = att_ref[...]
                lane = lane_iota(256, att.shape[1]) % LANES
                own = (lane < HEAD_DIM) if side == 0 else (lane >= HEAD_DIM)
                branch = branch + nt(jnp.where(own, att, jnp.zeros_like(att)), weight_ref[t, :, project])
            at = slice(side * 256, side * 256 + 256)
            rows = hidden_ref[at, :].astype(f32) + (branch + par_ref[2:3, :])
            normed, inv = norm_forward(rows)
            first = normed * par_ref[4:5, :] + par_ref[6:7, :]
            first_ref[at, :] = first
            normed_ref[at, :] = normed
            inv_ref[at, :] = jnp.broadcast_to(inv, (256, LANES))
            low_ref[at, :] = first.astype(bf16)
        sum_ref[...] = jnp.zeros_like(sum_ref)

    @pl.when((step >= 1) & (step <= 4))
    def _():
        j = step - 1
        for side in range(512 // TALL):
            at = slice(side * TALL, side * TALL + TALL)
            pre = nn(low_ref[at, :], weight_ref[j, :, :D]) + par_ref[pl.ds(8 + (place ^ j), 1), :]
            cdf = 0.5 * (1.0 + lax.erf(pre * (1.0 / math.sqrt(2.0))))
            slope_ref[j, at, :] = cdf + pre * jnp.exp(-0.5 * pre * pre) * (1.0 / math.sqrt(2.0 * math.pi))
            act = (pre * cdf).astype(bf16)
            act_ref[at, :] = act
            sum_ref[at, :] += nt(act, weight_ref[j, :, D : 2 * D])

    @pl.when(step == 4)
    def _():
        for side in range(4):
            at = slice(side * 128, side * 128 + 128)
            rows = first_ref[at, :] + (sum_ref[at, :] + par_ref[3:4, :])
            normed, inv = norm_forward(rows)
            out_ref[at, :] = (normed * par_ref[5:6, :] + par_ref[7:8, :]).astype(bf16)
            cot = cot_ref[at, :].astype(f32)
            grad = norm_backward(cot * par_ref[5:6, :], normed, inv)
            grad_low = grad.astype(bf16)
            h2_ref[at, :] = grad
            ffn_grad_ref[at, :] = grad_low
            vec_ref[3:4, :] += jnp.sum(grad_low.astype(f32), axis=0, keepdims=True)
            vec_ref[5:6, :] += jnp.sum(cot * normed, axis=0, keepdims=True)
            vec_ref[7:8, :] += jnp.sum(cot, axis=0, keepdims=True)
        sum_ref[...] = jnp.zeros_like(sum_ref)

    @pl.when(step >= 5)
    def _():
        j = 8 - step
        total = jnp.zeros((1, D), f32)
        for side in range(512 // TALL):
            at = slice(side * TALL, side * TALL + TALL)
            grad_act = nn(ffn_grad_ref[at, :], weight_ref[j, :, D : 2 * D])
            grad_pre = (grad_act * slope_ref[j, at, :]).astype(bf16)
            pre_ref[at, :] = grad_pre
            total = total + jnp.sum(grad_pre.astype(f32), axis=0, keepdims=True)
            sum_ref[at, :] += nt(grad_pre, weight_ref[j, :, :D])
        vec_ref[pl.ds(8 + (place ^ j), 1), :] = total

    @pl.when(step == 8)
    def _():
        for side in range(4):
            at = slice(side * 128, side * 128 + 128)
            grad_first = h2_ref[at, :] + sum_ref[at, :]
            normed = normed_ref[at, :]
            grad = norm_backward(grad_first * par_ref[4:5, :], normed, inv_ref[at, 0:1])
            grad_low = grad.astype(bf16)
            h1_ref[at, :] = grad
            branch_grad_ref[at, :] = grad_low
            vec_ref[2:3, :] += jnp.sum(grad_low.astype(f32), axis=0, keepdims=True)
            vec_ref[4:5, :] += jnp.sum(grad_first * normed, axis=0, keepdims=True)
            vec_ref[6:7, :] += jnp.sum(grad_first, axis=0, keepdims=True)
        for t, grad_ref in enumerate((grad0, grad1, grad2, grad3)):
            both = [
                nn(branch_grad_ref[s * 256 : s * 256 + 256, :], weight_ref[t, :, project])
                for s in range(2)
            ]
            lane = lane_iota(256, both[0].shape[1]) % LANES
            grad_ref[...] = jnp.where(lane < HEAD_DIM, both[0], both[1]).astype(bf16)


def middle(places, att, hidden, cotangent, params, weights):
    width = att[0].shape[1]
    rows = 512

    def up(s, q):
        return (0, jnp.clip(s - 1, 0, 3))

    def down(s, q):
        return (0, jnp.clip(8 - s, 0, 3))

    def whole(rank):
        return lambda s, q: (0,) * rank

    square = pl.BlockSpec((rows, D), whole(2))
    exchanged = pl.BlockSpec((256, width), whole(2))
    spec = pltpu.PrefetchScalarGridSpec(
        num_scalar_prefetch=1,
        grid=(9,),
        in_specs=[exchanged] * 4
        + [
            pl.BlockSpec((rows, D), lambda s, q: (q[1], 0)),
            pl.BlockSpec((rows, D), lambda s, q: (q[1], 0)),
            pl.BlockSpec((16, D), whole(2)),
        ]
        + [pl.BlockSpec(memory_space=pl.ANY)] * 4,
        out_specs=[
            square,
            pl.BlockSpec((rows, D), up),
            pl.BlockSpec((rows, D), down),
            square,
            square,
            square,
            square,
        ]
        + [exchanged] * 4
        + [pl.BlockSpec((16, D), whole(2))],
        scratch_shapes=[
            pltpu.VMEM((rows, D), f32),
            pltpu.VMEM((rows, D), f32),
            pltpu.VMEM((rows, LANES), f32),
            pltpu.VMEM((4, rows, D), f32),
            pltpu.VMEM((rows, D), f32),
            pltpu.VMEM((rows, D), f32),
            pltpu.VMEM((4, D, 2 * D + width), bf16),
            pltpu.SemaphoreType.DMA((2, 4)),
        ],
    )
    out = pl.pallas_call(
        middle_kernel,
        grid_spec=spec,
        out_shape=[
            jax.ShapeDtypeStruct((rows, D), bf16),
            jax.ShapeDtypeStruct((rows, FF), bf16),
            jax.ShapeDtypeStruct((rows, FF), bf16),
            jax.ShapeDtypeStruct((rows, D), bf16),
            jax.ShapeDtypeStruct((rows, D), bf16),
            jax.ShapeDtypeStruct((rows, D), bf16),
            jax.ShapeDtypeStruct((rows, D), f32),
        ]
        + [jax.ShapeDtypeStruct((256, width), bf16)] * 4
        + [jax.ShapeDtypeStruct((16, D), f32)],
        compiler_params=pltpu.CompilerParams(vmem_limit_bytes=VMEM),
        name="middle",
        cost_estimate=QUICK,
    )(places, *att, hidden, cotangent, params, *weights)
    return out[:7], out[7:11], out[11]


def weight_grad_kernel(chunks, adds, place_ref, act_ref, pre_ref, low_ref, ffn_ref, branch_ref, *refs):
    att_refs, add_refs, out_ref = refs[:chunks], refs[chunks : chunks + adds], refs[-1]

    def put(at, part):
        for ref in add_refs:
            part = part + ref[:, at].astype(f32)
        out_ref[:, at] = part.astype(bf16)

    put(slice(0, D), tn(low_ref[...], pre_ref[...]))
    put(slice(D, 2 * D), tn(ffn_ref[...], act_ref[...]))
    for i in range(chunks):

        @pl.when(pl.program_id(0) == i)
        def _():
            att = att_refs[i][...]
            low = lane_iota(256, att.shape[1]) % LANES < HEAD_DIM
            zero = jnp.zeros_like(att)
            both = jnp.concatenate([jnp.where(low, att, zero), jnp.where(low, zero, att)], axis=0)
            put(slice(2 * D, 2 * D + att.shape[1]), tn(branch_ref[...], both))


def weight_grads(places, saved, att, first, chunks, adds):
    act, pre, low, ffn_grad, branch_grad = saved
    rows = act.shape[0]
    width = att[0].shape[1]
    total = 2 * D + width
    cut = D // 2

    def chunk(s, i, q):
        return (0, first - 2 * s)

    part = pl.BlockSpec((rows, cut), lambda s, i, q: (0, i))
    spec = pltpu.PrefetchScalarGridSpec(
        num_scalar_prefetch=1,
        grid=(chunks, 2),
        in_specs=[pl.BlockSpec((rows, D), chunk)] * 2
        + [part] * 3
        + [pl.BlockSpec((256, width), lambda s, i, q: (0, 0))] * chunks
        + [pl.BlockSpec((cut, total), lambda s, i, q, k=k: (2 * k + i, 0)) for _, k in adds],
        out_specs=pl.BlockSpec((cut, total), lambda s, i, q: (2 * s + i, 0)),
    )
    return pl.pallas_call(
        partial(weight_grad_kernel, chunks, len(adds)),
        grid_spec=spec,
        out_shape=jax.ShapeDtypeStruct((chunks * D, total), bf16),
        compiler_params=pltpu.CompilerParams(vmem_limit_bytes=VMEM),
        name="weight_grads",
        cost_estimate=QUICK,
    )(
        places, act, pre, low, ffn_grad, branch_grad,
        *[att[first - 2 * s] for s in range(chunks)], *[a for a, _ in adds],
    )


def collect_kernel(lay, place_ref, *refs):
    rows_refs = refs[: lay.arrays]
    code_ref, dense_ref = refs[lay.arrays :]
    me = place_ref[0]
    tokens = dense_ref.shape[0]
    low = lane_iota(tokens) < HEAD_DIM
    firsts, seconds = [], []
    for h in range(lay.heads):
        column = as_column(code_ref[h, 0:1, :])
        half = as_column(code_ref[h, 1:2, :])
        planes = [block_rows(lay, rows_refs, (h * 3 + x) * lay.half_rows) for x in range(3)]
        found = nn(gather_matrix(lay, me, column), jnp.concatenate(planes, axis=1))
        one, two = [], []
        for x in range(3):
            part = found[:, x * LANES : (x + 1) * LANES]
            turned = pltpu.roll(part, HEAD_DIM, 1)
            one.append(jnp.where(half == 0, part, turned))
            two.append(jnp.where(half == 1, part, turned))
        firsts.append(one)
        seconds.append(two)
    tiles = [jnp.where(low, firsts[h][0], seconds[h][1]) for h in range(lay.heads)]
    for h in range(0, lay.heads, 2):
        right = seconds[h + 1][2] if h + 1 < lay.heads else jnp.zeros((tokens, LANES), f32)
        tiles.append(jnp.where(low, firsts[h][2], right))
    dense_ref[...] = jnp.concatenate(tiles, axis=1).astype(bf16)


def collect(lay, places, returned, code, width):
    tokens = COLLECT_ROWS
    spec = pltpu.PrefetchScalarGridSpec(
        num_scalar_prefetch=1,
        grid=(lay.tokens // tokens,),
        in_specs=lay.specs(lay.data_rows, only(0))
        + [pl.BlockSpec((lay.heads, 8, tokens), lambda c, q: (0, 0, c))],
        out_specs=pl.BlockSpec((tokens, width), lambda c, q: (c, 0)),
    )
    return pl.pallas_call(
        partial(collect_kernel, lay),
        grid_spec=spec,
        out_shape=jax.ShapeDtypeStruct((lay.tokens, width), bf16),
        compiler_params=pltpu.CompilerParams(vmem_limit_bytes=VMEM),
        name="collect",
        cost_estimate=cost(COLLECT_US),
    )(places, *returned, code)


def half_rows_at(g, s, place):
    core = place % 2
    return jnp.where(s == 0, 1 - core, core) * 2 + g


def spread_kernel(g, place_ref, dense_ref, w_ref, h1_ref, other_ref, mine_ref):
    step, place = pl.program_id(0), place_ref[1]
    own = (half_rows_at(g, step, place) == place).astype(f32)
    part = nt(dense_ref[...], w_ref[...]) + own * h1_ref[...]

    @pl.when(step == 0)
    def _():
        other_ref[...] = part.astype(bf16)

    @pl.when(step == 1)
    def _():
        mine_ref[...] = part.astype(bf16)


def spread_grads(g, places, dense, weights, grad_h1):
    width = weights.shape[1]
    whole = lambda s, q: (0, 0)
    spec = pltpu.PrefetchScalarGridSpec(
        num_scalar_prefetch=1,
        grid=(2,),
        in_specs=[
            pl.BlockSpec((512, width), lambda s, q: (half_rows_at(g, s, q[1]), 0)),
            pl.BlockSpec((D, width), whole),
            pl.BlockSpec((512, D), whole),
        ],
        out_specs=[pl.BlockSpec((512, D), whole)] * 2,
    )
    return pl.pallas_call(
        partial(spread_kernel, g),
        grid_spec=spec,
        out_shape=[jax.ShapeDtypeStruct((512, D), bf16)] * 2,
        compiler_params=pltpu.CompilerParams(vmem_limit_bytes=VMEM),
        name="spread_grads",
        cost_estimate=cost(SPREAD_US),
    )(places, dense, weights, grad_h1)


def head_grad_kernel(lay, place_ref, x_ref, dense_ref, vec_ref, *refs):
    out_ref, total_ref = refs
    step = pl.program_id(0)

    @pl.when(step == 0)
    def _():
        total_ref[...] = tn(x_ref[...], dense_ref[...])

    @pl.when(step > 0)
    def _():
        total_ref[...] += tn(x_ref[...], dense_ref[...])

    @pl.when(step == 3)
    def _():
        depth = D // lay.peers
        if not lay.direct:
            out_ref[...] = total_ref[...].astype(bf16)
            return
        for d in range(lay.peers):
            out_ref[d, :depth, :] = total_ref[d * depth : (d + 1) * depth, :].astype(bf16)
            vector = vec_ref[d]
            high = vector.astype(bf16).astype(f32)
            width = total_ref.shape[1]
            out_ref[d, depth:, :] = jnp.concatenate(
                [high, vector - high, jnp.zeros((16, width - 2 * LANES), f32)], axis=1
            ).astype(bf16)


def head_grads(lay, places, x, dense, vec):
    width = dense.shape[1]
    depth = D // lay.peers
    shape = (lay.peers, depth + 16, width) if lay.direct else (D, width)
    spec = pltpu.PrefetchScalarGridSpec(
        num_scalar_prefetch=1,
        grid=(4,),
        in_specs=[
            pl.BlockSpec((512, D), lambda s, q: (s, 0)),
            pl.BlockSpec((512, width), lambda s, q: (s, 0)),
            pl.BlockSpec(vec.shape, lambda s, q: (0, 0, 0)),
        ],
        out_specs=pl.BlockSpec(shape, lambda s, q: (0,) * len(shape)),
        scratch_shapes=[pltpu.VMEM((D, width), f32)],
    )
    return pl.pallas_call(
        partial(head_grad_kernel, lay),
        grid_spec=spec,
        out_shape=jax.ShapeDtypeStruct(shape, bf16),
        compiler_params=pltpu.CompilerParams(vmem_limit_bytes=VMEM),
        name="head_grads",
        cost_estimate=cost(HEAD_GRADS_US),
    )(places, x, dense, vec)


def finish_heads_kernel(*refs):
    parts, outs = refs[0], refs[1:]
    depth, width = outs[0].shape
    heads = width // HEAD_DIM
    total = parts[0].astype(f32)
    for d in range(1, parts.shape[0]):
        total = total + parts[d].astype(f32)
    grads = total[:depth]
    cut = [slice(h * LANES, h * LANES + HEAD_DIM) for h in range(heads)]
    outs[0][...] = jnp.concatenate([grads[:, at] for at in cut], axis=1)
    cut = [slice(h * LANES + HEAD_DIM, (h + 1) * LANES) for h in range(heads)]
    outs[1][...] = jnp.concatenate([grads[:, at] for at in cut], axis=1)
    outs[2][...] = grads[:, 2 * width : 3 * width]
    outs[3][...] = total[depth:, :LANES] + total[depth:, LANES : 2 * LANES]


def finish_heads(parts, depth, width):
    shapes = [(depth, width)] * 3 + [(16, LANES)]
    return pl.pallas_call(
        finish_heads_kernel,
        out_shape=[jax.ShapeDtypeStruct(s, f32) for s in shapes],
        name="finish_heads",
        cost_estimate=QUICK,
    )(parts)


def finish_vectors_kernel(depth, own_ref, other_ref, bias_ref, gain_ref, shift_ref, inner_ref):
    total = (own_ref[...] + other_ref[...])[:, :depth]
    bias_ref[...] = total[:4]
    gain_ref[...] = total[4:6]
    shift_ref[...] = total[6:8]
    inner_ref[...] = total[8:12]


def finish_vectors(own, other, depth):
    return pl.pallas_call(
        partial(finish_vectors_kernel, depth),
        out_shape=[jax.ShapeDtypeStruct((n, depth), f32) for n in (4, 2, 2, 4)],
        name="finish_vectors",
        cost_estimate=QUICK,
    )(own, other)


def finish_middle_kernel(grad_ref, inner_ref, outer_ref, output_ref):
    inner_ref[...] = grad_ref[:, :D].astype(f32)
    outer_ref[...] = grad_ref[:, D : 2 * D].astype(f32)
    rest = grad_ref[:, 2 * D :].astype(f32)
    planes = [rest[:, i * LANES : (i + 1) * LANES] for i in range(rest.shape[1] // LANES)]
    folded = [p[:, :HEAD_DIM] + p[:, HEAD_DIM:] for p in planes]
    output_ref[...] = jnp.concatenate(folded, axis=1).T


def finish_middle(grads):
    depth, total = grads.shape
    return pl.pallas_call(
        finish_middle_kernel,
        out_shape=[
            jax.ShapeDtypeStruct((depth, D), f32),
            jax.ShapeDtypeStruct((depth, D), f32),
            jax.ShapeDtypeStruct(((total - 2 * D) // 2, depth), f32),
        ],
        name="finish_middle",
        cost_estimate=QUICK,
    )(grads)


def order_kernel(place_ref, *refs):
    parts, out_ref, rows_ref, sems = refs[:4], refs[4], refs[5], refs[6]
    rows = rows_ref.shape[1]

    def take(i):
        return pltpu.make_async_copy(parts[i], rows_ref.at[i], sems.at[0, i])

    def put(i):
        at = pl.ds(pl.multiple_of(place_ref[i] * rows, rows), rows)
        return pltpu.make_async_copy(rows_ref.at[i], out_ref.at[at, :], sems.at[1, i])

    for i in range(4):
        take(i).start()
    for i in range(4):
        take(i).wait()
        put(i).start()
    for i in range(4):
        put(i).wait()


def order_quarters(order, quarters):
    rows, width = quarters[0].shape
    dtype = quarters[0].dtype
    return pl.pallas_call(
        order_kernel,
        in_specs=[pl.BlockSpec(memory_space=pltpu.SMEM)]
        + [pl.BlockSpec(memory_space=pl.ANY)] * 4,
        out_specs=pl.BlockSpec(memory_space=pl.ANY),
        out_shape=jax.ShapeDtypeStruct((4 * rows, width), dtype),
        scratch_shapes=[pltpu.VMEM((4, rows, width), dtype), pltpu.SemaphoreType.DMA((2, 4))],
        name="order_quarters",
        cost_estimate=QUICK,
    )(order, *quarters)


def over_rows(lay, blocks):
    if not lay.direct:
        return [lax.all_to_all(blocks[0], "dp", split_axis=0, concat_axis=0, tiled=True)]
    out = [blocks[0]]
    for s in range(1, lay.peers):
        out.append(lax.ppermute(blocks[s], "dp", [(i, i ^ s) for i in range(lay.peers)]))
    return out


def in_hbm(rows):
    return pltpu.with_memory_space_constraint(rows, pltpu.HBM)


def share_pieces(lay, piece):
    def flip(rows, s):
        return lax.ppermute(rows, "dp", [(i, i ^ s) for i in range(lay.peers)])

    half = lay.peers // 2
    far = flip(piece, half)
    near = [piece] + [flip(piece, s) for s in range(1, half)]
    return near + [far] + [flip(far, s) for s in range(1, half)]


def after(value, *others):
    return lax.optimization_barrier((value, *others))[0]


def swap(rows, flip):
    return lax.ppermute(rows, "mp", [(i, i ^ flip) for i in range(4)])


def over_heads(blocks):
    return [blocks[0]] + [swap(blocks[t], t) for t in range(1, 4)]


def on_device(
    hidden_in,
    cotangent,
    w_query,
    w_key,
    w_value,
    w_output,
    w_inner,
    w_outer,
    biases,
    gains,
    shifts,
    inner_bias,
    lengths,
    padding,
    cluster_perm,
):
    peers = lax.axis_size("dp")
    tokens = hidden_in.shape[0]
    heads = cluster_perm.shape[0]
    lay = Layout(peers, tokens, heads)
    place = lax.axis_index("mp")
    me = lax.axis_index("dp")
    places = jnp.stack([me, place]).astype(i32)
    hidden_in = in_hbm(hidden_in)
    depth = w_query.shape[0]
    width = heads * HEAD_DIM

    piece, shard = pack_weights(
        w_query, w_key, w_value, w_output, w_inner, w_outer.T,
        biases, gains, shifts, inner_bias.reshape(1, -1),
    )
    own_w = lax.all_gather(shard, "dp", axis=0, tiled=True)
    far_w = swap(own_w, 2)
    if lay.direct:
        weights, bias, params = assemble_weights(lay, places, share_pieces(lay, piece))
    else:
        weights, bias, params = gather_weights(lay, place, piece)

    weights = in_hbm(weights)
    code = in_hbm(place_tokens(lay, cluster_perm))
    sent = project_rows(lay, places, hidden_in, weights, bias, code, padding.reshape(1, tokens))
    arrived = over_rows(lay, sent)
    mixed = over_rows(lay, attend(lay, arrived))
    att = over_heads(unsort_rows(lay, places, mixed, code))
    far_w = after(far_w, *att)
    middle_w = [own_w, swap(own_w, 1), far_w, swap(far_w, 1)]
    saved, att_grad, vec = middle(places, att, hidden_in, cotangent, params, middle_w)
    out_quarter, act, pre_grad, first_low, ffn_grad, branch_grad, grad_h1 = saved
    saved = tuple(in_hbm(a) for a in (act, pre_grad, first_low, ffn_grad, branch_grad))
    att = [in_hbm(a) for a in att]

    got = over_heads(att_grad)
    far = swap(out_quarter, 2)
    ready = (after(act, *got),) + saved[1:]
    from_core = swap(weight_grads(places, ready, att, 3, 2, []), 1)
    grads = sort_rows(lay, places, got, code)
    ready = (after(act, grads[0], far),) + saved[1:]
    from_far = swap(weight_grads(places, ready, att, 2, 1, [(from_core, 0)]), 2)
    grads = over_rows(lay, grads)
    slot_grads, bias_sums = attend_back(lay, arrived, grads)

    returned = over_rows(lay, slot_grads)
    head_sums = bias_sums[:, :2].reshape(heads, 2, 2, HEAD_DIM).sum(axis=2)
    head_sums = head_sums.transpose(1, 0, 2).reshape(2, width)
    vec = lax.dynamic_update_slice(vec[:12], head_sums, (0, place * width))
    vec = jnp.concatenate(
        [vec[:8].reshape(8, peers, depth).transpose(1, 0, 2), vec[8:].reshape(peers, 4, depth)],
        axis=1,
    )
    spread = jnp.pad(vec, ((0, 0), (0, 4), (0, (-depth) % LANES)))
    summed = weight_grads(places, saved, att, 0, 1, [(from_core, 1), (from_far, 0)])
    reduced = lax.psum_scatter(summed, "dp", scatter_dimension=0, tiled=True)
    dense = collect(lay, places, returned, after(code, far), weights.shape[1])
    terms = head_grads(lay, places, hidden_in, dense, spread)
    dense = after(dense, terms)
    groups = [spread_grads(g, places, dense, weights, grad_h1) for g in range(2)]
    chips = [
        (mine.astype(f32) + swap(other, 1).astype(f32)).astype(bf16) for other, mine in groups
    ]
    far = after(far, terms)
    hidden_out = order_quarters(
        jnp.stack([place, place ^ 2, place ^ 1, place ^ 3]).astype(i32),
        [out_quarter, far, swap(out_quarter, 1), swap(far, 1)],
    )
    if lay.direct:
        terms = lax.all_to_all(terms, "dp", split_axis=0, concat_axis=0, tiled=True)
        ends = finish_heads(terms, depth, width)
    else:
        ends = reduce_heads(terms, vec, depth, width)
    ready = [
        (after(chip, ends[0]).astype(f32) + swap(chip, 2).astype(f32)).astype(bf16)
        for chip in chips
    ]
    core = place % 2
    grad_hidden = order_quarters(
        jnp.stack([2 * core, 2 * core + 1, 2 - 2 * core, 3 - 2 * core]).astype(i32),
        ready + [swap(part, 1) for part in ready],
    )

    small = ends[3] + swap(ends[3], 1)
    small = finish_vectors(small, swap(small, 2), depth)
    grad_inner, grad_outer, grad_output = finish_middle(reduced)
    return (
        hidden_out,
        grad_hidden,
        ends[0],
        ends[1],
        ends[2],
        grad_output,
        grad_inner,
        grad_outer.T,
        small[0],
        small[1],
        small[2],
        small[3].reshape(-1),
    )


def gather_weights(lay, place, piece):
    depth = D // lay.peers
    width = lay.heads * HEAD_DIM
    got = lax.all_gather(piece, "dp", axis=0, tiled=False)
    columns = piece.shape[1] - LANES
    weights = got[:, :depth, :columns].reshape(D, columns)
    vectors = got[:, :12, columns : columns + depth].astype(f32)
    params = vectors[:, :8].transpose(1, 0, 2).reshape(8, D)
    params = jnp.concatenate([params, vectors[:, 8:].reshape(4, D), jnp.zeros((4, D), f32)], axis=0)
    own = lax.dynamic_slice_in_dim(params[:2], place * width, width, 1)
    query = own[0].reshape(lay.heads, HEAD_DIM)
    query = jnp.concatenate([query, jnp.zeros_like(query)], axis=1).reshape(-1)
    row = jnp.concatenate([query, own[1], jnp.zeros(weights.shape[1] - 3 * width, f32)])
    return weights, jnp.broadcast_to(row[None], (8, row.shape[0])), params


def reduce_heads(grads, vec, depth, width):
    total = lax.psum_scatter(grads, "dp", scatter_dimension=0, tiled=True).astype(f32)
    pairs = total[:, : 2 * width].reshape(depth, -1, 2, HEAD_DIM)
    small = lax.psum_scatter(vec, "dp", scatter_dimension=0, tiled=False)
    small = jnp.pad(small, ((0, 4), (0, LANES - depth)))
    return (
        pairs[:, :, 0].reshape(depth, width),
        pairs[:, :, 1].reshape(depth, width),
        total[:, 2 * width : 3 * width],
        small,
    )


def solution(mesh):
    placed = (
        P("dp", None),
        P("dp", None),
        P("dp", "mp"),
        P("dp", "mp"),
        P("dp", "mp"),
        P("mp", "dp"),
        P("dp", "mp"),
        P("mp", "dp"),
        P(None, "dp"),
        P(None, "dp"),
        P(None, "dp"),
        P("dp"),
        P(),
        P("dp"),
        P("mp", "dp"),
    )
    return jax.shard_map(
        on_device,
        mesh=mesh,
        in_specs=placed,
        out_specs=(
            P("dp", None),
            P("dp", None),
            P("dp", "mp"),
            P("dp", "mp"),
            P("dp", "mp"),
            P("mp", "dp"),
            P("dp", "mp"),
            P("mp", "dp"),
            P(None, "dp"),
            P(None, "dp"),
            P(None, "dp"),
            P("dp"),
        ),
        check_vma=False,
    )
```

```python
from functools import partial
import math

import jax
import jax.numpy as jnp
from jax import lax
from jax.experimental import pallas as pl
from jax.experimental.pallas import tpu as pltpu
from jax.sharding import PartitionSpec as P

D = 768
HEAD_DIM = 64
FF = 3072
CLUSTER = 128
LANES = 128
EPSILON = 1e-05
MASKED = -1e30
SCALE = 1.0 / math.sqrt(HEAD_DIM)

bf16 = jnp.bfloat16
f32 = jnp.float32
i32 = jnp.int32

VMEM = 60 * 1024 * 1024


def cost(us):
    return pl.CostEstimate(flops=int(1e9 * us), bytes_accessed=int(3e6 * us), transcendentals=0)


QUICK = cost(0.001)
ATTEND_US = 46
COLLECT_US = 30
COLLECT_ROWS = 512
SPREAD_US = 3
HEAD_GRADS_US = 4
SORT_US = 80


def nn(a, b):
    return lax.dot_general(a, b, (((1,), (0,)), ((), ())), preferred_element_type=f32)


def nt(a, b):
    return lax.dot_general(a, b, (((1,), (1,)), ((), ())), preferred_element_type=f32)


def tn(a, b):
    return lax.dot_general(a, b, (((0,), (0,)), ((), ())), preferred_element_type=f32)


def lane_iota(rows, lanes=LANES):
    return lax.broadcasted_iota(i32, (rows, lanes), 1)


def sublane_iota(rows, lanes=LANES):
    return lax.broadcasted_iota(i32, (rows, lanes), 0)


def as_column(row):
    parts = [
        jnp.broadcast_to(row[:, i * LANES : (i + 1) * LANES], (LANES, LANES)).T
        for i in range(row.shape[1] // LANES)
    ]
    return parts[0] if len(parts) == 1 else jnp.concatenate(parts, axis=0)


def loop(count):
    def run(step):
        def body(i, carry):
            step(i)
            return carry

        lax.fori_loop(0, count, body, 0)

    return run


class Layout:
    def __init__(self, peers, tokens, heads):
        self.peers, self.tokens, self.heads = peers, tokens, heads
        self.stripe = min(16, peers)
        self.runs = peers // self.stripe
        self.per_dev = CLUSTER // self.stripe
        self.rows_peer = tokens // peers
        self.half_rows = self.rows_peer // 2
        self.pairs = self.half_rows // self.per_dev
        self.packed = tokens // 2
        self.clusters = peers * tokens // CLUSTER
        self.data_rows = 9 * self.half_rows
        self.direct = self.half_rows == LANES
        self.arrays = peers if self.direct else 1

    def peer(self, me, s):
        return (me ^ s) if self.direct else s

    def shapes(self, rows, dtype=bf16):
        lead = () if self.direct else (self.peers,)
        return [jax.ShapeDtypeStruct(lead + (rows, LANES), dtype)] * self.arrays

    def specs(self, rows, at):
        if self.direct:
            return [pl.BlockSpec((rows, LANES), lambda *g: (at(*g), 0))] * self.arrays
        return [pl.BlockSpec((self.peers, rows, LANES), lambda *g: (0, at(*g), 0))]

    def view(self, refs, s):
        return refs[s] if self.direct else refs[0].at[s]


def only(at):
    return lambda *g: at


def place_kernel(lay, perm_ref, code_ref):
    groups = lay.clusters
    shift = CLUSTER.bit_length() - 1
    blocks = lay.tokens // LANES
    before = sublane_iota(LANES, 2 * LANES)
    after = lane_iota(LANES, 2 * LANES)
    ahead_of = jnp.where((before < after) | (after >= LANES), 1.0, 0.0).astype(bf16)

    def members(h, b):
        row = lax.shift_right_logical(perm_ref[h : h + 1, b * LANES : (b + 1) * LANES], shift)
        return jnp.broadcast_to(row, (groups, LANES)) == sublane_iota(groups)

    for h in range(lay.heads):
        if lay.runs == 1:
            carry = (sublane_iota(groups) * lay.per_dev).astype(f32)
        else:
            counts = jnp.zeros((groups, LANES), f32)
            for b in range(blocks):
                member = jnp.where(members(h, b), 1.0, 0.0).astype(bf16)
                counts = counts + nn(member, ahead_of)[:, LANES:]
            lower = jnp.where(
                sublane_iota(groups, groups) > lane_iota(groups, groups), 1.0, 0.0
            ).astype(bf16)
            carry = nn(lower, counts.astype(bf16))
        for b in range(blocks):
            member = members(h, b)
            found = nn(jnp.where(member, 1.0, 0.0).astype(bf16), ahead_of)
            rank = jnp.sum(jnp.where(member, found[:, :LANES] + carry, 0.0), axis=0, keepdims=True)
            carry = carry + found[:, LANES:]
            rank = rank.astype(i32)
            peer = lax.shift_right_logical(rank, lay.rows_peer.bit_length() - 1)
            rest = rank & (lay.rows_peer - 1)
            half = lax.shift_right_logical(rest, lay.half_rows.bit_length() - 1)
            packed = peer * lay.half_rows + (rest & (lay.half_rows - 1))
            at = slice(b * LANES, (b + 1) * LANES)
            code_ref[h, 0:1, at] = packed
            code_ref[h, 1:2, at] = half


def place_tokens(lay, perm):
    return pl.pallas_call(
        partial(place_kernel, lay),
        out_shape=jax.ShapeDtypeStruct((lay.heads, 8, lay.tokens), i32),
        name="place_tokens",
        cost_estimate=QUICK,
    )(perm)


def one_hot(equal):
    return jnp.where(equal, 1.0, 0.0).astype(bf16)


def scatter_matrix(lay, me, packed, s, blocks):
    rows = blocks * lay.half_rows
    if lay.direct:
        parts = [
            one_hot(
                jnp.broadcast_to(packed, (lay.half_rows, lay.tokens))
                == sublane_iota(lay.half_rows, lay.tokens) + lay.peer(me, s + i) * lay.half_rows
            )
            for i in range(blocks)
        ]
        return jnp.concatenate(parts, axis=0)
    wanted = sublane_iota(rows, lay.tokens) + s * lay.half_rows
    return one_hot(jnp.broadcast_to(packed, (rows, lay.tokens)) == wanted)


def gather_matrix(lay, me, column):
    lane = lane_iota(column.shape[0])
    parts = [
        one_hot(column == lane + lay.peer(me, k) * LANES) for k in range(lay.packed // LANES)
    ]
    return jnp.concatenate(parts, axis=1)


def block_rows(lay, refs, first):
    at = slice(first, first + lay.half_rows)
    if lay.direct:
        return jnp.concatenate([refs[s][at, :] for s in range(lay.peers)], axis=0)
    return refs[0][:, at, :].astype(f32).reshape(lay.packed, LANES).astype(bf16)


def put_blocks(lay, refs, s, blocks, first, rows):
    at = slice(first, first + lay.half_rows) if isinstance(first, int) else pl.ds(first, lay.half_rows)
    if lay.direct:
        for i in range(blocks):
            refs[s + i][at, :] = rows[i * LANES : (i + 1) * LANES].astype(bf16)
    else:
        rows = rows.astype(f32).reshape(blocks, lay.half_rows, LANES).astype(bf16)
        refs[0][s : s + blocks, at, :] = rows


ROWS = 512
COUNT = 4


def project_kernel(lay, steps, place_ref, x_ref, w_ref, bias_ref, code_ref, pad_ref, *rest):
    outs = rest[: lay.arrays]
    rows_ref, flag_ref = rest[lay.arrays :]
    step = pl.program_id(0)
    me = place_ref[0]
    width = 4 * LANES

    @pl.when(step < steps)
    def _():
        at = pl.ds(pl.multiple_of(step * ROWS, ROWS), ROWS)
        values = nn(x_ref[...], w_ref[...]) + bias_ref[0:1, :]
        low = lane_iota(ROWS) < HEAD_DIM
        lane_half = jnp.where(low, 0, 1)
        live = as_column(pad_ref[0:1, at])
        tiles = [values[:, i * LANES : (i + 1) * LANES] for i in range(values.shape[1] // LANES)]
        turned = [pltpu.roll(tile, HEAD_DIM, 1) for tile in tiles]
        for h in range(lay.heads):
            half = as_column(code_ref[h, 1:2, at])
            keep = half == lane_half
            v, side = lay.heads + h // 2, h % 2
            planes = (
                jnp.where(low, tiles[h], turned[h]),
                jnp.where(low, turned[h], tiles[h]),
                jnp.where(low, tiles[v], turned[v]) if side == 0 else jnp.where(low, turned[v], tiles[v]),
            )
            for x, plane in enumerate(planes):
                rows_ref[h, at, x * LANES : (x + 1) * LANES] = jnp.where(keep, plane, 0.0).astype(bf16)
            flags = jnp.where((lane_iota(ROWS) == half) & (live == 1), 1.0, 0.0)
            rows_ref[h, at, 3 * LANES :] = flags.astype(bf16)

    count = COUNT if lay.direct else 32

    @pl.when(step >= steps)
    def _():
        h = step - steps
        for s in range(0, lay.peers, count):
            chosen = scatter_matrix(lay, me, code_ref[h, 0:1, :], s, count)
            moved = nn(chosen, rows_ref[h])
            for x in range(3):
                first = pl.multiple_of((h * 3 + x) * lay.half_rows, 16)
                put_blocks(lay, outs, s, count, first, moved[:, x * LANES : (x + 1) * LANES])
            for i in range(count * lay.half_rows // LANES):
                at = slice(s * lay.half_rows + i * LANES, s * lay.half_rows + (i + 1) * LANES)
                flag_ref[h, :, at] = moved[i * LANES : (i + 1) * LANES, 3 * LANES :].T[:8]

    @pl.when(step == steps + lay.heads - 1)
    def _():
        for s in range(lay.peers):
            at = slice(s * lay.half_rows, (s + 1) * lay.half_rows)
            rows = [flag_ref[k, 0:2, at] for k in range(lay.heads)]
            block = jnp.concatenate(rows + [jnp.zeros((16 - 2 * lay.heads, lay.half_rows), f32)], axis=0)
            if lay.half_rows < LANES:
                block = jnp.concatenate(
                    [block, jnp.zeros((16, LANES - lay.half_rows), f32)], axis=1
                )
            lay.view(outs, s)[lay.data_rows : lay.data_rows + 16, :] = block.astype(bf16)


def project_rows(lay, places, x, weights, bias, code, pad):
    width = weights.shape[1]
    steps = lay.tokens // ROWS
    spec = pltpu.PrefetchScalarGridSpec(
        num_scalar_prefetch=1,
        grid=(steps + lay.heads,),
        in_specs=[
            pl.BlockSpec((ROWS, D), lambda s, _: (jnp.minimum(s, steps - 1), 0)),
            pl.BlockSpec((D, width), lambda s, _: (0, 0)),
            pl.BlockSpec((8, width), lambda s, _: (0, 0)),
            pl.BlockSpec((lay.heads, 8, lay.tokens), lambda s, _: (0, 0, 0)),
            pl.BlockSpec((1, lay.tokens), lambda s, _: (0, 0)),
        ],
        out_specs=lay.specs(lay.data_rows + 16, only(0)),
        scratch_shapes=[
            pltpu.VMEM((lay.heads, lay.tokens, 4 * LANES), bf16),
            pltpu.VMEM((lay.heads, 8, lay.packed), f32),
        ],
    )
    return pl.pallas_call(
        partial(project_kernel, lay, steps),
        grid_spec=spec,
        out_shape=lay.shapes(lay.data_rows + 16),
        compiler_params=pltpu.CompilerParams(vmem_limit_bytes=VMEM),
        name="project_rows",
        cost_estimate=QUICK,
    )(places, x, weights, bias, code, pad)


def pair_rows(lay, refs, first, run, p):
    at = slice(first + p * lay.per_dev, first + (p + 1) * lay.per_dev)
    if lay.direct:
        return jnp.concatenate([refs[s][at, :] for s in range(lay.stripe)], axis=0)
    block = refs[0][run * lay.stripe : (run + 1) * lay.stripe, first : first + lay.half_rows, :]
    block = block.astype(f32)[:, p * lay.per_dev : (p + 1) * lay.per_dev, :]
    return block.reshape(CLUSTER, LANES).astype(bf16)


def put_pair(lay, refs, first, run, p, rows):
    at = slice(first + p * lay.per_dev, first + (p + 1) * lay.per_dev)
    for s in range(lay.stripe):
        part = rows[s * lay.per_dev : (s + 1) * lay.per_dev]
        lay.view(refs, run * lay.stripe + s)[at, :] = part.astype(bf16)


def live_columns(lay, flags, h):
    pick = one_hot(sublane_iota(16, 2 * LANES) == 2 * h + lane_iota(16, 2 * LANES) // LANES)
    return [tn(lay.view(flags, s)[...], pick) for s in range(lay.peers)]


def allowed_pair(lay, columns, run, p):
    at = slice(p * lay.per_dev, (p + 1) * lay.per_dev)
    live = jnp.concatenate([columns[run * lay.stripe + s][at] for s in range(lay.stripe)], axis=0)
    live = jnp.concatenate([live[:, :LANES], live[:, LANES:]], axis=0)
    same = sublane_iota(2 * CLUSTER) % CLUSTER == lane_iota(2 * CLUSTER)
    return (live > 0.5) | same


def stack_halves(rows):
    low = lane_iota(rows.shape[0], rows.shape[1]) < HEAD_DIM
    zero = jnp.zeros_like(rows)
    return jnp.concatenate([jnp.where(low, rows, zero), jnp.where(low, zero, rows)], axis=0)


def each_half(fold, rows):
    one, two = (
        jnp.broadcast_to(fold(part, axis=0, keepdims=True), part.shape)
        for part in (rows[:CLUSTER], rows[CLUSTER:])
    )
    return jnp.concatenate([one, two], axis=0)


def inverse_sum(rows, axis, keepdims):
    return 1.0 / jnp.sum(rows, axis=axis, keepdims=keepdims)


def soft_weights(queries, keys, allowed):
    scores = jnp.where(allowed, nt(keys, queries) * SCALE, MASKED)
    grown = jnp.exp(scores - each_half(jnp.max, scores))
    return grown * each_half(inverse_sum, grown)


def attend_kernel(lay, *refs):
    rows, flags, outs = (refs[i * lay.arrays : (i + 1) * lay.arrays] for i in range(3))
    live = live_columns(lay, flags, pl.program_id(0))
    for run in range(lay.runs):
        for p in range(lay.pairs):
            q, k, v = (pair_rows(lay, rows, x * lay.half_rows, run, p) for x in range(3))
            soft = soft_weights(q, stack_halves(k), allowed_pair(lay, live, run, p))
            put_pair(lay, outs, 0, run, p, tn(soft.astype(bf16), stack_halves(v)))


def attend(lay, arrived):
    head = lambda h: h
    return pl.pallas_call(
        partial(attend_kernel, lay),
        grid=(lay.heads,),
        in_specs=lay.specs(3 * lay.half_rows, head) + lay.specs(16, only(lay.data_rows // 16)),
        out_specs=lay.specs(lay.half_rows, head),
        out_shape=lay.shapes(lay.heads * lay.half_rows),
        name="attend",
        cost_estimate=cost(ATTEND_US),
    )(*arrived, *arrived)


def attend_back_kernel(lay, *refs):
    rows, flags, grads, outs = (refs[i * lay.arrays : (i + 1) * lay.arrays] for i in range(4))
    sum_ref = refs[-1]
    live = live_columns(lay, flags, pl.program_id(0))
    low = lane_iota(CLUSTER) < HEAD_DIM
    sums = [jnp.zeros((1, LANES), f32)] * 2
    for run in range(lay.runs):
        for p in range(lay.pairs):
            q, k, v = (pair_rows(lay, rows, x * lay.half_rows, run, p) for x in range(3))
            g = pair_rows(lay, grads, 0, run, p)
            keys = stack_halves(k)
            soft = soft_weights(q, keys, allowed_pair(lay, live, run, p))
            grad_soft = nt(stack_halves(v), g)
            delta = each_half(jnp.sum, soft * grad_soft)
            grad = (soft * (grad_soft - delta)).astype(bf16)
            grad_q = (tn(grad, keys) * SCALE).astype(bf16)
            part = nn(grad, q)
            grad_k = (jnp.where(low, part[:CLUSTER], part[CLUSTER:]) * SCALE).astype(bf16)
            part = nn(soft.astype(bf16), g)
            grad_v = jnp.where(low, part[:CLUSTER], part[CLUSTER:]).astype(bf16)
            for x, part in enumerate((grad_q, grad_k, grad_v)):
                put_pair(lay, outs, x * lay.half_rows, run, p, part)
            sums[0] = sums[0] + jnp.sum(grad_q.astype(f32), axis=0, keepdims=True)
            sums[1] = sums[1] + jnp.sum(grad_v.astype(f32), axis=0, keepdims=True)
    sum_ref[0] = jnp.concatenate(sums + [jnp.zeros((6, LANES), f32)], axis=0)


def attend_back(lay, arrived, grads):
    head = lambda h: h
    three = lay.specs(3 * lay.half_rows, head)
    out = pl.pallas_call(
        partial(attend_back_kernel, lay),
        grid=(lay.heads,),
        in_specs=three
        + lay.specs(16, only(lay.data_rows // 16))
        + lay.specs(lay.half_rows, head),
        out_specs=three + [pl.BlockSpec((1, 8, LANES), lambda h: (h, 0, 0))],
        out_shape=lay.shapes(lay.data_rows)
        + [jax.ShapeDtypeStruct((lay.heads, 8, LANES), f32)],
        name="attend_back",
        cost_estimate=QUICK,
    )(*arrived, *arrived, *grads)
    return list(out[:-1]), out[-1]


def side_rows(quarter, side):
    return pl.ds(pl.multiple_of(quarter * 512 + side * 256, 256), 256)


def unsort_kernel(lay, place_ref, *refs):
    rows_refs, code_ref, outs = refs[: lay.arrays], refs[lay.arrays], refs[lay.arrays + 1 :]
    rows = block_rows(lay, rows_refs, 0)
    low = lane_iota(256) < HEAD_DIM
    me, place = place_ref[0], place_ref[1]

    for t in range(4):
        sides = []
        for side in range(2):
            at = side_rows(place ^ t, side)
            column = as_column(code_ref[0, 0:1, at])
            half = as_column(code_ref[0, 1:2, at])
            found = nn(gather_matrix(lay, me, column), rows)
            sides.append(jnp.where(half == side, found, pltpu.roll(found, HEAD_DIM, 1)))
        outs[t][...] = jnp.where(low, sides[0], sides[1]).astype(bf16)


def unsort_rows(lay, places, returned, code):
    spec = pltpu.PrefetchScalarGridSpec(
        num_scalar_prefetch=1,
        grid=(lay.heads,),
        in_specs=lay.specs(lay.half_rows, lambda h, _: h)
        + [pl.BlockSpec((1, 8, lay.tokens), lambda h, _: (h, 0, 0))],
        out_specs=[pl.BlockSpec((256, LANES), lambda h, _: (0, h))] * 4,
    )
    return pl.pallas_call(
        partial(unsort_kernel, lay),
        grid_spec=spec,
        out_shape=[jax.ShapeDtypeStruct((256, lay.heads * LANES), bf16)] * 4,
        name="unsort_rows",
        cost_estimate=QUICK,
    )(places, *returned, code)


def sort_kernel(lay, place_ref, *refs):
    grads, code_ref, outs, rows_ref = refs[:4], refs[4], refs[5:-1], refs[-1]
    low = lane_iota(256) < HEAD_DIM
    lane_half = jnp.where(low, 0, 1)
    me, place = place_ref[0], place_ref[1]

    for t in range(4):
        block = grads[t][...].astype(f32)
        turned = pltpu.roll(block, HEAD_DIM, 1)
        for side in range(2):
            at = side_rows(place ^ t, side)
            half = as_column(code_ref[0, 1:2, at])
            both = jnp.where(low, block, turned) if side == 0 else jnp.where(low, turned, block)
            rows_ref[at, :] = jnp.where(half == lane_half, both, 0.0).astype(bf16)

    count = 4 if lay.direct else 32
    for s in range(0, lay.peers, count):
        chosen = scatter_matrix(lay, me, code_ref[0, 0:1, :], s, count)
        put_blocks(lay, outs, s, count, 0, nn(chosen, rows_ref[...]))


def sort_rows(lay, places, grads, code):
    spec = pltpu.PrefetchScalarGridSpec(
        num_scalar_prefetch=1,
        grid=(lay.heads,),
        in_specs=[pl.BlockSpec((256, LANES), lambda h, _: (0, h))] * 4
        + [pl.BlockSpec((1, 8, lay.tokens), lambda h, _: (h, 0, 0))],
        out_specs=lay.specs(lay.half_rows, lambda h, _: h),
        scratch_shapes=[pltpu.VMEM((lay.tokens, LANES), bf16)],
    )
    return pl.pallas_call(
        partial(sort_kernel, lay),
        grid_spec=spec,
        out_shape=lay.shapes(lay.heads * lay.half_rows),
        name="sort_rows",
        cost_estimate=cost(SORT_US),
    )(places, *grads, code)


def pack_kernel(
    query_ref, key_ref, value_ref, output_ref, inner_ref, outer_ref,
    bias_ref, gain_ref, shift_ref, inner_bias_ref, piece_ref, shard_ref,
):
    depth, width = query_ref.shape
    heads = width // HEAD_DIM
    query, key, value = (ref[...].astype(f32) for ref in (query_ref, key_ref, value_ref))
    cut = [slice(h * HEAD_DIM, (h + 1) * HEAD_DIM) for h in range(heads)]
    columns = [part for at in cut for part in (query[:, at], key[:, at])] + [value]
    have = 3 * width
    fill = -have % LANES
    if fill:
        columns.append(jnp.zeros((depth, fill), f32))
    columns = jnp.concatenate(columns, axis=1).astype(bf16)
    piece_ref[:depth, : have + fill] = columns
    inner_bias = inner_bias_ref[...].astype(f32)
    vectors = jnp.concatenate(
        [ref[...].astype(f32) for ref in (bias_ref, gain_ref, shift_ref)]
        + [inner_bias[:, i * depth : (i + 1) * depth] for i in range(4)]
        + [jnp.zeros((4, depth), f32)],
        axis=0,
    )
    if depth < LANES:
        vectors = jnp.concatenate([vectors, jnp.zeros((16, LANES - depth), f32)], axis=1)
    piece_ref[:16, have + fill :] = vectors.astype(bf16)
    shard_ref[:, :D] = inner_ref[...]
    turned = output_ref[...].astype(f32).T
    shard_ref[:, D : 2 * D] = outer_ref[...]
    shard_ref[:, 2 * D :] = jnp.concatenate(
        [turned[:, at] for at in cut for _ in range(2)], axis=1
    ).astype(bf16)


def pack_weights(*arrays):
    depth, width = arrays[0].shape
    columns = -(-3 * width // LANES) * LANES
    return pl.pallas_call(
        pack_kernel,
        out_shape=[
            jax.ShapeDtypeStruct((max(depth, 16), columns + LANES), bf16),
            jax.ShapeDtypeStruct((depth, 2 * D + 2 * width), bf16),
        ],
        name="pack_weights",
        cost_estimate=QUICK,
    )(*arrays)


def assemble_kernel(lay, place_ref, *refs):
    pieces, (weight_ref, bias_ref, par_ref, part_ref) = refs[: lay.peers], refs[lay.peers :]
    me, place = place_ref[0], place_ref[1]
    depth = D // lay.peers
    for s in range(lay.peers):
        d = me ^ s
        at = pl.ds(pl.multiple_of(d * depth, 16), depth)
        columns = weight_ref.shape[1]
        weight_ref[at, :] = pieces[s][:, :columns]
        part_ref[d] = pieces[s][:16, columns:].astype(f32)

    def whole(row, rows=1, peers=range(lay.peers)):
        return jnp.concatenate(
            [part_ref[d, row + i : row + i + 1, :depth] for d in peers for i in range(rows)], axis=1
        )

    vectors = [whole(r) for r in range(8)]
    each = lay.peers // 4
    vectors += [whole(8, 4, range(j * each, (j + 1) * each)) for j in range(4)]
    par_ref[...] = jnp.concatenate(vectors + [jnp.zeros((4, D), f32)], axis=0)
    width = lay.heads * HEAD_DIM

    def own(vector):
        out = vector[:, :width]
        for p in range(1, D // width):
            out = jnp.where(place == p, vector[:, p * width : (p + 1) * width], out)
        return out

    query = own(vectors[0])
    zero = jnp.zeros((1, HEAD_DIM), f32)
    columns = [
        part for h in range(lay.heads) for part in (query[:, h * HEAD_DIM : (h + 1) * HEAD_DIM], zero)
    ] + [own(vectors[1])]
    fill = bias_ref.shape[1] - 3 * width
    if fill:
        columns.append(jnp.zeros((1, fill), f32))
    bias_ref[...] = jnp.broadcast_to(jnp.concatenate(columns, axis=1), bias_ref.shape)


def assemble_weights(lay, places, pieces):
    columns = pieces[0].shape[1] - LANES
    vmem = pl.BlockSpec(memory_space=pltpu.VMEM)
    return pl.pallas_call(
        partial(assemble_kernel, lay),
        in_specs=[pl.BlockSpec(memory_space=pltpu.SMEM)] + [vmem] * lay.peers,
        out_specs=[vmem] * 3,
        out_shape=[
            jax.ShapeDtypeStruct((D, columns), bf16),
            jax.ShapeDtypeStruct((8, columns), f32),
            jax.ShapeDtypeStruct((16, D), f32),
        ],
        scratch_shapes=[pltpu.VMEM((lay.peers, 16, LANES), f32)],
        name="assemble_weights",
        cost_estimate=QUICK,
    )(places, *pieces)


def mean_rows(v):
    return jnp.sum(v, axis=1, keepdims=True) * (1.0 / D)


def norm_forward(rows):
    centred = rows - mean_rows(rows)
    inv = lax.rsqrt(mean_rows(centred * centred) + EPSILON)
    return centred * inv, inv


def norm_backward(scaled, normed, inv):
    return inv * (scaled - mean_rows(scaled) - normed * mean_rows(scaled * normed))


TALL = 512


def middle_kernel(
    place_ref,
    att0,
    att1,
    att2,
    att3,
    hidden_ref,
    cot_ref,
    par_ref,
    w0,
    w1,
    w2,
    w3,
    out_ref,
    act_ref,
    pre_ref,
    low_ref,
    ffn_grad_ref,
    branch_grad_ref,
    h1_ref,
    grad0,
    grad1,
    grad2,
    grad3,
    vec_ref,
    first_ref,
    normed_ref,
    inv_ref,
    slope_ref,
    sum_ref,
    h2_ref,
    weight_ref,
    sems,
):
    step = pl.program_id(0)
    place = place_ref[1]
    project = slice(2 * D, None)

    def fetch(t, part):
        width = att0.shape[1]
        at = (pl.ds(2 * D, width), pl.ds(0, 2 * D))[part]
        source = (w0, w1, w2, w3)[t]
        return pltpu.make_async_copy(source.at[:, at], weight_ref.at[t, :, at], sems.at[part, t])

    for t in range(4):

        @pl.when(step == t + 1)
        def _():
            fetch(t, 1).wait()

    @pl.when(step == 0)
    def _():
        for t in range(4):
            fetch(t, 0).start()
        for t in range(4):
            fetch(t, 1).start()
        for t in range(4):
            fetch(t, 0).wait()
        vec_ref[...] = jnp.zeros_like(vec_ref)

        @loop(2)
        def _(side):
            branch = jnp.zeros((256, D), f32)
            for t, att_ref in enumerate((att0, att1, att2, att3)):
                att = att_ref[...]
                lane = lane_iota(256, att.shape[1]) % LANES
                own = (lane >= HEAD_DIM).astype(i32) == side
                branch = branch + nt(jnp.where(own, att, jnp.zeros_like(att)), weight_ref[t, :, project])
            at = pl.ds(pl.multiple_of(side * 256, 256), 256)
            rows = hidden_ref[at, :].astype(f32) + (branch + par_ref[2:3, :])
            normed, inv = norm_forward(rows)
            first = normed * par_ref[4:5, :] + par_ref[6:7, :]
            first_ref[at, :] = first
            normed_ref[at, :] = normed
            inv_ref[at, :] = jnp.broadcast_to(inv, (256, LANES))
            low_ref[at, :] = first.astype(bf16)

        sum_ref[...] = jnp.zeros_like(sum_ref)

    @pl.when((step >= 1) & (step <= 4))
    def _():
        j = step - 1

        @loop(512 // TALL)
        def _(side):
            at = pl.ds(pl.multiple_of(side * TALL, TALL), TALL)
            pre = nn(low_ref[at, :], weight_ref[j, :, :D]) + par_ref[pl.ds(8 + (place ^ j), 1), :]
            cdf = 0.5 * (1.0 + lax.erf(pre * (1.0 / math.sqrt(2.0))))
            slope_ref[j, at, :] = cdf + pre * jnp.exp(-0.5 * pre * pre) * (1.0 / math.sqrt(2.0 * math.pi))
            act = (pre * cdf).astype(bf16)
            act_ref[at, :] = act
            sum_ref[at, :] += nt(act, weight_ref[j, :, D : 2 * D])

    @pl.when(step == 4)
    def _():

        @loop(4)
        def _(side):
            at = pl.ds(pl.multiple_of(side * 128, 128), 128)
            rows = first_ref[at, :] + (sum_ref[at, :] + par_ref[3:4, :])
            normed, inv = norm_forward(rows)
            out_ref[at, :] = (normed * par_ref[5:6, :] + par_ref[7:8, :]).astype(bf16)
            cot = cot_ref[at, :].astype(f32)
            grad = norm_backward(cot * par_ref[5:6, :], normed, inv)
            grad_low = grad.astype(bf16)
            h2_ref[at, :] = grad
            ffn_grad_ref[at, :] = grad_low
            vec_ref[3:4, :] += jnp.sum(grad_low.astype(f32), axis=0, keepdims=True)
            vec_ref[5:6, :] += jnp.sum(cot * normed, axis=0, keepdims=True)
            vec_ref[7:8, :] += jnp.sum(cot, axis=0, keepdims=True)

        sum_ref[...] = jnp.zeros_like(sum_ref)

    @pl.when(step >= 5)
    def _():
        j = 8 - step
        vec_ref[pl.ds(8 + (place ^ j), 1), :] = jnp.zeros((1, D), f32)

        @loop(512 // TALL)
        def _(side):
            at = pl.ds(pl.multiple_of(side * TALL, TALL), TALL)
            grad_act = nn(ffn_grad_ref[at, :], weight_ref[j, :, D : 2 * D])
            grad_pre = (grad_act * slope_ref[j, at, :]).astype(bf16)
            pre_ref[at, :] = grad_pre
            vec_ref[pl.ds(8 + (place ^ j), 1), :] += jnp.sum(grad_pre.astype(f32), axis=0, keepdims=True)
            sum_ref[at, :] += nt(grad_pre, weight_ref[j, :, :D])

    @pl.when(step == 8)
    def _():

        @loop(4)
        def _(side):
            at = pl.ds(pl.multiple_of(side * 128, 128), 128)
            grad_first = h2_ref[at, :] + sum_ref[at, :]
            normed = normed_ref[at, :]
            grad = norm_backward(grad_first * par_ref[4:5, :], normed, inv_ref[at, 0:1])
            grad_low = grad.astype(bf16)
            h1_ref[at, :] = grad
            branch_grad_ref[at, :] = grad_low
            vec_ref[2:3, :] += jnp.sum(grad_low.astype(f32), axis=0, keepdims=True)
            vec_ref[4:5, :] += jnp.sum(grad_first * normed, axis=0, keepdims=True)
            vec_ref[6:7, :] += jnp.sum(grad_first, axis=0, keepdims=True)

        for t, grad_ref in enumerate((grad0, grad1, grad2, grad3)):
            both = nn(branch_grad_ref[...], weight_ref[t, :, project])
            lane = lane_iota(256, both.shape[1]) % LANES
            grad_ref[...] = jnp.where(lane < HEAD_DIM, both[:256], both[256:]).astype(bf16)


def middle(places, att, hidden, cotangent, params, weights):
    width = att[0].shape[1]
    rows = 512

    def up(s, q):
        return (0, jnp.clip(s - 1, 0, 3))

    def down(s, q):
        return (0, jnp.clip(8 - s, 0, 3))

    def whole(rank):
        return lambda s, q: (0,) * rank

    square = pl.BlockSpec((rows, D), whole(2))
    exchanged = pl.BlockSpec((256, width), whole(2))
    spec = pltpu.PrefetchScalarGridSpec(
        num_scalar_prefetch=1,
        grid=(9,),
        in_specs=[exchanged] * 4
        + [
            pl.BlockSpec((rows, D), lambda s, q: (q[1], 0)),
            pl.BlockSpec((rows, D), lambda s, q: (q[1], 0)),
            pl.BlockSpec((16, D), whole(2)),
        ]
        + [pl.BlockSpec(memory_space=pl.ANY)] * 4,
        out_specs=[
            square,
            pl.BlockSpec((rows, D), up),
            pl.BlockSpec((rows, D), down),
            square,
            square,
            square,
            square,
        ]
        + [exchanged] * 4
        + [pl.BlockSpec((16, D), whole(2))],
        scratch_shapes=[
            pltpu.VMEM((rows, D), f32),
            pltpu.VMEM((rows, D), f32),
            pltpu.VMEM((rows, LANES), f32),
            pltpu.VMEM((4, rows, D), f32),
            pltpu.VMEM((rows, D), f32),
            pltpu.VMEM((rows, D), f32),
            pltpu.VMEM((4, D, 2 * D + width), bf16),
            pltpu.SemaphoreType.DMA((2, 4)),
        ],
    )
    out = pl.pallas_call(
        middle_kernel,
        grid_spec=spec,
        out_shape=[
            jax.ShapeDtypeStruct((rows, D), bf16),
            jax.ShapeDtypeStruct((rows, FF), bf16),
            jax.ShapeDtypeStruct((rows, FF), bf16),
            jax.ShapeDtypeStruct((rows, D), bf16),
            jax.ShapeDtypeStruct((rows, D), bf16),
            jax.ShapeDtypeStruct((rows, D), bf16),
            jax.ShapeDtypeStruct((rows, D), f32),
        ]
        + [jax.ShapeDtypeStruct((256, width), bf16)] * 4
        + [jax.ShapeDtypeStruct((16, D), f32)],
        compiler_params=pltpu.CompilerParams(vmem_limit_bytes=50 * 1024 * 1024),
        name="middle",
        cost_estimate=QUICK,
    )(places, *att, hidden, cotangent, params, *weights)
    return out[:7], out[7:11], out[11]


def weight_grad_kernel(chunks, adds, place_ref, act_ref, pre_ref, low_ref, ffn_ref, branch_ref, *refs):
    att_refs, add_refs, out_ref = refs[:chunks], refs[chunks : chunks + adds], refs[-1]

    def put(at, part):
        for ref in add_refs:
            part = part + ref[:, at].astype(f32)
        out_ref[:, at] = part.astype(bf16)

    put(slice(0, D), tn(low_ref[...], pre_ref[...]))
    put(slice(D, 2 * D), tn(ffn_ref[...], act_ref[...]))
    for i in range(chunks):

        @pl.when(pl.program_id(0) == i)
        def _():
            att = att_refs[i][...]
            low = lane_iota(256, att.shape[1]) % LANES < HEAD_DIM
            zero = jnp.zeros_like(att)
            both = jnp.concatenate([jnp.where(low, att, zero), jnp.where(low, zero, att)], axis=0)
            put(slice(2 * D, 2 * D + att.shape[1]), tn(branch_ref[...], both))


def weight_grads(places, saved, att, first, chunks, adds):
    act, pre, low, ffn_grad, branch_grad = saved
    rows = act.shape[0]
    width = att[0].shape[1]
    total = 2 * D + width
    cut = D // 2

    def chunk(s, i, q):
        return (0, first - 2 * s)

    part = pl.BlockSpec((rows, cut), lambda s, i, q: (0, i))
    spec = pltpu.PrefetchScalarGridSpec(
        num_scalar_prefetch=1,
        grid=(chunks, 2),
        in_specs=[pl.BlockSpec((rows, D), chunk)] * 2
        + [part] * 3
        + [pl.BlockSpec((256, width), lambda s, i, q: (0, 0))] * chunks
        + [pl.BlockSpec((cut, total), lambda s, i, q, k=k: (2 * k + i, 0)) for _, k in adds],
        out_specs=pl.BlockSpec((cut, total), lambda s, i, q: (2 * s + i, 0)),
    )
    return pl.pallas_call(
        partial(weight_grad_kernel, chunks, len(adds)),
        grid_spec=spec,
        out_shape=jax.ShapeDtypeStruct((chunks * D, total), bf16),
        compiler_params=pltpu.CompilerParams(vmem_limit_bytes=VMEM),
        name="weight_grads",
        cost_estimate=QUICK,
    )(
        places, act, pre, low, ffn_grad, branch_grad,
        *[att[first - 2 * s] for s in range(chunks)], *[a for a, _ in adds],
    )


def collect_kernel(lay, place_ref, *refs):
    rows_refs = refs[: lay.arrays]
    code_ref, dense_ref = refs[lay.arrays :]
    me = place_ref[0]
    tokens = dense_ref.shape[0]
    low = lane_iota(tokens) < HEAD_DIM
    firsts, seconds = [], []
    for h in range(lay.heads):
        column = as_column(code_ref[h, 0:1, :])
        half = as_column(code_ref[h, 1:2, :])
        planes = [block_rows(lay, rows_refs, (h * 3 + x) * lay.half_rows) for x in range(3)]
        found = nn(gather_matrix(lay, me, column), jnp.concatenate(planes, axis=1))
        one, two = [], []
        for x in range(3):
            part = found[:, x * LANES : (x + 1) * LANES]
            turned = pltpu.roll(part, HEAD_DIM, 1)
            one.append(jnp.where(half == 0, part, turned))
            two.append(jnp.where(half == 1, part, turned))
        firsts.append(one)
        seconds.append(two)
    tiles = [jnp.where(low, firsts[h][0], seconds[h][1]) for h in range(lay.heads)]
    for h in range(0, lay.heads, 2):
        right = seconds[h + 1][2] if h + 1 < lay.heads else jnp.zeros((tokens, LANES), f32)
        tiles.append(jnp.where(low, firsts[h][2], right))
    dense_ref[...] = jnp.concatenate(tiles, axis=1).astype(bf16)


def collect(lay, places, returned, code, width):
    tokens = COLLECT_ROWS
    spec = pltpu.PrefetchScalarGridSpec(
        num_scalar_prefetch=1,
        grid=(lay.tokens // tokens,),
        in_specs=lay.specs(lay.data_rows, only(0))
        + [pl.BlockSpec((lay.heads, 8, tokens), lambda c, q: (0, 0, c))],
        out_specs=pl.BlockSpec((tokens, width), lambda c, q: (c, 0)),
    )
    return pl.pallas_call(
        partial(collect_kernel, lay),
        grid_spec=spec,
        out_shape=jax.ShapeDtypeStruct((lay.tokens, width), bf16),
        compiler_params=pltpu.CompilerParams(vmem_limit_bytes=VMEM),
        name="collect",
        cost_estimate=cost(COLLECT_US),
    )(places, *returned, code)


def half_rows_at(g, s, place):
    core = place % 2
    return jnp.where(s == 0, 1 - core, core) * 2 + g


def spread_kernel(g, place_ref, dense_ref, w_ref, h1_ref, other_ref, mine_ref):
    step, place = pl.program_id(0), place_ref[1]
    own = (half_rows_at(g, step, place) == place).astype(f32)
    part = nt(dense_ref[...], w_ref[...]) + own * h1_ref[...]

    @pl.when(step == 0)
    def _():
        other_ref[...] = part.astype(bf16)

    @pl.when(step == 1)
    def _():
        mine_ref[...] = part.astype(bf16)


def spread_grads(g, places, dense, weights, grad_h1):
    width = weights.shape[1]
    whole = lambda s, q: (0, 0)
    spec = pltpu.PrefetchScalarGridSpec(
        num_scalar_prefetch=1,
        grid=(2,),
        in_specs=[
            pl.BlockSpec((512, width), lambda s, q: (half_rows_at(g, s, q[1]), 0)),
            pl.BlockSpec((D, width), whole),
            pl.BlockSpec((512, D), whole),
        ],
        out_specs=[pl.BlockSpec((512, D), whole)] * 2,
    )
    return pl.pallas_call(
        partial(spread_kernel, g),
        grid_spec=spec,
        out_shape=[jax.ShapeDtypeStruct((512, D), bf16)] * 2,
        compiler_params=pltpu.CompilerParams(vmem_limit_bytes=VMEM),
        name="spread_grads",
        cost_estimate=cost(SPREAD_US),
    )(places, dense, weights, grad_h1)


def head_grad_kernel(lay, place_ref, x_ref, dense_ref, vec_ref, *refs):
    out_ref, total_ref = refs
    step = pl.program_id(0)

    @pl.when(step == 0)
    def _():
        total_ref[...] = tn(x_ref[...], dense_ref[...])

    @pl.when(step > 0)
    def _():
        total_ref[...] += tn(x_ref[...], dense_ref[...])

    @pl.when(step == 3)
    def _():
        depth = D // lay.peers
        if not lay.direct:
            out_ref[...] = total_ref[...].astype(bf16)
            return
        for d in range(lay.peers):
            out_ref[d, :depth, :] = total_ref[d * depth : (d + 1) * depth, :].astype(bf16)
            vector = vec_ref[d]
            high = vector.astype(bf16).astype(f32)
            width = total_ref.shape[1]
            out_ref[d, depth:, :] = jnp.concatenate(
                [high, vector - high, jnp.zeros((16, width - 2 * LANES), f32)], axis=1
            ).astype(bf16)


def head_grads(lay, places, x, dense, vec):
    width = dense.shape[1]
    depth = D // lay.peers
    shape = (lay.peers, depth + 16, width) if lay.direct else (D, width)
    spec = pltpu.PrefetchScalarGridSpec(
        num_scalar_prefetch=1,
        grid=(4,),
        in_specs=[
            pl.BlockSpec((512, D), lambda s, q: (s, 0)),
            pl.BlockSpec((512, width), lambda s, q: (s, 0)),
            pl.BlockSpec(vec.shape, lambda s, q: (0, 0, 0)),
        ],
        out_specs=pl.BlockSpec(shape, lambda s, q: (0,) * len(shape)),
        scratch_shapes=[pltpu.VMEM((D, width), f32)],
    )
    return pl.pallas_call(
        partial(head_grad_kernel, lay),
        grid_spec=spec,
        out_shape=jax.ShapeDtypeStruct(shape, bf16),
        compiler_params=pltpu.CompilerParams(vmem_limit_bytes=VMEM),
        name="head_grads",
        cost_estimate=cost(HEAD_GRADS_US),
    )(places, x, dense, vec)


def finish_heads_kernel(*refs):
    parts, outs = refs[0], refs[1:]
    depth, width = outs[0].shape
    heads = width // HEAD_DIM
    total = parts[0].astype(f32)
    for d in range(1, parts.shape[0]):
        total = total + parts[d].astype(f32)
    grads = total[:depth]
    cut = [slice(h * LANES, h * LANES + HEAD_DIM) for h in range(heads)]
    outs[0][...] = jnp.concatenate([grads[:, at] for at in cut], axis=1)
    cut = [slice(h * LANES + HEAD_DIM, (h + 1) * LANES) for h in range(heads)]
    outs[1][...] = jnp.concatenate([grads[:, at] for at in cut], axis=1)
    outs[2][...] = grads[:, 2 * width : 3 * width]
    outs[3][...] = total[depth:, :LANES] + total[depth:, LANES : 2 * LANES]


def finish_heads(parts, depth, width):
    shapes = [(depth, width)] * 3 + [(16, LANES)]
    return pl.pallas_call(
        finish_heads_kernel,
        out_shape=[jax.ShapeDtypeStruct(s, f32) for s in shapes],
        name="finish_heads",
        cost_estimate=QUICK,
    )(parts)


def finish_vectors_kernel(depth, own_ref, other_ref, bias_ref, gain_ref, shift_ref, inner_ref):
    total = (own_ref[...] + other_ref[...])[:, :depth]
    bias_ref[...] = total[:4]
    gain_ref[...] = total[4:6]
    shift_ref[...] = total[6:8]
    inner_ref[...] = total[8:12]


def finish_vectors(own, other, depth):
    return pl.pallas_call(
        partial(finish_vectors_kernel, depth),
        out_shape=[jax.ShapeDtypeStruct((n, depth), f32) for n in (4, 2, 2, 4)],
        name="finish_vectors",
        cost_estimate=QUICK,
    )(own, other)


def finish_middle_kernel(grad_ref, inner_ref, outer_ref, output_ref):
    inner_ref[...] = grad_ref[:, :D].astype(f32)
    outer_ref[...] = grad_ref[:, D : 2 * D].astype(f32)
    rest = grad_ref[:, 2 * D :].astype(f32)
    planes = [rest[:, i * LANES : (i + 1) * LANES] for i in range(rest.shape[1] // LANES)]
    folded = [p[:, :HEAD_DIM] + p[:, HEAD_DIM:] for p in planes]
    output_ref[...] = jnp.concatenate(folded, axis=1).T


def finish_middle(grads):
    depth, total = grads.shape
    return pl.pallas_call(
        finish_middle_kernel,
        out_shape=[
            jax.ShapeDtypeStruct((depth, D), f32),
            jax.ShapeDtypeStruct((depth, D), f32),
            jax.ShapeDtypeStruct(((total - 2 * D) // 2, depth), f32),
        ],
        name="finish_middle",
        cost_estimate=QUICK,
    )(grads)


def order_kernel(place_ref, *refs):
    parts, out_ref, rows_ref, sems = refs[:4], refs[4], refs[5], refs[6]
    rows = rows_ref.shape[1]

    def take(i):
        return pltpu.make_async_copy(parts[i], rows_ref.at[i], sems.at[0, i])

    def put(i):
        at = pl.ds(pl.multiple_of(place_ref[i] * rows, rows), rows)
        return pltpu.make_async_copy(rows_ref.at[i], out_ref.at[at, :], sems.at[1, i])

    for i in range(4):
        take(i).start()
    for i in range(4):
        take(i).wait()
        put(i).start()
    for i in range(4):
        put(i).wait()


def order_quarters(order, quarters):
    rows, width = quarters[0].shape
    dtype = quarters[0].dtype
    return pl.pallas_call(
        order_kernel,
        in_specs=[pl.BlockSpec(memory_space=pltpu.SMEM)]
        + [pl.BlockSpec(memory_space=pl.ANY)] * 4,
        out_specs=pl.BlockSpec(memory_space=pl.ANY),
        out_shape=jax.ShapeDtypeStruct((4 * rows, width), dtype),
        scratch_shapes=[pltpu.VMEM((4, rows, width), dtype), pltpu.SemaphoreType.DMA((2, 4))],
        name="order_quarters",
        cost_estimate=QUICK,
    )(order, *quarters)


def over_rows(lay, blocks, near_first=False):
    if not lay.direct:
        return [lax.all_to_all(blocks[0], "dp", split_axis=0, concat_axis=0, tiled=True)]
    out = [blocks[0]]
    for s in range(1, lay.peers):
        rows = blocks[s]
        if near_first and s >= lay.peers - 2:
            rows = after(rows, out[s - lay.peers + 3])
        out.append(lax.ppermute(rows, "dp", [(i, i ^ s) for i in range(lay.peers)]))
    return out


def in_hbm(rows):
    return pltpu.with_memory_space_constraint(rows, pltpu.HBM)


def share_pieces(lay, piece):
    def flip(rows, s):
        return lax.ppermute(rows, "dp", [(i, i ^ s) for i in range(lay.peers)])

    half = lay.peers // 2
    far = flip(piece, half)
    near = [piece] + [flip(piece, s) for s in range(1, half)]
    return near + [far] + [flip(far, s) for s in range(1, half)]


def after(value, *others):
    return lax.optimization_barrier((value, *others))[0]


def swap(rows, flip):
    return lax.ppermute(rows, "mp", [(i, i ^ flip) for i in range(4)])


def over_heads(blocks):
    return [blocks[0]] + [swap(blocks[t], t) for t in range(1, 4)]


def on_device(
    hidden_in,
    cotangent,
    w_query,
    w_key,
    w_value,
    w_output,
    w_inner,
    w_outer,
    biases,
    gains,
    shifts,
    inner_bias,
    lengths,
    padding,
    cluster_perm,
):
    peers = lax.axis_size("dp")
    tokens = hidden_in.shape[0]
    heads = cluster_perm.shape[0]
    lay = Layout(peers, tokens, heads)
    place = lax.axis_index("mp")
    me = lax.axis_index("dp")
    places = jnp.stack([me, place]).astype(i32)
    hidden_in = in_hbm(hidden_in)
    depth = w_query.shape[0]
    width = heads * HEAD_DIM

    piece, shard = pack_weights(
        w_query, w_key, w_value, w_output, w_inner, w_outer.T,
        biases, gains, shifts, inner_bias.reshape(1, -1),
    )
    own_w = lax.all_gather(shard, "dp", axis=0, tiled=True)
    far_w = swap(own_w, 2)
    if lay.direct:
        weights, bias, params = assemble_weights(lay, places, share_pieces(lay, piece))
    else:
        weights, bias, params = gather_weights(lay, place, piece)

    weights = in_hbm(weights)
    code = in_hbm(place_tokens(lay, cluster_perm))
    sent = project_rows(lay, places, hidden_in, weights, bias, code, padding.reshape(1, tokens))
    arrived = over_rows(lay, sent, near_first=True)
    mixed = over_rows(lay, attend(lay, arrived))
    found = unsort_rows(lay, places, mixed, code)
    att = over_heads(found)
    far_w = after(far_w, found[0])
    middle_w = [own_w, swap(own_w, 1), far_w, swap(far_w, 1)]
    saved, att_grad, vec = middle(places, att, hidden_in, cotangent, params, middle_w)
    out_quarter, act, pre_grad, first_low, ffn_grad, branch_grad, grad_h1 = saved
    saved = tuple(in_hbm(a) for a in (act, pre_grad, first_low, ffn_grad, branch_grad))
    att = [in_hbm(a) for a in att]

    got = over_heads(att_grad)
    from_core = swap(weight_grads(places, saved, att, 3, 2, []), 1)
    grads = sort_rows(lay, places, got, code)
    ready = (after(act, grads[0]),) + saved[1:]
    from_far = swap(weight_grads(places, ready, att, 2, 1, [(from_core, 0)]), 2)
    grads = over_rows(lay, grads)
    slot_grads, bias_sums = attend_back(lay, arrived, grads)

    summed = weight_grads(places, saved, att, 0, 1, [(from_core, 1), (from_far, 0)])
    returned = over_rows(lay, slot_grads)
    head_sums = bias_sums[:, :2].reshape(heads, 2, 2, HEAD_DIM).sum(axis=2)
    head_sums = head_sums.transpose(1, 0, 2).reshape(2, width)
    vec = lax.dynamic_update_slice(vec[:12], head_sums, (0, place * width))
    vec = jnp.concatenate(
        [vec[:8].reshape(8, peers, depth).transpose(1, 0, 2), vec[8:].reshape(peers, 4, depth)],
        axis=1,
    )
    spread = jnp.pad(vec, ((0, 0), (0, 4), (0, (-depth) % LANES)))
    reduced = lax.psum_scatter(after(summed, *returned), "dp", scatter_dimension=0, tiled=True)
    far = swap(after(out_quarter, summed), 2)
    dense = collect(lay, places, returned, code, weights.shape[1])
    terms = head_grads(lay, places, hidden_in, dense, spread)
    dense = after(dense, terms, far)
    groups = [spread_grads(g, places, dense, weights, grad_h1) for g in range(2)]
    chips = [
        (mine.astype(f32) + swap(other, 1).astype(f32)).astype(bf16) for other, mine in groups
    ]
    hidden_out = order_quarters(
        jnp.stack([place, place ^ 2, place ^ 1, place ^ 3]).astype(i32),
        [out_quarter, far, swap(out_quarter, 1), swap(far, 1)],
    )
    if lay.direct:
        terms = lax.all_to_all(terms, "dp", split_axis=0, concat_axis=0, tiled=True)
        ends = finish_heads(terms, depth, width)
    else:
        ends = reduce_heads(terms, vec, depth, width)
    ready = [
        (after(chip, ends[0]).astype(f32) + swap(chip, 2).astype(f32)).astype(bf16)
        for chip in chips
    ]
    core = place % 2
    grad_hidden = order_quarters(
        jnp.stack([2 * core, 2 * core + 1, 2 - 2 * core, 3 - 2 * core]).astype(i32),
        ready + [swap(part, 1) for part in ready],
    )

    small = ends[3] + swap(ends[3], 1)
    small = finish_vectors(small, swap(small, 2), depth)
    grad_inner, grad_outer, grad_output = finish_middle(reduced)
    return (
        hidden_out,
        grad_hidden,
        ends[0],
        ends[1],
        ends[2],
        grad_output,
        grad_inner,
        grad_outer.T,
        small[0],
        small[1],
        small[2],
        small[3].reshape(-1),
    )


def gather_weights(lay, place, piece):
    depth = D // lay.peers
    width = lay.heads * HEAD_DIM
    got = lax.all_gather(piece, "dp", axis=0, tiled=False)
    columns = piece.shape[1] - LANES
    weights = got[:, :depth, :columns].reshape(D, columns)
    vectors = got[:, :12, columns : columns + depth].astype(f32)
    params = vectors[:, :8].transpose(1, 0, 2).reshape(8, D)
    params = jnp.concatenate([params, vectors[:, 8:].reshape(4, D), jnp.zeros((4, D), f32)], axis=0)
    own = lax.dynamic_slice_in_dim(params[:2], place * width, width, 1)
    query = own[0].reshape(lay.heads, HEAD_DIM)
    query = jnp.concatenate([query, jnp.zeros_like(query)], axis=1).reshape(-1)
    row = jnp.concatenate([query, own[1], jnp.zeros(weights.shape[1] - 3 * width, f32)])
    return weights, jnp.broadcast_to(row[None], (8, row.shape[0])), params


def reduce_heads(grads, vec, depth, width):
    total = lax.psum_scatter(grads, "dp", scatter_dimension=0, tiled=True).astype(f32)
    pairs = total[:, : 2 * width].reshape(depth, -1, 2, HEAD_DIM)
    small = lax.psum_scatter(vec, "dp", scatter_dimension=0, tiled=False)
    small = jnp.pad(small, ((0, 4), (0, LANES - depth)))
    return (
        pairs[:, :, 0].reshape(depth, width),
        pairs[:, :, 1].reshape(depth, width),
        total[:, 2 * width : 3 * width],
        small,
    )


def solution(mesh):
    placed = (
        P("dp", None),
        P("dp", None),
        P("dp", "mp"),
        P("dp", "mp"),
        P("dp", "mp"),
        P("mp", "dp"),
        P("dp", "mp"),
        P("mp", "dp"),
        P(None, "dp"),
        P(None, "dp"),
        P(None, "dp"),
        P("dp"),
        P(),
        P("dp"),
        P("mp", "dp"),
    )
    return jax.shard_map(
        on_device,
        mesh=mesh,
        in_specs=placed,
        out_specs=(
            P("dp", None),
            P("dp", None),
            P("dp", "mp"),
            P("dp", "mp"),
            P("dp", "mp"),
            P("mp", "dp"),
            P("dp", "mp"),
            P("mp", "dp"),
            P(None, "dp"),
            P(None, "dp"),
            P(None, "dp"),
            P("dp"),
        ),
        check_vma=False,
    )
```

```python
from functools import partial
import math

import jax
import jax.numpy as jnp
from jax import lax
from jax.experimental import pallas as pl
from jax.experimental.pallas import tpu as pltpu
from jax.sharding import PartitionSpec as P

D = 768
HEAD_DIM = 64
FF = 3072
CLUSTER = 128
LANES = 128
EPSILON = 1e-05
MASKED = -1e30
SCALE = 1.0 / math.sqrt(HEAD_DIM)

bf16 = jnp.bfloat16
f32 = jnp.float32
i32 = jnp.int32

VMEM = 60 * 1024 * 1024


def cost(us):
    return pl.CostEstimate(flops=int(1e9 * us), bytes_accessed=int(3e6 * us), transcendentals=0)


QUICK = cost(0.001)
ATTEND_US = 46
COLLECT_US = 30
COLLECT_ROWS = 512
SPREAD_US = 3
HEAD_GRADS_US = 4
SORT_US = 80
ATTEND_BACK_US = 40


def nn(a, b):
    return lax.dot_general(a, b, (((1,), (0,)), ((), ())), preferred_element_type=f32)


def nt(a, b):
    return lax.dot_general(a, b, (((1,), (1,)), ((), ())), preferred_element_type=f32)


def tn(a, b):
    return lax.dot_general(a, b, (((0,), (0,)), ((), ())), preferred_element_type=f32)


def lane_iota(rows, lanes=LANES):
    return lax.broadcasted_iota(i32, (rows, lanes), 1)


def sublane_iota(rows, lanes=LANES):
    return lax.broadcasted_iota(i32, (rows, lanes), 0)


def as_column(row):
    parts = [
        jnp.broadcast_to(row[:, i * LANES : (i + 1) * LANES], (LANES, LANES)).T
        for i in range(row.shape[1] // LANES)
    ]
    return parts[0] if len(parts) == 1 else jnp.concatenate(parts, axis=0)


def loop(count):
    def run(step):
        def body(i, carry):
            step(i)
            return carry

        lax.fori_loop(0, count, body, 0)

    return run


class Layout:
    def __init__(self, peers, tokens, heads):
        self.peers, self.tokens, self.heads = peers, tokens, heads
        self.stripe = min(16, peers)
        self.runs = peers // self.stripe
        self.per_dev = CLUSTER // self.stripe
        self.rows_peer = tokens // peers
        self.half_rows = self.rows_peer // 2
        self.pairs = self.half_rows // self.per_dev
        self.packed = tokens // 2
        self.clusters = peers * tokens // CLUSTER
        self.data_rows = 9 * self.half_rows
        self.direct = self.half_rows == LANES
        self.arrays = peers if self.direct else 1

    def peer(self, me, s):
        return (me ^ s) if self.direct else s

    def shapes(self, rows, dtype=bf16):
        lead = () if self.direct else (self.peers,)
        return [jax.ShapeDtypeStruct(lead + (rows, LANES), dtype)] * self.arrays

    def specs(self, rows, at):
        if self.direct:
            return [pl.BlockSpec((rows, LANES), lambda *g: (at(*g), 0))] * self.arrays
        return [pl.BlockSpec((self.peers, rows, LANES), lambda *g: (0, at(*g), 0))]

    def view(self, refs, s):
        return refs[s] if self.direct else refs[0].at[s]


def only(at):
    return lambda *g: at


def place_kernel(lay, perm_ref, code_ref):
    groups = lay.clusters
    shift = CLUSTER.bit_length() - 1
    blocks = lay.tokens // LANES
    before = sublane_iota(LANES, 2 * LANES)
    after = lane_iota(LANES, 2 * LANES)
    ahead_of = jnp.where((before < after) | (after >= LANES), 1.0, 0.0).astype(bf16)

    def members(h, b):
        row = lax.shift_right_logical(perm_ref[h : h + 1, b * LANES : (b + 1) * LANES], shift)
        return jnp.broadcast_to(row, (groups, LANES)) == sublane_iota(groups)

    for h in range(lay.heads):
        if lay.runs == 1:
            carry = (sublane_iota(groups) * lay.per_dev).astype(f32)
        else:
            counts = jnp.zeros((groups, LANES), f32)
            for b in range(blocks):
                member = jnp.where(members(h, b), 1.0, 0.0).astype(bf16)
                counts = counts + nn(member, ahead_of)[:, LANES:]
            lower = jnp.where(
                sublane_iota(groups, groups) > lane_iota(groups, groups), 1.0, 0.0
            ).astype(bf16)
            carry = nn(lower, counts.astype(bf16))
        for b in range(blocks):
            member = members(h, b)
            found = nn(jnp.where(member, 1.0, 0.0).astype(bf16), ahead_of)
            rank = jnp.sum(jnp.where(member, found[:, :LANES] + carry, 0.0), axis=0, keepdims=True)
            carry = carry + found[:, LANES:]
            rank = rank.astype(i32)
            peer = lax.shift_right_logical(rank, lay.rows_peer.bit_length() - 1)
            rest = rank & (lay.rows_peer - 1)
            half = lax.shift_right_logical(rest, lay.half_rows.bit_length() - 1)
            packed = peer * lay.half_rows + (rest & (lay.half_rows - 1))
            at = slice(b * LANES, (b + 1) * LANES)
            code_ref[h, 0:1, at] = packed
            code_ref[h, 1:2, at] = half


def place_tokens(lay, perm):
    return pl.pallas_call(
        partial(place_kernel, lay),
        out_shape=jax.ShapeDtypeStruct((lay.heads, 8, lay.tokens), i32),
        name="place_tokens",
        cost_estimate=QUICK,
    )(perm)


def one_hot(equal):
    return jnp.where(equal, 1.0, 0.0).astype(bf16)


def scatter_matrix(lay, me, packed, s, blocks):
    rows = blocks * lay.half_rows
    if lay.direct:
        parts = [
            one_hot(
                jnp.broadcast_to(packed, (lay.half_rows, lay.tokens))
                == sublane_iota(lay.half_rows, lay.tokens) + lay.peer(me, s + i) * lay.half_rows
            )
            for i in range(blocks)
        ]
        return jnp.concatenate(parts, axis=0)
    wanted = sublane_iota(rows, lay.tokens) + s * lay.half_rows
    return one_hot(jnp.broadcast_to(packed, (rows, lay.tokens)) == wanted)


def gather_matrix(lay, me, column):
    lane = lane_iota(column.shape[0])
    parts = [
        one_hot(column == lane + lay.peer(me, k) * LANES) for k in range(lay.packed // LANES)
    ]
    return jnp.concatenate(parts, axis=1)


def block_rows(lay, refs, first):
    at = slice(first, first + lay.half_rows)
    if lay.direct:
        return jnp.concatenate([refs[s][at, :] for s in range(lay.peers)], axis=0)
    return refs[0][:, at, :].astype(f32).reshape(lay.packed, LANES).astype(bf16)


def put_blocks(lay, refs, s, blocks, first, rows):
    at = slice(first, first + lay.half_rows) if isinstance(first, int) else pl.ds(first, lay.half_rows)
    if lay.direct:
        for i in range(blocks):
            refs[s + i][at, :] = rows[i * LANES : (i + 1) * LANES].astype(bf16)
    else:
        rows = rows.astype(f32).reshape(blocks, lay.half_rows, LANES).astype(bf16)
        refs[0][s : s + blocks, at, :] = rows


ROWS = 512
COUNT = 4


def project_kernel(lay, steps, place_ref, x_ref, w_ref, bias_ref, code_ref, pad_ref, *rest):
    outs = rest[: lay.arrays]
    rows_ref, flag_ref = rest[lay.arrays :]
    step = pl.program_id(0)
    me = place_ref[0]
    width = 4 * LANES

    @pl.when(step < steps)
    def _():
        at = pl.ds(pl.multiple_of(step * ROWS, ROWS), ROWS)
        values = nn(x_ref[...], w_ref[...]) + bias_ref[0:1, :]
        low = lane_iota(ROWS) < HEAD_DIM
        lane_half = jnp.where(low, 0, 1)
        live = as_column(pad_ref[0:1, at])
        tiles = [values[:, i * LANES : (i + 1) * LANES] for i in range(values.shape[1] // LANES)]
        turned = [pltpu.roll(tile, HEAD_DIM, 1) for tile in tiles]
        for h in range(lay.heads):
            half = as_column(code_ref[h, 1:2, at])
            keep = half == lane_half
            v, side = lay.heads + h // 2, h % 2
            planes = (
                jnp.where(low, tiles[h], turned[h]),
                jnp.where(low, turned[h], tiles[h]),
                jnp.where(low, tiles[v], turned[v]) if side == 0 else jnp.where(low, turned[v], tiles[v]),
            )
            for x, plane in enumerate(planes):
                rows_ref[h, at, x * LANES : (x + 1) * LANES] = jnp.where(keep, plane, 0.0).astype(bf16)
            flags = jnp.where((lane_iota(ROWS) == half) & (live == 1), 1.0, 0.0)
            rows_ref[h, at, 3 * LANES :] = flags.astype(bf16)

    count = COUNT if lay.direct else 32

    @pl.when(step >= steps)
    def _():
        h = step - steps
        for s in range(0, lay.peers, count):
            chosen = scatter_matrix(lay, me, code_ref[h, 0:1, :], s, count)
            moved = nn(chosen, rows_ref[h])
            for x in range(3):
                first = pl.multiple_of((h * 3 + x) * lay.half_rows, 16)
                put_blocks(lay, outs, s, count, first, moved[:, x * LANES : (x + 1) * LANES])
            for i in range(count * lay.half_rows // LANES):
                at = slice(s * lay.half_rows + i * LANES, s * lay.half_rows + (i + 1) * LANES)
                flag_ref[h, :, at] = moved[i * LANES : (i + 1) * LANES, 3 * LANES :].T[:8]

    @pl.when(step == steps + lay.heads - 1)
    def _():
        for s in range(lay.peers):
            at = slice(s * lay.half_rows, (s + 1) * lay.half_rows)
            rows = [flag_ref[k, 0:2, at] for k in range(lay.heads)]
            block = jnp.concatenate(rows + [jnp.zeros((16 - 2 * lay.heads, lay.half_rows), f32)], axis=0)
            if lay.half_rows < LANES:
                block = jnp.concatenate(
                    [block, jnp.zeros((16, LANES - lay.half_rows), f32)], axis=1
                )
            lay.view(outs, s)[lay.data_rows : lay.data_rows + 16, :] = block.astype(bf16)


def project_rows(lay, places, x, weights, bias, code, pad):
    width = weights.shape[1]
    steps = lay.tokens // ROWS
    spec = pltpu.PrefetchScalarGridSpec(
        num_scalar_prefetch=1,
        grid=(steps + lay.heads,),
        in_specs=[
            pl.BlockSpec((ROWS, D), lambda s, _: (jnp.minimum(s, steps - 1), 0)),
            pl.BlockSpec((D, width), lambda s, _: (0, 0)),
            pl.BlockSpec((8, width), lambda s, _: (0, 0)),
            pl.BlockSpec((lay.heads, 8, lay.tokens), lambda s, _: (0, 0, 0)),
            pl.BlockSpec((1, lay.tokens), lambda s, _: (0, 0)),
        ],
        out_specs=lay.specs(lay.data_rows + 16, only(0)),
        scratch_shapes=[
            pltpu.VMEM((lay.heads, lay.tokens, 4 * LANES), bf16),
            pltpu.VMEM((lay.heads, 8, lay.packed), f32),
        ],
    )
    return pl.pallas_call(
        partial(project_kernel, lay, steps),
        grid_spec=spec,
        out_shape=lay.shapes(lay.data_rows + 16),
        compiler_params=pltpu.CompilerParams(vmem_limit_bytes=VMEM),
        name="project_rows",
        cost_estimate=QUICK,
    )(places, x, weights, bias, code, pad)


def pair_rows(lay, refs, first, run, p):
    at = slice(first + p * lay.per_dev, first + (p + 1) * lay.per_dev)
    if lay.direct:
        return jnp.concatenate([refs[s][at, :] for s in range(lay.stripe)], axis=0)
    block = refs[0][run * lay.stripe : (run + 1) * lay.stripe, first : first + lay.half_rows, :]
    block = block.astype(f32)[:, p * lay.per_dev : (p + 1) * lay.per_dev, :]
    return block.reshape(CLUSTER, LANES).astype(bf16)


def put_pair(lay, refs, first, run, p, rows):
    at = slice(first + p * lay.per_dev, first + (p + 1) * lay.per_dev)
    for s in range(lay.stripe):
        part = rows[s * lay.per_dev : (s + 1) * lay.per_dev]
        lay.view(refs, run * lay.stripe + s)[at, :] = part.astype(bf16)


def live_columns(lay, flags, h):
    pick = one_hot(sublane_iota(16, 2 * LANES) == 2 * h + lane_iota(16, 2 * LANES) // LANES)
    return [tn(lay.view(flags, s)[...], pick) for s in range(lay.peers)]


def allowed_pair(lay, columns, run, p):
    at = slice(p * lay.per_dev, (p + 1) * lay.per_dev)
    live = jnp.concatenate([columns[run * lay.stripe + s][at] for s in range(lay.stripe)], axis=0)
    live = jnp.concatenate([live[:, :LANES], live[:, LANES:]], axis=0)
    same = sublane_iota(2 * CLUSTER) % CLUSTER == lane_iota(2 * CLUSTER)
    return (live > 0.5) | same


def stack_halves(rows):
    low = lane_iota(rows.shape[0], rows.shape[1]) < HEAD_DIM
    zero = jnp.zeros_like(rows)
    return jnp.concatenate([jnp.where(low, rows, zero), jnp.where(low, zero, rows)], axis=0)


def each_half(fold, rows):
    one, two = (
        jnp.broadcast_to(fold(part, axis=0, keepdims=True), part.shape)
        for part in (rows[:CLUSTER], rows[CLUSTER:])
    )
    return jnp.concatenate([one, two], axis=0)


def inverse_sum(rows, axis, keepdims):
    return 1.0 / jnp.sum(rows, axis=axis, keepdims=keepdims)


def soft_weights(queries, keys, allowed):
    scores = jnp.where(allowed, nt(keys, queries) * SCALE, MASKED)
    grown = jnp.exp(scores - each_half(jnp.max, scores))
    return grown * each_half(inverse_sum, grown)


def attend_kernel(lay, *refs):
    rows, flags, outs = (refs[i * lay.arrays : (i + 1) * lay.arrays] for i in range(3))
    live = live_columns(lay, flags, pl.program_id(0))
    for run in range(lay.runs):
        for p in range(lay.pairs):
            q, k, v = (pair_rows(lay, rows, x * lay.half_rows, run, p) for x in range(3))
            soft = soft_weights(q, stack_halves(k), allowed_pair(lay, live, run, p))
            put_pair(lay, outs, 0, run, p, tn(soft.astype(bf16), stack_halves(v)))


def attend(lay, arrived):
    head = lambda h: h
    return pl.pallas_call(
        partial(attend_kernel, lay),
        grid=(lay.heads,),
        in_specs=lay.specs(3 * lay.half_rows, head) + lay.specs(16, only(lay.data_rows // 16)),
        out_specs=lay.specs(lay.half_rows, head),
        out_shape=lay.shapes(lay.heads * lay.half_rows),
        name="attend",
        cost_estimate=cost(ATTEND_US),
    )(*arrived, *arrived)


def attend_back_kernel(lay, *refs):
    rows, flags, grads, outs = (refs[i * lay.arrays : (i + 1) * lay.arrays] for i in range(4))
    sum_ref = refs[-1]
    live = live_columns(lay, flags, pl.program_id(0))
    low = lane_iota(CLUSTER) < HEAD_DIM
    sums = [jnp.zeros((1, LANES), f32)] * 2
    for run in range(lay.runs):
        for p in range(lay.pairs):
            q, k, v = (pair_rows(lay, rows, x * lay.half_rows, run, p) for x in range(3))
            g = pair_rows(lay, grads, 0, run, p)
            keys = stack_halves(k)
            soft = soft_weights(q, keys, allowed_pair(lay, live, run, p))
            grad_soft = nt(stack_halves(v), g)
            delta = each_half(jnp.sum, soft * grad_soft)
            grad = (soft * (grad_soft - delta)).astype(bf16)
            grad_q = (tn(grad, keys) * SCALE).astype(bf16)
            part = nn(grad, q)
            grad_k = (jnp.where(low, part[:CLUSTER], part[CLUSTER:]) * SCALE).astype(bf16)
            part = nn(soft.astype(bf16), g)
            grad_v = jnp.where(low, part[:CLUSTER], part[CLUSTER:]).astype(bf16)
            for x, part in enumerate((grad_q, grad_k, grad_v)):
                put_pair(lay, outs, x * lay.half_rows, run, p, part)
            sums[0] = sums[0] + jnp.sum(grad_q.astype(f32), axis=0, keepdims=True)
            sums[1] = sums[1] + jnp.sum(grad_v.astype(f32), axis=0, keepdims=True)
    sum_ref[0] = jnp.concatenate(sums + [jnp.zeros((6, LANES), f32)], axis=0)


def attend_back(lay, arrived, grads):
    head = lambda h: h
    three = lay.specs(3 * lay.half_rows, head)
    out = pl.pallas_call(
        partial(attend_back_kernel, lay),
        grid=(lay.heads,),
        in_specs=three
        + lay.specs(16, only(lay.data_rows // 16))
        + lay.specs(lay.half_rows, head),
        out_specs=three + [pl.BlockSpec((1, 8, LANES), lambda h: (h, 0, 0))],
        out_shape=lay.shapes(lay.data_rows)
        + [jax.ShapeDtypeStruct((lay.heads, 8, LANES), f32)],
        name="attend_back",
        cost_estimate=cost(ATTEND_BACK_US),
    )(*arrived, *arrived, *grads)
    return list(out[:-1]), out[-1]


def side_rows(quarter, side):
    return pl.ds(pl.multiple_of(quarter * 512 + side * 256, 256), 256)


def unsort_kernel(lay, place_ref, *refs):
    rows_refs, code_ref, outs = refs[: lay.arrays], refs[lay.arrays], refs[lay.arrays + 1 :]
    rows = block_rows(lay, rows_refs, 0)
    low = lane_iota(256) < HEAD_DIM
    me, place = place_ref[0], place_ref[1]

    for t in range(4):
        sides = []
        for side in range(2):
            at = side_rows(place ^ t, side)
            column = as_column(code_ref[0, 0:1, at])
            half = as_column(code_ref[0, 1:2, at])
            found = nn(gather_matrix(lay, me, column), rows)
            sides.append(jnp.where(half == side, found, pltpu.roll(found, HEAD_DIM, 1)))
        outs[t][...] = jnp.where(low, sides[0], sides[1]).astype(bf16)


def unsort_rows(lay, places, returned, code):
    spec = pltpu.PrefetchScalarGridSpec(
        num_scalar_prefetch=1,
        grid=(lay.heads,),
        in_specs=lay.specs(lay.half_rows, lambda h, _: h)
        + [pl.BlockSpec((1, 8, lay.tokens), lambda h, _: (h, 0, 0))],
        out_specs=[pl.BlockSpec((256, LANES), lambda h, _: (0, h))] * 4,
    )
    return pl.pallas_call(
        partial(unsort_kernel, lay),
        grid_spec=spec,
        out_shape=[jax.ShapeDtypeStruct((256, lay.heads * LANES), bf16)] * 4,
        name="unsort_rows",
        cost_estimate=QUICK,
    )(places, *returned, code)


def sort_kernel(lay, place_ref, *refs):
    grads, code_ref, outs, rows_ref = refs[:4], refs[4], refs[5:-1], refs[-1]
    low = lane_iota(256) < HEAD_DIM
    lane_half = jnp.where(low, 0, 1)
    me, place = place_ref[0], place_ref[1]

    for t in range(4):
        block = grads[t][...].astype(f32)
        turned = pltpu.roll(block, HEAD_DIM, 1)
        for side in range(2):
            at = side_rows(place ^ t, side)
            half = as_column(code_ref[0, 1:2, at])
            both = jnp.where(low, block, turned) if side == 0 else jnp.where(low, turned, block)
            rows_ref[at, :] = jnp.where(half == lane_half, both, 0.0).astype(bf16)

    count = 4 if lay.direct else 32
    for s in range(0, lay.peers, count):
        chosen = scatter_matrix(lay, me, code_ref[0, 0:1, :], s, count)
        put_blocks(lay, outs, s, count, 0, nn(chosen, rows_ref[...]))


def sort_rows(lay, places, grads, code):
    spec = pltpu.PrefetchScalarGridSpec(
        num_scalar_prefetch=1,
        grid=(lay.heads,),
        in_specs=[pl.BlockSpec((256, LANES), lambda h, _: (0, h))] * 4
        + [pl.BlockSpec((1, 8, lay.tokens), lambda h, _: (h, 0, 0))],
        out_specs=lay.specs(lay.half_rows, lambda h, _: h),
        scratch_shapes=[pltpu.VMEM((lay.tokens, LANES), bf16)],
    )
    return pl.pallas_call(
        partial(sort_kernel, lay),
        grid_spec=spec,
        out_shape=lay.shapes(lay.heads * lay.half_rows),
        name="sort_rows",
        cost_estimate=cost(SORT_US),
    )(places, *grads, code)


def pack_kernel(
    query_ref, key_ref, value_ref, output_ref, inner_ref, outer_ref,
    bias_ref, gain_ref, shift_ref, inner_bias_ref, piece_ref, shard_ref,
):
    depth, width = query_ref.shape
    heads = width // HEAD_DIM
    query, key, value = (ref[...].astype(f32) for ref in (query_ref, key_ref, value_ref))
    cut = [slice(h * HEAD_DIM, (h + 1) * HEAD_DIM) for h in range(heads)]
    columns = [part for at in cut for part in (query[:, at], key[:, at])] + [value]
    have = 3 * width
    fill = -have % LANES
    if fill:
        columns.append(jnp.zeros((depth, fill), f32))
    columns = jnp.concatenate(columns, axis=1).astype(bf16)
    piece_ref[:depth, : have + fill] = columns
    inner_bias = inner_bias_ref[...].astype(f32)
    vectors = jnp.concatenate(
        [ref[...].astype(f32) for ref in (bias_ref, gain_ref, shift_ref)]
        + [inner_bias[:, i * depth : (i + 1) * depth] for i in range(4)]
        + [jnp.zeros((4, depth), f32)],
        axis=0,
    )
    if depth < LANES:
        vectors = jnp.concatenate([vectors, jnp.zeros((16, LANES - depth), f32)], axis=1)
    piece_ref[:16, have + fill :] = vectors.astype(bf16)
    shard_ref[:, :D] = inner_ref[...]
    turned = output_ref[...].astype(f32).T
    shard_ref[:, D : 2 * D] = outer_ref[...]
    shard_ref[:, 2 * D :] = jnp.concatenate(
        [turned[:, at] for at in cut for _ in range(2)], axis=1
    ).astype(bf16)


def pack_weights(*arrays):
    depth, width = arrays[0].shape
    columns = -(-3 * width // LANES) * LANES
    return pl.pallas_call(
        pack_kernel,
        out_shape=[
            jax.ShapeDtypeStruct((max(depth, 16), columns + LANES), bf16),
            jax.ShapeDtypeStruct((depth, 2 * D + 2 * width), bf16),
        ],
        name="pack_weights",
        cost_estimate=QUICK,
    )(*arrays)


def assemble_kernel(lay, place_ref, *refs):
    pieces, (weight_ref, bias_ref, par_ref, part_ref) = refs[: lay.peers], refs[lay.peers :]
    me, place = place_ref[0], place_ref[1]
    depth = D // lay.peers
    for s in range(lay.peers):
        d = me ^ s
        at = pl.ds(pl.multiple_of(d * depth, 16), depth)
        columns = weight_ref.shape[1]
        weight_ref[at, :] = pieces[s][:, :columns]
        part_ref[d] = pieces[s][:16, columns:].astype(f32)

    def whole(row, rows=1, peers=range(lay.peers)):
        return jnp.concatenate(
            [part_ref[d, row + i : row + i + 1, :depth] for d in peers for i in range(rows)], axis=1
        )

    vectors = [whole(r) for r in range(8)]
    each = lay.peers // 4
    vectors += [whole(8, 4, range(j * each, (j + 1) * each)) for j in range(4)]
    par_ref[...] = jnp.concatenate(vectors + [jnp.zeros((4, D), f32)], axis=0)
    width = lay.heads * HEAD_DIM

    def own(vector):
        out = vector[:, :width]
        for p in range(1, D // width):
            out = jnp.where(place == p, vector[:, p * width : (p + 1) * width], out)
        return out

    query = own(vectors[0])
    zero = jnp.zeros((1, HEAD_DIM), f32)
    columns = [
        part for h in range(lay.heads) for part in (query[:, h * HEAD_DIM : (h + 1) * HEAD_DIM], zero)
    ] + [own(vectors[1])]
    fill = bias_ref.shape[1] - 3 * width
    if fill:
        columns.append(jnp.zeros((1, fill), f32))
    bias_ref[...] = jnp.broadcast_to(jnp.concatenate(columns, axis=1), bias_ref.shape)


def assemble_weights(lay, places, pieces):
    columns = pieces[0].shape[1] - LANES
    vmem = pl.BlockSpec(memory_space=pltpu.VMEM)
    return pl.pallas_call(
        partial(assemble_kernel, lay),
        in_specs=[pl.BlockSpec(memory_space=pltpu.SMEM)] + [vmem] * lay.peers,
        out_specs=[vmem] * 3,
        out_shape=[
            jax.ShapeDtypeStruct((D, columns), bf16),
            jax.ShapeDtypeStruct((8, columns), f32),
            jax.ShapeDtypeStruct((16, D), f32),
        ],
        scratch_shapes=[pltpu.VMEM((lay.peers, 16, LANES), f32)],
        name="assemble_weights",
        cost_estimate=QUICK,
    )(places, *pieces)


def mean_rows(v):
    return jnp.sum(v, axis=1, keepdims=True) * (1.0 / D)


def norm_forward(rows):
    centred = rows - mean_rows(rows)
    inv = lax.rsqrt(mean_rows(centred * centred) + EPSILON)
    return centred * inv, inv


def norm_backward(scaled, normed, inv):
    return inv * (scaled - mean_rows(scaled) - normed * mean_rows(scaled * normed))


TALL = 512


def middle_kernel(
    place_ref,
    att0,
    att1,
    att2,
    att3,
    hidden_ref,
    cot_ref,
    par_ref,
    w0,
    w1,
    w2,
    w3,
    out_ref,
    act_ref,
    pre_ref,
    low_ref,
    ffn_grad_ref,
    branch_grad_ref,
    h1_ref,
    grad0,
    grad1,
    grad2,
    grad3,
    vec_ref,
    first_ref,
    normed_ref,
    inv_ref,
    slope_ref,
    sum_ref,
    h2_ref,
    weight_ref,
    sems,
):
    step = pl.program_id(0)
    place = place_ref[1]
    project = slice(2 * D, None)

    def fetch(t, part):
        width = att0.shape[1]
        at = (pl.ds(2 * D, width), pl.ds(0, 2 * D))[part]
        source = (w0, w1, w2, w3)[t]
        return pltpu.make_async_copy(source.at[:, at], weight_ref.at[t, :, at], sems.at[part, t])

    for t in range(4):

        @pl.when(step == t + 1)
        def _():
            fetch(t, 1).wait()

    @pl.when(step == 0)
    def _():
        for t in range(4):
            fetch(t, 0).start()
        for t in range(4):
            fetch(t, 1).start()
        for t in range(4):
            fetch(t, 0).wait()
        vec_ref[...] = jnp.zeros_like(vec_ref)

        @loop(2)
        def _(side):
            branch = jnp.zeros((256, D), f32)
            for t, att_ref in enumerate((att0, att1, att2, att3)):
                att = att_ref[...]
                lane = lane_iota(256, att.shape[1]) % LANES
                own = (lane >= HEAD_DIM).astype(i32) == side
                branch = branch + nt(jnp.where(own, att, jnp.zeros_like(att)), weight_ref[t, :, project])
            at = pl.ds(pl.multiple_of(side * 256, 256), 256)
            rows = hidden_ref[at, :].astype(f32) + (branch + par_ref[2:3, :])
            normed, inv = norm_forward(rows)
            first = normed * par_ref[4:5, :] + par_ref[6:7, :]
            first_ref[at, :] = first
            normed_ref[at, :] = normed
            inv_ref[at, :] = jnp.broadcast_to(inv, (256, LANES))
            low_ref[at, :] = first.astype(bf16)

        sum_ref[...] = jnp.zeros_like(sum_ref)

    @pl.when((step >= 1) & (step <= 4))
    def _():
        j = step - 1

        @loop(512 // TALL)
        def _(side):
            at = pl.ds(pl.multiple_of(side * TALL, TALL), TALL)
            pre = nn(low_ref[at, :], weight_ref[j, :, :D]) + par_ref[pl.ds(8 + (place ^ j), 1), :]
            cdf = 0.5 * (1.0 + lax.erf(pre * (1.0 / math.sqrt(2.0))))
            slope_ref[j, at, :] = cdf + pre * jnp.exp(-0.5 * pre * pre) * (1.0 / math.sqrt(2.0 * math.pi))
            act = (pre * cdf).astype(bf16)
            act_ref[at, :] = act
            sum_ref[at, :] += nt(act, weight_ref[j, :, D : 2 * D])

    @pl.when(step == 4)
    def _():

        @loop(4)
        def _(side):
            at = pl.ds(pl.multiple_of(side * 128, 128), 128)
            rows = first_ref[at, :] + (sum_ref[at, :] + par_ref[3:4, :])
            normed, inv = norm_forward(rows)
            out_ref[at, :] = (normed * par_ref[5:6, :] + par_ref[7:8, :]).astype(bf16)
            cot = cot_ref[at, :].astype(f32)
            grad = norm_backward(cot * par_ref[5:6, :], normed, inv)
            grad_low = grad.astype(bf16)
            h2_ref[at, :] = grad
            ffn_grad_ref[at, :] = grad_low
            vec_ref[3:4, :] += jnp.sum(grad_low.astype(f32), axis=0, keepdims=True)
            vec_ref[5:6, :] += jnp.sum(cot * normed, axis=0, keepdims=True)
            vec_ref[7:8, :] += jnp.sum(cot, axis=0, keepdims=True)

        sum_ref[...] = jnp.zeros_like(sum_ref)

    @pl.when(step >= 5)
    def _():
        j = 8 - step
        vec_ref[pl.ds(8 + (place ^ j), 1), :] = jnp.zeros((1, D), f32)

        @loop(512 // TALL)
        def _(side):
            at = pl.ds(pl.multiple_of(side * TALL, TALL), TALL)
            grad_act = nn(ffn_grad_ref[at, :], weight_ref[j, :, D : 2 * D])
            grad_pre = (grad_act * slope_ref[j, at, :]).astype(bf16)
            pre_ref[at, :] = grad_pre
            vec_ref[pl.ds(8 + (place ^ j), 1), :] += jnp.sum(grad_pre.astype(f32), axis=0, keepdims=True)
            sum_ref[at, :] += nt(grad_pre, weight_ref[j, :, :D])

    @pl.when(step == 8)
    def _():

        @loop(4)
        def _(side):
            at = pl.ds(pl.multiple_of(side * 128, 128), 128)
            grad_first = h2_ref[at, :] + sum_ref[at, :]
            normed = normed_ref[at, :]
            grad = norm_backward(grad_first * par_ref[4:5, :], normed, inv_ref[at, 0:1])
            grad_low = grad.astype(bf16)
            h1_ref[at, :] = grad
            branch_grad_ref[at, :] = grad_low
            vec_ref[2:3, :] += jnp.sum(grad_low.astype(f32), axis=0, keepdims=True)
            vec_ref[4:5, :] += jnp.sum(grad_first * normed, axis=0, keepdims=True)
            vec_ref[6:7, :] += jnp.sum(grad_first, axis=0, keepdims=True)

        for t, grad_ref in enumerate((grad0, grad1, grad2, grad3)):
            both = nn(branch_grad_ref[...], weight_ref[t, :, project])
            lane = lane_iota(256, both.shape[1]) % LANES
            grad_ref[...] = jnp.where(lane < HEAD_DIM, both[:256], both[256:]).astype(bf16)


def middle(places, att, hidden, cotangent, params, weights):
    width = att[0].shape[1]
    rows = 512

    def up(s, q):
        return (0, jnp.clip(s - 1, 0, 3))

    def down(s, q):
        return (0, jnp.clip(8 - s, 0, 3))

    def whole(rank):
        return lambda s, q: (0,) * rank

    square = pl.BlockSpec((rows, D), whole(2))
    exchanged = pl.BlockSpec((256, width), whole(2))
    spec = pltpu.PrefetchScalarGridSpec(
        num_scalar_prefetch=1,
        grid=(9,),
        in_specs=[exchanged] * 4
        + [
            pl.BlockSpec((rows, D), lambda s, q: (q[1], 0)),
            pl.BlockSpec((rows, D), lambda s, q: (q[1], 0)),
            pl.BlockSpec((16, D), whole(2)),
        ]
        + [pl.BlockSpec(memory_space=pl.ANY)] * 4,
        out_specs=[
            square,
            pl.BlockSpec((rows, D), up),
            pl.BlockSpec((rows, D), down),
            square,
            square,
            square,
            square,
        ]
        + [exchanged] * 4
        + [pl.BlockSpec((16, D), whole(2))],
        scratch_shapes=[
            pltpu.VMEM((rows, D), f32),
            pltpu.VMEM((rows, D), f32),
            pltpu.VMEM((rows, LANES), f32),
            pltpu.VMEM((4, rows, D), f32),
            pltpu.VMEM((rows, D), f32),
            pltpu.VMEM((rows, D), f32),
            pltpu.VMEM((4, D, 2 * D + width), bf16),
            pltpu.SemaphoreType.DMA((2, 4)),
        ],
    )
    out = pl.pallas_call(
        middle_kernel,
        grid_spec=spec,
        out_shape=[
            jax.ShapeDtypeStruct((rows, D), bf16),
            jax.ShapeDtypeStruct((rows, FF), bf16),
            jax.ShapeDtypeStruct((rows, FF), bf16),
            jax.ShapeDtypeStruct((rows, D), bf16),
            jax.ShapeDtypeStruct((rows, D), bf16),
            jax.ShapeDtypeStruct((rows, D), bf16),
            jax.ShapeDtypeStruct((rows, D), f32),
        ]
        + [jax.ShapeDtypeStruct((256, width), bf16)] * 4
        + [jax.ShapeDtypeStruct((16, D), f32)],
        compiler_params=pltpu.CompilerParams(vmem_limit_bytes=VMEM),
        name="middle",
        cost_estimate=QUICK,
    )(places, *att, hidden, cotangent, params, *weights)
    return out[:7], out[7:11], out[11]


def weight_grad_kernel(chunks, adds, place_ref, act_ref, pre_ref, low_ref, ffn_ref, branch_ref, *refs):
    att_refs, add_refs, out_ref = refs[:chunks], refs[chunks : chunks + adds], refs[-1]

    def put(at, part):
        for ref in add_refs:
            part = part + ref[:, at].astype(f32)
        out_ref[:, at] = part.astype(bf16)

    put(slice(0, D), tn(low_ref[...], pre_ref[...]))
    put(slice(D, 2 * D), tn(ffn_ref[...], act_ref[...]))
    for i in range(chunks):

        @pl.when(pl.program_id(0) == i)
        def _():
            att = att_refs[i][...]
            low = lane_iota(256, att.shape[1]) % LANES < HEAD_DIM
            zero = jnp.zeros_like(att)
            both = jnp.concatenate([jnp.where(low, att, zero), jnp.where(low, zero, att)], axis=0)
            put(slice(2 * D, 2 * D + att.shape[1]), tn(branch_ref[...], both))


def weight_grads(places, saved, att, first, chunks, adds):
    act, pre, low, ffn_grad, branch_grad = saved
    rows = act.shape[0]
    width = att[0].shape[1]
    total = 2 * D + width
    cut = D // 2

    def chunk(s, i, q):
        return (0, first - 2 * s)

    part = pl.BlockSpec((rows, cut), lambda s, i, q: (0, i))
    spec = pltpu.PrefetchScalarGridSpec(
        num_scalar_prefetch=1,
        grid=(chunks, 2),
        in_specs=[pl.BlockSpec((rows, D), chunk)] * 2
        + [part] * 3
        + [pl.BlockSpec((256, width), lambda s, i, q: (0, 0))] * chunks
        + [pl.BlockSpec((cut, total), lambda s, i, q, k=k: (2 * k + i, 0)) for _, k in adds],
        out_specs=pl.BlockSpec((cut, total), lambda s, i, q: (2 * s + i, 0)),
    )
    return pl.pallas_call(
        partial(weight_grad_kernel, chunks, len(adds)),
        grid_spec=spec,
        out_shape=jax.ShapeDtypeStruct((chunks * D, total), bf16),
        compiler_params=pltpu.CompilerParams(vmem_limit_bytes=VMEM),
        name="weight_grads",
        cost_estimate=QUICK,
    )(
        places, act, pre, low, ffn_grad, branch_grad,
        *[att[first - 2 * s] for s in range(chunks)], *[a for a, _ in adds],
    )


def collect_kernel(lay, place_ref, *refs):
    rows_refs = refs[: lay.arrays]
    code_ref, dense_ref = refs[lay.arrays :]
    me = place_ref[0]
    tokens = dense_ref.shape[0]
    low = lane_iota(tokens) < HEAD_DIM
    firsts, seconds = [], []
    for h in range(lay.heads):
        column = as_column(code_ref[h, 0:1, :])
        half = as_column(code_ref[h, 1:2, :])
        planes = [block_rows(lay, rows_refs, (h * 3 + x) * lay.half_rows) for x in range(3)]
        found = nn(gather_matrix(lay, me, column), jnp.concatenate(planes, axis=1))
        one, two = [], []
        for x in range(3):
            part = found[:, x * LANES : (x + 1) * LANES]
            turned = pltpu.roll(part, HEAD_DIM, 1)
            one.append(jnp.where(half == 0, part, turned))
            two.append(jnp.where(half == 1, part, turned))
        firsts.append(one)
        seconds.append(two)
    tiles = [jnp.where(low, firsts[h][0], seconds[h][1]) for h in range(lay.heads)]
    for h in range(0, lay.heads, 2):
        right = seconds[h + 1][2] if h + 1 < lay.heads else jnp.zeros((tokens, LANES), f32)
        tiles.append(jnp.where(low, firsts[h][2], right))
    dense_ref[...] = jnp.concatenate(tiles, axis=1).astype(bf16)


def collect(lay, places, returned, code, width):
    tokens = COLLECT_ROWS
    spec = pltpu.PrefetchScalarGridSpec(
        num_scalar_prefetch=1,
        grid=(lay.tokens // tokens,),
        in_specs=lay.specs(lay.data_rows, only(0))
        + [pl.BlockSpec((lay.heads, 8, tokens), lambda c, q: (0, 0, c))],
        out_specs=pl.BlockSpec((tokens, width), lambda c, q: (c, 0)),
    )
    return pl.pallas_call(
        partial(collect_kernel, lay),
        grid_spec=spec,
        out_shape=jax.ShapeDtypeStruct((lay.tokens, width), bf16),
        compiler_params=pltpu.CompilerParams(vmem_limit_bytes=VMEM),
        name="collect",
        cost_estimate=cost(COLLECT_US),
    )(places, *returned, code)


def half_rows_at(g, s, place):
    core = place % 2
    return jnp.where(s == 0, 1 - core, core) * 2 + g


def spread_kernel(g, place_ref, dense_ref, w_ref, h1_ref, other_ref, mine_ref):
    step, place = pl.program_id(0), place_ref[1]
    own = (half_rows_at(g, step, place) == place).astype(f32)
    part = nt(dense_ref[...], w_ref[...]) + own * h1_ref[...]

    @pl.when(step == 0)
    def _():
        other_ref[...] = part.astype(bf16)

    @pl.when(step == 1)
    def _():
        mine_ref[...] = part.astype(bf16)


def spread_grads(g, places, dense, weights, grad_h1):
    width = weights.shape[1]
    whole = lambda s, q: (0, 0)
    spec = pltpu.PrefetchScalarGridSpec(
        num_scalar_prefetch=1,
        grid=(2,),
        in_specs=[
            pl.BlockSpec((512, width), lambda s, q: (half_rows_at(g, s, q[1]), 0)),
            pl.BlockSpec((D, width), whole),
            pl.BlockSpec((512, D), whole),
        ],
        out_specs=[pl.BlockSpec((512, D), whole)] * 2,
    )
    return pl.pallas_call(
        partial(spread_kernel, g),
        grid_spec=spec,
        out_shape=[jax.ShapeDtypeStruct((512, D), bf16)] * 2,
        compiler_params=pltpu.CompilerParams(vmem_limit_bytes=VMEM),
        name="spread_grads",
        cost_estimate=cost(SPREAD_US),
    )(places, dense, weights, grad_h1)


def head_grad_kernel(lay, place_ref, x_ref, dense_ref, vec_ref, *refs):
    out_ref, total_ref = refs
    step = pl.program_id(0)

    @pl.when(step == 0)
    def _():
        total_ref[...] = tn(x_ref[...], dense_ref[...])

    @pl.when(step > 0)
    def _():
        total_ref[...] += tn(x_ref[...], dense_ref[...])

    @pl.when(step == 3)
    def _():
        depth = D // lay.peers
        if not lay.direct:
            out_ref[...] = total_ref[...].astype(bf16)
            return
        for d in range(lay.peers):
            out_ref[d, :depth, :] = total_ref[d * depth : (d + 1) * depth, :].astype(bf16)
            vector = vec_ref[d]
            high = vector.astype(bf16).astype(f32)
            width = total_ref.shape[1]
            out_ref[d, depth:, :] = jnp.concatenate(
                [high, vector - high, jnp.zeros((16, width - 2 * LANES), f32)], axis=1
            ).astype(bf16)


def head_grads(lay, places, x, dense, vec):
    width = dense.shape[1]
    depth = D // lay.peers
    shape = (lay.peers, depth + 16, width) if lay.direct else (D, width)
    spec = pltpu.PrefetchScalarGridSpec(
        num_scalar_prefetch=1,
        grid=(4,),
        in_specs=[
            pl.BlockSpec((512, D), lambda s, q: (s, 0)),
            pl.BlockSpec((512, width), lambda s, q: (s, 0)),
            pl.BlockSpec(vec.shape, lambda s, q: (0, 0, 0)),
        ],
        out_specs=pl.BlockSpec(shape, lambda s, q: (0,) * len(shape)),
        scratch_shapes=[pltpu.VMEM((D, width), f32)],
    )
    return pl.pallas_call(
        partial(head_grad_kernel, lay),
        grid_spec=spec,
        out_shape=jax.ShapeDtypeStruct(shape, bf16),
        compiler_params=pltpu.CompilerParams(vmem_limit_bytes=VMEM),
        name="head_grads",
        cost_estimate=cost(HEAD_GRADS_US),
    )(places, x, dense, vec)


def finish_heads_kernel(*refs):
    parts, outs = refs[0], refs[1:]
    depth, width = outs[0].shape
    heads = width // HEAD_DIM
    total = parts[0].astype(f32)
    for d in range(1, parts.shape[0]):
        total = total + parts[d].astype(f32)
    grads = total[:depth]
    cut = [slice(h * LANES, h * LANES + HEAD_DIM) for h in range(heads)]
    outs[0][...] = jnp.concatenate([grads[:, at] for at in cut], axis=1)
    cut = [slice(h * LANES + HEAD_DIM, (h + 1) * LANES) for h in range(heads)]
    outs[1][...] = jnp.concatenate([grads[:, at] for at in cut], axis=1)
    outs[2][...] = grads[:, 2 * width : 3 * width]
    outs[3][...] = total[depth:, :LANES] + total[depth:, LANES : 2 * LANES]


def finish_heads(parts, depth, width):
    shapes = [(depth, width)] * 3 + [(16, LANES)]
    return pl.pallas_call(
        finish_heads_kernel,
        out_shape=[jax.ShapeDtypeStruct(s, f32) for s in shapes],
        name="finish_heads",
        cost_estimate=QUICK,
    )(parts)


def finish_vectors_kernel(depth, own_ref, other_ref, bias_ref, gain_ref, shift_ref, inner_ref):
    total = (own_ref[...] + other_ref[...])[:, :depth]
    bias_ref[...] = total[:4]
    gain_ref[...] = total[4:6]
    shift_ref[...] = total[6:8]
    inner_ref[...] = total[8:12]


def finish_vectors(own, other, depth):
    return pl.pallas_call(
        partial(finish_vectors_kernel, depth),
        out_shape=[jax.ShapeDtypeStruct((n, depth), f32) for n in (4, 2, 2, 4)],
        name="finish_vectors",
        cost_estimate=QUICK,
    )(own, other)


def finish_middle_kernel(grad_ref, inner_ref, outer_ref, output_ref):
    inner_ref[...] = grad_ref[:, :D].astype(f32)
    outer_ref[...] = grad_ref[:, D : 2 * D].astype(f32)
    rest = grad_ref[:, 2 * D :].astype(f32)
    planes = [rest[:, i * LANES : (i + 1) * LANES] for i in range(rest.shape[1] // LANES)]
    folded = [p[:, :HEAD_DIM] + p[:, HEAD_DIM:] for p in planes]
    output_ref[...] = jnp.concatenate(folded, axis=1).T


def finish_middle(grads):
    depth, total = grads.shape
    return pl.pallas_call(
        finish_middle_kernel,
        out_shape=[
            jax.ShapeDtypeStruct((depth, D), f32),
            jax.ShapeDtypeStruct((depth, D), f32),
            jax.ShapeDtypeStruct(((total - 2 * D) // 2, depth), f32),
        ],
        name="finish_middle",
        cost_estimate=QUICK,
    )(grads)


def order_kernel(place_ref, *refs):
    parts, out_ref, rows_ref, sems = refs[:4], refs[4], refs[5], refs[6]
    rows = rows_ref.shape[1]

    def take(i):
        return pltpu.make_async_copy(parts[i], rows_ref.at[i], sems.at[0, i])

    def put(i):
        at = pl.ds(pl.multiple_of(place_ref[i] * rows, rows), rows)
        return pltpu.make_async_copy(rows_ref.at[i], out_ref.at[at, :], sems.at[1, i])

    for i in range(4):
        take(i).start()
    for i in range(4):
        take(i).wait()
        put(i).start()
    for i in range(4):
        put(i).wait()


def order_quarters(order, quarters):
    rows, width = quarters[0].shape
    dtype = quarters[0].dtype
    return pl.pallas_call(
        order_kernel,
        in_specs=[pl.BlockSpec(memory_space=pltpu.SMEM)]
        + [pl.BlockSpec(memory_space=pl.ANY)] * 4,
        out_specs=pl.BlockSpec(memory_space=pl.ANY),
        out_shape=jax.ShapeDtypeStruct((4 * rows, width), dtype),
        scratch_shapes=[pltpu.VMEM((4, rows, width), dtype), pltpu.SemaphoreType.DMA((2, 4))],
        name="order_quarters",
        cost_estimate=QUICK,
    )(order, *quarters)


def over_rows(lay, blocks, near_first=False):
    if not lay.direct:
        return [lax.all_to_all(blocks[0], "dp", split_axis=0, concat_axis=0, tiled=True)]
    out = [blocks[0]]
    for s in range(1, lay.peers):
        rows = blocks[s]
        if near_first and s >= lay.peers - 2:
            rows = after(rows, out[s - lay.peers + 3])
        out.append(lax.ppermute(rows, "dp", [(i, i ^ s) for i in range(lay.peers)]))
    return out


def in_hbm(rows):
    return pltpu.with_memory_space_constraint(rows, pltpu.HBM)


def share_pieces(lay, piece):
    def flip(rows, s):
        return lax.ppermute(rows, "dp", [(i, i ^ s) for i in range(lay.peers)])

    half = lay.peers // 2
    far = flip(piece, half)
    near = [piece] + [flip(piece, s) for s in range(1, half)]
    return near + [far] + [flip(far, s) for s in range(1, half)]


def after(value, *others):
    return lax.optimization_barrier((value, *others))[0]


def swap(rows, flip):
    return lax.ppermute(rows, "mp", [(i, i ^ flip) for i in range(4)])


def over_heads(blocks):
    return [blocks[0]] + [swap(blocks[t], t) for t in range(1, 4)]


def on_device(
    hidden_in,
    cotangent,
    w_query,
    w_key,
    w_value,
    w_output,
    w_inner,
    w_outer,
    biases,
    gains,
    shifts,
    inner_bias,
    lengths,
    padding,
    cluster_perm,
):
    peers = lax.axis_size("dp")
    tokens = hidden_in.shape[0]
    heads = cluster_perm.shape[0]
    lay = Layout(peers, tokens, heads)
    place = lax.axis_index("mp")
    me = lax.axis_index("dp")
    places = jnp.stack([me, place]).astype(i32)
    hidden_in = in_hbm(hidden_in)
    depth = w_query.shape[0]
    width = heads * HEAD_DIM

    piece, shard = pack_weights(
        w_query, w_key, w_value, w_output, w_inner, w_outer.T,
        biases, gains, shifts, inner_bias.reshape(1, -1),
    )
    own_w = lax.all_gather(shard, "dp", axis=0, tiled=True)
    far_w = swap(own_w, 2)
    if lay.direct:
        weights, bias, params = assemble_weights(lay, places, share_pieces(lay, piece))
    else:
        weights, bias, params = gather_weights(lay, place, piece)

    weights = in_hbm(weights)
    code = in_hbm(place_tokens(lay, cluster_perm))
    sent = project_rows(lay, places, hidden_in, weights, bias, code, padding.reshape(1, tokens))
    arrived = over_rows(lay, sent, near_first=True)
    mixed = over_rows(lay, attend(lay, arrived))
    found = unsort_rows(lay, places, mixed, code)
    att = over_heads(found)
    far_w = after(far_w, found[0])
    middle_w = [own_w, in_hbm(swap(own_w, 1)), far_w, in_hbm(swap(far_w, 1))]
    saved, att_grad, vec = middle(places, att, hidden_in, cotangent, params, middle_w)
    out_quarter, act, pre_grad, first_low, ffn_grad, branch_grad, grad_h1 = saved
    saved = tuple(in_hbm(a) for a in (act, pre_grad, first_low, ffn_grad, branch_grad))
    att = [in_hbm(a) for a in att]

    got = over_heads(att_grad)
    from_core = swap(weight_grads(places, saved, att, 3, 2, []), 1)
    grads = sort_rows(lay, places, got, code)
    ready = (after(act, grads[0]),) + saved[1:]
    from_far = swap(weight_grads(places, ready, att, 2, 1, [(from_core, 0)]), 2)
    grads = over_rows(lay, grads)
    slot_grads, bias_sums = attend_back(lay, arrived, grads)

    returned = over_rows(lay, slot_grads)
    ready = (after(act, *returned[1:4]),) + saved[1:]
    summed = weight_grads(places, ready, att, 0, 1, [(from_core, 1), (from_far, 0)])
    head_sums = bias_sums[:, :2].reshape(heads, 2, 2, HEAD_DIM).sum(axis=2)
    head_sums = head_sums.transpose(1, 0, 2).reshape(2, width)
    vec = lax.dynamic_update_slice(vec[:12], head_sums, (0, place * width))
    vec = jnp.concatenate(
        [vec[:8].reshape(8, peers, depth).transpose(1, 0, 2), vec[8:].reshape(peers, 4, depth)],
        axis=1,
    )
    spread = jnp.pad(vec, ((0, 0), (0, 4), (0, (-depth) % LANES)))
    reduced = lax.psum_scatter(after(summed, *returned), "dp", scatter_dimension=0, tiled=True)
    far = swap(after(out_quarter, summed), 2)
    dense = collect(lay, places, returned, code, weights.shape[1])
    terms = head_grads(lay, places, hidden_in, dense, spread)
    dense = after(dense, terms, far)
    groups = [spread_grads(g, places, dense, weights, grad_h1) for g in range(2)]
    chips = [
        (mine.astype(f32) + swap(other, 1).astype(f32)).astype(bf16) for other, mine in groups
    ]
    others = [swap(chip, 2) for chip in chips]
    hidden_out = order_quarters(
        jnp.stack([place, place ^ 2, place ^ 1, place ^ 3]).astype(i32),
        [out_quarter, far, swap(out_quarter, 1), swap(far, 1)],
    )
    if lay.direct:
        terms = lax.all_to_all(terms, "dp", split_axis=0, concat_axis=0, tiled=True)
        ends = finish_heads(terms, depth, width)
    else:
        ends = reduce_heads(terms, vec, depth, width)
    small = ends[3] + swap(ends[3], 1)
    small = finish_vectors(small, swap(small, 2), depth)
    chips[1] = after(chips[1], ends[0], hidden_out)
    ready = [
        (chip.astype(f32) + part.astype(f32)).astype(bf16) for chip, part in zip(chips, others)
    ]
    core = place % 2
    order = jnp.stack([2 * core, 2 * core + 1, 2 - 2 * core, 3 - 2 * core]).astype(i32)
    grad_hidden = order_quarters(
        after(order, small[0]),
        ready + [swap(part, 1) for part in ready],
    )

    grad_inner, grad_outer, grad_output = finish_middle(reduced)
    return (
        hidden_out,
        grad_hidden,
        ends[0],
        ends[1],
        ends[2],
        grad_output,
        grad_inner,
        grad_outer.T,
        small[0],
        small[1],
        small[2],
        small[3].reshape(-1),
    )


def gather_weights(lay, place, piece):
    depth = D // lay.peers
    width = lay.heads * HEAD_DIM
    got = lax.all_gather(piece, "dp", axis=0, tiled=False)
    columns = piece.shape[1] - LANES
    weights = got[:, :depth, :columns].reshape(D, columns)
    vectors = got[:, :12, columns : columns + depth].astype(f32)
    params = vectors[:, :8].transpose(1, 0, 2).reshape(8, D)
    params = jnp.concatenate([params, vectors[:, 8:].reshape(4, D), jnp.zeros((4, D), f32)], axis=0)
    own = lax.dynamic_slice_in_dim(params[:2], place * width, width, 1)
    query = own[0].reshape(lay.heads, HEAD_DIM)
    query = jnp.concatenate([query, jnp.zeros_like(query)], axis=1).reshape(-1)
    row = jnp.concatenate([query, own[1], jnp.zeros(weights.shape[1] - 3 * width, f32)])
    return weights, jnp.broadcast_to(row[None], (8, row.shape[0])), params


def reduce_heads(grads, vec, depth, width):
    total = lax.psum_scatter(grads, "dp", scatter_dimension=0, tiled=True).astype(f32)
    pairs = total[:, : 2 * width].reshape(depth, -1, 2, HEAD_DIM)
    small = lax.psum_scatter(vec, "dp", scatter_dimension=0, tiled=False)
    small = jnp.pad(small, ((0, 4), (0, LANES - depth)))
    return (
        pairs[:, :, 0].reshape(depth, width),
        pairs[:, :, 1].reshape(depth, width),
        total[:, 2 * width : 3 * width],
        small,
    )


def solution(mesh):
    placed = (
        P("dp", None),
        P("dp", None),
        P("dp", "mp"),
        P("dp", "mp"),
        P("dp", "mp"),
        P("mp", "dp"),
        P("dp", "mp"),
        P("mp", "dp"),
        P(None, "dp"),
        P(None, "dp"),
        P(None, "dp"),
        P("dp"),
        P(),
        P("dp"),
        P("mp", "dp"),
    )
    return jax.shard_map(
        on_device,
        mesh=mesh,
        in_specs=placed,
        out_specs=(
            P("dp", None),
            P("dp", None),
            P("dp", "mp"),
            P("dp", "mp"),
            P("dp", "mp"),
            P("mp", "dp"),
            P("dp", "mp"),
            P("mp", "dp"),
            P(None, "dp"),
            P(None, "dp"),
            P(None, "dp"),
            P("dp"),
        ),
        check_vma=False,
    )
```

```python
from functools import partial
import math

import jax
import jax.numpy as jnp
from jax import lax
from jax.experimental import pallas as pl
from jax.experimental.pallas import tpu as pltpu
from jax.sharding import PartitionSpec as P

D = 768
HEAD_DIM = 64
FF = 3072
CLUSTER = 128
LANES = 128
EPSILON = 1e-05
MASKED = -1e30
SCALE = 1.0 / math.sqrt(HEAD_DIM)

bf16 = jnp.bfloat16
f32 = jnp.float32
i32 = jnp.int32

VMEM = 60 * 1024 * 1024


def cost(us):
    return pl.CostEstimate(flops=int(1e9 * us), bytes_accessed=int(3e6 * us), transcendentals=0)


QUICK = cost(0.001)
ATTEND_US = 46
COLLECT_US = 30
COLLECT_ROWS = 512
SPREAD_US = 3
HEAD_GRADS_US = 4
SORT_US = 80
ATTEND_BACK_US = 40


def nn(a, b):
    return lax.dot_general(a, b, (((1,), (0,)), ((), ())), preferred_element_type=f32)


def nt(a, b):
    return lax.dot_general(a, b, (((1,), (1,)), ((), ())), preferred_element_type=f32)


def tn(a, b):
    return lax.dot_general(a, b, (((0,), (0,)), ((), ())), preferred_element_type=f32)


def lane_iota(rows, lanes=LANES):
    return lax.broadcasted_iota(i32, (rows, lanes), 1)


def sublane_iota(rows, lanes=LANES):
    return lax.broadcasted_iota(i32, (rows, lanes), 0)


def as_column(row):
    parts = [
        jnp.broadcast_to(row[:, i * LANES : (i + 1) * LANES], (LANES, LANES)).T
        for i in range(row.shape[1] // LANES)
    ]
    return parts[0] if len(parts) == 1 else jnp.concatenate(parts, axis=0)


def loop(count):
    def run(step):
        def body(i, carry):
            step(i)
            return carry

        lax.fori_loop(0, count, body, 0)

    return run


class Layout:
    def __init__(self, peers, tokens, heads):
        self.peers, self.tokens, self.heads = peers, tokens, heads
        self.stripe = min(16, peers)
        self.runs = peers // self.stripe
        self.per_dev = CLUSTER // self.stripe
        self.rows_peer = tokens // peers
        self.half_rows = self.rows_peer // 2
        self.pairs = self.half_rows // self.per_dev
        self.packed = tokens // 2
        self.clusters = peers * tokens // CLUSTER
        self.data_rows = 9 * self.half_rows
        self.direct = self.half_rows == LANES
        self.arrays = peers if self.direct else 1

    def peer(self, me, s):
        return (me ^ s) if self.direct else s

    def shapes(self, rows, dtype=bf16):
        lead = () if self.direct else (self.peers,)
        return [jax.ShapeDtypeStruct(lead + (rows, LANES), dtype)] * self.arrays

    def specs(self, rows, at):
        if self.direct:
            return [pl.BlockSpec((rows, LANES), lambda *g: (at(*g), 0))] * self.arrays
        return [pl.BlockSpec((self.peers, rows, LANES), lambda *g: (0, at(*g), 0))]

    def view(self, refs, s):
        return refs[s] if self.direct else refs[0].at[s]


def only(at):
    return lambda *g: at


def place_kernel(lay, perm_ref, code_ref):
    groups = lay.clusters
    shift = CLUSTER.bit_length() - 1
    blocks = lay.tokens // LANES
    before = sublane_iota(LANES, 2 * LANES)
    after = lane_iota(LANES, 2 * LANES)
    ahead_of = jnp.where((before < after) | (after >= LANES), 1.0, 0.0).astype(bf16)

    def members(h, b):
        row = lax.shift_right_logical(perm_ref[h : h + 1, b * LANES : (b + 1) * LANES], shift)
        return jnp.broadcast_to(row, (groups, LANES)) == sublane_iota(groups)

    for h in range(lay.heads):
        if lay.runs == 1:
            carry = (sublane_iota(groups) * lay.per_dev).astype(f32)
        else:
            counts = jnp.zeros((groups, LANES), f32)
            for b in range(blocks):
                member = jnp.where(members(h, b), 1.0, 0.0).astype(bf16)
                counts = counts + nn(member, ahead_of)[:, LANES:]
            lower = jnp.where(
                sublane_iota(groups, groups) > lane_iota(groups, groups), 1.0, 0.0
            ).astype(bf16)
            carry = nn(lower, counts.astype(bf16))
        for b in range(blocks):
            member = members(h, b)
            found = nn(jnp.where(member, 1.0, 0.0).astype(bf16), ahead_of)
            rank = jnp.sum(jnp.where(member, found[:, :LANES] + carry, 0.0), axis=0, keepdims=True)
            carry = carry + found[:, LANES:]
            rank = rank.astype(i32)
            peer = lax.shift_right_logical(rank, lay.rows_peer.bit_length() - 1)
            rest = rank & (lay.rows_peer - 1)
            half = lax.shift_right_logical(rest, lay.half_rows.bit_length() - 1)
            packed = peer * lay.half_rows + (rest & (lay.half_rows - 1))
            at = slice(b * LANES, (b + 1) * LANES)
            code_ref[h, 0:1, at] = packed
            code_ref[h, 1:2, at] = half


def place_tokens(lay, perm):
    return pl.pallas_call(
        partial(place_kernel, lay),
        out_shape=jax.ShapeDtypeStruct((lay.heads, 8, lay.tokens), i32),
        name="place_tokens",
        cost_estimate=QUICK,
    )(perm)


def one_hot(equal):
    return jnp.where(equal, 1.0, 0.0).astype(bf16)


def scatter_matrix(lay, me, packed, s, blocks):
    rows = blocks * lay.half_rows
    if lay.direct:
        parts = [
            one_hot(
                jnp.broadcast_to(packed, (lay.half_rows, lay.tokens))
                == sublane_iota(lay.half_rows, lay.tokens) + lay.peer(me, s + i) * lay.half_rows
            )
            for i in range(blocks)
        ]
        return jnp.concatenate(parts, axis=0)
    wanted = sublane_iota(rows, lay.tokens) + s * lay.half_rows
    return one_hot(jnp.broadcast_to(packed, (rows, lay.tokens)) == wanted)


def gather_matrix(lay, me, column):
    lane = lane_iota(column.shape[0])
    parts = [
        one_hot(column == lane + lay.peer(me, k) * LANES) for k in range(lay.packed // LANES)
    ]
    return jnp.concatenate(parts, axis=1)


def block_rows(lay, refs, first):
    at = slice(first, first + lay.half_rows)
    if lay.direct:
        return jnp.concatenate([refs[s][at, :] for s in range(lay.peers)], axis=0)
    return refs[0][:, at, :].astype(f32).reshape(lay.packed, LANES).astype(bf16)


def put_blocks(lay, refs, s, blocks, first, rows):
    at = slice(first, first + lay.half_rows) if isinstance(first, int) else pl.ds(first, lay.half_rows)
    if lay.direct:
        for i in range(blocks):
            refs[s + i][at, :] = rows[i * LANES : (i + 1) * LANES].astype(bf16)
    else:
        rows = rows.astype(f32).reshape(blocks, lay.half_rows, LANES).astype(bf16)
        refs[0][s : s + blocks, at, :] = rows


ROWS = 512
COUNT = 4


def project_kernel(lay, steps, place_ref, x_ref, w_ref, bias_ref, code_ref, pad_ref, *rest):
    outs = rest[: lay.arrays]
    rows_ref, flag_ref = rest[lay.arrays :]
    step = pl.program_id(0)
    me = place_ref[0]
    width = 4 * LANES

    @pl.when(step < steps)
    def _():
        at = pl.ds(pl.multiple_of(step * ROWS, ROWS), ROWS)
        values = nn(x_ref[...], w_ref[...]) + bias_ref[0:1, :]
        low = lane_iota(ROWS) < HEAD_DIM
        lane_half = jnp.where(low, 0, 1)
        live = as_column(pad_ref[0:1, at])
        tiles = [values[:, i * LANES : (i + 1) * LANES] for i in range(values.shape[1] // LANES)]
        turned = [pltpu.roll(tile, HEAD_DIM, 1) for tile in tiles]
        for h in range(lay.heads):
            half = as_column(code_ref[h, 1:2, at])
            keep = half == lane_half
            v, side = lay.heads + h // 2, h % 2
            planes = (
                jnp.where(low, tiles[h], turned[h]),
                jnp.where(low, turned[h], tiles[h]),
                jnp.where(low, tiles[v], turned[v]) if side == 0 else jnp.where(low, turned[v], tiles[v]),
            )
            for x, plane in enumerate(planes):
                rows_ref[h, at, x * LANES : (x + 1) * LANES] = jnp.where(keep, plane, 0.0).astype(bf16)
            flags = jnp.where((lane_iota(ROWS) == half) & (live == 1), 1.0, 0.0)
            rows_ref[h, at, 3 * LANES :] = flags.astype(bf16)

    count = COUNT if lay.direct else 32

    @pl.when(step >= steps)
    def _():
        h = step - steps
        for s in range(0, lay.peers, count):
            chosen = scatter_matrix(lay, me, code_ref[h, 0:1, :], s, count)
            moved = nn(chosen, rows_ref[h])
            for x in range(3):
                first = pl.multiple_of((h * 3 + x) * lay.half_rows, 16)
                put_blocks(lay, outs, s, count, first, moved[:, x * LANES : (x + 1) * LANES])
            for i in range(count * lay.half_rows // LANES):
                at = slice(s * lay.half_rows + i * LANES, s * lay.half_rows + (i + 1) * LANES)
                flag_ref[h, :, at] = moved[i * LANES : (i + 1) * LANES, 3 * LANES :].T[:8]

    @pl.when(step == steps + lay.heads - 1)
    def _():
        for s in range(lay.peers):
            at = slice(s * lay.half_rows, (s + 1) * lay.half_rows)
            rows = [flag_ref[k, 0:2, at] for k in range(lay.heads)]
            block = jnp.concatenate(rows + [jnp.zeros((16 - 2 * lay.heads, lay.half_rows), f32)], axis=0)
            if lay.half_rows < LANES:
                block = jnp.concatenate(
                    [block, jnp.zeros((16, LANES - lay.half_rows), f32)], axis=1
                )
            lay.view(outs, s)[lay.data_rows : lay.data_rows + 16, :] = block.astype(bf16)


def project_rows(lay, places, x, weights, bias, code, pad):
    width = weights.shape[1]
    steps = lay.tokens // ROWS
    spec = pltpu.PrefetchScalarGridSpec(
        num_scalar_prefetch=1,
        grid=(steps + lay.heads,),
        in_specs=[
            pl.BlockSpec((ROWS, D), lambda s, _: (jnp.minimum(s, steps - 1), 0)),
            pl.BlockSpec((D, width), lambda s, _: (0, 0)),
            pl.BlockSpec((8, width), lambda s, _: (0, 0)),
            pl.BlockSpec((lay.heads, 8, lay.tokens), lambda s, _: (0, 0, 0)),
            pl.BlockSpec((1, lay.tokens), lambda s, _: (0, 0)),
        ],
        out_specs=lay.specs(lay.data_rows + 16, only(0)),
        scratch_shapes=[
            pltpu.VMEM((lay.heads, lay.tokens, 4 * LANES), bf16),
            pltpu.VMEM((lay.heads, 8, lay.packed), f32),
        ],
    )
    return pl.pallas_call(
        partial(project_kernel, lay, steps),
        grid_spec=spec,
        out_shape=lay.shapes(lay.data_rows + 16),
        compiler_params=pltpu.CompilerParams(vmem_limit_bytes=VMEM),
        name="project_rows",
        cost_estimate=QUICK,
    )(places, x, weights, bias, code, pad)


def pair_rows(lay, refs, first, run, p):
    at = slice(first + p * lay.per_dev, first + (p + 1) * lay.per_dev)
    if lay.direct:
        return jnp.concatenate([refs[s][at, :] for s in range(lay.stripe)], axis=0)
    block = refs[0][run * lay.stripe : (run + 1) * lay.stripe, first : first + lay.half_rows, :]
    block = block.astype(f32)[:, p * lay.per_dev : (p + 1) * lay.per_dev, :]
    return block.reshape(CLUSTER, LANES).astype(bf16)


def put_pair(lay, refs, first, run, p, rows):
    at = slice(first + p * lay.per_dev, first + (p + 1) * lay.per_dev)
    for s in range(lay.stripe):
        part = rows[s * lay.per_dev : (s + 1) * lay.per_dev]
        lay.view(refs, run * lay.stripe + s)[at, :] = part.astype(bf16)


def live_columns(lay, flags, h):
    pick = one_hot(sublane_iota(16, 2 * LANES) == 2 * h + lane_iota(16, 2 * LANES) // LANES)
    return [tn(lay.view(flags, s)[...], pick) for s in range(lay.peers)]


def allowed_pair(lay, columns, run, p):
    at = slice(p * lay.per_dev, (p + 1) * lay.per_dev)
    live = jnp.concatenate([columns[run * lay.stripe + s][at] for s in range(lay.stripe)], axis=0)
    live = jnp.concatenate([live[:, :LANES], live[:, LANES:]], axis=0)
    same = sublane_iota(2 * CLUSTER) % CLUSTER == lane_iota(2 * CLUSTER)
    return (live > 0.5) | same


def stack_halves(rows):
    low = lane_iota(rows.shape[0], rows.shape[1]) < HEAD_DIM
    zero = jnp.zeros_like(rows)
    return jnp.concatenate([jnp.where(low, rows, zero), jnp.where(low, zero, rows)], axis=0)


def each_half(fold, rows):
    one, two = (
        jnp.broadcast_to(fold(part, axis=0, keepdims=True), part.shape)
        for part in (rows[:CLUSTER], rows[CLUSTER:])
    )
    return jnp.concatenate([one, two], axis=0)


def inverse_sum(rows, axis, keepdims):
    return 1.0 / jnp.sum(rows, axis=axis, keepdims=keepdims)


def soft_weights(queries, keys, allowed):
    scores = jnp.where(allowed, nt(keys, queries) * SCALE, MASKED)
    grown = jnp.exp(scores - each_half(jnp.max, scores))
    return grown * each_half(inverse_sum, grown)


def attend_kernel(lay, *refs):
    rows, flags, outs = (refs[i * lay.arrays : (i + 1) * lay.arrays] for i in range(3))
    live = live_columns(lay, flags, pl.program_id(0))
    for run in range(lay.runs):
        for p in range(lay.pairs):
            q, k, v = (pair_rows(lay, rows, x * lay.half_rows, run, p) for x in range(3))
            soft = soft_weights(q, stack_halves(k), allowed_pair(lay, live, run, p))
            put_pair(lay, outs, 0, run, p, tn(soft.astype(bf16), stack_halves(v)))


def attend(lay, arrived):
    head = lambda h: h
    return pl.pallas_call(
        partial(attend_kernel, lay),
        grid=(lay.heads,),
        in_specs=lay.specs(3 * lay.half_rows, head) + lay.specs(16, only(lay.data_rows // 16)),
        out_specs=lay.specs(lay.half_rows, head),
        out_shape=lay.shapes(lay.heads * lay.half_rows),
        name="attend",
        cost_estimate=cost(ATTEND_US),
    )(*arrived, *arrived)


def attend_back_kernel(lay, *refs):
    rows, flags, grads, outs = (refs[i * lay.arrays : (i + 1) * lay.arrays] for i in range(4))
    sum_ref = refs[-1]
    live = live_columns(lay, flags, pl.program_id(0))
    low = lane_iota(CLUSTER) < HEAD_DIM
    sums = [jnp.zeros((1, LANES), f32)] * 2
    for run in range(lay.runs):
        for p in range(lay.pairs):
            q, k, v = (pair_rows(lay, rows, x * lay.half_rows, run, p) for x in range(3))
            g = pair_rows(lay, grads, 0, run, p)
            keys = stack_halves(k)
            soft = soft_weights(q, keys, allowed_pair(lay, live, run, p))
            grad_soft = nt(stack_halves(v), g)
            delta = each_half(jnp.sum, soft * grad_soft)
            grad = (soft * (grad_soft - delta)).astype(bf16)
            grad_q = (tn(grad, keys) * SCALE).astype(bf16)
            part = nn(grad, q)
            grad_k = (jnp.where(low, part[:CLUSTER], part[CLUSTER:]) * SCALE).astype(bf16)
            part = nn(soft.astype(bf16), g)
            grad_v = jnp.where(low, part[:CLUSTER], part[CLUSTER:]).astype(bf16)
            for x, part in enumerate((grad_q, grad_k, grad_v)):
                put_pair(lay, outs, x * lay.half_rows, run, p, part)
            sums[0] = sums[0] + jnp.sum(grad_q.astype(f32), axis=0, keepdims=True)
            sums[1] = sums[1] + jnp.sum(grad_v.astype(f32), axis=0, keepdims=True)
    sum_ref[0] = jnp.concatenate(sums + [jnp.zeros((6, LANES), f32)], axis=0)


def attend_back(lay, arrived, grads):
    head = lambda h: h
    three = lay.specs(3 * lay.half_rows, head)
    out = pl.pallas_call(
        partial(attend_back_kernel, lay),
        grid=(lay.heads,),
        in_specs=three
        + lay.specs(16, only(lay.data_rows // 16))
        + lay.specs(lay.half_rows, head),
        out_specs=three + [pl.BlockSpec((1, 8, LANES), lambda h: (h, 0, 0))],
        out_shape=lay.shapes(lay.data_rows)
        + [jax.ShapeDtypeStruct((lay.heads, 8, LANES), f32)],
        name="attend_back",
        cost_estimate=cost(ATTEND_BACK_US),
    )(*arrived, *arrived, *grads)
    return list(out[:-1]), out[-1]


def side_rows(quarter, side):
    return pl.ds(pl.multiple_of(quarter * 512 + side * 256, 256), 256)


def unsort_kernel(lay, place_ref, *refs):
    rows_refs, code_ref, outs = refs[: lay.arrays], refs[lay.arrays], refs[lay.arrays + 1 :]
    rows = block_rows(lay, rows_refs, 0)
    low = lane_iota(256) < HEAD_DIM
    me, place = place_ref[0], place_ref[1]

    for t in range(4):
        sides = []
        for side in range(2):
            at = side_rows(place ^ t, side)
            column = as_column(code_ref[0, 0:1, at])
            half = as_column(code_ref[0, 1:2, at])
            found = nn(gather_matrix(lay, me, column), rows)
            sides.append(jnp.where(half == side, found, pltpu.roll(found, HEAD_DIM, 1)))
        outs[t][...] = jnp.where(low, sides[0], sides[1]).astype(bf16)


def unsort_rows(lay, places, returned, code):
    spec = pltpu.PrefetchScalarGridSpec(
        num_scalar_prefetch=1,
        grid=(lay.heads,),
        in_specs=lay.specs(lay.half_rows, lambda h, _: h)
        + [pl.BlockSpec((1, 8, lay.tokens), lambda h, _: (h, 0, 0))],
        out_specs=[pl.BlockSpec((256, LANES), lambda h, _: (0, h))] * 4,
    )
    return pl.pallas_call(
        partial(unsort_kernel, lay),
        grid_spec=spec,
        out_shape=[jax.ShapeDtypeStruct((256, lay.heads * LANES), bf16)] * 4,
        name="unsort_rows",
        cost_estimate=QUICK,
    )(places, *returned, code)


def sort_kernel(lay, place_ref, *refs):
    grads, code_ref, outs, rows_ref = refs[:4], refs[4], refs[5:-1], refs[-1]
    low = lane_iota(256) < HEAD_DIM
    lane_half = jnp.where(low, 0, 1)
    me, place = place_ref[0], place_ref[1]

    for t in range(4):
        block = grads[t][...].astype(f32)
        turned = pltpu.roll(block, HEAD_DIM, 1)
        for side in range(2):
            at = side_rows(place ^ t, side)
            half = as_column(code_ref[0, 1:2, at])
            both = jnp.where(low, block, turned) if side == 0 else jnp.where(low, turned, block)
            rows_ref[at, :] = jnp.where(half == lane_half, both, 0.0).astype(bf16)

    count = 4 if lay.direct else 32
    for s in range(0, lay.peers, count):
        chosen = scatter_matrix(lay, me, code_ref[0, 0:1, :], s, count)
        put_blocks(lay, outs, s, count, 0, nn(chosen, rows_ref[...]))


def sort_rows(lay, places, grads, code):
    spec = pltpu.PrefetchScalarGridSpec(
        num_scalar_prefetch=1,
        grid=(lay.heads,),
        in_specs=[pl.BlockSpec((256, LANES), lambda h, _: (0, h))] * 4
        + [pl.BlockSpec((1, 8, lay.tokens), lambda h, _: (h, 0, 0))],
        out_specs=lay.specs(lay.half_rows, lambda h, _: h),
        scratch_shapes=[pltpu.VMEM((lay.tokens, LANES), bf16)],
    )
    return pl.pallas_call(
        partial(sort_kernel, lay),
        grid_spec=spec,
        out_shape=lay.shapes(lay.heads * lay.half_rows),
        name="sort_rows",
        cost_estimate=cost(SORT_US),
    )(places, *grads, code)


def pack_kernel(
    query_ref, key_ref, value_ref, output_ref, inner_ref, outer_ref,
    bias_ref, gain_ref, shift_ref, inner_bias_ref, piece_ref, shard_ref,
):
    depth, width = query_ref.shape
    heads = width // HEAD_DIM
    query, key, value = (ref[...].astype(f32) for ref in (query_ref, key_ref, value_ref))
    cut = [slice(h * HEAD_DIM, (h + 1) * HEAD_DIM) for h in range(heads)]
    columns = [part for at in cut for part in (query[:, at], key[:, at])] + [value]
    have = 3 * width
    fill = -have % LANES
    if fill:
        columns.append(jnp.zeros((depth, fill), f32))
    columns = jnp.concatenate(columns, axis=1).astype(bf16)
    piece_ref[:depth, : have + fill] = columns
    inner_bias = inner_bias_ref[...].astype(f32)
    vectors = jnp.concatenate(
        [ref[...].astype(f32) for ref in (bias_ref, gain_ref, shift_ref)]
        + [inner_bias[:, i * depth : (i + 1) * depth] for i in range(4)]
        + [jnp.zeros((4, depth), f32)],
        axis=0,
    )
    if depth < LANES:
        vectors = jnp.concatenate([vectors, jnp.zeros((16, LANES - depth), f32)], axis=1)
    piece_ref[:16, have + fill :] = vectors.astype(bf16)
    shard_ref[:, :D] = inner_ref[...]
    turned = output_ref[...].astype(f32).T
    shard_ref[:, D : 2 * D] = outer_ref[...]
    shard_ref[:, 2 * D :] = jnp.concatenate(
        [turned[:, at] for at in cut for _ in range(2)], axis=1
    ).astype(bf16)


def pack_weights(*arrays):
    depth, width = arrays[0].shape
    columns = -(-3 * width // LANES) * LANES
    return pl.pallas_call(
        pack_kernel,
        out_shape=[
            jax.ShapeDtypeStruct((max(depth, 16), columns + LANES), bf16),
            jax.ShapeDtypeStruct((depth, 2 * D + 2 * width), bf16),
        ],
        name="pack_weights",
        cost_estimate=QUICK,
    )(*arrays)


def assemble_kernel(lay, place_ref, *refs):
    pieces, (weight_ref, bias_ref, par_ref, part_ref) = refs[: lay.peers], refs[lay.peers :]
    me, place = place_ref[0], place_ref[1]
    depth = D // lay.peers
    for s in range(lay.peers):
        d = me ^ s
        at = pl.ds(pl.multiple_of(d * depth, 16), depth)
        columns = weight_ref.shape[1]
        weight_ref[at, :] = pieces[s][:, :columns]
        part_ref[d] = pieces[s][:16, columns:].astype(f32)

    def whole(row, rows=1, peers=range(lay.peers)):
        return jnp.concatenate(
            [part_ref[d, row + i : row + i + 1, :depth] for d in peers for i in range(rows)], axis=1
        )

    vectors = [whole(r) for r in range(8)]
    each = lay.peers // 4
    vectors += [whole(8, 4, range(j * each, (j + 1) * each)) for j in range(4)]
    par_ref[...] = jnp.concatenate(vectors + [jnp.zeros((4, D), f32)], axis=0)
    width = lay.heads * HEAD_DIM

    def own(vector):
        out = vector[:, :width]
        for p in range(1, D // width):
            out = jnp.where(place == p, vector[:, p * width : (p + 1) * width], out)
        return out

    query = own(vectors[0])
    zero = jnp.zeros((1, HEAD_DIM), f32)
    columns = [
        part for h in range(lay.heads) for part in (query[:, h * HEAD_DIM : (h + 1) * HEAD_DIM], zero)
    ] + [own(vectors[1])]
    fill = bias_ref.shape[1] - 3 * width
    if fill:
        columns.append(jnp.zeros((1, fill), f32))
    bias_ref[...] = jnp.broadcast_to(jnp.concatenate(columns, axis=1), bias_ref.shape)


def assemble_weights(lay, places, pieces):
    columns = pieces[0].shape[1] - LANES
    vmem = pl.BlockSpec(memory_space=pltpu.VMEM)
    return pl.pallas_call(
        partial(assemble_kernel, lay),
        in_specs=[pl.BlockSpec(memory_space=pltpu.SMEM)] + [vmem] * lay.peers,
        out_specs=[vmem] * 3,
        out_shape=[
            jax.ShapeDtypeStruct((D, columns), bf16),
            jax.ShapeDtypeStruct((8, columns), f32),
            jax.ShapeDtypeStruct((16, D), f32),
        ],
        scratch_shapes=[pltpu.VMEM((lay.peers, 16, LANES), f32)],
        name="assemble_weights",
        cost_estimate=QUICK,
    )(places, *pieces)


def mean_rows(v):
    return jnp.sum(v, axis=1, keepdims=True) * (1.0 / D)


def norm_forward(rows):
    centred = rows - mean_rows(rows)
    inv = lax.rsqrt(mean_rows(centred * centred) + EPSILON)
    return centred * inv, inv


def norm_backward(scaled, normed, inv):
    return inv * (scaled - mean_rows(scaled) - normed * mean_rows(scaled * normed))


TALL = 512


def middle_kernel(
    place_ref,
    att0,
    att1,
    att2,
    att3,
    hidden_ref,
    cot_ref,
    par_ref,
    w0,
    w1,
    w2,
    w3,
    out_ref,
    act_ref,
    pre_ref,
    low_ref,
    ffn_grad_ref,
    branch_grad_ref,
    h1_ref,
    grad0,
    grad1,
    grad2,
    grad3,
    vec_ref,
    first_ref,
    normed_ref,
    inv_ref,
    slope_ref,
    sum_ref,
    h2_ref,
    weight_ref,
    sems,
):
    step = pl.program_id(0)
    place = place_ref[1]
    project = slice(2 * D, None)

    def fetch(t, part):
        width = att0.shape[1]
        at = (pl.ds(2 * D, width), pl.ds(0, 2 * D))[part]
        source = (w0, w1, w2, w3)[t]
        return pltpu.make_async_copy(source.at[:, at], weight_ref.at[t, :, at], sems.at[part, t])

    for t in range(4):

        @pl.when(step == t + 1)
        def _():
            fetch(t, 1).wait()

    @pl.when(step == 0)
    def _():
        for t in range(4):
            fetch(t, 0).start()
        for t in range(4):
            fetch(t, 1).start()
        for t in range(4):
            fetch(t, 0).wait()
        vec_ref[...] = jnp.zeros_like(vec_ref)

        @loop(2)
        def _(side):
            branch = jnp.zeros((256, D), f32)
            for t, att_ref in enumerate((att0, att1, att2, att3)):
                att = att_ref[...]
                lane = lane_iota(256, att.shape[1]) % LANES
                own = (lane >= HEAD_DIM).astype(i32) == side
                branch = branch + nt(jnp.where(own, att, jnp.zeros_like(att)), weight_ref[t, :, project])
            at = pl.ds(pl.multiple_of(side * 256, 256), 256)
            rows = hidden_ref[at, :].astype(f32) + (branch + par_ref[2:3, :])
            normed, inv = norm_forward(rows)
            first = normed * par_ref[4:5, :] + par_ref[6:7, :]
            first_ref[at, :] = first
            normed_ref[at, :] = normed
            inv_ref[at, :] = jnp.broadcast_to(inv, (256, LANES))
            low_ref[at, :] = first.astype(bf16)

        sum_ref[...] = jnp.zeros_like(sum_ref)

    @pl.when((step >= 1) & (step <= 4))
    def _():
        j = step - 1

        @loop(512 // TALL)
        def _(side):
            at = pl.ds(pl.multiple_of(side * TALL, TALL), TALL)
            pre = nn(low_ref[at, :], weight_ref[j, :, :D]) + par_ref[pl.ds(8 + (place ^ j), 1), :]
            cdf = 0.5 * (1.0 + lax.erf(pre * (1.0 / math.sqrt(2.0))))
            slope_ref[j, at, :] = cdf + pre * jnp.exp(-0.5 * pre * pre) * (1.0 / math.sqrt(2.0 * math.pi))
            act = (pre * cdf).astype(bf16)
            act_ref[at, :] = act
            sum_ref[at, :] += nt(act, weight_ref[j, :, D : 2 * D])

    @pl.when(step == 4)
    def _():

        @loop(4)
        def _(side):
            at = pl.ds(pl.multiple_of(side * 128, 128), 128)
            rows = first_ref[at, :] + (sum_ref[at, :] + par_ref[3:4, :])
            normed, inv = norm_forward(rows)
            out_ref[at, :] = (normed * par_ref[5:6, :] + par_ref[7:8, :]).astype(bf16)
            cot = cot_ref[at, :].astype(f32)
            grad = norm_backward(cot * par_ref[5:6, :], normed, inv)
            grad_low = grad.astype(bf16)
            h2_ref[at, :] = grad
            ffn_grad_ref[at, :] = grad_low
            vec_ref[3:4, :] += jnp.sum(grad_low.astype(f32), axis=0, keepdims=True)
            vec_ref[5:6, :] += jnp.sum(cot * normed, axis=0, keepdims=True)
            vec_ref[7:8, :] += jnp.sum(cot, axis=0, keepdims=True)

        sum_ref[...] = jnp.zeros_like(sum_ref)

    @pl.when(step >= 5)
    def _():
        j = 8 - step
        vec_ref[pl.ds(8 + (place ^ j), 1), :] = jnp.zeros((1, D), f32)

        @loop(512 // TALL)
        def _(side):
            at = pl.ds(pl.multiple_of(side * TALL, TALL), TALL)
            grad_act = nn(ffn_grad_ref[at, :], weight_ref[j, :, D : 2 * D])
            grad_pre = (grad_act * slope_ref[j, at, :]).astype(bf16)
            pre_ref[at, :] = grad_pre
            vec_ref[pl.ds(8 + (place ^ j), 1), :] += jnp.sum(grad_pre.astype(f32), axis=0, keepdims=True)
            sum_ref[at, :] += nt(grad_pre, weight_ref[j, :, :D])

    @pl.when(step == 8)
    def _():

        @loop(4)
        def _(side):
            at = pl.ds(pl.multiple_of(side * 128, 128), 128)
            grad_first = h2_ref[at, :] + sum_ref[at, :]
            normed = normed_ref[at, :]
            grad = norm_backward(grad_first * par_ref[4:5, :], normed, inv_ref[at, 0:1])
            grad_low = grad.astype(bf16)
            h1_ref[at, :] = grad
            branch_grad_ref[at, :] = grad_low
            vec_ref[2:3, :] += jnp.sum(grad_low.astype(f32), axis=0, keepdims=True)
            vec_ref[4:5, :] += jnp.sum(grad_first * normed, axis=0, keepdims=True)
            vec_ref[6:7, :] += jnp.sum(grad_first, axis=0, keepdims=True)

        for t, grad_ref in enumerate((grad0, grad1, grad2, grad3)):
            both = nn(branch_grad_ref[...], weight_ref[t, :, project])
            lane = lane_iota(256, both.shape[1]) % LANES
            grad_ref[...] = jnp.where(lane < HEAD_DIM, both[:256], both[256:]).astype(bf16)


def middle(places, att, hidden, cotangent, params, weights):
    width = att[0].shape[1]
    rows = 512

    def up(s, q):
        return (0, jnp.clip(s - 1, 0, 3))

    def down(s, q):
        return (0, jnp.clip(8 - s, 0, 3))

    def whole(rank):
        return lambda s, q: (0,) * rank

    square = pl.BlockSpec((rows, D), whole(2))
    exchanged = pl.BlockSpec((256, width), whole(2))
    spec = pltpu.PrefetchScalarGridSpec(
        num_scalar_prefetch=1,
        grid=(9,),
        in_specs=[exchanged] * 4
        + [
            pl.BlockSpec((rows, D), lambda s, q: (q[1], 0)),
            pl.BlockSpec((rows, D), lambda s, q: (q[1], 0)),
            pl.BlockSpec((16, D), whole(2)),
        ]
        + [pl.BlockSpec(memory_space=pl.ANY)] * 4,
        out_specs=[
            square,
            pl.BlockSpec((rows, D), up),
            pl.BlockSpec((rows, D), down),
            square,
            square,
            square,
            square,
        ]
        + [exchanged] * 4
        + [pl.BlockSpec((16, D), whole(2))],
        scratch_shapes=[
            pltpu.VMEM((rows, D), f32),
            pltpu.VMEM((rows, D), f32),
            pltpu.VMEM((rows, LANES), f32),
            pltpu.VMEM((4, rows, D), f32),
            pltpu.VMEM((rows, D), f32),
            pltpu.VMEM((rows, D), f32),
            pltpu.VMEM((4, D, 2 * D + width), bf16),
            pltpu.SemaphoreType.DMA((2, 4)),
        ],
    )
    out = pl.pallas_call(
        middle_kernel,
        grid_spec=spec,
        out_shape=[
            jax.ShapeDtypeStruct((rows, D), bf16),
            jax.ShapeDtypeStruct((rows, FF), bf16),
            jax.ShapeDtypeStruct((rows, FF), bf16),
            jax.ShapeDtypeStruct((rows, D), bf16),
            jax.ShapeDtypeStruct((rows, D), bf16),
            jax.ShapeDtypeStruct((rows, D), bf16),
            jax.ShapeDtypeStruct((rows, D), f32),
        ]
        + [jax.ShapeDtypeStruct((256, width), bf16)] * 4
        + [jax.ShapeDtypeStruct((16, D), f32)],
        compiler_params=pltpu.CompilerParams(vmem_limit_bytes=VMEM),
        name="middle",
        cost_estimate=QUICK,
    )(places, *att, hidden, cotangent, params, *weights)
    return out[:7], out[7:11], out[11]


def weight_grad_kernel(chunks, adds, place_ref, act_ref, pre_ref, low_ref, ffn_ref, branch_ref, *refs):
    att_refs, add_refs, out_ref = refs[:chunks], refs[chunks : chunks + adds], refs[-1]

    def put(at, part):
        for ref in add_refs:
            part = part + ref[:, at].astype(f32)
        out_ref[:, at] = part.astype(bf16)

    put(slice(0, D), tn(low_ref[...], pre_ref[...]))
    put(slice(D, 2 * D), tn(ffn_ref[...], act_ref[...]))
    for i in range(chunks):

        @pl.when(pl.program_id(0) == i)
        def _():
            att = att_refs[i][...]
            low = lane_iota(256, att.shape[1]) % LANES < HEAD_DIM
            zero = jnp.zeros_like(att)
            both = jnp.concatenate([jnp.where(low, att, zero), jnp.where(low, zero, att)], axis=0)
            part = tn(branch_ref[...], both)
            planes = [part[:, k * LANES : (k + 1) * LANES] for k in range(part.shape[1] // LANES)]
            planes = [plane + pltpu.roll(plane, HEAD_DIM, 1) for plane in planes]
            if len(planes) % 2:
                planes.append(jnp.zeros_like(planes[0]))
            first = lane_iota(part.shape[0]) < HEAD_DIM
            for k in range(0, len(planes), 2):
                at = slice(2 * D + k // 2 * LANES, 2 * D + (k // 2 + 1) * LANES)
                put(at, jnp.where(first, planes[k], planes[k + 1]))


def weight_grads(places, saved, att, first, chunks, adds):
    act, pre, low, ffn_grad, branch_grad = saved
    rows = act.shape[0]
    width = att[0].shape[1]
    total = 2 * D + -(-width // (2 * LANES)) * LANES
    cut = D // 2

    def chunk(s, i, q):
        return (0, first - 2 * s)

    part = pl.BlockSpec((rows, cut), lambda s, i, q: (0, i))
    spec = pltpu.PrefetchScalarGridSpec(
        num_scalar_prefetch=1,
        grid=(chunks, 2),
        in_specs=[pl.BlockSpec((rows, D), chunk)] * 2
        + [part] * 3
        + [pl.BlockSpec((256, width), lambda s, i, q: (0, 0))] * chunks
        + [pl.BlockSpec((cut, total), lambda s, i, q, k=k: (2 * k + i, 0)) for _, k in adds],
        out_specs=pl.BlockSpec((cut, total), lambda s, i, q: (2 * s + i, 0)),
    )
    return pl.pallas_call(
        partial(weight_grad_kernel, chunks, len(adds)),
        grid_spec=spec,
        out_shape=jax.ShapeDtypeStruct((chunks * D, total), bf16),
        compiler_params=pltpu.CompilerParams(vmem_limit_bytes=VMEM),
        name="weight_grads",
        cost_estimate=QUICK,
    )(
        places, act, pre, low, ffn_grad, branch_grad,
        *[att[first - 2 * s] for s in range(chunks)], *[a for a, _ in adds],
    )


def collect_kernel(lay, place_ref, *refs):
    rows_refs = refs[: lay.arrays]
    code_ref, dense_ref = refs[lay.arrays :]
    me = place_ref[0]
    tokens = dense_ref.shape[0]
    low = lane_iota(tokens) < HEAD_DIM
    firsts, seconds = [], []
    for h in range(lay.heads):
        column = as_column(code_ref[h, 0:1, :])
        half = as_column(code_ref[h, 1:2, :])
        planes = [block_rows(lay, rows_refs, (h * 3 + x) * lay.half_rows) for x in range(3)]
        found = nn(gather_matrix(lay, me, column), jnp.concatenate(planes, axis=1))
        one, two = [], []
        for x in range(3):
            part = found[:, x * LANES : (x + 1) * LANES]
            turned = pltpu.roll(part, HEAD_DIM, 1)
            one.append(jnp.where(half == 0, part, turned))
            two.append(jnp.where(half == 1, part, turned))
        firsts.append(one)
        seconds.append(two)
    tiles = [jnp.where(low, firsts[h][0], seconds[h][1]) for h in range(lay.heads)]
    for h in range(0, lay.heads, 2):
        right = seconds[h + 1][2] if h + 1 < lay.heads else jnp.zeros((tokens, LANES), f32)
        tiles.append(jnp.where(low, firsts[h][2], right))
    dense_ref[...] = jnp.concatenate(tiles, axis=1).astype(bf16)


def collect(lay, places, returned, code, width):
    tokens = COLLECT_ROWS
    spec = pltpu.PrefetchScalarGridSpec(
        num_scalar_prefetch=1,
        grid=(lay.tokens // tokens,),
        in_specs=lay.specs(lay.data_rows, only(0))
        + [pl.BlockSpec((lay.heads, 8, tokens), lambda c, q: (0, 0, c))],
        out_specs=pl.BlockSpec((tokens, width), lambda c, q: (c, 0)),
    )
    return pl.pallas_call(
        partial(collect_kernel, lay),
        grid_spec=spec,
        out_shape=jax.ShapeDtypeStruct((lay.tokens, width), bf16),
        compiler_params=pltpu.CompilerParams(vmem_limit_bytes=VMEM),
        name="collect",
        cost_estimate=cost(COLLECT_US),
    )(places, *returned, code)


def half_rows_at(g, s, place):
    core = place % 2
    return jnp.where(s == 0, 1 - core, core) * 2 + g


def spread_kernel(g, place_ref, dense_ref, w_ref, h1_ref, other_ref, mine_ref):
    step, place = pl.program_id(0), place_ref[1]
    own = (half_rows_at(g, step, place) == place).astype(f32)
    part = nt(dense_ref[...], w_ref[...]) + own * h1_ref[...]

    @pl.when(step == 0)
    def _():
        other_ref[...] = part.astype(bf16)

    @pl.when(step == 1)
    def _():
        mine_ref[...] = part.astype(bf16)


def spread_grads(g, places, dense, weights, grad_h1):
    width = weights.shape[1]
    whole = lambda s, q: (0, 0)
    spec = pltpu.PrefetchScalarGridSpec(
        num_scalar_prefetch=1,
        grid=(2,),
        in_specs=[
            pl.BlockSpec((512, width), lambda s, q: (half_rows_at(g, s, q[1]), 0)),
            pl.BlockSpec((D, width), whole),
            pl.BlockSpec((512, D), whole),
        ],
        out_specs=[pl.BlockSpec((512, D), whole)] * 2,
    )
    return pl.pallas_call(
        partial(spread_kernel, g),
        grid_spec=spec,
        out_shape=[jax.ShapeDtypeStruct((512, D), bf16)] * 2,
        compiler_params=pltpu.CompilerParams(vmem_limit_bytes=VMEM),
        name="spread_grads",
        cost_estimate=cost(SPREAD_US),
    )(places, dense, weights, grad_h1)


def head_grad_kernel(lay, place_ref, x_ref, dense_ref, vec_ref, *refs):
    out_ref, total_ref = refs
    step = pl.program_id(0)

    @pl.when(step == 0)
    def _():
        total_ref[...] = tn(x_ref[...], dense_ref[...])

    @pl.when(step > 0)
    def _():
        total_ref[...] += tn(x_ref[...], dense_ref[...])

    @pl.when(step == 3)
    def _():
        depth = D // lay.peers
        if not lay.direct:
            out_ref[...] = total_ref[...].astype(bf16)
            return
        for d in range(lay.peers):
            out_ref[d, :depth, :] = total_ref[d * depth : (d + 1) * depth, :].astype(bf16)
            vector = vec_ref[d]
            high = vector.astype(bf16).astype(f32)
            width = total_ref.shape[1]
            out_ref[d, depth:, :] = jnp.concatenate(
                [high, vector - high, jnp.zeros((16, width - 2 * LANES), f32)], axis=1
            ).astype(bf16)


def head_grads(lay, places, x, dense, vec):
    width = dense.shape[1]
    depth = D // lay.peers
    shape = (lay.peers, depth + 16, width) if lay.direct else (D, width)
    spec = pltpu.PrefetchScalarGridSpec(
        num_scalar_prefetch=1,
        grid=(4,),
        in_specs=[
            pl.BlockSpec((512, D), lambda s, q: (s, 0)),
            pl.BlockSpec((512, width), lambda s, q: (s, 0)),
            pl.BlockSpec(vec.shape, lambda s, q: (0, 0, 0)),
        ],
        out_specs=pl.BlockSpec(shape, lambda s, q: (0,) * len(shape)),
        scratch_shapes=[pltpu.VMEM((D, width), f32)],
    )
    return pl.pallas_call(
        partial(head_grad_kernel, lay),
        grid_spec=spec,
        out_shape=jax.ShapeDtypeStruct(shape, bf16),
        compiler_params=pltpu.CompilerParams(vmem_limit_bytes=VMEM),
        name="head_grads",
        cost_estimate=cost(HEAD_GRADS_US),
    )(places, x, dense, vec)


def finish_heads_kernel(*refs):
    parts, outs = refs[0], refs[1:]
    depth, width = outs[0].shape
    heads = width // HEAD_DIM
    total = parts[0].astype(f32)
    for d in range(1, parts.shape[0]):
        total = total + parts[d].astype(f32)
    grads = total[:depth]
    cut = [slice(h * LANES, h * LANES + HEAD_DIM) for h in range(heads)]
    outs[0][...] = jnp.concatenate([grads[:, at] for at in cut], axis=1)
    cut = [slice(h * LANES + HEAD_DIM, (h + 1) * LANES) for h in range(heads)]
    outs[1][...] = jnp.concatenate([grads[:, at] for at in cut], axis=1)
    outs[2][...] = grads[:, 2 * width : 3 * width]
    outs[3][...] = total[depth:, :LANES] + total[depth:, LANES : 2 * LANES]


def finish_heads(parts, depth, width):
    shapes = [(depth, width)] * 3 + [(16, LANES)]
    return pl.pallas_call(
        finish_heads_kernel,
        out_shape=[jax.ShapeDtypeStruct(s, f32) for s in shapes],
        name="finish_heads",
        cost_estimate=QUICK,
    )(parts)


def finish_vectors_kernel(depth, own_ref, other_ref, bias_ref, gain_ref, shift_ref, inner_ref):
    total = (own_ref[...] + other_ref[...])[:, :depth]
    bias_ref[...] = total[:4]
    gain_ref[...] = total[4:6]
    shift_ref[...] = total[6:8]
    inner_ref[...] = total[8:12]


def finish_vectors(own, other, depth):
    return pl.pallas_call(
        partial(finish_vectors_kernel, depth),
        out_shape=[jax.ShapeDtypeStruct((n, depth), f32) for n in (4, 2, 2, 4)],
        name="finish_vectors",
        cost_estimate=QUICK,
    )(own, other)


def finish_middle_kernel(grad_ref, inner_ref, outer_ref, output_ref):
    inner_ref[...] = grad_ref[:, :D].astype(f32)
    outer_ref[...] = grad_ref[:, D : 2 * D].astype(f32)
    rest = grad_ref[:, 2 * D :].astype(f32)
    output_ref[...] = rest[:, : output_ref.shape[0]].T


def finish_middle(grads, width):
    depth = grads.shape[0]
    return pl.pallas_call(
        finish_middle_kernel,
        out_shape=[
            jax.ShapeDtypeStruct((depth, D), f32),
            jax.ShapeDtypeStruct((depth, D), f32),
            jax.ShapeDtypeStruct((width, depth), f32),
        ],
        name="finish_middle",
        cost_estimate=QUICK,
    )(grads)


def order_kernel(place_ref, *refs):
    parts, out_ref, rows_ref, sems = refs[:4], refs[4], refs[5], refs[6]
    rows = rows_ref.shape[1]

    def take(i):
        return pltpu.make_async_copy(parts[i], rows_ref.at[i], sems.at[0, i])

    def put(i):
        at = pl.ds(pl.multiple_of(place_ref[i] * rows, rows), rows)
        return pltpu.make_async_copy(rows_ref.at[i], out_ref.at[at, :], sems.at[1, i])

    for i in range(4):
        take(i).start()
    for i in range(4):
        take(i).wait()
        put(i).start()
    for i in range(4):
        put(i).wait()


def order_quarters(order, quarters):
    rows, width = quarters[0].shape
    dtype = quarters[0].dtype
    return pl.pallas_call(
        order_kernel,
        in_specs=[pl.BlockSpec(memory_space=pltpu.SMEM)]
        + [pl.BlockSpec(memory_space=pl.ANY)] * 4,
        out_specs=pl.BlockSpec(memory_space=pl.ANY),
        out_shape=jax.ShapeDtypeStruct((4 * rows, width), dtype),
        scratch_shapes=[pltpu.VMEM((4, rows, width), dtype), pltpu.SemaphoreType.DMA((2, 4))],
        name="order_quarters",
        cost_estimate=QUICK,
    )(order, *quarters)


def over_rows(lay, blocks, near_first=False):
    if not lay.direct:
        return [lax.all_to_all(blocks[0], "dp", split_axis=0, concat_axis=0, tiled=True)]
    out = [blocks[0]]
    for s in range(1, lay.peers):
        rows = blocks[s]
        if near_first and s >= lay.peers - 2:
            rows = after(rows, out[s - lay.peers + 3])
        out.append(lax.ppermute(rows, "dp", [(i, i ^ s) for i in range(lay.peers)]))
    return out


def in_hbm(rows):
    return pltpu.with_memory_space_constraint(rows, pltpu.HBM)


def share_pieces(lay, piece):
    def flip(rows, s):
        return lax.ppermute(rows, "dp", [(i, i ^ s) for i in range(lay.peers)])

    half = lay.peers // 2
    far = flip(piece, half)
    near = [piece] + [flip(piece, s) for s in range(1, half)]
    return near + [far] + [flip(far, s) for s in range(1, half)]


def after(value, *others):
    return lax.optimization_barrier((value, *others))[0]


def swap(rows, flip):
    return lax.ppermute(rows, "mp", [(i, i ^ flip) for i in range(4)])


def over_heads(blocks):
    return [blocks[0]] + [swap(blocks[t], t) for t in range(1, 4)]


def on_device(
    hidden_in,
    cotangent,
    w_query,
    w_key,
    w_value,
    w_output,
    w_inner,
    w_outer,
    biases,
    gains,
    shifts,
    inner_bias,
    lengths,
    padding,
    cluster_perm,
):
    peers = lax.axis_size("dp")
    tokens = hidden_in.shape[0]
    heads = cluster_perm.shape[0]
    lay = Layout(peers, tokens, heads)
    place = lax.axis_index("mp")
    me = lax.axis_index("dp")
    places = jnp.stack([me, place]).astype(i32)
    hidden_in = in_hbm(hidden_in)
    depth = w_query.shape[0]
    width = heads * HEAD_DIM

    piece, shard = pack_weights(
        w_query, w_key, w_value, w_output, w_inner, w_outer.T,
        biases, gains, shifts, inner_bias.reshape(1, -1),
    )
    own_w = lax.all_gather(shard, "dp", axis=0, tiled=True)
    far_w = swap(own_w, 2)
    if lay.direct:
        weights, bias, params = assemble_weights(lay, places, share_pieces(lay, piece))
    else:
        weights, bias, params = gather_weights(lay, place, piece)

    weights = in_hbm(weights)
    code = in_hbm(place_tokens(lay, cluster_perm))
    sent = project_rows(lay, places, hidden_in, weights, bias, code, padding.reshape(1, tokens))
    arrived = over_rows(lay, sent, near_first=True)
    mixed = over_rows(lay, attend(lay, arrived))
    found = unsort_rows(lay, places, mixed, code)
    att = over_heads(found)
    far_w = after(far_w, found[0])
    middle_w = [own_w, in_hbm(swap(own_w, 1)), far_w, in_hbm(swap(far_w, 1))]
    saved, att_grad, vec = middle(places, att, hidden_in, cotangent, params, middle_w)
    out_quarter, act, pre_grad, first_low, ffn_grad, branch_grad, grad_h1 = saved
    saved = tuple(in_hbm(a) for a in (act, pre_grad, first_low, ffn_grad, branch_grad))
    att = [in_hbm(a) for a in att]

    got = over_heads(att_grad)
    from_core = swap(weight_grads(places, saved, att, 3, 2, []), 1)
    grads = sort_rows(lay, places, got, code)
    ready = (after(act, grads[0]),) + saved[1:]
    from_far = swap(weight_grads(places, ready, att, 2, 1, [(from_core, 0)]), 2)
    grads = over_rows(lay, grads)
    slot_grads, bias_sums = attend_back(lay, arrived, grads)

    returned = over_rows(lay, slot_grads)
    ready = (after(act, *returned[1:4]),) + saved[1:]
    summed = weight_grads(places, ready, att, 0, 1, [(from_core, 1), (from_far, 0)])
    head_sums = bias_sums[:, :2].reshape(heads, 2, 2, HEAD_DIM).sum(axis=2)
    head_sums = head_sums.transpose(1, 0, 2).reshape(2, width)
    vec = lax.dynamic_update_slice(vec[:12], head_sums, (0, place * width))
    vec = jnp.concatenate(
        [vec[:8].reshape(8, peers, depth).transpose(1, 0, 2), vec[8:].reshape(peers, 4, depth)],
        axis=1,
    )
    spread = jnp.pad(vec, ((0, 0), (0, 4), (0, (-depth) % LANES)))
    reduced = lax.psum_scatter(after(summed, *returned), "dp", scatter_dimension=0, tiled=True)
    far = swap(after(out_quarter, summed), 2)
    dense = collect(lay, places, returned, code, weights.shape[1])
    terms = head_grads(lay, places, hidden_in, dense, spread)
    dense = after(dense, terms, far)
    groups = [spread_grads(g, places, dense, weights, grad_h1) for g in range(2)]
    chips = [
        (mine.astype(f32) + swap(other, 1).astype(f32)).astype(bf16) for other, mine in groups
    ]
    others = [swap(chip, 2) for chip in chips]
    hidden_out = order_quarters(
        jnp.stack([place, place ^ 2, place ^ 1, place ^ 3]).astype(i32),
        [out_quarter, far, swap(out_quarter, 1), swap(far, 1)],
    )
    if lay.direct:
        terms = lax.all_to_all(terms, "dp", split_axis=0, concat_axis=0, tiled=True)
        ends = finish_heads(terms, depth, width)
    else:
        ends = reduce_heads(terms, vec, depth, width)
    small = ends[3] + swap(ends[3], 1)
    chips[1] = after(chips[1], small, hidden_out)
    small = finish_vectors(small, swap(small, 2), depth)
    ready = [
        (chip.astype(f32) + part.astype(f32)).astype(bf16) for chip, part in zip(chips, others)
    ]
    core = place % 2
    order = jnp.stack([2 * core, 2 * core + 1, 2 - 2 * core, 3 - 2 * core]).astype(i32)
    grad_hidden = order_quarters(
        after(order, small[0]),
        ready + [swap(part, 1) for part in ready],
    )

    grad_inner, grad_outer, grad_output = finish_middle(reduced, width)
    return (
        hidden_out,
        grad_hidden,
        ends[0],
        ends[1],
        ends[2],
        grad_output,
        grad_inner,
        grad_outer.T,
        small[0],
        small[1],
        small[2],
        small[3].reshape(-1),
    )


def gather_weights(lay, place, piece):
    depth = D // lay.peers
    width = lay.heads * HEAD_DIM
    got = lax.all_gather(piece, "dp", axis=0, tiled=False)
    columns = piece.shape[1] - LANES
    weights = got[:, :depth, :columns].reshape(D, columns)
    vectors = got[:, :12, columns : columns + depth].astype(f32)
    params = vectors[:, :8].transpose(1, 0, 2).reshape(8, D)
    params = jnp.concatenate([params, vectors[:, 8:].reshape(4, D), jnp.zeros((4, D), f32)], axis=0)
    own = lax.dynamic_slice_in_dim(params[:2], place * width, width, 1)
    query = own[0].reshape(lay.heads, HEAD_DIM)
    query = jnp.concatenate([query, jnp.zeros_like(query)], axis=1).reshape(-1)
    row = jnp.concatenate([query, own[1], jnp.zeros(weights.shape[1] - 3 * width, f32)])
    return weights, jnp.broadcast_to(row[None], (8, row.shape[0])), params


def reduce_heads(grads, vec, depth, width):
    total = lax.psum_scatter(grads, "dp", scatter_dimension=0, tiled=True).astype(f32)
    pairs = total[:, : 2 * width].reshape(depth, -1, 2, HEAD_DIM)
    small = lax.psum_scatter(vec, "dp", scatter_dimension=0, tiled=False)
    small = jnp.pad(small, ((0, 4), (0, LANES - depth)))
    return (
        pairs[:, :, 0].reshape(depth, width),
        pairs[:, :, 1].reshape(depth, width),
        total[:, 2 * width : 3 * width],
        small,
    )


def solution(mesh):
    placed = (
        P("dp", None),
        P("dp", None),
        P("dp", "mp"),
        P("dp", "mp"),
        P("dp", "mp"),
        P("mp", "dp"),
        P("dp", "mp"),
        P("mp", "dp"),
        P(None, "dp"),
        P(None, "dp"),
        P(None, "dp"),
        P("dp"),
        P(),
        P("dp"),
        P("mp", "dp"),
    )
    return jax.shard_map(
        on_device,
        mesh=mesh,
        in_specs=placed,
        out_specs=(
            P("dp", None),
            P("dp", None),
            P("dp", "mp"),
            P("dp", "mp"),
            P("dp", "mp"),
            P("mp", "dp"),
            P("dp", "mp"),
            P("mp", "dp"),
            P(None, "dp"),
            P(None, "dp"),
            P(None, "dp"),
            P("dp"),
        ),
        check_vma=False,
    )
```

```python
from functools import partial
import math

import jax
import jax.numpy as jnp
from jax import lax
from jax.experimental import pallas as pl
from jax.experimental.pallas import tpu as pltpu
from jax.sharding import PartitionSpec as P

D = 768
HEAD_DIM = 64
FF = 3072
CLUSTER = 128
LANES = 128
EPSILON = 1e-05
MASKED = -1e30
SCALE = 1.0 / math.sqrt(HEAD_DIM)

bf16 = jnp.bfloat16
f32 = jnp.float32
i32 = jnp.int32

VMEM = 60 * 1024 * 1024


def cost(us):
    return pl.CostEstimate(flops=int(1e9 * us), bytes_accessed=int(3e6 * us), transcendentals=0)


QUICK = cost(0.001)
ATTEND_US = 46
COLLECT_US = 30
COLLECT_ROWS = 512
SPREAD_US = 3
HEAD_GRADS_US = 4
SORT_US = 80
ATTEND_BACK_US = 40


def nn(a, b):
    return lax.dot_general(a, b, (((1,), (0,)), ((), ())), preferred_element_type=f32)


def nt(a, b):
    return lax.dot_general(a, b, (((1,), (1,)), ((), ())), preferred_element_type=f32)


def tn(a, b):
    return lax.dot_general(a, b, (((0,), (0,)), ((), ())), preferred_element_type=f32)


def lane_iota(rows, lanes=LANES):
    return lax.broadcasted_iota(i32, (rows, lanes), 1)


def sublane_iota(rows, lanes=LANES):
    return lax.broadcasted_iota(i32, (rows, lanes), 0)


def as_column(row):
    parts = [
        jnp.broadcast_to(row[:, i * LANES : (i + 1) * LANES], (LANES, LANES)).T
        for i in range(row.shape[1] // LANES)
    ]
    return parts[0] if len(parts) == 1 else jnp.concatenate(parts, axis=0)


def loop(count):
    def run(step):
        def body(i, carry):
            step(i)
            return carry

        lax.fori_loop(0, count, body, 0)

    return run


class Layout:
    def __init__(self, peers, tokens, heads):
        self.peers, self.tokens, self.heads = peers, tokens, heads
        self.stripe = min(16, peers)
        self.runs = peers // self.stripe
        self.per_dev = CLUSTER // self.stripe
        self.rows_peer = tokens // peers
        self.half_rows = self.rows_peer // 2
        self.pairs = self.half_rows // self.per_dev
        self.packed = tokens // 2
        self.clusters = peers * tokens // CLUSTER
        self.data_rows = 9 * self.half_rows
        self.direct = self.half_rows == LANES
        self.arrays = peers if self.direct else 1

    def peer(self, me, s):
        return (me ^ s) if self.direct else s

    def shapes(self, rows, dtype=bf16):
        lead = () if self.direct else (self.peers,)
        return [jax.ShapeDtypeStruct(lead + (rows, LANES), dtype)] * self.arrays

    def specs(self, rows, at):
        if self.direct:
            return [pl.BlockSpec((rows, LANES), lambda *g: (at(*g), 0))] * self.arrays
        return [pl.BlockSpec((self.peers, rows, LANES), lambda *g: (0, at(*g), 0))]

    def view(self, refs, s):
        return refs[s] if self.direct else refs[0].at[s]


def only(at):
    return lambda *g: at


def place_kernel(lay, perm_ref, code_ref):
    groups = lay.clusters
    shift = CLUSTER.bit_length() - 1
    blocks = lay.tokens // LANES
    before = sublane_iota(LANES, 2 * LANES)
    after = lane_iota(LANES, 2 * LANES)
    ahead_of = jnp.where((before < after) | (after >= LANES), 1.0, 0.0).astype(bf16)

    def members(h, b):
        row = lax.shift_right_logical(perm_ref[h : h + 1, b * LANES : (b + 1) * LANES], shift)
        return jnp.broadcast_to(row, (groups, LANES)) == sublane_iota(groups)

    for h in range(lay.heads):
        if lay.runs == 1:
            carry = (sublane_iota(groups) * lay.per_dev).astype(f32)
        else:
            counts = jnp.zeros((groups, LANES), f32)
            for b in range(blocks):
                member = jnp.where(members(h, b), 1.0, 0.0).astype(bf16)
                counts = counts + nn(member, ahead_of)[:, LANES:]
            lower = jnp.where(
                sublane_iota(groups, groups) > lane_iota(groups, groups), 1.0, 0.0
            ).astype(bf16)
            carry = nn(lower, counts.astype(bf16))
        for b in range(blocks):
            member = members(h, b)
            found = nn(jnp.where(member, 1.0, 0.0).astype(bf16), ahead_of)
            rank = jnp.sum(jnp.where(member, found[:, :LANES] + carry, 0.0), axis=0, keepdims=True)
            carry = carry + found[:, LANES:]
            rank = rank.astype(i32)
            peer = lax.shift_right_logical(rank, lay.rows_peer.bit_length() - 1)
            rest = rank & (lay.rows_peer - 1)
            half = lax.shift_right_logical(rest, lay.half_rows.bit_length() - 1)
            packed = peer * lay.half_rows + (rest & (lay.half_rows - 1))
            at = slice(b * LANES, (b + 1) * LANES)
            code_ref[h, 0:1, at] = packed
            code_ref[h, 1:2, at] = half


def place_tokens(lay, perm):
    return pl.pallas_call(
        partial(place_kernel, lay),
        out_shape=jax.ShapeDtypeStruct((lay.heads, 8, lay.tokens), i32),
        name="place_tokens",
        cost_estimate=QUICK,
    )(perm)


def one_hot(equal):
    return jnp.where(equal, 1.0, 0.0).astype(bf16)


def scatter_matrix(lay, me, packed, s, blocks):
    rows = blocks * lay.half_rows
    if lay.direct:
        parts = [
            one_hot(
                jnp.broadcast_to(packed, (lay.half_rows, lay.tokens))
                == sublane_iota(lay.half_rows, lay.tokens) + lay.peer(me, s + i) * lay.half_rows
            )
            for i in range(blocks)
        ]
        return jnp.concatenate(parts, axis=0)
    wanted = sublane_iota(rows, lay.tokens) + s * lay.half_rows
    return one_hot(jnp.broadcast_to(packed, (rows, lay.tokens)) == wanted)


def gather_matrix(lay, me, column):
    lane = lane_iota(column.shape[0])
    parts = [
        one_hot(column == lane + lay.peer(me, k) * LANES) for k in range(lay.packed // LANES)
    ]
    return jnp.concatenate(parts, axis=1)


def block_rows(lay, refs, first):
    at = slice(first, first + lay.half_rows)
    if lay.direct:
        return jnp.concatenate([refs[s][at, :] for s in range(lay.peers)], axis=0)
    return refs[0][:, at, :].astype(f32).reshape(lay.packed, LANES).astype(bf16)


def put_blocks(lay, refs, s, blocks, first, rows):
    at = slice(first, first + lay.half_rows) if isinstance(first, int) else pl.ds(first, lay.half_rows)
    if lay.direct:
        for i in range(blocks):
            refs[s + i][at, :] = rows[i * LANES : (i + 1) * LANES].astype(bf16)
    else:
        rows = rows.astype(f32).reshape(blocks, lay.half_rows, LANES).astype(bf16)
        refs[0][s : s + blocks, at, :] = rows


ROWS = 512
COUNT = 4


def project_kernel(lay, steps, place_ref, x_ref, w_ref, bias_ref, code_ref, pad_ref, *rest):
    outs = rest[: lay.arrays]
    rows_ref, flag_ref = rest[lay.arrays :]
    step = pl.program_id(0)
    me = place_ref[0]
    width = 4 * LANES

    @pl.when(step < steps)
    def _():
        at = pl.ds(pl.multiple_of(step * ROWS, ROWS), ROWS)
        values = nn(x_ref[...], w_ref[...]) + bias_ref[0:1, :]
        low = lane_iota(ROWS) < HEAD_DIM
        lane_half = jnp.where(low, 0, 1)
        live = as_column(pad_ref[0:1, at])
        tiles = [values[:, i * LANES : (i + 1) * LANES] for i in range(values.shape[1] // LANES)]
        turned = [pltpu.roll(tile, HEAD_DIM, 1) for tile in tiles]
        for h in range(lay.heads):
            half = as_column(code_ref[h, 1:2, at])
            keep = half == lane_half
            v, side = lay.heads + h // 2, h % 2
            planes = (
                jnp.where(low, tiles[h], turned[h]),
                jnp.where(low, turned[h], tiles[h]),
                jnp.where(low, tiles[v], turned[v]) if side == 0 else jnp.where(low, turned[v], tiles[v]),
            )
            for x, plane in enumerate(planes):
                rows_ref[h, at, x * LANES : (x + 1) * LANES] = jnp.where(keep, plane, 0.0).astype(bf16)
            flags = jnp.where((lane_iota(ROWS) == half) & (live == 1), 1.0, 0.0)
            rows_ref[h, at, 3 * LANES :] = flags.astype(bf16)

    count = COUNT if lay.direct else 32

    @pl.when(step >= steps)
    def _():
        h = step - steps
        for s in range(0, lay.peers, count):
            chosen = scatter_matrix(lay, me, code_ref[h, 0:1, :], s, count)
            moved = nn(chosen, rows_ref[h])
            for x in range(3):
                first = pl.multiple_of((h * 3 + x) * lay.half_rows, 16)
                put_blocks(lay, outs, s, count, first, moved[:, x * LANES : (x + 1) * LANES])
            for i in range(count * lay.half_rows // LANES):
                at = slice(s * lay.half_rows + i * LANES, s * lay.half_rows + (i + 1) * LANES)
                flag_ref[h, :, at] = moved[i * LANES : (i + 1) * LANES, 3 * LANES :].T[:8]

    @pl.when(step == steps + lay.heads - 1)
    def _():
        for s in range(lay.peers):
            at = slice(s * lay.half_rows, (s + 1) * lay.half_rows)
            rows = [flag_ref[k, 0:2, at] for k in range(lay.heads)]
            block = jnp.concatenate(rows + [jnp.zeros((16 - 2 * lay.heads, lay.half_rows), f32)], axis=0)
            if lay.half_rows < LANES:
                block = jnp.concatenate(
                    [block, jnp.zeros((16, LANES - lay.half_rows), f32)], axis=1
                )
            lay.view(outs, s)[lay.data_rows : lay.data_rows + 16, :] = block.astype(bf16)


def project_rows(lay, places, x, weights, bias, code, pad):
    width = weights.shape[1]
    steps = lay.tokens // ROWS
    spec = pltpu.PrefetchScalarGridSpec(
        num_scalar_prefetch=1,
        grid=(steps + lay.heads,),
        in_specs=[
            pl.BlockSpec((ROWS, D), lambda s, _: (jnp.minimum(s, steps - 1), 0)),
            pl.BlockSpec((D, width), lambda s, _: (0, 0)),
            pl.BlockSpec((8, width), lambda s, _: (0, 0)),
            pl.BlockSpec((lay.heads, 8, lay.tokens), lambda s, _: (0, 0, 0)),
            pl.BlockSpec((1, lay.tokens), lambda s, _: (0, 0)),
        ],
        out_specs=lay.specs(lay.data_rows + 16, only(0)),
        scratch_shapes=[
            pltpu.VMEM((lay.heads, lay.tokens, 4 * LANES), bf16),
            pltpu.VMEM((lay.heads, 8, lay.packed), f32),
        ],
    )
    return pl.pallas_call(
        partial(project_kernel, lay, steps),
        grid_spec=spec,
        out_shape=lay.shapes(lay.data_rows + 16),
        compiler_params=pltpu.CompilerParams(vmem_limit_bytes=VMEM),
        name="project_rows",
        cost_estimate=QUICK,
    )(places, x, weights, bias, code, pad)


def pair_rows(lay, refs, first, run, p):
    at = slice(first + p * lay.per_dev, first + (p + 1) * lay.per_dev)
    if lay.direct:
        return jnp.concatenate([refs[s][at, :] for s in range(lay.stripe)], axis=0)
    block = refs[0][run * lay.stripe : (run + 1) * lay.stripe, first : first + lay.half_rows, :]
    block = block.astype(f32)[:, p * lay.per_dev : (p + 1) * lay.per_dev, :]
    return block.reshape(CLUSTER, LANES).astype(bf16)


def put_pair(lay, refs, first, run, p, rows):
    at = slice(first + p * lay.per_dev, first + (p + 1) * lay.per_dev)
    for s in range(lay.stripe):
        part = rows[s * lay.per_dev : (s + 1) * lay.per_dev]
        lay.view(refs, run * lay.stripe + s)[at, :] = part.astype(bf16)


def live_columns(lay, flags, h):
    pick = one_hot(sublane_iota(16, 2 * LANES) == 2 * h + lane_iota(16, 2 * LANES) // LANES)
    return [tn(lay.view(flags, s)[...], pick) for s in range(lay.peers)]


def allowed_pair(lay, columns, run, p):
    at = slice(p * lay.per_dev, (p + 1) * lay.per_dev)
    live = jnp.concatenate([columns[run * lay.stripe + s][at] for s in range(lay.stripe)], axis=0)
    live = jnp.concatenate([live[:, :LANES], live[:, LANES:]], axis=0)
    same = sublane_iota(2 * CLUSTER) % CLUSTER == lane_iota(2 * CLUSTER)
    return (live > 0.5) | same


def stack_halves(rows):
    low = lane_iota(rows.shape[0], rows.shape[1]) < HEAD_DIM
    zero = jnp.zeros_like(rows)
    return jnp.concatenate([jnp.where(low, rows, zero), jnp.where(low, zero, rows)], axis=0)


def each_half(fold, rows):
    one, two = (
        jnp.broadcast_to(fold(part, axis=0, keepdims=True), part.shape)
        for part in (rows[:CLUSTER], rows[CLUSTER:])
    )
    return jnp.concatenate([one, two], axis=0)


def inverse_sum(rows, axis, keepdims):
    return 1.0 / jnp.sum(rows, axis=axis, keepdims=keepdims)


def soft_weights(queries, keys, allowed):
    scores = jnp.where(allowed, nt(keys, queries) * SCALE, MASKED)
    grown = jnp.exp(scores - each_half(jnp.max, scores))
    return grown * each_half(inverse_sum, grown)


def attend_kernel(lay, *refs):
    rows, flags, outs = (refs[i * lay.arrays : (i + 1) * lay.arrays] for i in range(3))
    live = live_columns(lay, flags, pl.program_id(0))
    for run in range(lay.runs):
        for p in range(lay.pairs):
            q, k, v = (pair_rows(lay, rows, x * lay.half_rows, run, p) for x in range(3))
            soft = soft_weights(q, stack_halves(k), allowed_pair(lay, live, run, p))
            put_pair(lay, outs, 0, run, p, tn(soft.astype(bf16), stack_halves(v)))


def attend(lay, arrived):
    head = lambda h: h
    return pl.pallas_call(
        partial(attend_kernel, lay),
        grid=(lay.heads,),
        in_specs=lay.specs(3 * lay.half_rows, head) + lay.specs(16, only(lay.data_rows // 16)),
        out_specs=lay.specs(lay.half_rows, head),
        out_shape=lay.shapes(lay.heads * lay.half_rows),
        name="attend",
        cost_estimate=cost(ATTEND_US),
    )(*arrived, *arrived)


def attend_back_kernel(lay, *refs):
    rows, flags, grads, outs = (refs[i * lay.arrays : (i + 1) * lay.arrays] for i in range(4))
    sum_ref = refs[-1]
    live = live_columns(lay, flags, pl.program_id(0))
    low = lane_iota(CLUSTER) < HEAD_DIM
    sums = [jnp.zeros((1, LANES), f32)] * 2
    for run in range(lay.runs):
        for p in range(lay.pairs):
            q, k, v = (pair_rows(lay, rows, x * lay.half_rows, run, p) for x in range(3))
            g = pair_rows(lay, grads, 0, run, p)
            keys = stack_halves(k)
            soft = soft_weights(q, keys, allowed_pair(lay, live, run, p))
            grad_soft = nt(stack_halves(v), g)
            delta = each_half(jnp.sum, soft * grad_soft)
            grad = (soft * (grad_soft - delta)).astype(bf16)
            grad_q = (tn(grad, keys) * SCALE).astype(bf16)
            part = nn(grad, q)
            grad_k = (jnp.where(low, part[:CLUSTER], part[CLUSTER:]) * SCALE).astype(bf16)
            part = nn(soft.astype(bf16), g)
            grad_v = jnp.where(low, part[:CLUSTER], part[CLUSTER:]).astype(bf16)
            for x, part in enumerate((grad_q, grad_k, grad_v)):
                put_pair(lay, outs, x * lay.half_rows, run, p, part)
            sums[0] = sums[0] + jnp.sum(grad_q.astype(f32), axis=0, keepdims=True)
            sums[1] = sums[1] + jnp.sum(grad_v.astype(f32), axis=0, keepdims=True)
    sum_ref[0] = jnp.concatenate(sums + [jnp.zeros((6, LANES), f32)], axis=0)


def attend_back(lay, arrived, grads):
    head = lambda h: h
    three = lay.specs(3 * lay.half_rows, head)
    out = pl.pallas_call(
        partial(attend_back_kernel, lay),
        grid=(lay.heads,),
        in_specs=three
        + lay.specs(16, only(lay.data_rows // 16))
        + lay.specs(lay.half_rows, head),
        out_specs=three + [pl.BlockSpec((1, 8, LANES), lambda h: (h, 0, 0))],
        out_shape=lay.shapes(lay.data_rows)
        + [jax.ShapeDtypeStruct((lay.heads, 8, LANES), f32)],
        name="attend_back",
        cost_estimate=cost(ATTEND_BACK_US),
    )(*arrived, *arrived, *grads)
    return list(out[:-1]), out[-1]


def side_rows(quarter, side):
    return pl.ds(pl.multiple_of(quarter * 512 + side * 256, 256), 256)


def unsort_kernel(lay, place_ref, *refs):
    rows_refs, code_ref, outs = refs[: lay.arrays], refs[lay.arrays], refs[lay.arrays + 1 :]
    rows = block_rows(lay, rows_refs, 0)
    low = lane_iota(256) < HEAD_DIM
    me, place = place_ref[0], place_ref[1]

    for t in range(4):
        sides = []
        for side in range(2):
            at = side_rows(place ^ t, side)
            column = as_column(code_ref[0, 0:1, at])
            half = as_column(code_ref[0, 1:2, at])
            found = nn(gather_matrix(lay, me, column), rows)
            sides.append(jnp.where(half == side, found, pltpu.roll(found, HEAD_DIM, 1)))
        outs[t][...] = jnp.where(low, sides[0], sides[1]).astype(bf16)


def unsort_rows(lay, places, returned, code):
    spec = pltpu.PrefetchScalarGridSpec(
        num_scalar_prefetch=1,
        grid=(lay.heads,),
        in_specs=lay.specs(lay.half_rows, lambda h, _: h)
        + [pl.BlockSpec((1, 8, lay.tokens), lambda h, _: (h, 0, 0))],
        out_specs=[pl.BlockSpec((256, LANES), lambda h, _: (0, h))] * 4,
    )
    return pl.pallas_call(
        partial(unsort_kernel, lay),
        grid_spec=spec,
        out_shape=[jax.ShapeDtypeStruct((256, lay.heads * LANES), bf16)] * 4,
        name="unsort_rows",
        cost_estimate=QUICK,
    )(places, *returned, code)


def sort_kernel(lay, place_ref, *refs):
    grads, code_ref, outs, rows_ref = refs[:4], refs[4], refs[5:-1], refs[-1]
    low = lane_iota(256) < HEAD_DIM
    lane_half = jnp.where(low, 0, 1)
    me, place = place_ref[0], place_ref[1]

    for t in range(4):
        block = grads[t][...].astype(f32)
        turned = pltpu.roll(block, HEAD_DIM, 1)
        for side in range(2):
            at = side_rows(place ^ t, side)
            half = as_column(code_ref[0, 1:2, at])
            both = jnp.where(low, block, turned) if side == 0 else jnp.where(low, turned, block)
            rows_ref[at, :] = jnp.where(half == lane_half, both, 0.0).astype(bf16)

    count = 4 if lay.direct else 32
    for s in range(0, lay.peers, count):
        chosen = scatter_matrix(lay, me, code_ref[0, 0:1, :], s, count)
        put_blocks(lay, outs, s, count, 0, nn(chosen, rows_ref[...]))


def sort_rows(lay, places, grads, code):
    spec = pltpu.PrefetchScalarGridSpec(
        num_scalar_prefetch=1,
        grid=(lay.heads,),
        in_specs=[pl.BlockSpec((256, LANES), lambda h, _: (0, h))] * 4
        + [pl.BlockSpec((1, 8, lay.tokens), lambda h, _: (h, 0, 0))],
        out_specs=lay.specs(lay.half_rows, lambda h, _: h),
        scratch_shapes=[pltpu.VMEM((lay.tokens, LANES), bf16)],
    )
    return pl.pallas_call(
        partial(sort_kernel, lay),
        grid_spec=spec,
        out_shape=lay.shapes(lay.heads * lay.half_rows),
        name="sort_rows",
        cost_estimate=cost(SORT_US),
    )(places, *grads, code)


def pack_kernel(
    query_ref, key_ref, value_ref, output_ref, inner_ref, outer_ref,
    bias_ref, gain_ref, shift_ref, inner_bias_ref, piece_ref, shard_ref,
):
    depth, width = query_ref.shape
    heads = width // HEAD_DIM
    query, key, value = (ref[...].astype(f32) for ref in (query_ref, key_ref, value_ref))
    cut = [slice(h * HEAD_DIM, (h + 1) * HEAD_DIM) for h in range(heads)]
    columns = [part for at in cut for part in (query[:, at], key[:, at])] + [value]
    have = 3 * width
    fill = -have % LANES
    if fill:
        columns.append(jnp.zeros((depth, fill), f32))
    columns = jnp.concatenate(columns, axis=1).astype(bf16)
    piece_ref[:depth, : have + fill] = columns
    inner_bias = inner_bias_ref[...].astype(f32)
    vectors = jnp.concatenate(
        [ref[...].astype(f32) for ref in (bias_ref, gain_ref, shift_ref)]
        + [inner_bias[:, i * depth : (i + 1) * depth] for i in range(4)]
        + [jnp.zeros((4, depth), f32)],
        axis=0,
    )
    if depth < LANES:
        vectors = jnp.concatenate([vectors, jnp.zeros((16, LANES - depth), f32)], axis=1)
    piece_ref[:16, have + fill :] = vectors.astype(bf16)
    shard_ref[:, :D] = inner_ref[...]
    turned = output_ref[...].astype(f32).T
    shard_ref[:, D : 2 * D] = outer_ref[...]
    fill = -width % (2 * LANES)
    if fill:
        turned = jnp.concatenate([turned, jnp.zeros((depth, fill), f32)], axis=1)
    shard_ref[:, 2 * D :] = turned.astype(bf16)


def pack_weights(*arrays):
    depth, width = arrays[0].shape
    columns = -(-3 * width // LANES) * LANES
    return pl.pallas_call(
        pack_kernel,
        out_shape=[
            jax.ShapeDtypeStruct((max(depth, 16), columns + LANES), bf16),
            jax.ShapeDtypeStruct((depth, 2 * D + width + -width % (2 * LANES)), bf16),
        ],
        name="pack_weights",
        cost_estimate=QUICK,
    )(*arrays)


def assemble_kernel(lay, place_ref, *refs):
    pieces, (weight_ref, bias_ref, par_ref, part_ref) = refs[: lay.peers], refs[lay.peers :]
    me, place = place_ref[0], place_ref[1]
    depth = D // lay.peers
    for s in range(lay.peers):
        d = me ^ s
        at = pl.ds(pl.multiple_of(d * depth, 16), depth)
        columns = weight_ref.shape[1]
        weight_ref[at, :] = pieces[s][:, :columns]
        part_ref[d] = pieces[s][:16, columns:].astype(f32)

    def whole(row, rows=1, peers=range(lay.peers)):
        return jnp.concatenate(
            [part_ref[d, row + i : row + i + 1, :depth] for d in peers for i in range(rows)], axis=1
        )

    vectors = [whole(r) for r in range(8)]
    each = lay.peers // 4
    vectors += [whole(8, 4, range(j * each, (j + 1) * each)) for j in range(4)]
    par_ref[...] = jnp.concatenate(vectors + [jnp.zeros((4, D), f32)], axis=0)
    width = lay.heads * HEAD_DIM

    def own(vector):
        out = vector[:, :width]
        for p in range(1, D // width):
            out = jnp.where(place == p, vector[:, p * width : (p + 1) * width], out)
        return out

    query = own(vectors[0])
    zero = jnp.zeros((1, HEAD_DIM), f32)
    columns = [
        part for h in range(lay.heads) for part in (query[:, h * HEAD_DIM : (h + 1) * HEAD_DIM], zero)
    ] + [own(vectors[1])]
    fill = bias_ref.shape[1] - 3 * width
    if fill:
        columns.append(jnp.zeros((1, fill), f32))
    bias_ref[...] = jnp.broadcast_to(jnp.concatenate(columns, axis=1), bias_ref.shape)


def assemble_weights(lay, places, pieces):
    columns = pieces[0].shape[1] - LANES
    vmem = pl.BlockSpec(memory_space=pltpu.VMEM)
    return pl.pallas_call(
        partial(assemble_kernel, lay),
        in_specs=[pl.BlockSpec(memory_space=pltpu.SMEM)] + [vmem] * lay.peers,
        out_specs=[vmem] * 3,
        out_shape=[
            jax.ShapeDtypeStruct((D, columns), bf16),
            jax.ShapeDtypeStruct((8, columns), f32),
            jax.ShapeDtypeStruct((16, D), f32),
        ],
        scratch_shapes=[pltpu.VMEM((lay.peers, 16, LANES), f32)],
        name="assemble_weights",
        cost_estimate=QUICK,
    )(places, *pieces)


def mean_rows(v):
    return jnp.sum(v, axis=1, keepdims=True) * (1.0 / D)


def norm_forward(rows):
    centred = rows - mean_rows(rows)
    inv = lax.rsqrt(mean_rows(centred * centred) + EPSILON)
    return centred * inv, inv


def norm_backward(scaled, normed, inv):
    return inv * (scaled - mean_rows(scaled) - normed * mean_rows(scaled * normed))


TALL = 512


def middle_kernel(
    place_ref,
    att0,
    att1,
    att2,
    att3,
    hidden_ref,
    cot_ref,
    par_ref,
    w0,
    w1,
    w2,
    w3,
    out_ref,
    act_ref,
    pre_ref,
    low_ref,
    ffn_grad_ref,
    branch_grad_ref,
    h1_ref,
    grad0,
    grad1,
    grad2,
    grad3,
    vec_ref,
    first_ref,
    normed_ref,
    inv_ref,
    slope_ref,
    sum_ref,
    h2_ref,
    weight_ref,
    double_ref,
    sems,
):
    step = pl.program_id(0)
    place = place_ref[1]

    def fetch(t, part):
        at = (pl.ds(2 * D, weight_ref.shape[2] - 2 * D), pl.ds(0, 2 * D))[part]
        source = (w0, w1, w2, w3)[t]
        return pltpu.make_async_copy(source.at[:, at], weight_ref.at[t, :, at], sems.at[part, t])

    for t in range(4):

        @pl.when(step == t + 1)
        def _():
            fetch(t, 1).wait()

    @pl.when(step == 0)
    def _():
        for t in range(4):
            fetch(t, 0).start()
        for t in range(4):
            fetch(t, 1).start()
        for t in range(4):
            fetch(t, 0).wait()

        @loop(4)
        def _(t):
            low = lane_iota(D) < HEAD_DIM
            for k in range(double_ref.shape[2] // LANES):
                tile = weight_ref[t, :, 2 * D + k // 2 * LANES : 2 * D + (k // 2 + 1) * LANES]
                tile = tile.astype(f32)
                turned = pltpu.roll(tile, HEAD_DIM, 1)
                both = jnp.where(low, tile, turned) if k % 2 == 0 else jnp.where(low, turned, tile)
                double_ref[t, :, k * LANES : (k + 1) * LANES] = both.astype(bf16)

        vec_ref[...] = jnp.zeros_like(vec_ref)

        @loop(2)
        def _(side):
            branch = jnp.zeros((256, D), f32)
            for t, att_ref in enumerate((att0, att1, att2, att3)):
                att = att_ref[...]
                lane = lane_iota(256, att.shape[1]) % LANES
                own = (lane >= HEAD_DIM).astype(i32) == side
                branch = branch + nt(jnp.where(own, att, jnp.zeros_like(att)), double_ref[t])
            at = pl.ds(pl.multiple_of(side * 256, 256), 256)
            rows = hidden_ref[at, :].astype(f32) + (branch + par_ref[2:3, :])
            normed, inv = norm_forward(rows)
            first = normed * par_ref[4:5, :] + par_ref[6:7, :]
            first_ref[at, :] = first
            normed_ref[at, :] = normed
            inv_ref[at, :] = jnp.broadcast_to(inv, (256, LANES))
            low_ref[at, :] = first.astype(bf16)

        sum_ref[...] = jnp.zeros_like(sum_ref)

    @pl.when((step >= 1) & (step <= 4))
    def _():
        j = step - 1

        @loop(512 // TALL)
        def _(side):
            at = pl.ds(pl.multiple_of(side * TALL, TALL), TALL)
            pre = nn(low_ref[at, :], weight_ref[j, :, :D]) + par_ref[pl.ds(8 + (place ^ j), 1), :]
            cdf = 0.5 * (1.0 + lax.erf(pre * (1.0 / math.sqrt(2.0))))
            slope_ref[j, at, :] = cdf + pre * jnp.exp(-0.5 * pre * pre) * (1.0 / math.sqrt(2.0 * math.pi))
            act = (pre * cdf).astype(bf16)
            act_ref[at, :] = act
            sum_ref[at, :] += nt(act, weight_ref[j, :, D : 2 * D])

    @pl.when(step == 4)
    def _():

        @loop(4)
        def _(side):
            at = pl.ds(pl.multiple_of(side * 128, 128), 128)
            rows = first_ref[at, :] + (sum_ref[at, :] + par_ref[3:4, :])
            normed, inv = norm_forward(rows)
            out_ref[at, :] = (normed * par_ref[5:6, :] + par_ref[7:8, :]).astype(bf16)
            cot = cot_ref[at, :].astype(f32)
            grad = norm_backward(cot * par_ref[5:6, :], normed, inv)
            grad_low = grad.astype(bf16)
            h2_ref[at, :] = grad
            ffn_grad_ref[at, :] = grad_low
            vec_ref[3:4, :] += jnp.sum(grad_low.astype(f32), axis=0, keepdims=True)
            vec_ref[5:6, :] += jnp.sum(cot * normed, axis=0, keepdims=True)
            vec_ref[7:8, :] += jnp.sum(cot, axis=0, keepdims=True)

        sum_ref[...] = jnp.zeros_like(sum_ref)

    @pl.when(step >= 5)
    def _():
        j = 8 - step
        vec_ref[pl.ds(8 + (place ^ j), 1), :] = jnp.zeros((1, D), f32)

        @loop(512 // TALL)
        def _(side):
            at = pl.ds(pl.multiple_of(side * TALL, TALL), TALL)
            grad_act = nn(ffn_grad_ref[at, :], weight_ref[j, :, D : 2 * D])
            grad_pre = (grad_act * slope_ref[j, at, :]).astype(bf16)
            pre_ref[at, :] = grad_pre
            vec_ref[pl.ds(8 + (place ^ j), 1), :] += jnp.sum(grad_pre.astype(f32), axis=0, keepdims=True)
            sum_ref[at, :] += nt(grad_pre, weight_ref[j, :, :D])

    @pl.when(step == 8)
    def _():

        @loop(4)
        def _(side):
            at = pl.ds(pl.multiple_of(side * 128, 128), 128)
            grad_first = h2_ref[at, :] + sum_ref[at, :]
            normed = normed_ref[at, :]
            grad = norm_backward(grad_first * par_ref[4:5, :], normed, inv_ref[at, 0:1])
            grad_low = grad.astype(bf16)
            h1_ref[at, :] = grad
            branch_grad_ref[at, :] = grad_low
            vec_ref[2:3, :] += jnp.sum(grad_low.astype(f32), axis=0, keepdims=True)
            vec_ref[4:5, :] += jnp.sum(grad_first * normed, axis=0, keepdims=True)
            vec_ref[6:7, :] += jnp.sum(grad_first, axis=0, keepdims=True)

        for t, grad_ref in enumerate((grad0, grad1, grad2, grad3)):
            both = nn(branch_grad_ref[...], double_ref[t])
            lane = lane_iota(256, both.shape[1]) % LANES
            grad_ref[...] = jnp.where(lane < HEAD_DIM, both[:256], both[256:]).astype(bf16)


def middle(places, att, hidden, cotangent, params, weights):
    width = att[0].shape[1]
    rows = 512

    def up(s, q):
        return (0, jnp.clip(s - 1, 0, 3))

    def down(s, q):
        return (0, jnp.clip(8 - s, 0, 3))

    def whole(rank):
        return lambda s, q: (0,) * rank

    square = pl.BlockSpec((rows, D), whole(2))
    exchanged = pl.BlockSpec((256, width), whole(2))
    spec = pltpu.PrefetchScalarGridSpec(
        num_scalar_prefetch=1,
        grid=(9,),
        in_specs=[exchanged] * 4
        + [
            pl.BlockSpec((rows, D), lambda s, q: (q[1], 0)),
            pl.BlockSpec((rows, D), lambda s, q: (q[1], 0)),
            pl.BlockSpec((16, D), whole(2)),
        ]
        + [pl.BlockSpec(memory_space=pl.ANY)] * 4,
        out_specs=[
            square,
            pl.BlockSpec((rows, D), up),
            pl.BlockSpec((rows, D), down),
            square,
            square,
            square,
            square,
        ]
        + [exchanged] * 4
        + [pl.BlockSpec((16, D), whole(2))],
        scratch_shapes=[
            pltpu.VMEM((rows, D), f32),
            pltpu.VMEM((rows, D), f32),
            pltpu.VMEM((rows, LANES), f32),
            pltpu.VMEM((4, rows, D), f32),
            pltpu.VMEM((rows, D), f32),
            pltpu.VMEM((rows, D), f32),
            pltpu.VMEM((4,) + weights[0].shape, bf16),
            pltpu.VMEM((4, D, width), bf16),
            pltpu.SemaphoreType.DMA((2, 4)),
        ],
    )
    out = pl.pallas_call(
        middle_kernel,
        grid_spec=spec,
        out_shape=[
            jax.ShapeDtypeStruct((rows, D), bf16),
            jax.ShapeDtypeStruct((rows, FF), bf16),
            jax.ShapeDtypeStruct((rows, FF), bf16),
            jax.ShapeDtypeStruct((rows, D), bf16),
            jax.ShapeDtypeStruct((rows, D), bf16),
            jax.ShapeDtypeStruct((rows, D), bf16),
            jax.ShapeDtypeStruct((rows, D), f32),
        ]
        + [jax.ShapeDtypeStruct((256, width), bf16)] * 4
        + [jax.ShapeDtypeStruct((16, D), f32)],
        compiler_params=pltpu.CompilerParams(vmem_limit_bytes=VMEM),
        name="middle",
        cost_estimate=QUICK,
    )(places, *att, hidden, cotangent, params, *weights)
    return out[:7], out[7:11], out[11]


def weight_grad_kernel(chunks, adds, place_ref, act_ref, pre_ref, low_ref, ffn_ref, branch_ref, *refs):
    att_refs, add_refs, out_ref = refs[:chunks], refs[chunks : chunks + adds], refs[-1]

    def put(at, part):
        for ref in add_refs:
            part = part + ref[:, at].astype(f32)
        out_ref[:, at] = part.astype(bf16)

    put(slice(0, D), tn(low_ref[...], pre_ref[...]))
    put(slice(D, 2 * D), tn(ffn_ref[...], act_ref[...]))
    for i in range(chunks):

        @pl.when(pl.program_id(0) == i)
        def _():
            att = att_refs[i][...]
            low = lane_iota(256, att.shape[1]) % LANES < HEAD_DIM
            zero = jnp.zeros_like(att)
            both = jnp.concatenate([jnp.where(low, att, zero), jnp.where(low, zero, att)], axis=0)
            part = tn(branch_ref[...], both)
            planes = [part[:, k * LANES : (k + 1) * LANES] for k in range(part.shape[1] // LANES)]
            planes = [plane + pltpu.roll(plane, HEAD_DIM, 1) for plane in planes]
            if len(planes) % 2:
                planes.append(jnp.zeros_like(planes[0]))
            first = lane_iota(part.shape[0]) < HEAD_DIM
            for k in range(0, len(planes), 2):
                at = slice(2 * D + k // 2 * LANES, 2 * D + (k // 2 + 1) * LANES)
                put(at, jnp.where(first, planes[k], planes[k + 1]))


def weight_grads(places, saved, att, first, chunks, adds):
    act, pre, low, ffn_grad, branch_grad = saved
    rows = act.shape[0]
    width = att[0].shape[1]
    total = 2 * D + -(-width // (2 * LANES)) * LANES
    cut = D // 2

    def chunk(s, i, q):
        return (0, first - 2 * s)

    part = pl.BlockSpec((rows, cut), lambda s, i, q: (0, i))
    spec = pltpu.PrefetchScalarGridSpec(
        num_scalar_prefetch=1,
        grid=(chunks, 2),
        in_specs=[pl.BlockSpec((rows, D), chunk)] * 2
        + [part] * 3
        + [pl.BlockSpec((256, width), lambda s, i, q: (0, 0))] * chunks
        + [pl.BlockSpec((cut, total), lambda s, i, q, k=k: (2 * k + i, 0)) for _, k in adds],
        out_specs=pl.BlockSpec((cut, total), lambda s, i, q: (2 * s + i, 0)),
    )
    return pl.pallas_call(
        partial(weight_grad_kernel, chunks, len(adds)),
        grid_spec=spec,
        out_shape=jax.ShapeDtypeStruct((chunks * D, total), bf16),
        compiler_params=pltpu.CompilerParams(vmem_limit_bytes=VMEM),
        name="weight_grads",
        cost_estimate=QUICK,
    )(
        places, act, pre, low, ffn_grad, branch_grad,
        *[att[first - 2 * s] for s in range(chunks)], *[a for a, _ in adds],
    )


def collect_kernel(lay, place_ref, *refs):
    rows_refs = refs[: lay.arrays]
    code_ref, dense_ref = refs[lay.arrays :]
    me = place_ref[0]
    tokens = dense_ref.shape[0]
    low = lane_iota(tokens) < HEAD_DIM
    firsts, seconds = [], []
    for h in range(lay.heads):
        column = as_column(code_ref[h, 0:1, :])
        half = as_column(code_ref[h, 1:2, :])
        planes = [block_rows(lay, rows_refs, (h * 3 + x) * lay.half_rows) for x in range(3)]
        found = nn(gather_matrix(lay, me, column), jnp.concatenate(planes, axis=1))
        one, two = [], []
        for x in range(3):
            part = found[:, x * LANES : (x + 1) * LANES]
            turned = pltpu.roll(part, HEAD_DIM, 1)
            one.append(jnp.where(half == 0, part, turned))
            two.append(jnp.where(half == 1, part, turned))
        firsts.append(one)
        seconds.append(two)
    tiles = [jnp.where(low, firsts[h][0], seconds[h][1]) for h in range(lay.heads)]
    for h in range(0, lay.heads, 2):
        right = seconds[h + 1][2] if h + 1 < lay.heads else jnp.zeros((tokens, LANES), f32)
        tiles.append(jnp.where(low, firsts[h][2], right))
    dense_ref[...] = jnp.concatenate(tiles, axis=1).astype(bf16)


def collect(lay, places, returned, code, width):
    tokens = COLLECT_ROWS
    spec = pltpu.PrefetchScalarGridSpec(
        num_scalar_prefetch=1,
        grid=(lay.tokens // tokens,),
        in_specs=lay.specs(lay.data_rows, only(0))
        + [pl.BlockSpec((lay.heads, 8, tokens), lambda c, q: (0, 0, c))],
        out_specs=pl.BlockSpec((tokens, width), lambda c, q: (c, 0)),
    )
    return pl.pallas_call(
        partial(collect_kernel, lay),
        grid_spec=spec,
        out_shape=jax.ShapeDtypeStruct((lay.tokens, width), bf16),
        compiler_params=pltpu.CompilerParams(vmem_limit_bytes=VMEM),
        name="collect",
        cost_estimate=cost(COLLECT_US),
    )(places, *returned, code)


def half_rows_at(g, s, place):
    core = place % 2
    return jnp.where(s == 0, 1 - core, core) * 2 + g


def spread_kernel(g, place_ref, dense_ref, w_ref, h1_ref, other_ref, mine_ref):
    step, place = pl.program_id(0), place_ref[1]
    own = (half_rows_at(g, step, place) == place).astype(f32)
    part = nt(dense_ref[...], w_ref[...]) + own * h1_ref[...]

    @pl.when(step == 0)
    def _():
        other_ref[...] = part.astype(bf16)

    @pl.when(step == 1)
    def _():
        mine_ref[...] = part.astype(bf16)


def spread_grads(g, places, dense, weights, grad_h1):
    width = weights.shape[1]
    whole = lambda s, q: (0, 0)
    spec = pltpu.PrefetchScalarGridSpec(
        num_scalar_prefetch=1,
        grid=(2,),
        in_specs=[
            pl.BlockSpec((512, width), lambda s, q: (half_rows_at(g, s, q[1]), 0)),
            pl.BlockSpec((D, width), whole),
            pl.BlockSpec((512, D), whole),
        ],
        out_specs=[pl.BlockSpec((512, D), whole)] * 2,
    )
    return pl.pallas_call(
        partial(spread_kernel, g),
        grid_spec=spec,
        out_shape=[jax.ShapeDtypeStruct((512, D), bf16)] * 2,
        compiler_params=pltpu.CompilerParams(vmem_limit_bytes=VMEM),
        name="spread_grads",
        cost_estimate=cost(SPREAD_US),
    )(places, dense, weights, grad_h1)


def head_grad_kernel(lay, place_ref, x_ref, dense_ref, vec_ref, *refs):
    out_ref, total_ref = refs
    step = pl.program_id(0)

    @pl.when(step == 0)
    def _():
        total_ref[...] = tn(x_ref[...], dense_ref[...])

    @pl.when(step > 0)
    def _():
        total_ref[...] += tn(x_ref[...], dense_ref[...])

    @pl.when(step == 3)
    def _():
        depth = D // lay.peers
        if not lay.direct:
            out_ref[...] = total_ref[...].astype(bf16)
            return
        for d in range(lay.peers):
            out_ref[d, :depth, :] = total_ref[d * depth : (d + 1) * depth, :].astype(bf16)
            vector = vec_ref[d]
            high = vector.astype(bf16).astype(f32)
            width = total_ref.shape[1]
            out_ref[d, depth:, :] = jnp.concatenate(
                [high, vector - high, jnp.zeros((16, width - 2 * LANES), f32)], axis=1
            ).astype(bf16)


def head_grads(lay, places, x, dense, vec):
    width = dense.shape[1]
    depth = D // lay.peers
    shape = (lay.peers, depth + 16, width) if lay.direct else (D, width)
    spec = pltpu.PrefetchScalarGridSpec(
        num_scalar_prefetch=1,
        grid=(4,),
        in_specs=[
            pl.BlockSpec((512, D), lambda s, q: (s, 0)),
            pl.BlockSpec((512, width), lambda s, q: (s, 0)),
            pl.BlockSpec(vec.shape, lambda s, q: (0, 0, 0)),
        ],
        out_specs=pl.BlockSpec(shape, lambda s, q: (0,) * len(shape)),
        scratch_shapes=[pltpu.VMEM((D, width), f32)],
    )
    return pl.pallas_call(
        partial(head_grad_kernel, lay),
        grid_spec=spec,
        out_shape=jax.ShapeDtypeStruct(shape, bf16),
        compiler_params=pltpu.CompilerParams(vmem_limit_bytes=VMEM),
        name="head_grads",
        cost_estimate=cost(HEAD_GRADS_US),
    )(places, x, dense, vec)


def finish_heads_kernel(*refs):
    parts, outs = refs[0], refs[1:]
    depth, width = outs[0].shape
    heads = width // HEAD_DIM
    total = parts[0].astype(f32)
    for d in range(1, parts.shape[0]):
        total = total + parts[d].astype(f32)
    grads = total[:depth]
    cut = [slice(h * LANES, h * LANES + HEAD_DIM) for h in range(heads)]
    outs[0][...] = jnp.concatenate([grads[:, at] for at in cut], axis=1)
    cut = [slice(h * LANES + HEAD_DIM, (h + 1) * LANES) for h in range(heads)]
    outs[1][...] = jnp.concatenate([grads[:, at] for at in cut], axis=1)
    outs[2][...] = grads[:, 2 * width : 3 * width]
    outs[3][...] = total[depth:, :LANES] + total[depth:, LANES : 2 * LANES]


def finish_heads(parts, depth, width):
    shapes = [(depth, width)] * 3 + [(16, LANES)]
    return pl.pallas_call(
        finish_heads_kernel,
        out_shape=[jax.ShapeDtypeStruct(s, f32) for s in shapes],
        name="finish_heads",
        cost_estimate=QUICK,
    )(parts)


def finish_vectors_kernel(depth, own_ref, other_ref, bias_ref, gain_ref, shift_ref, inner_ref):
    total = (own_ref[...] + other_ref[...])[:, :depth]
    bias_ref[...] = total[:4]
    gain_ref[...] = total[4:6]
    shift_ref[...] = total[6:8]
    inner_ref[...] = total[8:12]


def finish_vectors(own, other, depth):
    return pl.pallas_call(
        partial(finish_vectors_kernel, depth),
        out_shape=[jax.ShapeDtypeStruct((n, depth), f32) for n in (4, 2, 2, 4)],
        name="finish_vectors",
        cost_estimate=QUICK,
    )(own, other)


def finish_middle_kernel(grad_ref, inner_ref, outer_ref, output_ref):
    inner_ref[...] = grad_ref[:, :D].astype(f32)
    outer_ref[...] = grad_ref[:, D : 2 * D].astype(f32)
    rest = grad_ref[:, 2 * D :].astype(f32)
    output_ref[...] = rest[:, : output_ref.shape[0]].T


def finish_middle(grads, width):
    depth = grads.shape[0]
    return pl.pallas_call(
        finish_middle_kernel,
        out_shape=[
            jax.ShapeDtypeStruct((depth, D), f32),
            jax.ShapeDtypeStruct((depth, D), f32),
            jax.ShapeDtypeStruct((width, depth), f32),
        ],
        name="finish_middle",
        cost_estimate=QUICK,
    )(grads)


def order_kernel(place_ref, *refs):
    parts, out_ref, rows_ref, sems = refs[:4], refs[4], refs[5], refs[6]
    rows = rows_ref.shape[1]

    def take(i):
        return pltpu.make_async_copy(parts[i], rows_ref.at[i], sems.at[0, i])

    def put(i):
        at = pl.ds(pl.multiple_of(place_ref[i] * rows, rows), rows)
        return pltpu.make_async_copy(rows_ref.at[i], out_ref.at[at, :], sems.at[1, i])

    for i in range(4):
        take(i).start()
    for i in range(4):
        take(i).wait()
        put(i).start()
    for i in range(4):
        put(i).wait()


def order_quarters(order, quarters):
    rows, width = quarters[0].shape
    dtype = quarters[0].dtype
    return pl.pallas_call(
        order_kernel,
        in_specs=[pl.BlockSpec(memory_space=pltpu.SMEM)]
        + [pl.BlockSpec(memory_space=pl.ANY)] * 4,
        out_specs=pl.BlockSpec(memory_space=pl.ANY),
        out_shape=jax.ShapeDtypeStruct((4 * rows, width), dtype),
        scratch_shapes=[pltpu.VMEM((4, rows, width), dtype), pltpu.SemaphoreType.DMA((2, 4))],
        name="order_quarters",
        cost_estimate=QUICK,
    )(order, *quarters)


def over_rows(lay, blocks, near_first=False):
    if not lay.direct:
        return [lax.all_to_all(blocks[0], "dp", split_axis=0, concat_axis=0, tiled=True)]
    out = [blocks[0]]
    for s in range(1, lay.peers):
        rows = blocks[s]
        if near_first and s >= lay.peers - 2:
            rows = after(rows, out[s - lay.peers + 3])
        out.append(lax.ppermute(rows, "dp", [(i, i ^ s) for i in range(lay.peers)]))
    return out


def in_hbm(rows):
    return pltpu.with_memory_space_constraint(rows, pltpu.HBM)


def share_pieces(lay, piece):
    def flip(rows, s):
        return lax.ppermute(rows, "dp", [(i, i ^ s) for i in range(lay.peers)])

    half = lay.peers // 2
    far = flip(piece, half)
    near = [piece] + [flip(piece, s) for s in range(1, half)]
    return near + [far] + [flip(far, s) for s in range(1, half)]


def after(value, *others):
    return lax.optimization_barrier((value, *others))[0]


def swap(rows, flip):
    return lax.ppermute(rows, "mp", [(i, i ^ flip) for i in range(4)])


def over_heads(blocks):
    return [blocks[0]] + [swap(blocks[t], t) for t in range(1, 4)]


def on_device(
    hidden_in,
    cotangent,
    w_query,
    w_key,
    w_value,
    w_output,
    w_inner,
    w_outer,
    biases,
    gains,
    shifts,
    inner_bias,
    lengths,
    padding,
    cluster_perm,
):
    peers = lax.axis_size("dp")
    tokens = hidden_in.shape[0]
    heads = cluster_perm.shape[0]
    lay = Layout(peers, tokens, heads)
    place = lax.axis_index("mp")
    me = lax.axis_index("dp")
    places = jnp.stack([me, place]).astype(i32)
    hidden_in = in_hbm(hidden_in)
    depth = w_query.shape[0]
    width = heads * HEAD_DIM

    piece, shard = pack_weights(
        w_query, w_key, w_value, w_output, w_inner, w_outer.T,
        biases, gains, shifts, inner_bias.reshape(1, -1),
    )
    own_w = lax.all_gather(shard, "dp", axis=0, tiled=True)
    far_w = swap(own_w, 2)
    if lay.direct:
        weights, bias, params = assemble_weights(lay, places, share_pieces(lay, piece))
    else:
        weights, bias, params = gather_weights(lay, place, piece)

    weights = in_hbm(weights)
    code = in_hbm(place_tokens(lay, cluster_perm))
    sent = project_rows(lay, places, hidden_in, weights, bias, code, padding.reshape(1, tokens))
    arrived = over_rows(lay, sent, near_first=True)
    mixed = over_rows(lay, attend(lay, arrived))
    found = unsort_rows(lay, places, mixed, code)
    att = over_heads(found)
    far_w = after(far_w, found[0])
    middle_w = [own_w, in_hbm(swap(own_w, 1)), far_w, in_hbm(swap(far_w, 1))]
    saved, att_grad, vec = middle(places, att, hidden_in, cotangent, params, middle_w)
    out_quarter, act, pre_grad, first_low, ffn_grad, branch_grad, grad_h1 = saved
    saved = tuple(in_hbm(a) for a in (act, pre_grad, first_low, ffn_grad, branch_grad))
    att = [in_hbm(a) for a in att]

    got = over_heads(att_grad)
    from_core = swap(weight_grads(places, saved, att, 3, 2, []), 1)
    grads = sort_rows(lay, places, got, code)
    ready = (after(act, grads[0]),) + saved[1:]
    from_far = swap(weight_grads(places, ready, att, 2, 1, [(from_core, 0)]), 2)
    grads = over_rows(lay, grads)
    slot_grads, bias_sums = attend_back(lay, arrived, grads)

    returned = over_rows(lay, slot_grads)
    ready = (after(act, *returned[1:4]),) + saved[1:]
    summed = weight_grads(places, ready, att, 0, 1, [(from_core, 1), (from_far, 0)])
    head_sums = bias_sums[:, :2].reshape(heads, 2, 2, HEAD_DIM).sum(axis=2)
    head_sums = head_sums.transpose(1, 0, 2).reshape(2, width)
    vec = lax.dynamic_update_slice(vec[:12], head_sums, (0, place * width))
    vec = jnp.concatenate(
        [vec[:8].reshape(8, peers, depth).transpose(1, 0, 2), vec[8:].reshape(peers, 4, depth)],
        axis=1,
    )
    spread = jnp.pad(vec, ((0, 0), (0, 4), (0, (-depth) % LANES)))
    reduced = lax.psum_scatter(after(summed, *returned), "dp", scatter_dimension=0, tiled=True)
    far = swap(after(out_quarter, summed), 2)
    dense = collect(lay, places, returned, code, weights.shape[1])
    terms = head_grads(lay, places, hidden_in, dense, spread)
    dense = after(dense, terms, far)
    groups = [spread_grads(g, places, dense, weights, grad_h1) for g in range(2)]
    chips = [
        (mine.astype(f32) + swap(other, 1).astype(f32)).astype(bf16) for other, mine in groups
    ]
    others = [swap(chip, 2) for chip in chips]
    hidden_out = order_quarters(
        jnp.stack([place, place ^ 2, place ^ 1, place ^ 3]).astype(i32),
        [out_quarter, far, swap(out_quarter, 1), swap(far, 1)],
    )
    if lay.direct:
        terms = lax.all_to_all(terms, "dp", split_axis=0, concat_axis=0, tiled=True)
        ends = finish_heads(terms, depth, width)
    else:
        ends = reduce_heads(terms, vec, depth, width)
    small = ends[3] + swap(ends[3], 1)
    chips[1] = after(chips[1], small, hidden_out)
    small = finish_vectors(small, swap(small, 2), depth)
    ready = [
        (chip.astype(f32) + part.astype(f32)).astype(bf16) for chip, part in zip(chips, others)
    ]
    core = place % 2
    order = jnp.stack([2 * core, 2 * core + 1, 2 - 2 * core, 3 - 2 * core]).astype(i32)
    grad_hidden = order_quarters(
        after(order, small[0]),
        ready + [swap(part, 1) for part in ready],
    )

    grad_inner, grad_outer, grad_output = finish_middle(reduced, width)
    return (
        hidden_out,
        grad_hidden,
        ends[0],
        ends[1],
        ends[2],
        grad_output,
        grad_inner,
        grad_outer.T,
        small[0],
        small[1],
        small[2],
        small[3].reshape(-1),
    )


def gather_weights(lay, place, piece):
    depth = D // lay.peers
    width = lay.heads * HEAD_DIM
    got = lax.all_gather(piece, "dp", axis=0, tiled=False)
    columns = piece.shape[1] - LANES
    weights = got[:, :depth, :columns].reshape(D, columns)
    vectors = got[:, :12, columns : columns + depth].astype(f32)
    params = vectors[:, :8].transpose(1, 0, 2).reshape(8, D)
    params = jnp.concatenate([params, vectors[:, 8:].reshape(4, D), jnp.zeros((4, D), f32)], axis=0)
    own = lax.dynamic_slice_in_dim(params[:2], place * width, width, 1)
    query = own[0].reshape(lay.heads, HEAD_DIM)
    query = jnp.concatenate([query, jnp.zeros_like(query)], axis=1).reshape(-1)
    row = jnp.concatenate([query, own[1], jnp.zeros(weights.shape[1] - 3 * width, f32)])
    return weights, jnp.broadcast_to(row[None], (8, row.shape[0])), params


def reduce_heads(grads, vec, depth, width):
    total = lax.psum_scatter(grads, "dp", scatter_dimension=0, tiled=True).astype(f32)
    pairs = total[:, : 2 * width].reshape(depth, -1, 2, HEAD_DIM)
    small = lax.psum_scatter(vec, "dp", scatter_dimension=0, tiled=False)
    small = jnp.pad(small, ((0, 4), (0, LANES - depth)))
    return (
        pairs[:, :, 0].reshape(depth, width),
        pairs[:, :, 1].reshape(depth, width),
        total[:, 2 * width : 3 * width],
        small,
    )


def solution(mesh):
    placed = (
        P("dp", None),
        P("dp", None),
        P("dp", "mp"),
        P("dp", "mp"),
        P("dp", "mp"),
        P("mp", "dp"),
        P("dp", "mp"),
        P("mp", "dp"),
        P(None, "dp"),
        P(None, "dp"),
        P(None, "dp"),
        P("dp"),
        P(),
        P("dp"),
        P("mp", "dp"),
    )
    return jax.shard_map(
        on_device,
        mesh=mesh,
        in_specs=placed,
        out_specs=(
            P("dp", None),
            P("dp", None),
            P("dp", "mp"),
            P("dp", "mp"),
            P("dp", "mp"),
            P("mp", "dp"),
            P("dp", "mp"),
            P("mp", "dp"),
            P(None, "dp"),
            P(None, "dp"),
            P(None, "dp"),
            P("dp"),
        ),
        check_vma=False,
    )
```

```python
from functools import partial
import math

import jax
import jax.numpy as jnp
from jax import lax
from jax.experimental import pallas as pl
from jax.experimental.pallas import tpu as pltpu
from jax.sharding import PartitionSpec as P

D = 768
HEAD_DIM = 64
FF = 3072
CLUSTER = 128
LANES = 128
EPSILON = 1e-05
MASKED = -1e30
SCALE = 1.0 / math.sqrt(HEAD_DIM)

bf16 = jnp.bfloat16
f32 = jnp.float32
i32 = jnp.int32

VMEM = 60 * 1024 * 1024


def cost(us):
    return pl.CostEstimate(flops=int(1e9 * us), bytes_accessed=int(3e6 * us), transcendentals=0)


QUICK = cost(0.001)
ATTEND_US = 46
COLLECT_US = 30
COLLECT_ROWS = 512
SPREAD_US = 3
HEAD_GRADS_US = 4
SORT_US = 80
ATTEND_BACK_US = 40


def nn(a, b):
    return lax.dot_general(a, b, (((1,), (0,)), ((), ())), preferred_element_type=f32)


def nt(a, b):
    return lax.dot_general(a, b, (((1,), (1,)), ((), ())), preferred_element_type=f32)


def tn(a, b):
    return lax.dot_general(a, b, (((0,), (0,)), ((), ())), preferred_element_type=f32)


def lane_iota(rows, lanes=LANES):
    return lax.broadcasted_iota(i32, (rows, lanes), 1)


def sublane_iota(rows, lanes=LANES):
    return lax.broadcasted_iota(i32, (rows, lanes), 0)


def as_column(row):
    parts = [
        jnp.broadcast_to(row[:, i * LANES : (i + 1) * LANES], (LANES, LANES)).T
        for i in range(row.shape[1] // LANES)
    ]
    return parts[0] if len(parts) == 1 else jnp.concatenate(parts, axis=0)


def loop(count):
    def run(step):
        def body(i, carry):
            step(i)
            return carry

        lax.fori_loop(0, count, body, 0)

    return run


class Layout:
    def __init__(self, peers, tokens, heads):
        self.peers, self.tokens, self.heads = peers, tokens, heads
        self.stripe = min(16, peers)
        self.runs = peers // self.stripe
        self.per_dev = CLUSTER // self.stripe
        self.rows_peer = tokens // peers
        self.half_rows = self.rows_peer // 2
        self.pairs = self.half_rows // self.per_dev
        self.packed = tokens // 2
        self.clusters = peers * tokens // CLUSTER
        self.data_rows = 9 * self.half_rows
        self.direct = self.half_rows == LANES
        self.arrays = peers if self.direct else 1

    def peer(self, me, s):
        return (me ^ s) if self.direct else s

    def shapes(self, rows, dtype=bf16):
        lead = () if self.direct else (self.peers,)
        return [jax.ShapeDtypeStruct(lead + (rows, LANES), dtype)] * self.arrays

    def specs(self, rows, at):
        if self.direct:
            return [pl.BlockSpec((rows, LANES), lambda *g: (at(*g), 0))] * self.arrays
        return [pl.BlockSpec((self.peers, rows, LANES), lambda *g: (0, at(*g), 0))]

    def view(self, refs, s):
        return refs[s] if self.direct else refs[0].at[s]


def only(at):
    return lambda *g: at


def place_kernel(lay, perm_ref, code_ref):
    groups = lay.clusters
    shift = CLUSTER.bit_length() - 1
    blocks = lay.tokens // LANES
    before = sublane_iota(LANES, 2 * LANES)
    after = lane_iota(LANES, 2 * LANES)
    ahead_of = jnp.where((before < after) | (after >= LANES), 1.0, 0.0).astype(bf16)

    def members(h, b):
        row = lax.shift_right_logical(perm_ref[h : h + 1, b * LANES : (b + 1) * LANES], shift)
        return jnp.broadcast_to(row, (groups, LANES)) == sublane_iota(groups)

    for h in range(lay.heads):
        if lay.runs == 1:
            carry = (sublane_iota(groups) * lay.per_dev).astype(f32)
        else:
            counts = jnp.zeros((groups, LANES), f32)
            for b in range(blocks):
                member = jnp.where(members(h, b), 1.0, 0.0).astype(bf16)
                counts = counts + nn(member, ahead_of)[:, LANES:]
            lower = jnp.where(
                sublane_iota(groups, groups) > lane_iota(groups, groups), 1.0, 0.0
            ).astype(bf16)
            carry = nn(lower, counts.astype(bf16))
        for b in range(blocks):
            member = members(h, b)
            found = nn(jnp.where(member, 1.0, 0.0).astype(bf16), ahead_of)
            rank = jnp.sum(jnp.where(member, found[:, :LANES] + carry, 0.0), axis=0, keepdims=True)
            carry = carry + found[:, LANES:]
            rank = rank.astype(i32)
            peer = lax.shift_right_logical(rank, lay.rows_peer.bit_length() - 1)
            rest = rank & (lay.rows_peer - 1)
            half = lax.shift_right_logical(rest, lay.half_rows.bit_length() - 1)
            packed = peer * lay.half_rows + (rest & (lay.half_rows - 1))
            at = slice(b * LANES, (b + 1) * LANES)
            code_ref[h, 0:1, at] = packed
            code_ref[h, 1:2, at] = half


def place_tokens(lay, perm):
    return pl.pallas_call(
        partial(place_kernel, lay),
        out_shape=jax.ShapeDtypeStruct((lay.heads, 8, lay.tokens), i32),
        name="place_tokens",
        cost_estimate=QUICK,
    )(perm)


def one_hot(equal):
    return jnp.where(equal, 1.0, 0.0).astype(bf16)


def scatter_matrix(lay, me, packed, s, blocks):
    rows = blocks * lay.half_rows
    if lay.direct:
        parts = [
            one_hot(
                jnp.broadcast_to(packed, (lay.half_rows, lay.tokens))
                == sublane_iota(lay.half_rows, lay.tokens) + lay.peer(me, s + i) * lay.half_rows
            )
            for i in range(blocks)
        ]
        return jnp.concatenate(parts, axis=0)
    wanted = sublane_iota(rows, lay.tokens) + s * lay.half_rows
    return one_hot(jnp.broadcast_to(packed, (rows, lay.tokens)) == wanted)


def gather_matrix(lay, me, column):
    lane = lane_iota(column.shape[0])
    parts = [
        one_hot(column == lane + lay.peer(me, k) * LANES) for k in range(lay.packed // LANES)
    ]
    return jnp.concatenate(parts, axis=1)


def block_rows(lay, refs, first):
    at = slice(first, first + lay.half_rows)
    if lay.direct:
        return jnp.concatenate([refs[s][at, :] for s in range(lay.peers)], axis=0)
    return refs[0][:, at, :].astype(f32).reshape(lay.packed, LANES).astype(bf16)


def put_blocks(lay, refs, s, blocks, first, rows):
    at = slice(first, first + lay.half_rows) if isinstance(first, int) else pl.ds(first, lay.half_rows)
    if lay.direct:
        for i in range(blocks):
            refs[s + i][at, :] = rows[i * LANES : (i + 1) * LANES].astype(bf16)
    else:
        rows = rows.astype(f32).reshape(blocks, lay.half_rows, LANES).astype(bf16)
        refs[0][s : s + blocks, at, :] = rows


ROWS = 512
COUNT = 4


def project_kernel(lay, steps, place_ref, x_ref, w_ref, bias_ref, code_ref, pad_ref, *rest):
    outs = rest[: lay.arrays]
    rows_ref, flag_ref = rest[lay.arrays :]
    step = pl.program_id(0)
    me = place_ref[0]
    width = 4 * LANES

    @pl.when(step < steps)
    def _():
        at = pl.ds(pl.multiple_of(step * ROWS, ROWS), ROWS)
        values = nn(x_ref[...], w_ref[...]) + bias_ref[0:1, :]
        low = lane_iota(ROWS) < HEAD_DIM
        lane_half = jnp.where(low, 0, 1)
        live = as_column(pad_ref[0:1, at])
        tiles = [values[:, i * LANES : (i + 1) * LANES] for i in range(values.shape[1] // LANES)]
        turned = [pltpu.roll(tile, HEAD_DIM, 1) for tile in tiles]
        for h in range(lay.heads):
            half = as_column(code_ref[h, 1:2, at])
            keep = half == lane_half
            v, side = lay.heads + h // 2, h % 2
            planes = (
                jnp.where(low, tiles[h], turned[h]),
                jnp.where(low, turned[h], tiles[h]),
                jnp.where(low, tiles[v], turned[v]) if side == 0 else jnp.where(low, turned[v], tiles[v]),
            )
            for x, plane in enumerate(planes):
                rows_ref[h, at, x * LANES : (x + 1) * LANES] = jnp.where(keep, plane, 0.0).astype(bf16)
            flags = jnp.where((lane_iota(ROWS) == half) & (live == 1), 1.0, 0.0)
            rows_ref[h, at, 3 * LANES :] = flags.astype(bf16)

    count = COUNT if lay.direct else 32

    @pl.when(step >= steps)
    def _():
        h = step - steps
        for s in range(0, lay.peers, count):
            chosen = scatter_matrix(lay, me, code_ref[h, 0:1, :], s, count)
            moved = nn(chosen, rows_ref[h])
            for x in range(3):
                first = pl.multiple_of((h * 3 + x) * lay.half_rows, 16)
                put_blocks(lay, outs, s, count, first, moved[:, x * LANES : (x + 1) * LANES])
            for i in range(count * lay.half_rows // LANES):
                at = slice(s * lay.half_rows + i * LANES, s * lay.half_rows + (i + 1) * LANES)
                flag_ref[h, :, at] = moved[i * LANES : (i + 1) * LANES, 3 * LANES :].T[:8]

    @pl.when(step == steps + lay.heads - 1)
    def _():
        for s in range(lay.peers):
            at = slice(s * lay.half_rows, (s + 1) * lay.half_rows)
            rows = [flag_ref[k, 0:2, at] for k in range(lay.heads)]
            block = jnp.concatenate(rows + [jnp.zeros((16 - 2 * lay.heads, lay.half_rows), f32)], axis=0)
            if lay.half_rows < LANES:
                block = jnp.concatenate(
                    [block, jnp.zeros((16, LANES - lay.half_rows), f32)], axis=1
                )
            lay.view(outs, s)[lay.data_rows : lay.data_rows + 16, :] = block.astype(bf16)


def project_rows(lay, places, x, weights, bias, code, pad):
    width = weights.shape[1]
    steps = lay.tokens // ROWS
    spec = pltpu.PrefetchScalarGridSpec(
        num_scalar_prefetch=1,
        grid=(steps + lay.heads,),
        in_specs=[
            pl.BlockSpec((ROWS, D), lambda s, _: (jnp.minimum(s, steps - 1), 0)),
            pl.BlockSpec((D, width), lambda s, _: (0, 0)),
            pl.BlockSpec((8, width), lambda s, _: (0, 0)),
            pl.BlockSpec((lay.heads, 8, lay.tokens), lambda s, _: (0, 0, 0)),
            pl.BlockSpec((1, lay.tokens), lambda s, _: (0, 0)),
        ],
        out_specs=lay.specs(lay.data_rows + 16, only(0)),
        scratch_shapes=[
            pltpu.VMEM((lay.heads, lay.tokens, 4 * LANES), bf16),
            pltpu.VMEM((lay.heads, 8, lay.packed), f32),
        ],
    )
    return pl.pallas_call(
        partial(project_kernel, lay, steps),
        grid_spec=spec,
        out_shape=lay.shapes(lay.data_rows + 16),
        compiler_params=pltpu.CompilerParams(vmem_limit_bytes=VMEM),
        name="project_rows",
        cost_estimate=QUICK,
    )(places, x, weights, bias, code, pad)


def pair_rows(lay, refs, first, run, p):
    at = slice(first + p * lay.per_dev, first + (p + 1) * lay.per_dev)
    if lay.direct:
        return jnp.concatenate([refs[s][at, :] for s in range(lay.stripe)], axis=0)
    block = refs[0][run * lay.stripe : (run + 1) * lay.stripe, first : first + lay.half_rows, :]
    block = block.astype(f32)[:, p * lay.per_dev : (p + 1) * lay.per_dev, :]
    return block.reshape(CLUSTER, LANES).astype(bf16)


def put_pair(lay, refs, first, run, p, rows):
    at = slice(first + p * lay.per_dev, first + (p + 1) * lay.per_dev)
    for s in range(lay.stripe):
        part = rows[s * lay.per_dev : (s + 1) * lay.per_dev]
        lay.view(refs, run * lay.stripe + s)[at, :] = part.astype(bf16)


def live_columns(lay, flags, h):
    pick = one_hot(sublane_iota(16, 2 * LANES) == 2 * h + lane_iota(16, 2 * LANES) // LANES)
    return [tn(lay.view(flags, s)[...], pick) for s in range(lay.peers)]


def allowed_pair(lay, columns, run, p):
    at = slice(p * lay.per_dev, (p + 1) * lay.per_dev)
    live = jnp.concatenate([columns[run * lay.stripe + s][at] for s in range(lay.stripe)], axis=0)
    live = jnp.concatenate([live[:, :LANES], live[:, LANES:]], axis=0)
    same = sublane_iota(2 * CLUSTER) % CLUSTER == lane_iota(2 * CLUSTER)
    return (live > 0.5) | same


def stack_halves(rows):
    low = lane_iota(rows.shape[0], rows.shape[1]) < HEAD_DIM
    zero = jnp.zeros_like(rows)
    return jnp.concatenate([jnp.where(low, rows, zero), jnp.where(low, zero, rows)], axis=0)


def each_half(fold, rows):
    one, two = (
        jnp.broadcast_to(fold(part, axis=0, keepdims=True), part.shape)
        for part in (rows[:CLUSTER], rows[CLUSTER:])
    )
    return jnp.concatenate([one, two], axis=0)


def inverse_sum(rows, axis, keepdims):
    return 1.0 / jnp.sum(rows, axis=axis, keepdims=keepdims)


def soft_weights(queries, keys, allowed):
    scores = jnp.where(allowed, nt(keys, queries) * SCALE, MASKED)
    grown = jnp.exp(scores - each_half(jnp.max, scores))
    return grown * each_half(inverse_sum, grown)


def attend_kernel(lay, *refs):
    rows, flags, outs = (refs[i * lay.arrays : (i + 1) * lay.arrays] for i in range(3))
    live = live_columns(lay, flags, pl.program_id(0))
    for run in range(lay.runs):
        for p in range(lay.pairs):
            q, k, v = (pair_rows(lay, rows, x * lay.half_rows, run, p) for x in range(3))
            soft = soft_weights(q, stack_halves(k), allowed_pair(lay, live, run, p))
            put_pair(lay, outs, 0, run, p, tn(soft.astype(bf16), stack_halves(v)))


def attend(lay, arrived):
    head = lambda h: h
    return pl.pallas_call(
        partial(attend_kernel, lay),
        grid=(lay.heads,),
        in_specs=lay.specs(3 * lay.half_rows, head) + lay.specs(16, only(lay.data_rows // 16)),
        out_specs=lay.specs(lay.half_rows, head),
        out_shape=lay.shapes(lay.heads * lay.half_rows),
        name="attend",
        cost_estimate=cost(ATTEND_US),
    )(*arrived, *arrived)


def attend_back_kernel(lay, *refs):
    rows, flags, grads, outs = (refs[i * lay.arrays : (i + 1) * lay.arrays] for i in range(4))
    sum_ref = refs[-1]
    live = live_columns(lay, flags, pl.program_id(0))
    low = lane_iota(CLUSTER) < HEAD_DIM
    sums = [jnp.zeros((1, LANES), f32)] * 2
    for run in range(lay.runs):
        for p in range(lay.pairs):
            q, k, v = (pair_rows(lay, rows, x * lay.half_rows, run, p) for x in range(3))
            g = pair_rows(lay, grads, 0, run, p)
            keys = stack_halves(k)
            soft = soft_weights(q, keys, allowed_pair(lay, live, run, p))
            grad_soft = nt(stack_halves(v), g)
            delta = each_half(jnp.sum, soft * grad_soft)
            grad = (soft * (grad_soft - delta)).astype(bf16)
            grad_q = (tn(grad, keys) * SCALE).astype(bf16)
            part = nn(grad, q)
            grad_k = (jnp.where(low, part[:CLUSTER], part[CLUSTER:]) * SCALE).astype(bf16)
            part = nn(soft.astype(bf16), g)
            grad_v = jnp.where(low, part[:CLUSTER], part[CLUSTER:]).astype(bf16)
            for x, part in enumerate((grad_q, grad_k, grad_v)):
                put_pair(lay, outs, x * lay.half_rows, run, p, part)
            sums[0] = sums[0] + jnp.sum(grad_q.astype(f32), axis=0, keepdims=True)
            sums[1] = sums[1] + jnp.sum(grad_v.astype(f32), axis=0, keepdims=True)
    sum_ref[0] = jnp.concatenate(sums + [jnp.zeros((6, LANES), f32)], axis=0)


def attend_back(lay, arrived, grads):
    head = lambda h: h
    three = lay.specs(3 * lay.half_rows, head)
    out = pl.pallas_call(
        partial(attend_back_kernel, lay),
        grid=(lay.heads,),
        in_specs=three
        + lay.specs(16, only(lay.data_rows // 16))
        + lay.specs(lay.half_rows, head),
        out_specs=three + [pl.BlockSpec((1, 8, LANES), lambda h: (h, 0, 0))],
        out_shape=lay.shapes(lay.data_rows)
        + [jax.ShapeDtypeStruct((lay.heads, 8, LANES), f32)],
        name="attend_back",
        cost_estimate=cost(ATTEND_BACK_US),
    )(*arrived, *arrived, *grads)
    return list(out[:-1]), out[-1]


def side_rows(quarter, side):
    return pl.ds(pl.multiple_of(quarter * 512 + side * 256, 256), 256)


def unsort_kernel(lay, place_ref, *refs):
    rows_refs, code_ref, outs = refs[: lay.arrays], refs[lay.arrays], refs[lay.arrays + 1 :]
    rows = block_rows(lay, rows_refs, 0)
    low = lane_iota(256) < HEAD_DIM
    me, place = place_ref[0], place_ref[1]

    for t in range(4):
        sides = []
        for side in range(2):
            at = side_rows(place ^ t, side)
            column = as_column(code_ref[0, 0:1, at])
            half = as_column(code_ref[0, 1:2, at])
            found = nn(gather_matrix(lay, me, column), rows)
            sides.append(jnp.where(half == side, found, pltpu.roll(found, HEAD_DIM, 1)))
        outs[t][...] = jnp.where(low, sides[0], sides[1]).astype(bf16)


def unsort_rows(lay, places, returned, code):
    spec = pltpu.PrefetchScalarGridSpec(
        num_scalar_prefetch=1,
        grid=(lay.heads,),
        in_specs=lay.specs(lay.half_rows, lambda h, _: h)
        + [pl.BlockSpec((1, 8, lay.tokens), lambda h, _: (h, 0, 0))],
        out_specs=[pl.BlockSpec((256, LANES), lambda h, _: (0, h))] * 4,
    )
    return pl.pallas_call(
        partial(unsort_kernel, lay),
        grid_spec=spec,
        out_shape=[jax.ShapeDtypeStruct((256, lay.heads * LANES), bf16)] * 4,
        name="unsort_rows",
        cost_estimate=QUICK,
    )(places, *returned, code)


def sort_kernel(lay, place_ref, *refs):
    grads, code_ref, outs, rows_ref = refs[:4], refs[4], refs[5:-1], refs[-1]
    low = lane_iota(256) < HEAD_DIM
    lane_half = jnp.where(low, 0, 1)
    me, place = place_ref[0], place_ref[1]

    for t in range(4):
        block = grads[t][...].astype(f32)
        turned = pltpu.roll(block, HEAD_DIM, 1)
        for side in range(2):
            at = side_rows(place ^ t, side)
            half = as_column(code_ref[0, 1:2, at])
            both = jnp.where(low, block, turned) if side == 0 else jnp.where(low, turned, block)
            rows_ref[at, :] = jnp.where(half == lane_half, both, 0.0).astype(bf16)

    count = 4 if lay.direct else 32
    for s in range(0, lay.peers, count):
        chosen = scatter_matrix(lay, me, code_ref[0, 0:1, :], s, count)
        put_blocks(lay, outs, s, count, 0, nn(chosen, rows_ref[...]))


def sort_rows(lay, places, grads, code):
    spec = pltpu.PrefetchScalarGridSpec(
        num_scalar_prefetch=1,
        grid=(lay.heads,),
        in_specs=[pl.BlockSpec((256, LANES), lambda h, _: (0, h))] * 4
        + [pl.BlockSpec((1, 8, lay.tokens), lambda h, _: (h, 0, 0))],
        out_specs=lay.specs(lay.half_rows, lambda h, _: h),
        scratch_shapes=[pltpu.VMEM((lay.tokens, LANES), bf16)],
    )
    return pl.pallas_call(
        partial(sort_kernel, lay),
        grid_spec=spec,
        out_shape=lay.shapes(lay.heads * lay.half_rows),
        name="sort_rows",
        cost_estimate=cost(SORT_US),
    )(places, *grads, code)


def pack_kernel(
    query_ref, key_ref, value_ref, output_ref, inner_ref, outer_ref,
    bias_ref, gain_ref, shift_ref, inner_bias_ref, piece_ref, shard_ref,
):
    depth, width = query_ref.shape
    heads = width // HEAD_DIM
    query, key, value = (ref[...].astype(f32) for ref in (query_ref, key_ref, value_ref))
    cut = [slice(h * HEAD_DIM, (h + 1) * HEAD_DIM) for h in range(heads)]
    columns = [part for at in cut for part in (query[:, at], key[:, at])] + [value]
    have = 3 * width
    fill = -have % LANES
    if fill:
        columns.append(jnp.zeros((depth, fill), f32))
    columns = jnp.concatenate(columns, axis=1).astype(bf16)
    piece_ref[:depth, : have + fill] = columns
    inner_bias = inner_bias_ref[...].astype(f32).reshape(1, -1)
    vectors = jnp.concatenate(
        [ref[...].astype(f32) for ref in (bias_ref, gain_ref, shift_ref)]
        + [inner_bias[:, i * depth : (i + 1) * depth] for i in range(4)]
        + [jnp.zeros((4, depth), f32)],
        axis=0,
    )
    if depth < LANES:
        vectors = jnp.concatenate([vectors, jnp.zeros((16, LANES - depth), f32)], axis=1)
    piece_ref[:16, have + fill :] = vectors.astype(bf16)
    shard_ref[:, :D] = inner_ref[...]
    turned = output_ref[...].astype(f32).T
    shard_ref[:, D : 2 * D] = outer_ref[...]
    fill = -width % (2 * LANES)
    if fill:
        turned = jnp.concatenate([turned, jnp.zeros((depth, fill), f32)], axis=1)
    shard_ref[:, 2 * D :] = turned.astype(bf16)


def pack_weights(*arrays):
    depth, width = arrays[0].shape
    columns = -(-3 * width // LANES) * LANES
    return pl.pallas_call(
        pack_kernel,
        out_shape=[
            jax.ShapeDtypeStruct((max(depth, 16), columns + LANES), bf16),
            jax.ShapeDtypeStruct((depth, 2 * D + width + -width % (2 * LANES)), bf16),
        ],
        name="pack_weights",
        cost_estimate=QUICK,
    )(*arrays)


def assemble_kernel(lay, place_ref, *refs):
    pieces, (weight_ref, bias_ref, par_ref, part_ref) = refs[: lay.peers], refs[lay.peers :]
    me, place = place_ref[0], place_ref[1]
    depth = D // lay.peers
    for s in range(lay.peers):
        d = me ^ s
        at = pl.ds(pl.multiple_of(d * depth, 16), depth)
        columns = weight_ref.shape[1]
        weight_ref[at, :] = pieces[s][:, :columns]
        part_ref[d] = pieces[s][:16, columns:].astype(f32)

    def whole(row, rows=1, peers=range(lay.peers)):
        return jnp.concatenate(
            [part_ref[d, row + i : row + i + 1, :depth] for d in peers for i in range(rows)], axis=1
        )

    vectors = [whole(r) for r in range(8)]
    each = lay.peers // 4
    vectors += [whole(8, 4, range(j * each, (j + 1) * each)) for j in range(4)]
    par_ref[...] = jnp.concatenate(vectors + [jnp.zeros((4, D), f32)], axis=0)
    width = lay.heads * HEAD_DIM

    def own(vector):
        out = vector[:, :width]
        for p in range(1, D // width):
            out = jnp.where(place == p, vector[:, p * width : (p + 1) * width], out)
        return out

    query = own(vectors[0])
    zero = jnp.zeros((1, HEAD_DIM), f32)
    columns = [
        part for h in range(lay.heads) for part in (query[:, h * HEAD_DIM : (h + 1) * HEAD_DIM], zero)
    ] + [own(vectors[1])]
    fill = bias_ref.shape[1] - 3 * width
    if fill:
        columns.append(jnp.zeros((1, fill), f32))
    bias_ref[...] = jnp.broadcast_to(jnp.concatenate(columns, axis=1), bias_ref.shape)


def assemble_weights(lay, places, pieces):
    columns = pieces[0].shape[1] - LANES
    vmem = pl.BlockSpec(memory_space=pltpu.VMEM)
    return pl.pallas_call(
        partial(assemble_kernel, lay),
        in_specs=[pl.BlockSpec(memory_space=pltpu.SMEM)] + [vmem] * lay.peers,
        out_specs=[vmem] * 3,
        out_shape=[
            jax.ShapeDtypeStruct((D, columns), bf16),
            jax.ShapeDtypeStruct((8, columns), f32),
            jax.ShapeDtypeStruct((16, D), f32),
        ],
        scratch_shapes=[pltpu.VMEM((lay.peers, 16, LANES), f32)],
        name="assemble_weights",
        cost_estimate=QUICK,
    )(places, *pieces)


def mean_rows(v):
    return jnp.sum(v, axis=1, keepdims=True) * (1.0 / D)


def norm_forward(rows):
    centred = rows - mean_rows(rows)
    inv = lax.rsqrt(mean_rows(centred * centred) + EPSILON)
    return centred * inv, inv


def norm_backward(scaled, normed, inv):
    return inv * (scaled - mean_rows(scaled) - normed * mean_rows(scaled * normed))


TALL = 512


def middle_kernel(
    place_ref,
    att0,
    att1,
    att2,
    att3,
    hidden_ref,
    cot_ref,
    par_ref,
    w0,
    w1,
    w2,
    w3,
    out_ref,
    act_ref,
    pre_ref,
    low_ref,
    ffn_grad_ref,
    branch_grad_ref,
    h1_ref,
    grad0,
    grad1,
    grad2,
    grad3,
    vec_ref,
    first_ref,
    normed_ref,
    inv_ref,
    slope_ref,
    sum_ref,
    h2_ref,
    weight_ref,
    double_ref,
    sems,
):
    step = pl.program_id(0)
    place = place_ref[1]

    def fetch(t, part):
        at = (pl.ds(2 * D, weight_ref.shape[2] - 2 * D), pl.ds(0, 2 * D))[part]
        source = (w0, w1, w2, w3)[t]
        return pltpu.make_async_copy(source.at[:, at], weight_ref.at[t, :, at], sems.at[part, t])

    for t in range(4):

        @pl.when(step == t + 1)
        def _():
            fetch(t, 1).wait()

    @pl.when(step == 0)
    def _():
        for t in range(4):
            fetch(t, 0).start()
        for t in range(4):
            fetch(t, 1).start()
        for t in range(4):
            fetch(t, 0).wait()

        @loop(4)
        def _(t):
            low = lane_iota(D) < HEAD_DIM
            for k in range(double_ref.shape[2] // LANES):
                tile = weight_ref[t, :, 2 * D + k // 2 * LANES : 2 * D + (k // 2 + 1) * LANES]
                tile = tile.astype(f32)
                turned = pltpu.roll(tile, HEAD_DIM, 1)
                both = jnp.where(low, tile, turned) if k % 2 == 0 else jnp.where(low, turned, tile)
                double_ref[t, :, k * LANES : (k + 1) * LANES] = both.astype(bf16)

        vec_ref[...] = jnp.zeros_like(vec_ref)

        @loop(2)
        def _(side):
            branch = jnp.zeros((256, D), f32)
            for t, att_ref in enumerate((att0, att1, att2, att3)):
                att = att_ref[...]
                lane = lane_iota(256, att.shape[1]) % LANES
                own = (lane >= HEAD_DIM).astype(i32) == side
                branch = branch + nt(jnp.where(own, att, jnp.zeros_like(att)), double_ref[t])
            at = pl.ds(pl.multiple_of(side * 256, 256), 256)
            rows = hidden_ref[at, :].astype(f32) + (branch + par_ref[2:3, :])
            normed, inv = norm_forward(rows)
            first = normed * par_ref[4:5, :] + par_ref[6:7, :]
            first_ref[at, :] = first
            normed_ref[at, :] = normed
            inv_ref[at, :] = jnp.broadcast_to(inv, (256, LANES))
            low_ref[at, :] = first.astype(bf16)

        sum_ref[...] = jnp.zeros_like(sum_ref)

    @pl.when((step >= 1) & (step <= 4))
    def _():
        j = step - 1

        @loop(512 // TALL)
        def _(side):
            at = pl.ds(pl.multiple_of(side * TALL, TALL), TALL)
            pre = nn(low_ref[at, :], weight_ref[j, :, :D]) + par_ref[pl.ds(8 + (place ^ j), 1), :]
            cdf = 0.5 * (1.0 + lax.erf(pre * (1.0 / math.sqrt(2.0))))
            slope_ref[j, at, :] = cdf + pre * jnp.exp(-0.5 * pre * pre) * (1.0 / math.sqrt(2.0 * math.pi))
            act = (pre * cdf).astype(bf16)
            act_ref[at, :] = act
            sum_ref[at, :] += nt(act, weight_ref[j, :, D : 2 * D])

    @pl.when(step == 4)
    def _():

        @loop(4)
        def _(side):
            at = pl.ds(pl.multiple_of(side * 128, 128), 128)
            rows = first_ref[at, :] + (sum_ref[at, :] + par_ref[3:4, :])
            normed, inv = norm_forward(rows)
            out_ref[at, :] = (normed * par_ref[5:6, :] + par_ref[7:8, :]).astype(bf16)
            cot = cot_ref[at, :].astype(f32)
            grad = norm_backward(cot * par_ref[5:6, :], normed, inv)
            grad_low = grad.astype(bf16)
            h2_ref[at, :] = grad
            ffn_grad_ref[at, :] = grad_low
            vec_ref[3:4, :] += jnp.sum(grad_low.astype(f32), axis=0, keepdims=True)
            vec_ref[5:6, :] += jnp.sum(cot * normed, axis=0, keepdims=True)
            vec_ref[7:8, :] += jnp.sum(cot, axis=0, keepdims=True)

        sum_ref[...] = jnp.zeros_like(sum_ref)

    @pl.when(step >= 5)
    def _():
        j = 8 - step
        vec_ref[pl.ds(8 + (place ^ j), 1), :] = jnp.zeros((1, D), f32)

        @loop(512 // TALL)
        def _(side):
            at = pl.ds(pl.multiple_of(side * TALL, TALL), TALL)
            grad_act = nn(ffn_grad_ref[at, :], weight_ref[j, :, D : 2 * D])
            grad_pre = (grad_act * slope_ref[j, at, :]).astype(bf16)
            pre_ref[at, :] = grad_pre
            vec_ref[pl.ds(8 + (place ^ j), 1), :] += jnp.sum(grad_pre.astype(f32), axis=0, keepdims=True)
            sum_ref[at, :] += nt(grad_pre, weight_ref[j, :, :D])

    @pl.when(step == 8)
    def _():

        @loop(4)
        def _(side):
            at = pl.ds(pl.multiple_of(side * 128, 128), 128)
            grad_first = h2_ref[at, :] + sum_ref[at, :]
            normed = normed_ref[at, :]
            grad = norm_backward(grad_first * par_ref[4:5, :], normed, inv_ref[at, 0:1])
            grad_low = grad.astype(bf16)
            h1_ref[at, :] = grad
            branch_grad_ref[at, :] = grad_low
            vec_ref[2:3, :] += jnp.sum(grad_low.astype(f32), axis=0, keepdims=True)
            vec_ref[4:5, :] += jnp.sum(grad_first * normed, axis=0, keepdims=True)
            vec_ref[6:7, :] += jnp.sum(grad_first, axis=0, keepdims=True)

        for t, grad_ref in enumerate((grad0, grad1, grad2, grad3)):
            both = nn(branch_grad_ref[...], double_ref[t])
            lane = lane_iota(256, both.shape[1]) % LANES
            grad_ref[...] = jnp.where(lane < HEAD_DIM, both[:256], both[256:]).astype(bf16)


def middle(places, att, hidden, cotangent, params, weights):
    width = att[0].shape[1]
    rows = 512

    def up(s, q):
        return (0, jnp.clip(s - 1, 0, 3))

    def down(s, q):
        return (0, jnp.clip(8 - s, 0, 3))

    def whole(rank):
        return lambda s, q: (0,) * rank

    square = pl.BlockSpec((rows, D), whole(2))
    exchanged = pl.BlockSpec((256, width), whole(2))
    spec = pltpu.PrefetchScalarGridSpec(
        num_scalar_prefetch=1,
        grid=(9,),
        in_specs=[exchanged] * 4
        + [
            pl.BlockSpec((rows, D), lambda s, q: (q[1], 0)),
            pl.BlockSpec((rows, D), lambda s, q: (q[1], 0)),
            pl.BlockSpec((16, D), whole(2)),
        ]
        + [pl.BlockSpec(memory_space=pl.ANY)] * 4,
        out_specs=[
            square,
            pl.BlockSpec((rows, D), up),
            pl.BlockSpec((rows, D), down),
            square,
            square,
            square,
            square,
        ]
        + [exchanged] * 4
        + [pl.BlockSpec((16, D), whole(2))],
        scratch_shapes=[
            pltpu.VMEM((rows, D), f32),
            pltpu.VMEM((rows, D), f32),
            pltpu.VMEM((rows, LANES), f32),
            pltpu.VMEM((4, rows, D), f32),
            pltpu.VMEM((rows, D), f32),
            pltpu.VMEM((rows, D), f32),
            pltpu.VMEM((4,) + weights[0].shape, bf16),
            pltpu.VMEM((4, D, width), bf16),
            pltpu.SemaphoreType.DMA((2, 4)),
        ],
    )
    out = pl.pallas_call(
        middle_kernel,
        grid_spec=spec,
        out_shape=[
            jax.ShapeDtypeStruct((rows, D), bf16),
            jax.ShapeDtypeStruct((rows, FF), bf16),
            jax.ShapeDtypeStruct((rows, FF), bf16),
            jax.ShapeDtypeStruct((rows, D), bf16),
            jax.ShapeDtypeStruct((rows, D), bf16),
            jax.ShapeDtypeStruct((rows, D), bf16),
            jax.ShapeDtypeStruct((rows, D), f32),
        ]
        + [jax.ShapeDtypeStruct((256, width), bf16)] * 4
        + [jax.ShapeDtypeStruct((16, D), f32)],
        compiler_params=pltpu.CompilerParams(vmem_limit_bytes=VMEM),
        name="middle",
        cost_estimate=QUICK,
    )(places, *att, hidden, cotangent, params, *weights)
    return out[:7], out[7:11], out[11]


def weight_grad_kernel(chunks, adds, place_ref, act_ref, pre_ref, low_ref, ffn_ref, branch_ref, *refs):
    att_refs, add_refs, out_ref = refs[:chunks], refs[chunks : chunks + adds], refs[-1]

    def put(at, part):
        for ref in add_refs:
            part = part + ref[:, at].astype(f32)
        out_ref[:, at] = part.astype(bf16)

    put(slice(0, D), tn(low_ref[...], pre_ref[...]))
    put(slice(D, 2 * D), tn(ffn_ref[...], act_ref[...]))
    for i in range(chunks):

        @pl.when(pl.program_id(0) == i)
        def _():
            att = att_refs[i][...]
            low = lane_iota(256, att.shape[1]) % LANES < HEAD_DIM
            zero = jnp.zeros_like(att)
            both = jnp.concatenate([jnp.where(low, att, zero), jnp.where(low, zero, att)], axis=0)
            part = tn(branch_ref[...], both)
            planes = [part[:, k * LANES : (k + 1) * LANES] for k in range(part.shape[1] // LANES)]
            planes = [plane + pltpu.roll(plane, HEAD_DIM, 1) for plane in planes]
            if len(planes) % 2:
                planes.append(jnp.zeros_like(planes[0]))
            first = lane_iota(part.shape[0]) < HEAD_DIM
            for k in range(0, len(planes), 2):
                at = slice(2 * D + k // 2 * LANES, 2 * D + (k // 2 + 1) * LANES)
                put(at, jnp.where(first, planes[k], planes[k + 1]))


def weight_grads(places, saved, att, first, chunks, adds):
    act, pre, low, ffn_grad, branch_grad = saved
    rows = act.shape[0]
    width = att[0].shape[1]
    total = 2 * D + -(-width // (2 * LANES)) * LANES
    cut = D // 2

    def chunk(s, i, q):
        return (0, first - 2 * s)

    part = pl.BlockSpec((rows, cut), lambda s, i, q: (0, i))
    spec = pltpu.PrefetchScalarGridSpec(
        num_scalar_prefetch=1,
        grid=(chunks, 2),
        in_specs=[pl.BlockSpec((rows, D), chunk)] * 2
        + [part] * 3
        + [pl.BlockSpec((256, width), lambda s, i, q: (0, 0))] * chunks
        + [pl.BlockSpec((cut, total), lambda s, i, q, k=k: (2 * k + i, 0)) for _, k in adds],
        out_specs=pl.BlockSpec((cut, total), lambda s, i, q: (2 * s + i, 0)),
    )
    return pl.pallas_call(
        partial(weight_grad_kernel, chunks, len(adds)),
        grid_spec=spec,
        out_shape=jax.ShapeDtypeStruct((chunks * D, total), bf16),
        compiler_params=pltpu.CompilerParams(vmem_limit_bytes=VMEM),
        name="weight_grads",
        cost_estimate=QUICK,
    )(
        places, act, pre, low, ffn_grad, branch_grad,
        *[att[first - 2 * s] for s in range(chunks)], *[a for a, _ in adds],
    )


def collect_kernel(lay, place_ref, *refs):
    rows_refs = refs[: lay.arrays]
    code_ref, dense_ref = refs[lay.arrays :]
    me = place_ref[0]
    tokens = dense_ref.shape[0]
    low = lane_iota(tokens) < HEAD_DIM
    firsts, seconds = [], []
    for h in range(lay.heads):
        column = as_column(code_ref[h, 0:1, :])
        half = as_column(code_ref[h, 1:2, :])
        planes = [block_rows(lay, rows_refs, (h * 3 + x) * lay.half_rows) for x in range(3)]
        found = nn(gather_matrix(lay, me, column), jnp.concatenate(planes, axis=1))
        one, two = [], []
        for x in range(3):
            part = found[:, x * LANES : (x + 1) * LANES]
            turned = pltpu.roll(part, HEAD_DIM, 1)
            one.append(jnp.where(half == 0, part, turned))
            two.append(jnp.where(half == 1, part, turned))
        firsts.append(one)
        seconds.append(two)
    tiles = [jnp.where(low, firsts[h][0], seconds[h][1]) for h in range(lay.heads)]
    for h in range(0, lay.heads, 2):
        right = seconds[h + 1][2] if h + 1 < lay.heads else jnp.zeros((tokens, LANES), f32)
        tiles.append(jnp.where(low, firsts[h][2], right))
    dense_ref[...] = jnp.concatenate(tiles, axis=1).astype(bf16)


def collect(lay, places, returned, code, width):
    tokens = COLLECT_ROWS
    spec = pltpu.PrefetchScalarGridSpec(
        num_scalar_prefetch=1,
        grid=(lay.tokens // tokens,),
        in_specs=lay.specs(lay.data_rows, only(0))
        + [pl.BlockSpec((lay.heads, 8, tokens), lambda c, q: (0, 0, c))],
        out_specs=pl.BlockSpec((tokens, width), lambda c, q: (c, 0)),
    )
    return pl.pallas_call(
        partial(collect_kernel, lay),
        grid_spec=spec,
        out_shape=jax.ShapeDtypeStruct((lay.tokens, width), bf16),
        compiler_params=pltpu.CompilerParams(vmem_limit_bytes=VMEM),
        name="collect",
        cost_estimate=cost(COLLECT_US),
    )(places, *returned, code)


def half_rows_at(g, s, place):
    core = place % 2
    return jnp.where(s == 0, 1 - core, core) * 2 + g


def spread_kernel(g, place_ref, dense_ref, w_ref, h1_ref, other_ref, mine_ref):
    step, place = pl.program_id(0), place_ref[1]
    own = (half_rows_at(g, step, place) == place).astype(f32)
    part = nt(dense_ref[...], w_ref[...]) + own * h1_ref[...]

    @pl.when(step == 0)
    def _():
        other_ref[...] = part.astype(bf16)

    @pl.when(step == 1)
    def _():
        mine_ref[...] = part.astype(bf16)


def spread_grads(g, places, dense, weights, grad_h1):
    width = weights.shape[1]
    whole = lambda s, q: (0, 0)
    spec = pltpu.PrefetchScalarGridSpec(
        num_scalar_prefetch=1,
        grid=(2,),
        in_specs=[
            pl.BlockSpec((512, width), lambda s, q: (half_rows_at(g, s, q[1]), 0)),
            pl.BlockSpec((D, width), whole),
            pl.BlockSpec((512, D), whole),
        ],
        out_specs=[pl.BlockSpec((512, D), whole)] * 2,
    )
    return pl.pallas_call(
        partial(spread_kernel, g),
        grid_spec=spec,
        out_shape=[jax.ShapeDtypeStruct((512, D), bf16)] * 2,
        compiler_params=pltpu.CompilerParams(vmem_limit_bytes=VMEM),
        name="spread_grads",
        cost_estimate=cost(SPREAD_US),
    )(places, dense, weights, grad_h1)


def head_grad_kernel(lay, place_ref, x_ref, dense_ref, vec_ref, *refs):
    out_ref, total_ref = refs
    step = pl.program_id(0)

    @pl.when(step == 0)
    def _():
        total_ref[...] = tn(x_ref[...], dense_ref[...])

    @pl.when(step > 0)
    def _():
        total_ref[...] += tn(x_ref[...], dense_ref[...])

    @pl.when(step == 3)
    def _():
        depth = D // lay.peers
        if not lay.direct:
            out_ref[...] = total_ref[...].astype(bf16)
            return
        for d in range(lay.peers):
            out_ref[d, :depth, :] = total_ref[d * depth : (d + 1) * depth, :].astype(bf16)
            vector = vec_ref[d]
            high = vector.astype(bf16).astype(f32)
            width = total_ref.shape[1]
            out_ref[d, depth:, :] = jnp.concatenate(
                [high, vector - high, jnp.zeros((16, width - 2 * LANES), f32)], axis=1
            ).astype(bf16)


def head_grads(lay, places, x, dense, vec):
    width = dense.shape[1]
    depth = D // lay.peers
    shape = (lay.peers, depth + 16, width) if lay.direct else (D, width)
    spec = pltpu.PrefetchScalarGridSpec(
        num_scalar_prefetch=1,
        grid=(4,),
        in_specs=[
            pl.BlockSpec((512, D), lambda s, q: (s, 0)),
            pl.BlockSpec((512, width), lambda s, q: (s, 0)),
            pl.BlockSpec(vec.shape, lambda s, q: (0, 0, 0)),
        ],
        out_specs=pl.BlockSpec(shape, lambda s, q: (0,) * len(shape)),
        scratch_shapes=[pltpu.VMEM((D, width), f32)],
    )
    return pl.pallas_call(
        partial(head_grad_kernel, lay),
        grid_spec=spec,
        out_shape=jax.ShapeDtypeStruct(shape, bf16),
        compiler_params=pltpu.CompilerParams(vmem_limit_bytes=VMEM),
        name="head_grads",
        cost_estimate=cost(HEAD_GRADS_US),
    )(places, x, dense, vec)


def finish_heads_kernel(*refs):
    parts, outs = refs[0], refs[1:]
    depth, width = outs[0].shape
    heads = width // HEAD_DIM
    total = parts[0].astype(f32)
    for d in range(1, parts.shape[0]):
        total = total + parts[d].astype(f32)
    grads = total[:depth]
    cut = [slice(h * LANES, h * LANES + HEAD_DIM) for h in range(heads)]
    outs[0][...] = jnp.concatenate([grads[:, at] for at in cut], axis=1)
    cut = [slice(h * LANES + HEAD_DIM, (h + 1) * LANES) for h in range(heads)]
    outs[1][...] = jnp.concatenate([grads[:, at] for at in cut], axis=1)
    outs[2][...] = grads[:, 2 * width : 3 * width]
    outs[3][...] = total[depth:, :LANES] + total[depth:, LANES : 2 * LANES]


def finish_heads(parts, depth, width):
    shapes = [(depth, width)] * 3 + [(16, LANES)]
    return pl.pallas_call(
        finish_heads_kernel,
        out_shape=[jax.ShapeDtypeStruct(s, f32) for s in shapes],
        name="finish_heads",
        cost_estimate=QUICK,
    )(parts)


def finish_vectors_kernel(depth, own_ref, other_ref, bias_ref, gain_ref, shift_ref, inner_ref):
    total = (own_ref[...] + other_ref[...])[:, :depth]
    bias_ref[...] = total[:4]
    gain_ref[...] = total[4:6]
    shift_ref[...] = total[6:8]
    inner_ref[...] = total[8:12]


def finish_vectors(own, other, depth):
    return pl.pallas_call(
        partial(finish_vectors_kernel, depth),
        out_shape=[jax.ShapeDtypeStruct((n, depth), f32) for n in (4, 2, 2, 4)],
        name="finish_vectors",
        cost_estimate=QUICK,
    )(own, other)


def finish_middle_kernel(grad_ref, inner_ref, outer_ref, output_ref):
    inner_ref[...] = grad_ref[:, :D].astype(f32)
    outer_ref[...] = grad_ref[:, D : 2 * D].astype(f32)
    rest = grad_ref[:, 2 * D :].astype(f32)
    output_ref[...] = rest[:, : output_ref.shape[0]].T


def finish_middle(grads, width):
    depth = grads.shape[0]
    return pl.pallas_call(
        finish_middle_kernel,
        out_shape=[
            jax.ShapeDtypeStruct((depth, D), f32),
            jax.ShapeDtypeStruct((depth, D), f32),
            jax.ShapeDtypeStruct((width, depth), f32),
        ],
        name="finish_middle",
        cost_estimate=QUICK,
    )(grads)


def order_kernel(place_ref, *refs):
    parts, out_ref, rows_ref, sems = refs[:4], refs[4], refs[5], refs[6]
    rows = rows_ref.shape[1]

    def take(i):
        return pltpu.make_async_copy(parts[i], rows_ref.at[i], sems.at[0, i])

    def put(i):
        at = pl.ds(pl.multiple_of(place_ref[i] * rows, rows), rows)
        return pltpu.make_async_copy(rows_ref.at[i], out_ref.at[at, :], sems.at[1, i])

    for i in range(4):
        take(i).start()
    for i in range(4):
        take(i).wait()
        put(i).start()
    for i in range(4):
        put(i).wait()


def order_quarters(order, quarters):
    rows, width = quarters[0].shape
    dtype = quarters[0].dtype
    return pl.pallas_call(
        order_kernel,
        in_specs=[pl.BlockSpec(memory_space=pltpu.SMEM)]
        + [pl.BlockSpec(memory_space=pl.ANY)] * 4,
        out_specs=pl.BlockSpec(memory_space=pl.ANY),
        out_shape=jax.ShapeDtypeStruct((4 * rows, width), dtype),
        scratch_shapes=[pltpu.VMEM((4, rows, width), dtype), pltpu.SemaphoreType.DMA((2, 4))],
        name="order_quarters",
        cost_estimate=QUICK,
    )(order, *quarters)


def over_rows(lay, blocks, near_first=False):
    if not lay.direct:
        return [lax.all_to_all(blocks[0], "dp", split_axis=0, concat_axis=0, tiled=True)]
    out = [blocks[0]]
    for s in range(1, lay.peers):
        rows = blocks[s]
        if near_first and s >= lay.peers - 2:
            rows = after(rows, out[s - lay.peers + 3])
        out.append(lax.ppermute(rows, "dp", [(i, i ^ s) for i in range(lay.peers)]))
    return out


def in_hbm(rows):
    return pltpu.with_memory_space_constraint(rows, pltpu.HBM)


def share_pieces(lay, piece):
    def flip(rows, s):
        return lax.ppermute(rows, "dp", [(i, i ^ s) for i in range(lay.peers)])

    half = lay.peers // 2
    far = flip(piece, half)
    near = [piece] + [flip(piece, s) for s in range(1, half)]
    return near + [far] + [flip(far, s) for s in range(1, half)]


def after(value, *others):
    return lax.optimization_barrier((value, *others))[0]


def swap(rows, flip):
    return lax.ppermute(rows, "mp", [(i, i ^ flip) for i in range(4)])


def over_heads(blocks):
    return [blocks[0]] + [swap(blocks[t], t) for t in range(1, 4)]


def on_device(
    hidden_in,
    cotangent,
    w_query,
    w_key,
    w_value,
    w_output,
    w_inner,
    w_outer,
    biases,
    gains,
    shifts,
    inner_bias,
    lengths,
    padding,
    cluster_perm,
):
    peers = lax.axis_size("dp")
    tokens = hidden_in.shape[0]
    heads = cluster_perm.shape[0]
    lay = Layout(peers, tokens, heads)
    place = lax.axis_index("mp")
    me = lax.axis_index("dp")
    places = jnp.stack([me, place]).astype(i32)
    hidden_in = in_hbm(hidden_in)
    depth = w_query.shape[0]
    width = heads * HEAD_DIM

    piece, shard = pack_weights(
        w_query, w_key, w_value, w_output, w_inner, w_outer.T,
        biases, gains, shifts, inner_bias,
    )
    own_w = lax.all_gather(shard, "dp", axis=0, tiled=True)
    far_w = swap(own_w, 2)
    if lay.direct:
        weights, bias, params = assemble_weights(lay, places, share_pieces(lay, piece))
    else:
        weights, bias, params = gather_weights(lay, place, piece)

    weights = in_hbm(weights)
    code = in_hbm(place_tokens(lay, cluster_perm))
    sent = project_rows(lay, places, hidden_in, weights, bias, code, padding.reshape(1, tokens))
    arrived = over_rows(lay, sent, near_first=True)
    mixed = over_rows(lay, attend(lay, arrived))
    found = unsort_rows(lay, places, mixed, code)
    att = over_heads(found)
    far_w = after(far_w, found[0])
    middle_w = [own_w, in_hbm(swap(own_w, 1)), far_w, in_hbm(swap(far_w, 1))]
    saved, att_grad, vec = middle(places, att, hidden_in, cotangent, params, middle_w)
    out_quarter, act, pre_grad, first_low, ffn_grad, branch_grad, grad_h1 = saved
    saved = tuple(in_hbm(a) for a in (act, pre_grad, first_low, ffn_grad, branch_grad))
    att = [in_hbm(a) for a in att]

    got = over_heads(att_grad)
    from_core = swap(weight_grads(places, saved, att, 3, 2, []), 1)
    grads = sort_rows(lay, places, got, code)
    ready = (after(act, grads[0]),) + saved[1:]
    from_far = swap(weight_grads(places, ready, att, 2, 1, [(from_core, 0)]), 2)
    grads = over_rows(lay, grads)
    slot_grads, bias_sums = attend_back(lay, arrived, grads)

    returned = over_rows(lay, slot_grads)
    ready = (after(act, *returned[1:4]),) + saved[1:]
    summed = weight_grads(places, ready, att, 0, 1, [(from_core, 1), (from_far, 0)])
    head_sums = bias_sums[:, :2].reshape(heads, 2, 2, HEAD_DIM).sum(axis=2)
    head_sums = head_sums.transpose(1, 0, 2).reshape(2, width)
    vec = lax.dynamic_update_slice(vec[:12], head_sums, (0, place * width))
    vec = jnp.concatenate(
        [vec[:8].reshape(8, peers, depth).transpose(1, 0, 2), vec[8:].reshape(peers, 4, depth)],
        axis=1,
    )
    spread = jnp.pad(vec, ((0, 0), (0, 4), (0, (-depth) % LANES)))
    reduced = lax.psum_scatter(after(summed, *returned), "dp", scatter_dimension=0, tiled=True)
    far = swap(after(out_quarter, summed), 2)
    dense = collect(lay, places, returned, code, weights.shape[1])
    terms = head_grads(lay, places, hidden_in, dense, spread)
    dense = after(dense, terms, far)
    groups = [spread_grads(g, places, dense, weights, grad_h1) for g in range(2)]
    chips = [
        (mine.astype(f32) + swap(other, 1).astype(f32)).astype(bf16) for other, mine in groups
    ]
    others = [swap(chip, 2) for chip in chips]
    hidden_out = order_quarters(
        jnp.stack([place, place ^ 2, place ^ 1, place ^ 3]).astype(i32),
        [out_quarter, far, swap(out_quarter, 1), swap(far, 1)],
    )
    if lay.direct:
        terms = lax.all_to_all(terms, "dp", split_axis=0, concat_axis=0, tiled=True)
        ends = finish_heads(terms, depth, width)
    else:
        ends = reduce_heads(terms, vec, depth, width)
    small = ends[3] + swap(ends[3], 1)
    chips[1] = after(chips[1], small, hidden_out)
    small = finish_vectors(small, swap(small, 2), depth)
    ready = [
        (chip.astype(f32) + part.astype(f32)).astype(bf16) for chip, part in zip(chips, others)
    ]
    core = place % 2
    order = jnp.stack([2 * core, 2 * core + 1, 2 - 2 * core, 3 - 2 * core]).astype(i32)
    grad_hidden = order_quarters(
        after(order, small[0]),
        ready + [swap(part, 1) for part in ready],
    )

    grad_inner, grad_outer, grad_output = finish_middle(reduced, width)
    return (
        hidden_out,
        grad_hidden,
        ends[0],
        ends[1],
        ends[2],
        grad_output,
        grad_inner,
        grad_outer.T,
        small[0],
        small[1],
        small[2],
        small[3].reshape(-1),
    )


def gather_weights(lay, place, piece):
    depth = D // lay.peers
    width = lay.heads * HEAD_DIM
    got = lax.all_gather(piece, "dp", axis=0, tiled=False)
    columns = piece.shape[1] - LANES
    weights = got[:, :depth, :columns].reshape(D, columns)
    vectors = got[:, :12, columns : columns + depth].astype(f32)
    params = vectors[:, :8].transpose(1, 0, 2).reshape(8, D)
    params = jnp.concatenate([params, vectors[:, 8:].reshape(4, D), jnp.zeros((4, D), f32)], axis=0)
    own = lax.dynamic_slice_in_dim(params[:2], place * width, width, 1)
    query = own[0].reshape(lay.heads, HEAD_DIM)
    query = jnp.concatenate([query, jnp.zeros_like(query)], axis=1).reshape(-1)
    row = jnp.concatenate([query, own[1], jnp.zeros(weights.shape[1] - 3 * width, f32)])
    return weights, jnp.broadcast_to(row[None], (8, row.shape[0])), params


def reduce_heads(grads, vec, depth, width):
    total = lax.psum_scatter(grads, "dp", scatter_dimension=0, tiled=True).astype(f32)
    pairs = total[:, : 2 * width].reshape(depth, -1, 2, HEAD_DIM)
    small = lax.psum_scatter(vec, "dp", scatter_dimension=0, tiled=False)
    small = jnp.pad(small, ((0, 4), (0, LANES - depth)))
    return (
        pairs[:, :, 0].reshape(depth, width),
        pairs[:, :, 1].reshape(depth, width),
        total[:, 2 * width : 3 * width],
        small,
    )


def solution(mesh):
    placed = (
        P("dp", None),
        P("dp", None),
        P("dp", "mp"),
        P("dp", "mp"),
        P("dp", "mp"),
        P("mp", "dp"),
        P("dp", "mp"),
        P("mp", "dp"),
        P(None, "dp"),
        P(None, "dp"),
        P(None, "dp"),
        P("dp"),
        P(),
        P("dp"),
        P("mp", "dp"),
    )
    return jax.shard_map(
        on_device,
        mesh=mesh,
        in_specs=placed,
        out_specs=(
            P("dp", None),
            P("dp", None),
            P("dp", "mp"),
            P("dp", "mp"),
            P("dp", "mp"),
            P("mp", "dp"),
            P("dp", "mp"),
            P("mp", "dp"),
            P(None, "dp"),
            P(None, "dp"),
            P(None, "dp"),
            P("dp"),
        ),
        check_vma=False,
    )
```
